32 devices in a mesh: dp: 8 (over z, y), hg: 2 (over x), hid: 2 (over core).
Axes of the slice: x: 2, y: 2, z: 4, core: 2. Of those that a mesh axis runs over, the one named last changes fastest.
Arguments:
- tokens: bfloat16 [18816, 768], P(('dp', 'hid')), may hold values from -6 to 6
- big_images: int32 [16], P(('dp', 'hid')), may hold values from 0 to 1, as said below
- norm_gain: bfloat16 [768], replicated, may hold values from 0.5 to 1.5
- w_qkv: bfloat16 [768, 2304], P(None, 'hg'), may hold values from -0.21875 to 0.21875
- qk_gains: bfloat16 [2, 64], replicated, may hold values from 0.099609375 to 1.8984375
- w_out_t: bfloat16 [768, 768], P(None, 'hg'), may hold values from -0.625 to 0.625
- w_in: bfloat16 [768, 3072], P(None, ('hg', 'hid')), may hold values from -0.21875 to 0.21875
- w_back: bfloat16 [768, 3072], P(None, ('hg', 'hid')), may hold values from -0.109375 to 0.109375
- cotangent: bfloat16 [18816, 768], P(('dp', 'hid'), 'hg'), may hold values from -6 to 6
Outputs:
- output: bfloat16 [18816, 768], P(('dp', 'hid'), 'hg')
- token_grad: bfloat16 [18816, 768], P(('dp', 'hid'))
- norm_gain_grad: float32 [768], P(('dp', 'hid'))
- w_qkv_grad: float32 [768, 2304], P(('dp', 'hid'), 'hg')
- qk_gains_grad: float32 [2, 64], replicated
- w_out_t_grad: float32 [768, 768], P(('dp', 'hid'), 'hg')
- w_in_grad: float32 [768, 3072], P('dp', ('hg', 'hid'))
- w_back_grad: float32 [768, 3072], P('dp', ('hg', 'hid'))
The draws below stay inside these ranges and needn't reach their ends.
Inputs may be any that keep to these rules, and one draw needn't show every extreme that they name: `big_images`: 1 where the 1176 tokens of a group form one image, 0 where they form 6 images of 196 tokens each in order; every draw has groups of both kinds.
All inputs are finite; a program needn't handle non-finite values.
Results may differ from the reference program's by a relative error of at most 0.012.
Values may be sent and summed in bfloat16 or wider, within the bound.
No kernel may reach another device: no remote copies, remote signals or barrier semaphores. Data moves between devices by JAX's collectives and lax.ppermute only.
A program may use at most 256 MiB of HBM per device.

```python
import jax
import jax.numpy as jnp
from jax import lax

D = 768
H = 12
HD = 64
FF = 3072
PATCHES = 196
TOK_DEV = 1176
GROUPS = 16
TOKENS = 18816


def draw_big_images(key, part):
    base = jax.random.randint(key, (GROUPS,), 0, 8)
    flags = (base == 0).astype(jnp.int32)
    order = jax.random.permutation(jax.random.fold_in(key, 7), GROUPS)
    flags = flags.at[order[0]].set(1)
    flags = flags.at[order[1]].set(0)
    return flags


def raised(values, key, source, target, blocks, factor):
    def block_of(position):
        return (jnp.arange(values.shape[position]) // (values.shape[position] // blocks)).reshape((-1,) + (1,) * (values.ndim - 1 - position))

    first = jax.random.permutation(key, blocks)[block_of(target)]
    other_side = (block_of(target) + blocks // 2) % blocks
    return jnp.where((block_of(source) == first) | (block_of(source) == other_side), factor * values, values)


def block_scale(rng, dims, split, low, high):
    level, own = 1.0, jax.random.fold_in(rng, 6)
    for dim, shards_of in split:
        heights = jnp.exp(jax.random.uniform(jax.random.fold_in(own, dim), (shards_of,), jnp.float32, low / len(split), high / len(split)))
        level = level * jnp.repeat(heights, dims[dim] // shards_of).reshape([-1 if axis == dim else 1 for axis in range(len(dims))])
    return level


def gaussian(own_key, shape, width, bound, cuts=(), kind=jnp.bfloat16):
    array = jax.random.normal(own_key, shape, jnp.float32) * width
    if len(cuts) > 0:
        array = block_scale(own_key, shape, cuts, -0.22, 0.18) * array
    return jnp.clip(array, min=-bound, max=bound).astype(kind)


def bell_draw_with(key, shape, width, bound, split, heavy, dtype=jnp.bfloat16):
    values = width * jax.random.normal(key, shape, jnp.float32)
    if split:
        values = values * block_scale(key, shape, split, -0.22, 0.18)
    return jnp.clip(raised(values, jax.random.fold_in(key, 3), *heavy), -bound, bound).astype(dtype)


def setup_inputs(seed: int = 0) -> dict:
    seeds = jax.random.split(jax.random.key(seed), 10)
    tokens = bell_draw_with(seeds[0], (TOKENS, D), 1.0, 6.0, ((0, 16),), (0, 1, 16, 2.0))
    big_images = draw_big_images(jax.random.fold_in(seeds[9], 71), 0)
    norm_gain = jnp.clip(1.0 + 0.1 * jax.random.normal(seeds[2], (D,), jnp.float32), 0.5, 1.5).astype(jnp.bfloat16)
    w_qkv = gaussian(seeds[3], (D, 3 * D), D ** -0.5, 0.21875, ((1, 2),))
    qk_gains = jnp.clip(1.0 + 0.18 * jax.random.normal(seeds[4], (2, HD), jnp.float32), 0.099609375, 1.8984375).astype(jnp.bfloat16)
    w_out_t = gaussian(seeds[5], (D, D), (D // 8) ** -0.5, 0.625, ((1, 2),))
    w_in = gaussian(seeds[6], (D, FF), D ** -0.5, 0.21875, ((1, 4),))
    w_back = gaussian(seeds[7], (D, FF), FF ** -0.5, 0.109375, ((1, 4),))
    cotangent = bell_draw_with(seeds[8], (TOKENS, D), 1.0, 6.0, ((0, 16), (1, 2)), (0, 1, 16, 2.0))
    return dict(tokens=tokens, big_images=big_images, norm_gain=norm_gain, w_qkv=w_qkv, qk_gains=qk_gains, w_out_t=w_out_t, w_in=w_in, w_back=w_back, cotangent=cotangent)


@jax.custom_vjp
def low(v):
    return lax.optimization_barrier(v.astype(jnp.bfloat16)).astype(jnp.float32)

@jax.custom_vjp
def low_back(v):
    return v

def low_keep(v):
    return (low(v), None)

def low_pass(kept, grad):
    return (grad,)

def back_keep(v):
    return (v, None)

def back_low(kept, grad):
    return (low(grad),)
low.defvjp(low_keep, low_pass)
low_back.defvjp(back_keep, back_low)
EPSILON = 1e-06
HIGHEST = lax.Precision.HIGHEST

def normalize(values):
    centred = values - lax.optimization_barrier(jnp.mean(values, axis=-1, keepdims=True))
    return centred * lax.rsqrt(lax.optimization_barrier(jnp.mean(centred * centred, axis=-1, keepdims=True)) + EPSILON)

def group_forward(inputs, big_flag, norm_gain, w_qkv, qk_gains, w_out_t, w_in, w_back):
    normed = low(normalize(inputs) * norm_gain)
    joined = low_back(jnp.dot(normed, w_qkv, precision=HIGHEST)).reshape(TOK_DEV, H, 3, HD)
    queries = low(normalize(joined[:, :, 0]) * qk_gains[0] * HD ** (-0.5))
    keys_all = low(normalize(joined[:, :, 1]) * qk_gains[1])
    values_all = low(joined[:, :, 2])
    scores = low_back(jnp.einsum('qhe,khe->hqk', queries, keys_all, precision=HIGHEST))
    image_of = jnp.arange(TOK_DEV) // PATCHES
    same_image = (image_of[:, None] == image_of[None, :]) | (big_flag > 0)
    scores = jnp.where(same_image[None], scores, -1e+30)
    weights = low(jax.nn.softmax(scores, axis=-1))
    attended = jnp.einsum('hqk,khe->qhe', weights, values_all, precision=HIGHEST)
    attended = low(low_back(attended)).reshape(TOK_DEV, D)
    branch_attn = jnp.dot(attended, w_out_t.T, precision=HIGHEST)
    hidden_pre = low_back(jnp.dot(normed, w_in, precision=HIGHEST))
    hidden_act = low(jax.nn.gelu(hidden_pre))
    branch_mlp = jnp.dot(hidden_act, w_back.T, precision=HIGHEST)
    return inputs + branch_attn + branch_mlp

def reference(tokens, big_images, norm_gain, w_qkv, qk_gains, w_out_t, w_in, w_back, cotangent):
    params = tuple((weight_arg.astype(jnp.float32) for weight_arg in (norm_gain, w_qkv, qk_gains, w_out_t, w_in, w_back)))
    inputs = tokens.astype(jnp.float32).reshape(GROUPS, TOK_DEV, D)
    cot_groups = cotangent.astype(jnp.float32).reshape(GROUPS, TOK_DEV, D)

    def forward(inputs, params):
        stepper = jax.checkpoint(group_forward)
        return lax.map(lambda grouped: stepper(grouped[0], grouped[1], *params), (inputs, big_images))
    result, pullback = jax.vjp(forward, inputs, params)
    token_grad, param_grads = pullback(cot_groups)
    return (result.reshape(TOKENS, D).astype(jnp.bfloat16), token_grad.reshape(TOKENS, D).astype(jnp.bfloat16), param_grads[0], param_grads[1], param_grads[2], param_grads[3], param_grads[4], param_grads[5])
```

```python
import jax
import jax.numpy as jnp
from jax import lax
from jax.sharding import PartitionSpec as P

PATCHES = 196


EPSILON = 1e-06


def normalize(values):
    centred = values - jnp.mean(values, axis=-1, keepdims=True)
    inverse = lax.rsqrt(jnp.mean(centred * centred, axis=-1, keepdims=True) + EPSILON)
    return (centred * inverse, inverse)


def normalize_back(upstream, normed, inverse):
    inner = jnp.mean(upstream * normed, axis=-1, keepdims=True)
    return inverse * (upstream - jnp.mean(upstream, axis=-1, keepdims=True) - normed * inner)


def times_t(left, right):
    return lax.dot_general(
        left, right, (((1,), (1,)), ((), ())), preferred_element_type=jnp.float32
    )


def rows_t(left, right):
    return lax.dot_general(
        left, right, (((0,), (0,)), ((), ())), preferred_element_type=jnp.float32
    )


def masked_scores(queries, keys_in, allowed):
    scores = jnp.einsum("gqe,gke->gqk", queries, keys_in, preferred_element_type=jnp.float32)
    return jnp.where(allowed, scores, -1e30)


def head_forward(queries, keys_in, values_in, allowed):
    scores = masked_scores(queries, keys_in, allowed)
    highest = jnp.max(scores, axis=-1, keepdims=True)
    expo_scores = jnp.exp(scores - highest)
    totals = jnp.sum(expo_scores, axis=-1, keepdims=True)
    weights = (expo_scores / totals).astype(jnp.bfloat16)
    attended = jnp.einsum("gqk,gke->gqe", weights, values_in, preferred_element_type=jnp.float32)
    return (attended, (highest + jnp.log(totals))[..., 0])


def head_back(queries, keys_in, values_in, log_total, grad_out, allowed):
    scores = masked_scores(queries, keys_in, allowed)
    probs = jnp.exp(scores - log_total[..., None])
    grad_probs = jnp.einsum("gqe,gke->gqk", grad_out, values_in, preferred_element_type=jnp.float32)
    inner = jnp.sum(grad_probs * probs, axis=-1, keepdims=True)
    grad_scores = (probs * (grad_probs - inner)).astype(jnp.bfloat16)
    grad_values = jnp.einsum(
        "gqk,gqe->gke", probs.astype(jnp.bfloat16), grad_out, preferred_element_type=jnp.float32
    )
    grad_queries = jnp.einsum(
        "gqk,gke->gqe", grad_scores, keys_in, preferred_element_type=jnp.float32
    )
    grad_keys = jnp.einsum("gqk,gqe->gke", grad_scores, queries, preferred_element_type=jnp.float32)
    return (grad_queries, grad_keys, grad_values)


def attention_pass(step_fn, arrays, big_flag):
    heads_here = arrays[0].shape[0]
    tok_rows = arrays[0].shape[1]
    image_of = jnp.arange(tok_rows) // PATCHES
    allowed = (image_of[:, None] == image_of[None, :]) | (big_flag > 0)
    run_allowed = allowed[None]
    shaped = tuple(
        (member.reshape((heads_here, 1, tok_rows // 1) + member.shape[2:]) for member in arrays)
    )
    results = lax.map(lambda blocks: step_fn(*blocks, run_allowed), shaped)
    return tuple((member.reshape((heads_here, tok_rows) + member.shape[3:]) for member in results))


def swap(value, axis, bit):
    size = lax.axis_size(axis)
    return lax.ppermute(value, axis, [(place, place ^ bit) for place in range(size)])


def bits_of(axis):
    size = lax.axis_size(axis)
    return [1 << place for place in range(size.bit_length() - 1)]


def gather_columns(block, axis):
    for bit in bits_of(axis):
        block = jnp.concatenate([block, swap(block, axis, bit)], axis=1)
    return block


def scatter_columns(grad, axis):
    for bit in reversed(bits_of(axis)):
        half = grad.shape[1] // 2
        sent = swap(grad[:, half:].astype(jnp.bfloat16), axis, bit)
        grad = grad[:, :half] + sent.astype(jnp.float32)
    return grad


def scatter_rows(grad, axes):
    levels = []
    for axis in axes:
        levels += [(axis, bit) for bit in reversed(bits_of(axis))]
    rows, columns = grad.shape
    blocks = rows >> len(levels)
    shaped = grad.reshape((2,) * len(levels) + (blocks, columns))
    for axis, bit in reversed(levels):
        place = len(shaped.shape) - 3
        mine = (lax.axis_index(axis) & bit) > 0
        low, high = (lax.index_in_dim(shaped, side, place, keepdims=False) for side in (0, 1))
        sent = jnp.where(mine, low, high).astype(jnp.bfloat16)
        shaped = jnp.where(mine, high, low) + swap(sent, axis, bit).astype(jnp.float32)
    return shaped


def sum_everywhere(value, axes):
    for axis in axes:
        for bit in bits_of(axis):
            value = value + swap(value, axis, bit)
    return value


def both_halves(mine, axis):
    other = swap(mine, axis, 1)
    first = lax.axis_index(axis) == 0
    return jnp.concatenate(
        [jnp.where(first, mine, other), jnp.where(first, other, mine)], axis=1
    )


def shards(tokens, big_images, norm_gain, w_qkv, qk_gains, w_out_t, w_in, w_back, cotangent):
    tok_rows, width = tokens.shape
    head_size = qk_gains.shape[1]
    heads_here = w_qkv.shape[1] // (3 * head_size)
    half_width = heads_here * head_size
    big_flag = big_images[0]
    head_scale = head_size ** (-0.5)
    grad_out = both_halves(cotangent, "hg")
    w_in = gather_columns(w_in, "hid")
    w_back = gather_columns(w_back, "hid")
    inputs = tokens.astype(jnp.float32)
    normed, inverse = normalize(inputs)
    gain_vec = norm_gain.astype(jnp.float32)
    normed_low = (normed * gain_vec).astype(jnp.bfloat16)
    joined = jnp.dot(normed_low, w_qkv, preferred_element_type=jnp.float32).reshape(
        tok_rows, heads_here, 3, head_size
    )
    q_hat, q_inverse = normalize(joined[:, :, 0])
    k_hat, k_inverse = normalize(joined[:, :, 1])
    q_gain = qk_gains[0].astype(jnp.float32)
    k_gain = qk_gains[1].astype(jnp.float32)
    queries = (q_hat * q_gain * head_scale).astype(jnp.bfloat16).transpose(1, 0, 2)
    keys_in = (k_hat * k_gain).astype(jnp.bfloat16).transpose(1, 0, 2)
    values_in = joined[:, :, 2].astype(jnp.bfloat16).transpose(1, 0, 2)
    attended, log_total = attention_pass(head_forward, (queries, keys_in, values_in), big_flag)
    attended_low = attended.astype(jnp.bfloat16).transpose(1, 0, 2).reshape(tok_rows, half_width)
    hidden_pre = jnp.dot(normed_low, w_in, preferred_element_type=jnp.float32)
    hidden_act = jax.nn.gelu(hidden_pre).astype(jnp.bfloat16)
    mixed = times_t(attended_low, w_out_t) + times_t(hidden_act, w_back)
    out_cols = width // lax.axis_size("hg")
    place = lax.axis_index("hg") * out_cols
    sent = lax.dynamic_slice_in_dim(mixed, out_cols - place, out_cols, 1).astype(jnp.bfloat16)
    kept = lax.dynamic_slice_in_dim(mixed + inputs, place, out_cols, 1)
    output = (kept + swap(sent, "hg", 1).astype(jnp.float32)).astype(jnp.bfloat16)

    grad_act = jnp.dot(grad_out, w_back, preferred_element_type=jnp.float32)
    grad_up = jax.vjp(jax.nn.gelu, hidden_pre)[1](grad_act)[0].astype(jnp.bfloat16)
    grad_w_back = scatter_columns(rows_t(grad_out, hidden_act), "hid")
    grad_w_in = scatter_columns(rows_t(normed_low, grad_up), "hid")
    w_in_grad = scatter_rows(grad_w_in, ("dp",))
    w_back_grad = scatter_rows(grad_w_back, ("dp",))
    w_out_t_grad = scatter_rows(rows_t(grad_out, attended_low), ("dp", "hid"))

    grad_attended = jnp.dot(grad_out, w_out_t, preferred_element_type=jnp.float32)
    grad_att_low = (
        grad_attended.astype(jnp.bfloat16)
        .reshape(tok_rows, heads_here, head_size)
        .transpose(1, 0, 2)
    )
    grad_queries, grad_keys, grad_values = attention_pass(
        head_back, (queries, keys_in, values_in, log_total, grad_att_low), big_flag
    )
    grad_query = grad_queries.transpose(1, 0, 2) * head_scale
    grad_key = grad_keys.transpose(1, 0, 2)
    qk_partial = jnp.stack(
        [jnp.sum(grad_query * q_hat, axis=(0, 1)), jnp.sum(grad_key * k_hat, axis=(0, 1))]
    )
    grad_q_raw = normalize_back(grad_query * q_gain, q_hat, q_inverse)
    grad_k_raw = normalize_back(grad_key * k_gain, k_hat, k_inverse)
    grad_joined = jnp.stack([grad_q_raw, grad_k_raw, grad_values.transpose(1, 0, 2)], axis=2)
    grad_joined = grad_joined.reshape(tok_rows, 3 * half_width).astype(jnp.bfloat16)
    grad_normed = times_t(grad_joined, w_qkv) + times_t(grad_up, w_in)
    normed_sent = grad_normed.astype(jnp.bfloat16)
    w_qkv_grad = scatter_rows(rows_t(normed_low, grad_joined), ("dp", "hid"))
    gain_partial = jnp.sum(grad_normed * normed, axis=0)
    small = sum_everywhere(
        jnp.concatenate([gain_partial, qk_partial.reshape(-1)]), ("hid", "hg", "dp")
    )
    shard_count = lax.axis_size("dp") * lax.axis_size("hid")
    own = lax.axis_index("dp") * lax.axis_size("hid") + lax.axis_index("hid")
    gain_rows = width // shard_count
    norm_gain_grad = lax.dynamic_slice_in_dim(small, own * gain_rows, gain_rows, 0)
    qk_gains_grad = small[width:].reshape(2, head_size)
    grad_normed = normed_sent.astype(jnp.float32) + swap(normed_sent, "hg", 1).astype(jnp.float32)
    token_grad = (
        normalize_back(grad_normed * gain_vec, normed, inverse) + grad_out.astype(jnp.float32)
    ).astype(jnp.bfloat16)
    return (
        output,
        token_grad,
        norm_gain_grad,
        w_qkv_grad,
        qk_gains_grad,
        w_out_t_grad,
        w_in_grad,
        w_back_grad,
    )


def solution(mesh):
    return jax.shard_map(
        shards,
        mesh=mesh,
        in_specs=(
            P(("dp", "hid"), None),
            P(("dp", "hid")),
            P(),
            P(None, "hg"),
            P(),
            P(None, "hg"),
            P(None, ("hg", "hid")),
            P(None, ("hg", "hid")),
            P(("dp", "hid"), "hg"),
        ),
        out_specs=(
            P(("dp", "hid"), "hg"),
            P(("dp", "hid"), None),
            P(("dp", "hid")),
            P(("dp", "hid"), "hg"),
            P(),
            P(("dp", "hid"), "hg"),
            P("dp", ("hg", "hid")),
            P("dp", ("hg", "hid")),
        ),
        check_vma=False,
    )
```

```python
import functools
import math

import jax
import jax.numpy as jnp
from jax import lax
from jax.experimental import pallas as pl
from jax.experimental.pallas import tpu as pltpu
from jax.sharding import PartitionSpec as P

PATCHES = 196
EPSILON = 1e-06
LOG2E = math.log2(math.e)
LANES = 128
VMEM = pltpu.VMEM


def times_t(left, right):
    return lax.dot_general(
        left, right, (((1,), (1,)), ((), ())), preferred_element_type=jnp.float32
    )


def rows_t(left, right):
    return lax.dot_general(
        left, right, (((0,), (0,)), ((), ())), preferred_element_type=jnp.float32
    )


def times(left, right):
    return jnp.dot(left, right, preferred_element_type=jnp.float32)


def low(value):
    return value.astype(jnp.bfloat16)


def wide(value):
    return value.astype(jnp.float32)


def lane_of(shape):
    return lax.broadcasted_iota(jnp.int32, shape, 1)


def row_of(shape):
    return lax.broadcasted_iota(jnp.int32, shape, 0)


def other_half(value):
    return pltpu.roll(value, LANES // 2, 1)


def three_terms(column, shape):
    lane = lane_of(shape)
    whole = jnp.broadcast_to(column, shape)
    first = wide(low(whole))
    second = wide(low(whole - first))
    third = whole - first - second
    return jnp.where(lane == 64, first, jnp.where(lane == 65, second, jnp.where(lane == 66, third, 0.0)))


def pair_mask(block, shape, first_lane):
    start = 2 * PATCHES * block - first_lane
    place = lane_of(shape) - start
    second = row_of(shape) >= PATCHES
    begin = jnp.where(second, PATCHES, 0)
    return (place >= begin) & (place < begin + PATCHES)


def window_of(block):
    return (2 * PATCHES * block // LANES) * LANES, 4 * LANES


def forward_kernel(
    flag_ref, tok_ref, gain_ref, w_ref, qk_ref, normed_ref, q_ref, k_ref, v_ref, att_ref, inv_ref
):
    rows = tok_ref.shape[0]
    heads, padded, _ = q_ref.shape
    tile = 2 * PATCHES
    size = qk_ref.shape[1]
    columns = w_ref.shape[1]
    gain = wide(gain_ref[...])
    q_gain = wide(qk_ref[0:1, :]) * (size**-0.5 * LOG2E)
    k_gain = wide(qk_ref[1:2, :])
    ones = jnp.ones_like(k_gain)
    gains = jnp.concatenate([q_gain, k_gain, ones, q_gain, k_gain, ones], axis=1)
    is_value = jnp.concatenate([0 * ones, 0 * ones, ones, 0 * ones, 0 * ones, ones], axis=1)
    group_a = row_of((256, 256)) // size
    group_b = lane_of((256, 256)) // size
    mean_of = low(jnp.where(group_a == group_b, 1.0 / size, 0.0))
    lane = lane_of((tile, LANES))
    for start in range(0, rows, tile):
        here = slice(start, start + tile)
        x = wide(tok_ref[here, :])
        x = x - jnp.mean(x, axis=1, keepdims=True)
        x = x * lax.rsqrt(jnp.mean(x * x, axis=1, keepdims=True) + EPSILON)
        normed = low(x * gain)
        normed_ref[here, :] = normed
        compact = jnp.zeros((tile, LANES), jnp.float32)
        for pair in range(heads // 2):
            joined = times(normed, w_ref[:, 384 * pair : 384 * pair + 384])
            parts = []
            for at in (0, 256):
                wid = min(256, 384 - at)
                block = joined[:, at : at + wid]
                means = mean_of[:wid, :wid]
                centred = block - times(low(block), means)
                squares = low(centred * centred)
                variance = times(squares, means)
                place = 6 * pair + at // size
                pick = low(
                    jnp.where(
                        row_of((wid, LANES)) // size + place == lane_of((wid, LANES)), 1.0 / size, 0.0
                    )
                )
                compact = compact + times(squares, pick)
                hat = centred * lax.rsqrt(variance + EPSILON)
                parts.append(
                    jnp.where(is_value[:, at : at + wid] > 0, block, hat * gains[:, at : at + wid])
                )
            b0, b1, b2 = parts[0][:, :128], parts[0][:, 128:], parts[1]
            first = lane < 64
            unit = jnp.where(lane < 67, 1.0, 0.0)
            q_ref[2 * pair, here, :] = low(jnp.where(first, b0, 0.0))
            k_ref[2 * pair, here, :] = low(jnp.where(first, other_half(b0), unit))
            v_ref[2 * pair, here, :] = low(jnp.where(first, b1, unit))
            q_ref[2 * pair + 1, here, :] = low(jnp.where(first, other_half(b1), 0.0))
            k_ref[2 * pair + 1, here, :] = low(jnp.where(first, b2, unit))
            v_ref[2 * pair + 1, here, :] = low(jnp.where(first, other_half(b2), unit))
        inv_ref[here, :] = lax.rsqrt(compact + EPSILON)
    for ref in (q_ref, k_ref, v_ref):
        ref[:, rows:, :] = jnp.zeros((heads, padded - rows, LANES), jnp.bfloat16)

    def attend(pair, _, big):
        for start in range(0, rows, tile):
            here = slice(start, start + tile)
            if big:
                keys = slice(0, padded)
            else:
                begin, length = window_of(start // tile)
                keys = slice(begin, begin + length)
            found = []
            for side in range(2):
                head = 2 * pair + side
                queries = q_ref[head, here, :]
                scores = times_t(queries, k_ref[head, keys, :])
                if not big:
                    scores = jnp.where(
                        pair_mask(start // tile, scores.shape, keys.start), scores, -1e30
                    )
                expo = low(jnp.exp2(scores))
                out = times(expo, v_ref[head, keys, :])
                total = out[:, 64:65]
                found.append(out * (1.0 / total))
                log_total = jnp.log(total) * (-LOG2E)
                q_ref[head, here, :] = low(
                    jnp.where(lane < 64, wide(queries), three_terms(log_total, lane.shape))
                )
            att_ref[here, pl.ds(pl.multiple_of(pair * LANES, LANES), LANES)] = low(
                jnp.where(lane < 64, found[0], other_half(found[1]))
            )
        return 0

    @pl.when(flag_ref[0] > 0)
    def _():
        lax.fori_loop(0, heads // 2, functools.partial(attend, big=True), 0)

    @pl.when(flag_ref[0] <= 0)
    def _():
        lax.fori_loop(0, heads // 2, functools.partial(attend, big=False), 0)


def forward(big_images, tokens, norm_gain, w_qkv, qk_gains):
    rows, width = tokens.shape
    size = qk_gains.shape[1]
    heads = w_qkv.shape[1] // (3 * size)
    padded = -(-rows // 256) * 256
    whole = pl.BlockSpec(memory_space=VMEM)
    head_rows = jax.ShapeDtypeStruct((heads, padded, LANES), jnp.bfloat16)
    return pl.pallas_call(
        forward_kernel,
        name="forward",
        out_shape=[
            jax.ShapeDtypeStruct((rows, width), jnp.bfloat16),
            head_rows,
            head_rows,
            head_rows,
            jax.ShapeDtypeStruct((rows, heads * size), jnp.bfloat16),
            jax.ShapeDtypeStruct((rows, LANES), jnp.float32),
        ],
        in_specs=[pl.BlockSpec(memory_space=pltpu.SMEM)] + [whole] * 4,
        out_specs=[whole] * 6,
        compiler_params=pltpu.CompilerParams(vmem_limit_bytes=56 * 2**20),
        cost_estimate=pl.CostEstimate(
            flops=2 * rows * (width * w_qkv.shape[1] + heads * padded * 2 * LANES),
            bytes_accessed=20 * 2**20,
            transcendentals=heads * rows * padded,
        ),
    )(big_images, tokens, norm_gain.reshape(1, -1), w_qkv, qk_gains)


def backward_kernel(
    flag_ref, q_ref, k_ref, v_ref, do_ref, inv_ref, qk_ref, joined_ref, small_ref, dq_ref, dk_ref, dv_ref
):
    pair = pl.program_id(0)
    rows = inv_ref.shape[0]
    padded = q_ref.shape[1]
    tile = 2 * PATCHES
    size = qk_ref.shape[1]
    scale = size**-0.5
    zeros = jnp.zeros((1, LANES - size), jnp.float32)
    q_gain = wide(qk_ref[0:1, :])
    k_gain = wide(qk_ref[1:2, :])
    q_back = jnp.concatenate([1.0 / (q_gain * (scale * LOG2E)), zeros], axis=1)
    k_back = jnp.concatenate([1.0 / k_gain, zeros], axis=1)
    q_gain = jnp.concatenate([q_gain, zeros], axis=1)
    k_gain = jnp.concatenate([k_gain, zeros], axis=1)

    def attend(side, _, big):
        for start in range(0, rows, tile):
            here = slice(start, start + tile)
            if big:
                over = slice(0, padded)
            else:
                begin, length = window_of(start // tile)
                over = slice(begin, begin + length)
            keys = k_ref[side, here, :]
            queries = q_ref[side, over, :]
            grads = do_ref[side, over, :]
            scores = times_t(keys, queries)
            if not big:
                scores = jnp.where(pair_mask(start // tile, scores.shape, over.start), scores, -1e30)
            probs = jnp.exp2(scores)
            grad_probs = times_t(v_ref[side, here, :], grads)
            grad_scores = low(probs * grad_probs)
            dv_ref[side, here, :] = times(low(probs), grads)
            dk_ref[side, here, :] = times(grad_scores, queries)
            more = rows_t(keys, grad_scores)
            if big and start == 0:
                dq_ref[side, :, over] = more
            elif big:
                dq_ref[side, :, over] += more
            else:
                place = lane_of(more.shape) - (start - over.start)
                dq_ref[side, :, over] = jnp.where(
                    (place >= 0) & (place < tile), more, dq_ref[side, :, over]
                )
        return 0

    @pl.when(flag_ref[0] > 0)
    def _():
        lax.fori_loop(0, 2, functools.partial(attend, big=True), 0)

    @pl.when(flag_ref[0] <= 0)
    def _():
        lax.fori_loop(0, 2, functools.partial(attend, big=False), 0)

    @pl.when(pair == 0)
    def _():
        small_ref[...] = jnp.zeros_like(small_ref)

    lane = lane_of((tile, LANES))
    first = lane < 64
    all_places = lane_of((rows, LANES)) - 6 * pair

    def undo(grad, hat, gain, inverse):
        grad_hat = grad * gain
        mean = jnp.sum(grad_hat, axis=1, keepdims=True) * (1.0 / size)
        inner = jnp.sum(grad_hat * hat, axis=1, keepdims=True) * (1.0 / size)
        return inverse * (grad_hat - mean - hat * inner)

    for start in range(0, rows, tile):
        here = slice(start, start + tile)
        blocks = []
        for side in range(2):
            inverses = inv_ref[here, :]
            place = lane - 6 * pair
            q_at, k_at = (0, 1) if side == 0 else (3, 4)
            q_inv = jnp.sum(jnp.where(place == q_at, inverses, 0.0), axis=1, keepdims=True)
            k_inv = jnp.sum(jnp.where(place == k_at, inverses, 0.0), axis=1, keepdims=True)
            q_hat = wide(q_ref[side, here, :]) * q_back
            k_hat = wide(k_ref[side, here, :]) * k_back
            grad_q = dq_ref[side, :, here].T * scale
            grad_k = dk_ref[side, here, :] * math.log(2.0)
            small_ref[0:1, :] += jnp.sum(jnp.where(first, grad_q * q_hat, 0.0), axis=0, keepdims=True)
            small_ref[1:2, :] += jnp.sum(jnp.where(first, grad_k * k_hat, 0.0), axis=0, keepdims=True)
            blocks.append(
                (
                    undo(grad_q, q_hat, q_gain, q_inv),
                    undo(grad_k, k_hat, k_gain, k_inv),
                    dv_ref[side, here, :],
                )
            )
        (q0, k0, v0), (q1, k1, v1) = blocks
        joined_ref[here, 0:128] = low(jnp.where(first, q0, other_half(k0)))
        joined_ref[here, 128:256] = low(jnp.where(first, v0, other_half(q1)))
        joined_ref[here, 256:384] = low(jnp.where(first, k1, other_half(v1)))


def backward(big_images, q_rows, k_rows, v_rows, do_rows, inverses, qk_gains):
    heads, padded, _ = q_rows.shape
    rows = inverses.shape[0]
    pair_spec = pl.BlockSpec((2, padded, LANES), lambda pair: (pair, 0, 0))
    return pl.pallas_call(
        backward_kernel,
        name="backward",
        grid=(heads // 2,),
        out_shape=[
            jax.ShapeDtypeStruct((rows, heads * 3 * LANES // 2), jnp.bfloat16),
            jax.ShapeDtypeStruct((8, LANES), jnp.float32),
        ],
        in_specs=[pl.BlockSpec(memory_space=pltpu.SMEM)]
        + [pair_spec] * 4
        + [pl.BlockSpec((rows, LANES), lambda pair: (0, 0)), pl.BlockSpec(qk_gains.shape, lambda pair: (0, 0))],
        out_specs=[
            pl.BlockSpec((rows, 3 * LANES), lambda pair: (0, pair)),
            pl.BlockSpec((8, LANES), lambda pair: (0, 0)),
        ],
        scratch_shapes=[
            VMEM((2, LANES, padded), jnp.float32),
            VMEM((2, rows, LANES), jnp.float32),
            VMEM((2, rows, LANES), jnp.float32),
        ],
        compiler_params=pltpu.CompilerParams(vmem_limit_bytes=56 * 2**20),
        cost_estimate=pl.CostEstimate(
            flops=2 * rows * heads * padded * 5 * LANES,
            bytes_accessed=16 * 2**20,
            transcendentals=heads * rows * padded,
        ),
    )(big_images, q_rows, k_rows, v_rows, do_rows, inverses, qk_gains)


def dense_kernel(count, place_ref, tok_ref, normed_ref, att_ref, mine_ref, other_ref, w_out_ref, *refs):
    w_in_refs, w_back_refs = refs[:count], refs[count : 2 * count]
    refs = refs[2 * count :]
    keep_ref, send_ref, grad_ref, do_ref, w_out_grad_ref = refs[:5]
    gin_refs, gback_refs = refs[5 : 5 + count], refs[5 + count : 5 + 2 * count]
    refs = refs[5 + 2 * count :]
    dy_ref, left_ref, act_refs, gup_refs = refs[0], refs[1], refs[2 : 2 + count], refs[2 + count :]
    rows, width = normed_ref.shape
    half = width // 2
    heads, padded, _ = do_ref.shape
    tile = 2 * PATCHES
    here_lane = pl.multiple_of(place_ref[0] * half, LANES)
    other_lane = pl.multiple_of((1 - place_ref[0]) * half, LANES)
    dy_ref[:, pl.ds(here_lane, half)] = mine_ref[...]
    dy_ref[:, pl.ds(other_lane, half)] = other_ref[...]
    curve = math.sqrt(2.0 / math.pi)
    lane = lane_of((tile, LANES))

    for start in range(0, rows, tile):
        here = slice(start, start + tile)
        for w_in_ref, w_back_ref, act_ref, gup_ref in zip(w_in_refs, w_back_refs, act_refs, gup_refs):
            columns = w_in_ref.shape[1]
            step = min(256, columns)
            normed = normed_ref[here, :]
            dy = dy_ref[here, :]
            for at in range(0, columns, step):
                cols = slice(at, min(at + step, columns))
                up = times(normed, w_in_ref[:, cols])
                grad_act = times(dy, w_back_ref[:, cols])
                square = up * up
                bent = jnp.tanh(up * (curve + (curve * 0.044715) * square))
                gate = 0.5 + 0.5 * bent
                act = up * gate
                slope = gate + act * ((1.0 - gate) * (2 * curve + (6 * curve * 0.044715) * square))
                act_ref[here, cols] = low(act)
                gup_ref[here, cols] = low(grad_act * slope)
        attended = att_ref[here, :]
        total = times_t(attended, w_out_ref[...])
        for act_ref, w_back_ref in zip(act_refs, w_back_refs):
            total = total + times_t(act_ref[here, :], w_back_ref[...])
        left_ref[...] = total
        keep_ref[here, :] = left_ref[:, pl.ds(here_lane, half)] + wide(tok_ref[here, pl.ds(here_lane, half)])
        send_ref[here, :] = low(left_ref[:, pl.ds(other_lane, half)])
        grad = None
        for gup_ref, w_in_ref in zip(gup_refs, w_in_refs):
            part = times_t(gup_ref[here, :], w_in_ref[...])
            grad = part if grad is None else grad + part
        grad_ref[here, :] = low(grad)
        grad_att = times(dy_ref[here, :], w_out_ref[...])
        for pair in range(heads // 2):
            cols = slice(pair * LANES, pair * LANES + LANES)
            block = grad_att[:, cols]
            low_block = wide(low(block))
            weighed = low_block * wide(attended[:, cols])
            for side in range(2):
                mine = lane < 64 if side == 0 else lane >= 64
                inner = jnp.sum(jnp.where(mine, weighed, 0.0), axis=1, keepdims=True)
                value = low_block if side == 0 else other_half(low_block)
                do_ref[2 * pair + side, here, :] = low(
                    jnp.where(lane < 64, value, three_terms(-inner, lane.shape))
                )
    do_ref[:, rows:, :] = jnp.zeros((heads, padded - rows, LANES), jnp.bfloat16)
    for act_ref, gup_ref, gin_ref, gback_ref in zip(act_refs, gup_refs, gin_refs, gback_refs):
        gback_ref[...] = rows_t(dy_ref[...], act_ref[...]).astype(gback_ref.dtype)
        gin_ref[...] = rows_t(normed_ref[...], gup_ref[...]).astype(gin_ref.dtype)
    w_out_grad_ref[...] = rows_t(dy_ref[...], att_ref[...])


def dense(place, tokens, normed, attended, mine, other, w_out_t, w_in_pieces, w_back_pieces):
    rows, width = tokens.shape
    heads = w_out_t.shape[1] // 64
    padded = -(-rows // 256) * 256
    count = len(w_in_pieces)
    whole = pl.BlockSpec(memory_space=VMEM)
    shape = jax.ShapeDtypeStruct
    sizes = [piece.shape[1] for piece in w_in_pieces]
    kinds = [jnp.float32] * (count - 1) + [jnp.bfloat16] if count > 1 else [jnp.float32]
    grads = [shape((width, size), kind) for size, kind in zip(sizes, kinds)]
    hidden = sum(sizes)
    return pl.pallas_call(
        functools.partial(dense_kernel, count),
        name="dense",
        out_shape=[
            shape((rows, width // 2), jnp.float32),
            shape((rows, width // 2), jnp.bfloat16),
            shape((rows, width), jnp.bfloat16),
            shape((heads, padded, LANES), jnp.bfloat16),
            shape((width, w_out_t.shape[1]), jnp.float32),
        ]
        + grads
        + grads,
        in_specs=[pl.BlockSpec(memory_space=pltpu.SMEM)] + [whole] * (6 + 2 * count),
        out_specs=[whole] * (5 + 2 * count),
        scratch_shapes=[VMEM((rows, width), jnp.bfloat16), VMEM((2 * PATCHES, width), jnp.float32)]
        + [VMEM((rows, size), jnp.bfloat16) for size in sizes] * 2,
        compiler_params=pltpu.CompilerParams(vmem_limit_bytes=60 * 2**20),
        cost_estimate=pl.CostEstimate(
            flops=2 * rows * width * (6 * hidden + 3 * w_out_t.shape[1]),
            bytes_accessed=26 * 2**20,
            transcendentals=rows * hidden,
        ),
    )(place, tokens, normed, attended, mine, other, w_out_t, *w_in_pieces, *w_back_pieces)


def swap(value, axis, bit):
    size = lax.axis_size(axis)
    return lax.ppermute(value, axis, [(place, place ^ bit) for place in range(size)])


def bits_of(axis):
    size = lax.axis_size(axis)
    return [1 << place for place in range(size.bit_length() - 1)]


def gather_pieces(block, axis):
    pieces = [block]
    for bit in bits_of(axis):
        held = pieces[0] if len(pieces) == 1 else jnp.concatenate(pieces, axis=1)
        pieces.append(swap(held, axis, bit))
    return pieces


def scatter_pieces(pieces, axis):
    for bit in reversed(bits_of(axis)):
        sent = swap(low(pieces[-1]), axis, bit)
        kept, at = [], 0
        for piece in pieces[:-1]:
            kept.append(wide(piece) + wide(sent[:, at : at + piece.shape[1]]))
            at += piece.shape[1]
        pieces = kept
    return pieces[0]


def scatter_rows(grad, axes):
    levels = []
    for axis in axes:
        levels += [(axis, bit) for bit in reversed(bits_of(axis))]
    rows, columns = grad.shape
    blocks = rows >> len(levels)
    shaped = grad.reshape((2,) * len(levels) + (blocks, columns))
    for axis, bit in reversed(levels):
        place = len(shaped.shape) - 3
        mine = (lax.axis_index(axis) & bit) > 0
        first, second = (lax.index_in_dim(shaped, side, place, keepdims=False) for side in (0, 1))
        sent = low(jnp.where(mine, first, second))
        shaped = wide(jnp.where(mine, second, first)) + wide(swap(sent, axis, bit))
    return shaped


def sum_everywhere(value, axes):
    for axis in axes:
        for bit in bits_of(axis):
            value = value + swap(value, axis, bit)
    return value


def normalize(values):
    centred = values - jnp.mean(values, axis=-1, keepdims=True)
    inverse = lax.rsqrt(jnp.mean(centred * centred, axis=-1, keepdims=True) + EPSILON)
    return (centred * inverse, inverse)


def normalize_back(upstream, normed, inverse):
    inner = jnp.mean(upstream * normed, axis=-1, keepdims=True)
    return inverse * (upstream - jnp.mean(upstream, axis=-1, keepdims=True) - normed * inner)


def shards(tokens, big_images, norm_gain, w_qkv, qk_gains, w_out_t, w_in, w_back, cotangent):
    tok_rows, width = tokens.shape
    size = qk_gains.shape[1]
    place = lax.axis_index("hg").astype(jnp.int32)
    other = swap(cotangent, "hg", 1)
    w_in_pieces = gather_pieces(w_in, "hid")
    w_back_pieces = gather_pieces(w_back, "hid")
    normed_low, q_rows, k_rows, v_rows, attended, inverses = forward(
        big_images, tokens, norm_gain, w_qkv, qk_gains
    )
    kept, sent, grad_mlp, do_rows, grad_w_out, *grads = dense(
        place.reshape(1), tokens, normed_low, attended, cotangent, other, w_out_t, w_in_pieces, w_back_pieces
    )
    count = len(w_in_pieces)
    output = low(kept + wide(swap(sent, "hg", 1)))
    w_in_grad = scatter_rows(scatter_pieces(grads[:count], "hid"), ("dp",))
    w_back_grad = scatter_rows(scatter_pieces(grads[count:], "hid"), ("dp",))
    w_out_t_grad = scatter_rows(grad_w_out, ("dp", "hid"))

    grad_joined, small = backward(big_images, q_rows, k_rows, v_rows, do_rows, inverses, qk_gains)
    grad_normed = times_t(grad_joined, w_qkv) + wide(grad_mlp)
    normed_sent = low(grad_normed)
    w_qkv_grad = scatter_rows(rows_t(normed_low, grad_joined), ("dp", "hid"))
    normed, inverse = normalize(wide(tokens))
    gain_vec = wide(norm_gain)
    gain_partial = jnp.sum(grad_normed * normed, axis=0)
    small = sum_everywhere(
        jnp.concatenate([gain_partial, small[:2, :size].reshape(-1)]), ("hid", "hg", "dp")
    )
    shard_count = lax.axis_size("dp") * lax.axis_size("hid")
    own = lax.axis_index("dp") * lax.axis_size("hid") + lax.axis_index("hid")
    gain_rows = width // shard_count
    norm_gain_grad = lax.dynamic_slice_in_dim(small, own * gain_rows, gain_rows, 0)
    qk_gains_grad = small[width:].reshape(2, size)
    grad_normed = wide(normed_sent) + wide(swap(normed_sent, "hg", 1))
    first = place == 0
    grad_out = jnp.concatenate(
        [jnp.where(first, cotangent, other), jnp.where(first, other, cotangent)], axis=1
    )
    token_grad = low(normalize_back(grad_normed * gain_vec, normed, inverse) + wide(grad_out))
    return (
        output,
        token_grad,
        norm_gain_grad,
        w_qkv_grad,
        qk_gains_grad,
        w_out_t_grad,
        w_in_grad,
        w_back_grad,
    )


def solution(mesh):
    return jax.shard_map(
        shards,
        mesh=mesh,
        in_specs=(
            P(("dp", "hid"), None),
            P(("dp", "hid")),
            P(),
            P(None, "hg"),
            P(),
            P(None, "hg"),
            P(None, ("hg", "hid")),
            P(None, ("hg", "hid")),
            P(("dp", "hid"), "hg"),
        ),
        out_specs=(
            P(("dp", "hid"), "hg"),
            P(("dp", "hid"), None),
            P(("dp", "hid")),
            P(("dp", "hid"), "hg"),
            P(),
            P(("dp", "hid"), "hg"),
            P("dp", ("hg", "hid")),
            P("dp", ("hg", "hid")),
        ),
        check_vma=False,
    )
```

```python
import functools
import math

import jax
import jax.numpy as jnp
from jax import lax
from jax.experimental import pallas as pl
from jax.experimental.pallas import tpu as pltpu
from jax.sharding import PartitionSpec as P

PATCHES = 196
EPSILON = 1e-06
LOG2E = math.log2(math.e)
LANES = 128
VMEM = pltpu.VMEM
SCALE = 1.0


def cost(microseconds):
    return pl.CostEstimate(
        flops=int(microseconds * SCALE * 1e9), bytes_accessed=2**20, transcendentals=0
    )


def times_t(left, right):
    return lax.dot_general(
        left, right, (((1,), (1,)), ((), ())), preferred_element_type=jnp.float32
    )


def rows_t(left, right):
    return lax.dot_general(
        left, right, (((0,), (0,)), ((), ())), preferred_element_type=jnp.float32
    )


def times(left, right):
    return jnp.dot(left, right, preferred_element_type=jnp.float32)


def low(value):
    return value.astype(jnp.bfloat16)


def wide(value):
    return value.astype(jnp.float32)


def lane_of(shape):
    return lax.broadcasted_iota(jnp.int32, shape, 1)


def row_of(shape):
    return lax.broadcasted_iota(jnp.int32, shape, 0)


def other_half(value):
    return pltpu.roll(value, LANES // 2, 1)


def three_terms(column, shape):
    lane = lane_of(shape)
    whole = jnp.broadcast_to(column, shape)
    first = wide(low(whole))
    second = wide(low(whole - first))
    third = whole - first - second
    return jnp.where(lane == 64, first, jnp.where(lane == 65, second, jnp.where(lane == 66, third, 0.0)))


def pair_mask(block, shape, first_lane):
    start = 2 * PATCHES * block - first_lane
    place = lane_of(shape) - start
    second = row_of(shape) >= PATCHES
    begin = jnp.where(second, PATCHES, 0)
    return (place >= begin) & (place < begin + PATCHES)


def window_of(block):
    return (2 * PATCHES * block // LANES) * LANES, 4 * LANES


def forward_kernel(
    flag_ref, tok_ref, gain_ref, w_ref, qk_ref, normed_ref, q_ref, k_ref, v_ref, att_ref, inv_ref
):
    rows = tok_ref.shape[0]
    heads, padded, _ = q_ref.shape
    tile = 2 * PATCHES
    size = qk_ref.shape[1]
    columns = w_ref.shape[1]
    gain = wide(gain_ref[...])
    q_gain = wide(qk_ref[0:1, :]) * (size**-0.5 * LOG2E)
    k_gain = wide(qk_ref[1:2, :])
    ones = jnp.ones_like(k_gain)
    gains = jnp.concatenate([q_gain, k_gain, ones, q_gain, k_gain, ones], axis=1)
    is_value = jnp.concatenate([0 * ones, 0 * ones, ones, 0 * ones, 0 * ones, ones], axis=1)
    group_a = row_of((256, 256)) // size
    group_b = lane_of((256, 256)) // size
    mean_of = low(jnp.where(group_a == group_b, 1.0 / size, 0.0))
    lane = lane_of((tile, LANES))
    for start in range(0, rows, tile):
        here = slice(start, start + tile)
        x = wide(tok_ref[here, :])
        x = x - jnp.mean(x, axis=1, keepdims=True)
        x = x * lax.rsqrt(jnp.mean(x * x, axis=1, keepdims=True) + EPSILON)
        normed = low(x * gain)
        normed_ref[here, :] = normed
        compact = jnp.zeros((tile, LANES), jnp.float32)
        for pair in range(heads // 2):
            joined = times(normed, w_ref[:, 384 * pair : 384 * pair + 384])
            parts = []
            for at in (0, 256):
                wid = min(256, 384 - at)
                block = joined[:, at : at + wid]
                means = mean_of[:wid, :wid]
                centred = block - times(low(block), means)
                squares = low(centred * centred)
                variance = times(squares, means)
                place = 6 * pair + at // size
                pick = low(
                    jnp.where(
                        row_of((wid, LANES)) // size + place == lane_of((wid, LANES)), 1.0 / size, 0.0
                    )
                )
                compact = compact + times(squares, pick)
                hat = centred * lax.rsqrt(variance + EPSILON)
                parts.append(
                    jnp.where(is_value[:, at : at + wid] > 0, block, hat * gains[:, at : at + wid])
                )
            b0, b1, b2 = parts[0][:, :128], parts[0][:, 128:], parts[1]
            first = lane < 64
            unit = jnp.where(lane < 67, 1.0, 0.0)
            q_ref[2 * pair, here, :] = low(jnp.where(first, b0, 0.0))
            k_ref[2 * pair, here, :] = low(jnp.where(first, other_half(b0), unit))
            v_ref[2 * pair, here, :] = low(jnp.where(first, b1, unit))
            q_ref[2 * pair + 1, here, :] = low(jnp.where(first, other_half(b1), 0.0))
            k_ref[2 * pair + 1, here, :] = low(jnp.where(first, b2, unit))
            v_ref[2 * pair + 1, here, :] = low(jnp.where(first, other_half(b2), unit))
        inv_ref[here, :] = lax.rsqrt(compact + EPSILON)
    for ref in (q_ref, k_ref, v_ref):
        ref[:, rows:, :] = jnp.zeros((heads, padded - rows, LANES), jnp.bfloat16)

    def attend(pair, _, big):
        for start in range(0, rows, tile):
            here = slice(start, start + tile)
            if big:
                keys = slice(0, padded)
            else:
                begin, length = window_of(start // tile)
                keys = slice(begin, begin + length)
            found = []
            for side in range(2):
                head = 2 * pair + side
                queries = q_ref[head, here, :]
                scores = times_t(queries, k_ref[head, keys, :])
                if not big:
                    scores = jnp.where(
                        pair_mask(start // tile, scores.shape, keys.start), scores, -1e30
                    )
                expo = low(jnp.exp2(scores))
                out = times(expo, v_ref[head, keys, :])
                total = out[:, 64:65]
                found.append(out * (1.0 / total))
                log_total = jnp.log(total) * (-LOG2E)
                q_ref[head, here, :] = low(
                    jnp.where(lane < 64, wide(queries), three_terms(log_total, lane.shape))
                )
            att_ref[here, pl.ds(pl.multiple_of(pair * LANES, LANES), LANES)] = low(
                jnp.where(lane < 64, found[0], other_half(found[1]))
            )
        return 0

    @pl.when(flag_ref[0] > 0)
    def _():
        lax.fori_loop(0, heads // 2, functools.partial(attend, big=True), 0)

    @pl.when(flag_ref[0] <= 0)
    def _():
        lax.fori_loop(0, heads // 2, functools.partial(attend, big=False), 0)


def forward(big_images, tokens, norm_gain, w_qkv, qk_gains):
    rows, width = tokens.shape
    size = qk_gains.shape[1]
    heads = w_qkv.shape[1] // (3 * size)
    padded = -(-rows // 256) * 256
    whole = pl.BlockSpec(memory_space=VMEM)
    head_rows = jax.ShapeDtypeStruct((heads, padded, LANES), jnp.bfloat16)
    return pl.pallas_call(
        forward_kernel,
        name="forward",
        out_shape=[
            jax.ShapeDtypeStruct((rows, width), jnp.bfloat16),
            head_rows,
            head_rows,
            head_rows,
            jax.ShapeDtypeStruct((rows, heads * size), jnp.bfloat16),
            jax.ShapeDtypeStruct((rows, LANES), jnp.float32),
        ],
        in_specs=[pl.BlockSpec(memory_space=pltpu.SMEM)] + [whole] * 4,
        out_specs=[whole] * 6,
        compiler_params=pltpu.CompilerParams(vmem_limit_bytes=56 * 2**20),
        cost_estimate=cost(24),
    )(big_images, tokens, norm_gain.reshape(1, -1), w_qkv, qk_gains)


def backward_kernel(
    flag_ref, q_ref, k_ref, v_ref, do_ref, inv_ref, qk_ref, joined_ref, small_ref, dq_ref, dk_ref, dv_ref
):
    pair = pl.program_id(0)
    rows = inv_ref.shape[0]
    padded = q_ref.shape[1]
    tile = 2 * PATCHES
    size = qk_ref.shape[1]
    scale = size**-0.5
    zeros = jnp.zeros((1, LANES - size), jnp.float32)
    q_gain = wide(qk_ref[0:1, :])
    k_gain = wide(qk_ref[1:2, :])
    q_back = jnp.concatenate([1.0 / (q_gain * (scale * LOG2E)), zeros], axis=1)
    k_back = jnp.concatenate([1.0 / k_gain, zeros], axis=1)
    q_gain = jnp.concatenate([q_gain, zeros], axis=1)
    k_gain = jnp.concatenate([k_gain, zeros], axis=1)

    def attend(side, _, big):
        for start in range(0, rows, tile):
            here = slice(start, start + tile)
            if big:
                over = slice(0, padded)
            else:
                begin, length = window_of(start // tile)
                over = slice(begin, begin + length)
            keys = k_ref[side, here, :]
            queries = q_ref[side, over, :]
            grads = do_ref[side, over, :]
            scores = times_t(keys, queries)
            if not big:
                scores = jnp.where(pair_mask(start // tile, scores.shape, over.start), scores, -1e30)
            probs = jnp.exp2(scores)
            grad_probs = times_t(v_ref[side, here, :], grads)
            grad_scores = low(probs * grad_probs)
            dv_ref[side, here, :] = times(low(probs), grads)
            dk_ref[side, here, :] = times(grad_scores, queries)
            more = rows_t(keys, grad_scores)
            if big and start == 0:
                dq_ref[side, :, over] = more
            elif big:
                dq_ref[side, :, over] += more
            else:
                place = lane_of(more.shape) - (start - over.start)
                dq_ref[side, :, over] = jnp.where(
                    (place >= 0) & (place < tile), more, dq_ref[side, :, over]
                )
        return 0

    @pl.when(flag_ref[0] > 0)
    def _():
        lax.fori_loop(0, 2, functools.partial(attend, big=True), 0)

    @pl.when(flag_ref[0] <= 0)
    def _():
        lax.fori_loop(0, 2, functools.partial(attend, big=False), 0)

    @pl.when(pair == 0)
    def _():
        small_ref[...] = jnp.zeros_like(small_ref)

    lane = lane_of((tile, LANES))
    first = lane < 64
    all_places = lane_of((rows, LANES)) - 6 * pair

    def undo(grad, hat, gain, inverse):
        grad_hat = grad * gain
        mean = jnp.sum(grad_hat, axis=1, keepdims=True) * (1.0 / size)
        inner = jnp.sum(grad_hat * hat, axis=1, keepdims=True) * (1.0 / size)
        return inverse * (grad_hat - mean - hat * inner)

    for start in range(0, rows, tile):
        here = slice(start, start + tile)
        blocks = []
        for side in range(2):
            inverses = inv_ref[here, :]
            place = lane - 6 * pair
            q_at, k_at = (0, 1) if side == 0 else (3, 4)
            q_inv = jnp.sum(jnp.where(place == q_at, inverses, 0.0), axis=1, keepdims=True)
            k_inv = jnp.sum(jnp.where(place == k_at, inverses, 0.0), axis=1, keepdims=True)
            q_hat = wide(q_ref[side, here, :]) * q_back
            k_hat = wide(k_ref[side, here, :]) * k_back
            grad_q = dq_ref[side, :, here].T * scale
            grad_k = dk_ref[side, here, :] * math.log(2.0)
            small_ref[0:1, :] += jnp.sum(jnp.where(first, grad_q * q_hat, 0.0), axis=0, keepdims=True)
            small_ref[1:2, :] += jnp.sum(jnp.where(first, grad_k * k_hat, 0.0), axis=0, keepdims=True)
            blocks.append(
                (
                    undo(grad_q, q_hat, q_gain, q_inv),
                    undo(grad_k, k_hat, k_gain, k_inv),
                    dv_ref[side, here, :],
                )
            )
        (q0, k0, v0), (q1, k1, v1) = blocks
        joined_ref[here, 0:128] = low(jnp.where(first, q0, other_half(k0)))
        joined_ref[here, 128:256] = low(jnp.where(first, v0, other_half(q1)))
        joined_ref[here, 256:384] = low(jnp.where(first, k1, other_half(v1)))


def backward(big_images, q_rows, k_rows, v_rows, do_rows, inverses, qk_gains):
    heads, padded, _ = q_rows.shape
    rows = inverses.shape[0]
    pair_spec = pl.BlockSpec((2, padded, LANES), lambda pair: (pair, 0, 0))
    return pl.pallas_call(
        backward_kernel,
        name="backward",
        grid=(heads // 2,),
        out_shape=[
            jax.ShapeDtypeStruct((rows, heads * 3 * LANES // 2), jnp.bfloat16),
            jax.ShapeDtypeStruct((8, LANES), jnp.float32),
        ],
        in_specs=[pl.BlockSpec(memory_space=pltpu.SMEM)]
        + [pair_spec] * 4
        + [pl.BlockSpec((rows, LANES), lambda pair: (0, 0)), pl.BlockSpec(qk_gains.shape, lambda pair: (0, 0))],
        out_specs=[
            pl.BlockSpec((rows, 3 * LANES), lambda pair: (0, pair)),
            pl.BlockSpec((8, LANES), lambda pair: (0, 0)),
        ],
        scratch_shapes=[
            VMEM((2, LANES, padded), jnp.float32),
            VMEM((2, rows, LANES), jnp.float32),
            VMEM((2, rows, LANES), jnp.float32),
        ],
        compiler_params=pltpu.CompilerParams(vmem_limit_bytes=56 * 2**20),
        cost_estimate=cost(36),
    )(big_images, q_rows, k_rows, v_rows, do_rows, inverses, qk_gains)


def in_order(mine, other):
    first = lax.axis_index("hg") == 0
    return jnp.where(first, mine, other), jnp.where(first, other, mine)


def dense_kernel(count, normed_ref, mine_ref, other_ref, *refs):
    w_in_refs, w_back_refs = refs[:count], refs[count : 2 * count]
    refs = refs[2 * count :]
    part_ref, grad_ref, dy_ref = refs[:3]
    grad_refs, refs = refs[3 : 3 + count], refs[3 + count :]
    act_refs, gup_refs = refs[:count], refs[count:]
    rows, width = normed_ref.shape
    half = width // 2
    tile = 2 * PATCHES
    dy_ref[:, :half], dy_ref[:, half:] = in_order(mine_ref[...], other_ref[...])
    curve = math.sqrt(2.0 / math.pi)

    for start in range(0, rows, tile):
        here = slice(start, start + tile)
        for w_in_ref, w_back_ref, act_ref, gup_ref in zip(w_in_refs, w_back_refs, act_refs, gup_refs):
            columns = w_in_ref.shape[1]
            step = min(256, columns)
            normed = normed_ref[here, :]
            dy = dy_ref[here, :]
            for at in range(0, columns, step):
                cols = slice(at, min(at + step, columns))
                up = times(normed, w_in_ref[:, cols])
                grad_act = times(dy, w_back_ref[:, cols])
                square = up * up
                bent = jnp.tanh(up * (curve + (curve * 0.044715) * square))
                gate = 0.5 + 0.5 * bent
                act = up * gate
                slope = gate + act * ((1.0 - gate) * (2 * curve + (6 * curve * 0.044715) * square))
                act_ref[here, cols] = low(act)
                gup_ref[here, cols] = low(grad_act * slope)
        total, grad = None, None
        for act_ref, w_back_ref, gup_ref, w_in_ref in zip(act_refs, w_back_refs, gup_refs, w_in_refs):
            part = times_t(act_ref[here, :], w_back_ref[...])
            total = part if total is None else total + part
            part = times_t(gup_ref[here, :], w_in_ref[...])
            grad = part if grad is None else grad + part
        part_ref[here, :] = total
        grad_ref[here, :] = low(grad)
    for act_ref, gup_ref, ref in zip(act_refs, gup_refs, grad_refs):
        columns = act_ref.shape[1]
        ref[:, :columns] = rows_t(normed_ref[...], gup_ref[...]).astype(ref.dtype)
        ref[:, columns:] = rows_t(dy_ref[...], act_ref[...]).astype(ref.dtype)


def dense(normed, mine, other, w_in_pieces, w_back_pieces):
    rows, width = normed.shape
    count = len(w_in_pieces)
    whole = pl.BlockSpec(memory_space=VMEM)
    shape = jax.ShapeDtypeStruct
    sizes = [piece.shape[1] for piece in w_in_pieces]
    kinds = [jnp.float32] * (count - 1) + [jnp.bfloat16] if count > 1 else [jnp.float32]
    hidden = sum(sizes)
    return pl.pallas_call(
        functools.partial(dense_kernel, count),
        name="dense",
        out_shape=[
            shape((rows, width), jnp.float32),
            shape((rows, width), jnp.bfloat16),
            shape((rows, width), jnp.bfloat16),
        ]
        + [shape((width, 2 * size), kind) for size, kind in zip(sizes, kinds)],
        in_specs=[whole] * (3 + 2 * count),
        out_specs=[whole] * (3 + count),
        scratch_shapes=[VMEM((rows, size), jnp.bfloat16) for size in sizes] * 2,
        compiler_params=pltpu.CompilerParams(vmem_limit_bytes=60 * 2**20),
        cost_estimate=cost(24),
    )(normed, mine, other, *w_in_pieces, *w_back_pieces)


def outputs_kernel(
    part_ref, tok_ref, att_ref, mine_ref, other_ref, w_out_ref, keep_ref, send_ref, do_ref
):
    rows, width = part_ref.shape
    half = width // 2
    heads, padded, _ = do_ref.shape
    tile = 2 * PATCHES
    lane = lane_of((tile, LANES))
    for start in range(0, rows, tile):
        here = slice(start, start + tile)
        attended = att_ref[here, :]
        left = times_t(attended, w_out_ref[...]) + part_ref[here, :]
        token = tok_ref[here, :]
        keep, send = in_order(left[:, :half], left[:, half:])
        keep_ref[here, :] = keep + in_order(wide(token[:, :half]), wide(token[:, half:]))[0]
        send_ref[here, :] = low(send)
        first, second = in_order(mine_ref[here, :], other_ref[here, :])
        grad_att = times(first, w_out_ref[:half, :]) + times(second, w_out_ref[half:, :])
        for pair in range(heads // 2):
            cols = slice(pair * LANES, pair * LANES + LANES)
            low_block = wide(low(grad_att[:, cols]))
            weighed = low_block * wide(attended[:, cols])
            for side in range(2):
                mine = lane < 64 if side == 0 else lane >= 64
                inner = jnp.sum(jnp.where(mine, weighed, 0.0), axis=1, keepdims=True)
                value = low_block if side == 0 else other_half(low_block)
                do_ref[2 * pair + side, here, :] = low(
                    jnp.where(lane < 64, value, three_terms(-inner, lane.shape))
                )
    do_ref[:, rows:, :] = jnp.zeros((heads, padded - rows, LANES), jnp.bfloat16)


def outputs(part, tokens, attended, mine, other, w_out_t):
    rows, width = tokens.shape
    heads = w_out_t.shape[1] // 64
    padded = -(-rows // 256) * 256
    whole = pl.BlockSpec(memory_space=VMEM)
    shape = jax.ShapeDtypeStruct
    return pl.pallas_call(
        outputs_kernel,
        name="outputs",
        out_shape=[
            shape((rows, width // 2), jnp.float32),
            shape((rows, width // 2), jnp.bfloat16),
            shape((heads, padded, LANES), jnp.bfloat16),
        ],
        in_specs=[whole] * 6,
        out_specs=[whole] * 3,
        compiler_params=pltpu.CompilerParams(vmem_limit_bytes=56 * 2**20),
        cost_estimate=cost(6),
    )(part, tokens, attended, mine, other, w_out_t)


def features_kernel(joined_ref, w_ref, mlp_ref, tok_ref, sent_ref, gain_ref):
    grad = times_t(joined_ref[...], w_ref[...]) + wide(mlp_ref[...])
    sent_ref[...] = low(grad)
    x = wide(tok_ref[...])
    x = x - jnp.mean(x, axis=1, keepdims=True)
    x = x * lax.rsqrt(jnp.mean(x * x, axis=1, keepdims=True) + EPSILON)

    @pl.when(pl.program_id(0) == 0)
    def _():
        gain_ref[...] = jnp.zeros_like(gain_ref)

    gain_ref[0:1, :] += jnp.sum(grad * x, axis=0, keepdims=True)


def features(first, count, grad_joined, w_qkv, grad_mlp, tokens):
    rows, width = tokens.shape
    tile = 2 * PATCHES
    row_tile = lambda columns: pl.BlockSpec((tile, columns), lambda step: (step + first, 0))
    return pl.pallas_call(
        features_kernel,
        name="features",
        grid=(count,),
        out_shape=[
            jax.ShapeDtypeStruct((tile * count, width), jnp.bfloat16),
            jax.ShapeDtypeStruct((8, width), jnp.float32),
        ],
        in_specs=[
            row_tile(grad_joined.shape[1]),
            pl.BlockSpec(w_qkv.shape, lambda step: (0, 0)),
            row_tile(width),
            row_tile(width),
        ],
        out_specs=[
            pl.BlockSpec((tile, width), lambda step: (step, 0)),
            pl.BlockSpec((8, width), lambda step: (0, 0)),
        ],
        compiler_params=pltpu.CompilerParams(vmem_limit_bytes=40 * 2**20),
        cost_estimate=cost(0.3 * count),
    )(grad_joined, w_qkv, grad_mlp, tokens)


def weights_kernel(*refs):
    keep_ref, send_ref = refs[-2:]
    groups, rows, _ = keep_ref.shape
    first_side = lax.axis_index("hid") == 0
    at = 0
    for left_ref, right_ref in zip(refs[:-2:2], refs[1:-2:2]):
        total = rows_t(left_ref[...], right_ref[...])
        cols = slice(at, at + total.shape[1])
        at = cols.stop
        for group in range(groups):
            even, odd = (total[(2 * group + side) * rows : (2 * group + side + 1) * rows] for side in (0, 1))
            keep_ref[group, :, cols] = jnp.where(first_side, even, odd)
            send_ref[group, :, cols] = low(jnp.where(first_side, odd, even))


def weights(*pairs):
    whole = pl.BlockSpec(memory_space=VMEM)
    groups = lax.axis_size("dp")
    columns = sum(right.shape[1] for right in pairs[1::2])
    shape = (groups, pairs[0].shape[1] // (2 * groups), columns)
    return pl.pallas_call(
        weights_kernel,
        name="weights",
        out_shape=[jax.ShapeDtypeStruct(shape, jnp.float32), jax.ShapeDtypeStruct(shape, jnp.bfloat16)],
        in_specs=[whole] * len(pairs),
        out_specs=[whole] * 2,
        compiler_params=pltpu.CompilerParams(vmem_limit_bytes=48 * 2**20),
        cost_estimate=cost(1),
    )(*pairs)


def tokens_kernel(sent_ref, came_ref, tok_ref, gain_ref, mine_ref, other_ref, *refs):
    out_ref = refs[-1]
    half = mine_ref.shape[1]
    grad = (wide(sent_ref[...]) + wide(came_ref[...])) * wide(gain_ref[...])
    x = wide(tok_ref[...])
    x = x - jnp.mean(x, axis=1, keepdims=True)
    inverse = lax.rsqrt(jnp.mean(x * x, axis=1, keepdims=True) + EPSILON)
    x = x * inverse
    inner = jnp.mean(grad * x, axis=1, keepdims=True)
    grad = inverse * (grad - jnp.mean(grad, axis=1, keepdims=True) - x * inner)
    first, second = in_order(wide(mine_ref[...]), wide(other_ref[...]))
    out_ref[:, :half] = low(grad[:, :half] + first)
    out_ref[:, half:] = low(grad[:, half:] + second)


def token_rows(first, sent, came, tokens, norm_gain, mine, other, before):
    rows, width = tokens.shape
    tile = 2 * PATCHES
    count = sent.shape[0] // tile
    near = lambda columns: pl.BlockSpec((tile, columns), lambda step: (step, 0))
    far = lambda columns: pl.BlockSpec((tile, columns), lambda step: (step + first, 0))
    more = [] if before is None else [before]
    return pl.pallas_call(
        tokens_kernel,
        name="token_rows",
        grid=(count,),
        out_shape=jax.ShapeDtypeStruct((rows, width), jnp.bfloat16),
        in_specs=[
            near(width),
            near(width),
            far(width),
            pl.BlockSpec((1, width), lambda step: (0, 0)),
            far(width // 2),
            far(width // 2),
        ]
        + [pl.BlockSpec(memory_space=pl.ANY)] * len(more),
        out_specs=far(width),
        input_output_aliases={6: 0} if more else {},
        compiler_params=pltpu.CompilerParams(vmem_limit_bytes=40 * 2**20),
        cost_estimate=cost(0.3 * count),
    )(sent, came, tokens, norm_gain.reshape(1, -1), mine, other, *more)


def swap(value, axis, bit):
    size = lax.axis_size(axis)
    return lax.ppermute(value, axis, [(place, place ^ bit) for place in range(size)])


def bits_of(axis):
    size = lax.axis_size(axis)
    return [1 << place for place in range(size.bit_length() - 1)]


def gather_pieces(block, axis):
    pieces = [block]
    for bit in bits_of(axis):
        held = pieces[0] if len(pieces) == 1 else jnp.concatenate(pieces, axis=1)
        pieces.append(swap(held, axis, bit))
    return pieces


def scatter_pieces(pieces, axis):
    for bit in reversed(bits_of(axis)):
        sent = swap(low(pieces[-1]), axis, bit)
        kept, at, half = [], 0, sent.shape[1] // 2
        for piece in pieces[:-1]:
            size = piece.shape[1] // 2
            parts = (sent[:, at : at + size], sent[:, half + at : half + at + size])
            kept.append(wide(piece) + wide(jnp.concatenate(parts, axis=1) if size < half else sent))
            at += size
        pieces = kept
    return pieces[0]


def row_blocks(*pairs):
    groups, sides = lax.axis_size("dp"), lax.axis_size("hid")
    if sides == 2 and pairs[0].shape[1] % (16 * groups * sides) == 0:
        keep, send = weights(*pairs)
        return keep + wide(swap(send, "hid", 1))
    total = jnp.concatenate([rows_t(*pairs[at : at + 2]) for at in range(0, len(pairs), 2)], axis=1)
    shaped = total.reshape(groups, sides, -1, total.shape[1])
    shaped = shaped[:, lax.axis_index("hid") ^ jnp.arange(sides)]
    for bit in reversed(bits_of("hid")):
        shaped = shaped[:, :bit] + wide(swap(low(shaped[:, bit:]), "hid", bit))
    return shaped[:, 0]


def halve(shaped):
    count, rows, columns = shaped.shape
    shaped = shaped.reshape(count // 2, 2, rows, columns)
    odd = (lax.axis_index("dp") & 1) > 0
    sent = low(jnp.where(odd, shaped[:, 0], shaped[:, 1]))
    return jnp.where(odd, shaped[:, 1], shaped[:, 0]), swap(sent, "dp", 1)


def sum_rest(kept, came):
    count = lax.axis_size("dp")
    groups = [list(range(odd, count, 2)) for odd in (0, 1)]
    total = low(wide(kept) + wide(came))
    total = lax.all_to_all(total, "dp", 0, 0, axis_index_groups=groups, tiled=True)
    return jnp.sum(wide(total), axis=0)


def sum_everywhere(value, axes):
    for axis in axes:
        for bit in bits_of(axis):
            value = value + swap(value, axis, bit)
    return value


def shards(tokens, big_images, norm_gain, w_qkv, qk_gains, w_out_t, w_in, w_back, cotangent):
    width = tokens.shape[1]
    size = qk_gains.shape[1]
    groups = lax.axis_size("dp")
    other = swap(cotangent, "hg", 1)
    w_in_pieces = gather_pieces(w_in, "hid")
    w_back_pieces = gather_pieces(w_back, "hid")
    normed, q_rows, k_rows, v_rows, attended, inverses = forward(
        big_images, tokens, norm_gain, w_qkv, qk_gains
    )
    part, grad_mlp, grad_out, *grads = dense(normed, cotangent, other, w_in_pieces, w_back_pieces)
    kept, sent, do_rows = outputs(part, tokens, attended, cotangent, other, w_out_t)
    out_came = swap(sent, "hg", 1)
    mlp_kept, mlp_came = halve(scatter_pieces(grads, "hid").reshape(groups, width // groups, -1))
    do_rows, mlp_kept = lax.optimization_barrier((do_rows, mlp_kept))

    grad_joined, qk_part = backward(big_images, q_rows, k_rows, v_rows, do_rows, inverses, qk_gains)
    grad_joined, out_came, mlp_came = lax.optimization_barrier((grad_joined, out_came, mlp_came))
    output = low(kept + wide(out_came))
    token_grad, gain_part, mine, came = None, 0.0, [], []
    for tile in range(tokens.shape[0] // (2 * PATCHES)):
        rows, gains = features(tile, 1, grad_joined, w_qkv, grad_mlp, tokens)
        grad_joined, rows = lax.optimization_barrier((grad_joined, rows))
        mine.append(rows)
        gain_part = gain_part + gains[0]
    for rows in mine:
        came.append(swap(rows, "hg", 1))
    mlp_grads = sum_rest(mlp_kept, mlp_came)
    w_in_grad, w_back_grad = jnp.split(mlp_grads, 2, axis=1)

    blocks = row_blocks(normed, grad_joined, grad_out, attended)
    blocks, came[0] = lax.optimization_barrier((blocks, came[0]))
    kept, blocks_came = halve(blocks)
    blocks_came, came[1] = lax.optimization_barrier((blocks_came, came[1]))
    both = sum_rest(kept, blocks_came)
    w_qkv_grad, w_out_t_grad = both[:, : w_qkv.shape[1]], both[:, w_qkv.shape[1] :]

    small = jnp.concatenate([gain_part, qk_part[:2, :size].reshape(-1)])
    small = sum_everywhere(small, ("hid", "hg", "dp"))
    own = lax.axis_index("dp") * lax.axis_size("hid") + lax.axis_index("hid")
    gain_rows = width // (groups * lax.axis_size("hid"))
    norm_gain_grad = lax.dynamic_slice_in_dim(small, own * gain_rows, gain_rows, 0)
    qk_gains_grad = small[width:].reshape(2, size)
    for tile, (rows, others) in enumerate(zip(mine, came)):
        token_grad = token_rows(tile, rows, others, tokens, norm_gain, cotangent, other, token_grad)
    return (
        output,
        token_grad,
        norm_gain_grad,
        w_qkv_grad,
        qk_gains_grad,
        w_out_t_grad,
        w_in_grad,
        w_back_grad,
    )


def solution(mesh):
    return jax.shard_map(
        shards,
        mesh=mesh,
        in_specs=(
            P(("dp", "hid"), None),
            P(("dp", "hid")),
            P(),
            P(None, "hg"),
            P(),
            P(None, "hg"),
            P(None, ("hg", "hid")),
            P(None, ("hg", "hid")),
            P(("dp", "hid"), "hg"),
        ),
        out_specs=(
            P(("dp", "hid"), "hg"),
            P(("dp", "hid"), None),
            P(("dp", "hid")),
            P(("dp", "hid"), "hg"),
            P(),
            P(("dp", "hid"), "hg"),
            P("dp", ("hg", "hid")),
            P("dp", ("hg", "hid")),
        ),
        check_vma=False,
    )
```

```python
import functools
import math

import jax
import jax.numpy as jnp
from jax import lax
from jax.experimental import pallas as pl
from jax.experimental.pallas import tpu as pltpu
from jax.sharding import PartitionSpec as P

PATCHES = 196
EPSILON = 1e-06
LOG2E = math.log2(math.e)
LANES = 128
VMEM = pltpu.VMEM
SCALE = 1.0


def cost(microseconds):
    return pl.CostEstimate(
        flops=int(microseconds * SCALE * 1e9), bytes_accessed=2**20, transcendentals=0
    )


def times_t(left, right):
    return lax.dot_general(
        left, right, (((1,), (1,)), ((), ())), preferred_element_type=jnp.float32
    )


def rows_t(left, right):
    return lax.dot_general(
        left, right, (((0,), (0,)), ((), ())), preferred_element_type=jnp.float32
    )


def times(left, right):
    return jnp.dot(left, right, preferred_element_type=jnp.float32)


def low(value):
    return value.astype(jnp.bfloat16)


def wide(value):
    return value.astype(jnp.float32)


def lane_of(shape):
    return lax.broadcasted_iota(jnp.int32, shape, 1)


def row_of(shape):
    return lax.broadcasted_iota(jnp.int32, shape, 0)


def other_half(value):
    return pltpu.roll(value, LANES // 2, 1)


def three_terms(column, shape):
    lane = lane_of(shape)
    whole = jnp.broadcast_to(column, shape)
    first = wide(low(whole))
    second = wide(low(whole - first))
    third = whole - first - second
    return jnp.where(lane == 64, first, jnp.where(lane == 65, second, jnp.where(lane == 66, third, 0.0)))


def pair_mask(block, shape, first_lane):
    start = 2 * PATCHES * block - first_lane
    place = lane_of(shape) - start
    second = row_of(shape) >= PATCHES
    begin = jnp.where(second, PATCHES, 0)
    return (place >= begin) & (place < begin + PATCHES)


def window_of(block):
    return (2 * PATCHES * block // LANES) * LANES, 4 * LANES


def forward_kernel(
    flag_ref, tok_ref, gain_ref, w_ref, qk_ref, normed_ref, q_ref, k_ref, v_ref, att_ref, inv_ref
):
    rows = tok_ref.shape[0]
    heads, padded, _ = q_ref.shape
    tile = 2 * PATCHES
    size = qk_ref.shape[1]
    columns = w_ref.shape[1]
    gain = wide(gain_ref[...])
    q_gain = wide(qk_ref[0:1, :]) * (size**-0.5 * LOG2E)
    k_gain = wide(qk_ref[1:2, :])
    ones = jnp.ones_like(k_gain)
    gains = jnp.concatenate([q_gain, k_gain, ones, q_gain, k_gain, ones], axis=1)
    is_value = jnp.concatenate([0 * ones, 0 * ones, ones, 0 * ones, 0 * ones, ones], axis=1)
    group_a = row_of((256, 256)) // size
    group_b = lane_of((256, 256)) // size
    mean_of = low(jnp.where(group_a == group_b, 1.0 / size, 0.0))
    lane = lane_of((tile, LANES))
    for start in range(0, rows, tile):
        here = slice(start, start + tile)
        x = wide(tok_ref[here, :])
        x = x - jnp.mean(x, axis=1, keepdims=True)
        x = x * lax.rsqrt(jnp.mean(x * x, axis=1, keepdims=True) + EPSILON)
        normed = low(x * gain)
        normed_ref[here, :] = normed
        compact = jnp.zeros((tile, LANES), jnp.float32)
        for pair in range(heads // 2):
            joined = times(normed, w_ref[:, 384 * pair : 384 * pair + 384])
            parts = []
            for at in (0, 256):
                wid = min(256, 384 - at)
                block = joined[:, at : at + wid]
                means = mean_of[:wid, :wid]
                centred = block - times(low(block), means)
                squares = low(centred * centred)
                variance = times(squares, means)
                place = 6 * pair + at // size
                pick = low(
                    jnp.where(
                        row_of((wid, LANES)) // size + place == lane_of((wid, LANES)), 1.0 / size, 0.0
                    )
                )
                compact = compact + times(squares, pick)
                hat = centred * lax.rsqrt(variance + EPSILON)
                parts.append(
                    jnp.where(is_value[:, at : at + wid] > 0, block, hat * gains[:, at : at + wid])
                )
            b0, b1, b2 = parts[0][:, :128], parts[0][:, 128:], parts[1]
            first = lane < 64
            unit = jnp.where(lane < 67, 1.0, 0.0)
            q_ref[2 * pair, here, :] = low(jnp.where(first, b0, 0.0))
            k_ref[2 * pair, here, :] = low(jnp.where(first, other_half(b0), unit))
            v_ref[2 * pair, here, :] = low(jnp.where(first, b1, unit))
            q_ref[2 * pair + 1, here, :] = low(jnp.where(first, other_half(b1), 0.0))
            k_ref[2 * pair + 1, here, :] = low(jnp.where(first, b2, unit))
            v_ref[2 * pair + 1, here, :] = low(jnp.where(first, other_half(b2), unit))
        inv_ref[here, :] = lax.rsqrt(compact + EPSILON)
    for ref in (q_ref, k_ref, v_ref):
        ref[:, rows:, :] = jnp.zeros((heads, padded - rows, LANES), jnp.bfloat16)

    def attend(pair, _, big):
        for start in range(0, rows, tile):
            here = slice(start, start + tile)
            if big:
                keys = slice(0, padded)
            else:
                begin, length = window_of(start // tile)
                keys = slice(begin, begin + length)
            found = []
            for side in range(2):
                head = 2 * pair + side
                queries = q_ref[head, here, :]
                scores = times_t(queries, k_ref[head, keys, :])
                if not big:
                    scores = jnp.where(
                        pair_mask(start // tile, scores.shape, keys.start), scores, -1e30
                    )
                expo = low(jnp.exp2(scores))
                out = times(expo, v_ref[head, keys, :])
                total = out[:, 64:65]
                found.append(out * (1.0 / total))
                log_total = jnp.log(total) * (-LOG2E)
                q_ref[head, here, :] = low(
                    jnp.where(lane < 64, wide(queries), three_terms(log_total, lane.shape))
                )
            att_ref[here, pl.ds(pl.multiple_of(pair * LANES, LANES), LANES)] = low(
                jnp.where(lane < 64, found[0], other_half(found[1]))
            )
        return 0

    @pl.when(flag_ref[0] > 0)
    def _():
        lax.fori_loop(0, heads // 2, functools.partial(attend, big=True), 0)

    @pl.when(flag_ref[0] <= 0)
    def _():
        lax.fori_loop(0, heads // 2, functools.partial(attend, big=False), 0)


def forward(big_images, tokens, norm_gain, w_qkv, qk_gains):
    rows, width = tokens.shape
    size = qk_gains.shape[1]
    heads = w_qkv.shape[1] // (3 * size)
    padded = -(-rows // 256) * 256
    whole = pl.BlockSpec(memory_space=VMEM)
    head_rows = jax.ShapeDtypeStruct((heads, padded, LANES), jnp.bfloat16)
    return pl.pallas_call(
        forward_kernel,
        name="forward",
        out_shape=[
            jax.ShapeDtypeStruct((rows, width), jnp.bfloat16),
            head_rows,
            head_rows,
            head_rows,
            jax.ShapeDtypeStruct((rows, heads * size), jnp.bfloat16),
            jax.ShapeDtypeStruct((rows, LANES), jnp.float32),
        ],
        in_specs=[pl.BlockSpec(memory_space=pltpu.SMEM)] + [whole] * 4,
        out_specs=[whole] * 6,
        compiler_params=pltpu.CompilerParams(vmem_limit_bytes=56 * 2**20),
        cost_estimate=cost(24),
    )(big_images, tokens, norm_gain.reshape(1, -1), w_qkv, qk_gains)


def backward_kernel(
    flag_ref, q_ref, k_ref, v_ref, do_ref, inv_ref, qk_ref, joined_ref, small_ref, dq_ref, dk_ref, dv_ref
):
    pair = pl.program_id(0)
    rows = inv_ref.shape[0]
    padded = q_ref.shape[1]
    tile = 2 * PATCHES
    size = qk_ref.shape[1]
    scale = size**-0.5
    zeros = jnp.zeros((1, LANES - size), jnp.float32)
    q_gain = wide(qk_ref[0:1, :])
    k_gain = wide(qk_ref[1:2, :])
    q_back = jnp.concatenate([1.0 / (q_gain * (scale * LOG2E)), zeros], axis=1)
    k_back = jnp.concatenate([1.0 / k_gain, zeros], axis=1)
    q_gain = jnp.concatenate([q_gain, zeros], axis=1)
    k_gain = jnp.concatenate([k_gain, zeros], axis=1)

    def attend(side, _, big):
        for start in range(0, rows, tile):
            here = slice(start, start + tile)
            if big:
                over = slice(0, padded)
            else:
                begin, length = window_of(start // tile)
                over = slice(begin, begin + length)
            keys = k_ref[side, here, :]
            queries = q_ref[side, over, :]
            grads = do_ref[side, over, :]
            scores = times_t(keys, queries)
            if not big:
                scores = jnp.where(pair_mask(start // tile, scores.shape, over.start), scores, -1e30)
            probs = jnp.exp2(scores)
            grad_probs = times_t(v_ref[side, here, :], grads)
            grad_scores = low(probs * grad_probs)
            dv_ref[side, here, :] = times(low(probs), grads)
            dk_ref[side, here, :] = times(grad_scores, queries)
            more = rows_t(keys, grad_scores)
            if big and start == 0:
                dq_ref[side, :, over] = more
            elif big:
                dq_ref[side, :, over] += more
            else:
                place = lane_of(more.shape) - (start - over.start)
                dq_ref[side, :, over] = jnp.where(
                    (place >= 0) & (place < tile), more, dq_ref[side, :, over]
                )
        return 0

    @pl.when(flag_ref[0] > 0)
    def _():
        lax.fori_loop(0, 2, functools.partial(attend, big=True), 0)

    @pl.when(flag_ref[0] <= 0)
    def _():
        lax.fori_loop(0, 2, functools.partial(attend, big=False), 0)

    @pl.when(pair == 0)
    def _():
        small_ref[...] = jnp.zeros_like(small_ref)

    lane = lane_of((tile, LANES))
    first = lane < 64
    all_places = lane_of((rows, LANES)) - 6 * pair

    def undo(grad, hat, gain, inverse):
        grad_hat = grad * gain
        mean = jnp.sum(grad_hat, axis=1, keepdims=True) * (1.0 / size)
        inner = jnp.sum(grad_hat * hat, axis=1, keepdims=True) * (1.0 / size)
        return inverse * (grad_hat - mean - hat * inner)

    for start in range(0, rows, tile):
        here = slice(start, start + tile)
        blocks = []
        for side in range(2):
            inverses = inv_ref[here, :]
            place = lane - 6 * pair
            q_at, k_at = (0, 1) if side == 0 else (3, 4)
            q_inv = jnp.sum(jnp.where(place == q_at, inverses, 0.0), axis=1, keepdims=True)
            k_inv = jnp.sum(jnp.where(place == k_at, inverses, 0.0), axis=1, keepdims=True)
            q_hat = wide(q_ref[side, here, :]) * q_back
            k_hat = wide(k_ref[side, here, :]) * k_back
            grad_q = dq_ref[side, :, here].T * scale
            grad_k = dk_ref[side, here, :] * math.log(2.0)
            small_ref[0:1, :] += jnp.sum(jnp.where(first, grad_q * q_hat, 0.0), axis=0, keepdims=True)
            small_ref[1:2, :] += jnp.sum(jnp.where(first, grad_k * k_hat, 0.0), axis=0, keepdims=True)
            blocks.append(
                (
                    undo(grad_q, q_hat, q_gain, q_inv),
                    undo(grad_k, k_hat, k_gain, k_inv),
                    dv_ref[side, here, :],
                )
            )
        (q0, k0, v0), (q1, k1, v1) = blocks
        joined_ref[here, 0:128] = low(jnp.where(first, q0, other_half(k0)))
        joined_ref[here, 128:256] = low(jnp.where(first, v0, other_half(q1)))
        joined_ref[here, 256:384] = low(jnp.where(first, k1, other_half(v1)))


def backward(big_images, q_rows, k_rows, v_rows, do_rows, inverses, qk_gains):
    heads, padded, _ = q_rows.shape
    rows = inverses.shape[0]
    pair_spec = pl.BlockSpec((2, padded, LANES), lambda pair: (pair, 0, 0))
    return pl.pallas_call(
        backward_kernel,
        name="backward",
        grid=(heads // 2,),
        out_shape=[
            jax.ShapeDtypeStruct((rows, heads * 3 * LANES // 2), jnp.bfloat16),
            jax.ShapeDtypeStruct((8, LANES), jnp.float32),
        ],
        in_specs=[pl.BlockSpec(memory_space=pltpu.SMEM)]
        + [pair_spec] * 4
        + [pl.BlockSpec((rows, LANES), lambda pair: (0, 0)), pl.BlockSpec(qk_gains.shape, lambda pair: (0, 0))],
        out_specs=[
            pl.BlockSpec((rows, 3 * LANES), lambda pair: (0, pair)),
            pl.BlockSpec((8, LANES), lambda pair: (0, 0)),
        ],
        scratch_shapes=[
            VMEM((2, LANES, padded), jnp.float32),
            VMEM((2, rows, LANES), jnp.float32),
            VMEM((2, rows, LANES), jnp.float32),
        ],
        compiler_params=pltpu.CompilerParams(vmem_limit_bytes=56 * 2**20),
        cost_estimate=cost(36),
    )(big_images, q_rows, k_rows, v_rows, do_rows, inverses, qk_gains)


def in_order(mine, other):
    first = lax.axis_index("hg") == 0
    return jnp.where(first, mine, other), jnp.where(first, other, mine)


def dense_kernel(count, normed_ref, mine_ref, other_ref, *refs):
    w_in_refs, w_back_refs = refs[:count], refs[count : 2 * count]
    refs = refs[2 * count :]
    part_ref, grad_ref, dy_ref = refs[:3]
    grad_refs, refs = refs[3 : 3 + count], refs[3 + count :]
    act_refs, gup_refs = refs[:count], refs[count:]
    rows, width = normed_ref.shape
    half = width // 2
    tile = 2 * PATCHES
    dy_ref[:, :half], dy_ref[:, half:] = in_order(mine_ref[...], other_ref[...])
    curve = math.sqrt(2.0 / math.pi)

    for start in range(0, rows, tile):
        here = slice(start, start + tile)
        for w_in_ref, w_back_ref, act_ref, gup_ref in zip(w_in_refs, w_back_refs, act_refs, gup_refs):
            columns = w_in_ref.shape[1]
            step = min(256, columns)
            normed = normed_ref[here, :]
            dy = dy_ref[here, :]
            for at in range(0, columns, step):
                cols = slice(at, min(at + step, columns))
                up = times(normed, w_in_ref[:, cols])
                grad_act = times(dy, w_back_ref[:, cols])
                square = up * up
                bent = jnp.tanh(up * (curve + (curve * 0.044715) * square))
                gate = 0.5 + 0.5 * bent
                act = up * gate
                slope = gate + act * ((1.0 - gate) * (2 * curve + (6 * curve * 0.044715) * square))
                act_ref[here, cols] = low(act)
                gup_ref[here, cols] = low(grad_act * slope)
        total, grad = None, None
        for act_ref, w_back_ref, gup_ref, w_in_ref in zip(act_refs, w_back_refs, gup_refs, w_in_refs):
            part = times_t(act_ref[here, :], w_back_ref[...])
            total = part if total is None else total + part
            part = times_t(gup_ref[here, :], w_in_ref[...])
            grad = part if grad is None else grad + part
        part_ref[here, :] = total
        grad_ref[here, :] = low(grad)
    for act_ref, gup_ref, ref in zip(act_refs, gup_refs, grad_refs):
        columns = act_ref.shape[1]
        ref[:, :columns] = rows_t(normed_ref[...], gup_ref[...]).astype(ref.dtype)
        ref[:, columns:] = rows_t(dy_ref[...], act_ref[...]).astype(ref.dtype)


def dense(normed, mine, other, w_in_pieces, w_back_pieces):
    rows, width = normed.shape
    count = len(w_in_pieces)
    whole = pl.BlockSpec(memory_space=VMEM)
    shape = jax.ShapeDtypeStruct
    sizes = [piece.shape[1] for piece in w_in_pieces]
    kinds = [jnp.float32] * (count - 1) + [jnp.bfloat16] if count > 1 else [jnp.float32]
    hidden = sum(sizes)
    return pl.pallas_call(
        functools.partial(dense_kernel, count),
        name="dense",
        out_shape=[
            shape((rows, width), jnp.float32),
            shape((rows, width), jnp.bfloat16),
            shape((rows, width), jnp.bfloat16),
        ]
        + [shape((width, 2 * size), kind) for size, kind in zip(sizes, kinds)],
        in_specs=[whole] * (3 + 2 * count),
        out_specs=[whole] * (3 + count),
        scratch_shapes=[VMEM((rows, size), jnp.bfloat16) for size in sizes] * 2,
        compiler_params=pltpu.CompilerParams(vmem_limit_bytes=60 * 2**20),
        cost_estimate=cost(24),
    )(normed, mine, other, *w_in_pieces, *w_back_pieces)


def outputs_kernel(
    part_ref, tok_ref, att_ref, mine_ref, other_ref, w_out_ref, keep_ref, send_ref, do_ref
):
    rows, width = part_ref.shape
    half = width // 2
    heads, padded, _ = do_ref.shape
    tile = 2 * PATCHES
    lane = lane_of((tile, LANES))
    for start in range(0, rows, tile):
        here = slice(start, start + tile)
        attended = att_ref[here, :]
        left = times_t(attended, w_out_ref[...]) + part_ref[here, :]
        token = tok_ref[here, :]
        keep, send = in_order(left[:, :half], left[:, half:])
        keep_ref[here, :] = keep + in_order(wide(token[:, :half]), wide(token[:, half:]))[0]
        send_ref[here, :] = low(send)
        first, second = in_order(mine_ref[here, :], other_ref[here, :])
        grad_att = times(first, w_out_ref[:half, :]) + times(second, w_out_ref[half:, :])
        for pair in range(heads // 2):
            cols = slice(pair * LANES, pair * LANES + LANES)
            low_block = wide(low(grad_att[:, cols]))
            weighed = low_block * wide(attended[:, cols])
            for side in range(2):
                mine = lane < 64 if side == 0 else lane >= 64
                inner = jnp.sum(jnp.where(mine, weighed, 0.0), axis=1, keepdims=True)
                value = low_block if side == 0 else other_half(low_block)
                do_ref[2 * pair + side, here, :] = low(
                    jnp.where(lane < 64, value, three_terms(-inner, lane.shape))
                )
    do_ref[:, rows:, :] = jnp.zeros((heads, padded - rows, LANES), jnp.bfloat16)


def outputs(part, tokens, attended, mine, other, w_out_t):
    rows, width = tokens.shape
    heads = w_out_t.shape[1] // 64
    padded = -(-rows // 256) * 256
    whole = pl.BlockSpec(memory_space=VMEM)
    shape = jax.ShapeDtypeStruct
    return pl.pallas_call(
        outputs_kernel,
        name="outputs",
        out_shape=[
            shape((rows, width // 2), jnp.float32),
            shape((rows, width // 2), jnp.bfloat16),
            shape((heads, padded, LANES), jnp.bfloat16),
        ],
        in_specs=[whole] * 6,
        out_specs=[whole] * 3,
        compiler_params=pltpu.CompilerParams(vmem_limit_bytes=56 * 2**20),
        cost_estimate=cost(6),
    )(part, tokens, attended, mine, other, w_out_t)


def features_kernel(joined_ref, w_ref, mlp_ref, tok_ref, sent_ref, gain_ref):
    grad = times_t(joined_ref[...], w_ref[...]) + wide(mlp_ref[...])
    sent_ref[...] = low(grad)
    x = wide(tok_ref[...])
    x = x - jnp.mean(x, axis=1, keepdims=True)
    x = x * lax.rsqrt(jnp.mean(x * x, axis=1, keepdims=True) + EPSILON)

    @pl.when(pl.program_id(0) == 0)
    def _():
        gain_ref[...] = jnp.zeros_like(gain_ref)

    gain_ref[0:1, :] += jnp.sum(grad * x, axis=0, keepdims=True)


def features(first, count, grad_joined, w_qkv, grad_mlp, tokens):
    rows, width = tokens.shape
    tile = 2 * PATCHES
    row_tile = lambda columns: pl.BlockSpec((tile, columns), lambda step: (step + first, 0))
    return pl.pallas_call(
        features_kernel,
        name="features",
        grid=(count,),
        out_shape=[
            jax.ShapeDtypeStruct((tile * count, width), jnp.bfloat16),
            jax.ShapeDtypeStruct((8, width), jnp.float32),
        ],
        in_specs=[
            row_tile(grad_joined.shape[1]),
            pl.BlockSpec(w_qkv.shape, lambda step: (0, 0)),
            row_tile(width),
            row_tile(width),
        ],
        out_specs=[
            pl.BlockSpec((tile, width), lambda step: (step, 0)),
            pl.BlockSpec((8, width), lambda step: (0, 0)),
        ],
        compiler_params=pltpu.CompilerParams(vmem_limit_bytes=40 * 2**20),
        cost_estimate=cost(0.3 * count),
    )(grad_joined, w_qkv, grad_mlp, tokens)


def weights_kernel(*refs):
    keep_ref, send_ref = refs[-2:]
    groups, rows, _ = keep_ref.shape
    first_side = lax.axis_index("hid") == 0
    at = 0
    for left_ref, right_ref in zip(refs[:-2:2], refs[1:-2:2]):
        total = rows_t(left_ref[...], right_ref[...])
        cols = slice(at, at + total.shape[1])
        at = cols.stop
        for group in range(groups):
            even, odd = (total[(2 * group + side) * rows : (2 * group + side + 1) * rows] for side in (0, 1))
            keep_ref[group, :, cols] = jnp.where(first_side, even, odd)
            send_ref[group, :, cols] = low(jnp.where(first_side, odd, even))


def weights(*pairs):
    whole = pl.BlockSpec(memory_space=VMEM)
    groups = lax.axis_size("dp")
    columns = sum(right.shape[1] for right in pairs[1::2])
    shape = (groups, pairs[0].shape[1] // (2 * groups), columns)
    return pl.pallas_call(
        weights_kernel,
        name="weights",
        out_shape=[jax.ShapeDtypeStruct(shape, jnp.float32), jax.ShapeDtypeStruct(shape, jnp.bfloat16)],
        in_specs=[whole] * len(pairs),
        out_specs=[whole] * 2,
        compiler_params=pltpu.CompilerParams(vmem_limit_bytes=48 * 2**20),
        cost_estimate=cost(1),
    )(*pairs)


def tokens_kernel(sent_ref, came_ref, tok_ref, gain_ref, mine_ref, other_ref, *refs):
    out_ref = refs[-1]
    half = mine_ref.shape[1]
    grad = (wide(sent_ref[...]) + wide(came_ref[...])) * wide(gain_ref[...])
    x = wide(tok_ref[...])
    x = x - jnp.mean(x, axis=1, keepdims=True)
    inverse = lax.rsqrt(jnp.mean(x * x, axis=1, keepdims=True) + EPSILON)
    x = x * inverse
    inner = jnp.mean(grad * x, axis=1, keepdims=True)
    grad = inverse * (grad - jnp.mean(grad, axis=1, keepdims=True) - x * inner)
    first, second = in_order(wide(mine_ref[...]), wide(other_ref[...]))
    out_ref[:, :half] = low(grad[:, :half] + first)
    out_ref[:, half:] = low(grad[:, half:] + second)


def token_rows(first, sent, came, tokens, norm_gain, mine, other, before):
    rows, width = tokens.shape
    tile = 2 * PATCHES
    count = sent.shape[0] // tile
    near = lambda columns: pl.BlockSpec((tile, columns), lambda step: (step, 0))
    far = lambda columns: pl.BlockSpec((tile, columns), lambda step: (step + first, 0))
    more = [] if before is None else [before]
    return pl.pallas_call(
        tokens_kernel,
        name="token_rows",
        grid=(count,),
        out_shape=jax.ShapeDtypeStruct((rows, width), jnp.bfloat16),
        in_specs=[
            near(width),
            near(width),
            far(width),
            pl.BlockSpec((1, width), lambda step: (0, 0)),
            far(width // 2),
            far(width // 2),
        ]
        + [pl.BlockSpec(memory_space=pl.ANY)] * len(more),
        out_specs=far(width),
        input_output_aliases={6: 0} if more else {},
        compiler_params=pltpu.CompilerParams(vmem_limit_bytes=40 * 2**20),
        cost_estimate=cost(0.3 * count),
    )(sent, came, tokens, norm_gain.reshape(1, -1), mine, other, *more)


def swap(value, axis, bit):
    size = lax.axis_size(axis)
    return lax.ppermute(value, axis, [(place, place ^ bit) for place in range(size)])


def bits_of(axis):
    size = lax.axis_size(axis)
    return [1 << place for place in range(size.bit_length() - 1)]


def gather_pieces(block, axis):
    pieces = [block]
    for bit in bits_of(axis):
        held = pieces[0] if len(pieces) == 1 else jnp.concatenate(pieces, axis=1)
        pieces.append(swap(held, axis, bit))
    return pieces


def scatter_pieces(pieces, axis):
    for bit in reversed(bits_of(axis)):
        sent = swap(low(pieces[-1]), axis, bit)
        kept, at, half = [], 0, sent.shape[1] // 2
        for piece in pieces[:-1]:
            size = piece.shape[1] // 2
            parts = (sent[:, at : at + size], sent[:, half + at : half + at + size])
            kept.append(wide(piece) + wide(jnp.concatenate(parts, axis=1) if size < half else sent))
            at += size
        pieces = kept
    return pieces[0]


def row_blocks(*pairs):
    groups, sides = lax.axis_size("dp"), lax.axis_size("hid")
    if sides == 2 and pairs[0].shape[1] % (16 * groups * sides) == 0:
        keep, send = weights(*pairs)
        return keep + wide(swap(send, "hid", 1))
    total = jnp.concatenate([rows_t(*pairs[at : at + 2]) for at in range(0, len(pairs), 2)], axis=1)
    shaped = total.reshape(groups, sides, -1, total.shape[1])
    shaped = shaped[:, lax.axis_index("hid") ^ jnp.arange(sides)]
    for bit in reversed(bits_of("hid")):
        shaped = shaped[:, :bit] + wide(swap(low(shaped[:, bit:]), "hid", bit))
    return shaped[:, 0]


def halve(shaped):
    count, rows, columns = shaped.shape
    shaped = shaped.reshape(count // 2, 2, rows, columns)
    odd = (lax.axis_index("dp") & 1) > 0
    sent = low(jnp.where(odd, shaped[:, 0], shaped[:, 1]))
    return jnp.where(odd, shaped[:, 1], shaped[:, 0]), swap(sent, "dp", 1)


def sum_rest(kept, came):
    count = lax.axis_size("dp")
    groups = [list(range(odd, count, 2)) for odd in (0, 1)]
    total = low(wide(kept) + wide(came))
    total = lax.all_to_all(total, "dp", 0, 0, axis_index_groups=groups, tiled=True)
    return jnp.sum(wide(total), axis=0)


def sum_far(kept, came):
    total = low(wide(kept) + wide(came))
    me = lax.axis_index("dp") // 2
    terms = [lax.dynamic_index_in_dim(total, me, keepdims=False)]
    for step in range(1, total.shape[0]):
        block = lax.dynamic_index_in_dim(total, me ^ step, keepdims=False)
        terms.append(swap(block, "dp", 2 * step))
    return sum(wide(term) for term in terms)


def sum_everywhere(value, axes):
    for axis in axes:
        for bit in bits_of(axis):
            value = value + swap(value, axis, bit)
    return value


def shards(tokens, big_images, norm_gain, w_qkv, qk_gains, w_out_t, w_in, w_back, cotangent):
    width = tokens.shape[1]
    size = qk_gains.shape[1]
    groups = lax.axis_size("dp")
    other = swap(cotangent, "hg", 1)
    w_in_pieces = gather_pieces(w_in, "hid")
    w_back_pieces = gather_pieces(w_back, "hid")
    normed, q_rows, k_rows, v_rows, attended, inverses = forward(
        big_images, tokens, norm_gain, w_qkv, qk_gains
    )
    part, grad_mlp, grad_out, *grads = dense(normed, cotangent, other, w_in_pieces, w_back_pieces)
    kept, sent, do_rows = outputs(part, tokens, attended, cotangent, other, w_out_t)
    out_came = swap(sent, "hg", 1)
    mlp_kept, mlp_came = halve(scatter_pieces(grads, "hid").reshape(groups, width // groups, -1))
    do_rows, mlp_kept = lax.optimization_barrier((do_rows, mlp_kept))

    grad_joined, qk_part = backward(big_images, q_rows, k_rows, v_rows, do_rows, inverses, qk_gains)
    grad_joined, out_came, mlp_came = lax.optimization_barrier((grad_joined, out_came, mlp_came))
    output = low(kept + wide(out_came))
    mine, gain_part = features(0, tokens.shape[0] // (2 * PATCHES), grad_joined, w_qkv, grad_mlp, tokens)
    came = swap(mine, "hg", 1)

    def weight_sums(normed, grad_joined, grad_out, attended, mlp_kept, mlp_came, gain_part, qk_part):
        blocks = row_blocks(normed, grad_joined, grad_out, attended)
        mlp_grads = sum_rest(mlp_kept, mlp_came)
        both = sum_far(*halve(blocks))
        small = jnp.concatenate([gain_part[0], qk_part[:2, :size].reshape(-1)])
        return mlp_grads, both, sum_everywhere(small, ("hid", "hg", "dp"))

    def no_sums(*operands):
        return tuple(jnp.zeros(kind.shape, kind.dtype) for kind in kinds)

    operands = (normed, grad_joined, grad_out, attended, mlp_kept, mlp_came, gain_part, qk_part)
    kinds = jax.eval_shape(weight_sums, *operands)
    mlp_grads, both, small = lax.cond(big_images[0] >= 0, weight_sums, no_sums, *operands)
    came, small = lax.optimization_barrier((came, small))
    w_in_grad, w_back_grad = jnp.split(mlp_grads, 2, axis=1)
    w_qkv_grad, w_out_t_grad = both[:, : w_qkv.shape[1]], both[:, w_qkv.shape[1] :]
    own = lax.axis_index("dp") * lax.axis_size("hid") + lax.axis_index("hid")
    gain_rows = width // (groups * lax.axis_size("hid"))
    norm_gain_grad = lax.dynamic_slice_in_dim(small, own * gain_rows, gain_rows, 0)
    qk_gains_grad = small[width:].reshape(2, size)
    token_grad = token_rows(0, mine, came, tokens, norm_gain, cotangent, other, None)
    return (
        output,
        token_grad,
        norm_gain_grad,
        w_qkv_grad,
        qk_gains_grad,
        w_out_t_grad,
        w_in_grad,
        w_back_grad,
    )


def solution(mesh):
    return jax.shard_map(
        shards,
        mesh=mesh,
        in_specs=(
            P(("dp", "hid"), None),
            P(("dp", "hid")),
            P(),
            P(None, "hg"),
            P(),
            P(None, "hg"),
            P(None, ("hg", "hid")),
            P(None, ("hg", "hid")),
            P(("dp", "hid"), "hg"),
        ),
        out_specs=(
            P(("dp", "hid"), "hg"),
            P(("dp", "hid"), None),
            P(("dp", "hid")),
            P(("dp", "hid"), "hg"),
            P(),
            P(("dp", "hid"), "hg"),
            P("dp", ("hg", "hid")),
            P("dp", ("hg", "hid")),
        ),
        check_vma=False,
    )
```

```python
import functools
import math

import jax
import jax.numpy as jnp
from jax import lax
from jax.experimental import pallas as pl
from jax.experimental.pallas import tpu as pltpu
from jax.sharding import PartitionSpec as P

PATCHES = 196
EPSILON = 1e-06
LOG2E = math.log2(math.e)
LANES = 128
VMEM = pltpu.VMEM
SCALE = 1.0


def cost(microseconds):
    return pl.CostEstimate(
        flops=int(microseconds * SCALE * 1e9), bytes_accessed=2**20, transcendentals=0
    )


def times_t(left, right):
    return lax.dot_general(
        left, right, (((1,), (1,)), ((), ())), preferred_element_type=jnp.float32
    )


def rows_t(left, right):
    return lax.dot_general(
        left, right, (((0,), (0,)), ((), ())), preferred_element_type=jnp.float32
    )


def times(left, right):
    return jnp.dot(left, right, preferred_element_type=jnp.float32)


def low(value):
    return value.astype(jnp.bfloat16)


def wide(value):
    return value.astype(jnp.float32)


def lane_of(shape):
    return lax.broadcasted_iota(jnp.int32, shape, 1)


def row_of(shape):
    return lax.broadcasted_iota(jnp.int32, shape, 0)


def other_half(value):
    return pltpu.roll(value, LANES // 2, 1)


def spread_terms(whole):
    lane = lane_of(whole.shape)
    first = wide(low(whole))
    second = wide(low(whole - first))
    third = whole - first - second
    return jnp.where(lane == 64, first, jnp.where(lane == 65, second, jnp.where(lane == 66, third, 0.0)))


def three_terms(column, shape):
    return spread_terms(jnp.broadcast_to(column, shape))


def two_terms(value):
    first = low(value)
    return first, low(value - wide(first))


def pair_mask(block, shape, first_lane):
    start = 2 * PATCHES * block - first_lane
    place = lane_of(shape) - start
    second = row_of(shape) >= PATCHES
    begin = jnp.where(second, PATCHES, 0)
    return (place >= begin) & (place < begin + PATCHES)


def window_of(block):
    return (2 * PATCHES * block // LANES) * LANES, 4 * LANES


def forward_kernel(
    flag_ref, tok_ref, gain_ref, w_ref, qk_ref, normed_ref, q_ref, k_ref, v_ref, att_ref, inv_ref
):
    rows = tok_ref.shape[0]
    heads, padded, _ = q_ref.shape
    tile = 2 * PATCHES
    size = qk_ref.shape[1]
    columns = w_ref.shape[1]
    gain = wide(gain_ref[...])
    q_gain = wide(qk_ref[0:1, :]) * (size**-0.5 * LOG2E)
    k_gain = wide(qk_ref[1:2, :])
    ones = jnp.ones_like(k_gain)
    gains = jnp.concatenate([q_gain, k_gain, ones, q_gain, k_gain, ones], axis=1)
    is_value = jnp.concatenate([0 * ones, 0 * ones, ones, 0 * ones, 0 * ones, ones], axis=1)
    group_a = row_of((256, 256)) // size
    group_b = lane_of((256, 256)) // size
    mean_of = low(jnp.where(group_a == group_b, 1.0 / size, 0.0))
    stride = rows // (3 * LANES) and 3 * LANES
    strip = rows - (rows // stride - 1) * stride
    lane = lane_of((strip, LANES))

    def project(step, _):
        here = pl.ds(pl.multiple_of(step * stride, LANES), strip)
        x = wide(tok_ref[here, :])
        x = x - jnp.mean(x, axis=1, keepdims=True)
        x = x * lax.rsqrt(jnp.mean(x * x, axis=1, keepdims=True) + EPSILON)
        normed = low(x * gain)
        normed_ref[here, :] = normed
        compact = jnp.zeros((strip, LANES), jnp.float32)
        for pair in range(heads // 2):
            joined = times(normed, w_ref[:, 384 * pair : 384 * pair + 384])
            parts = []
            for at in (0, 256):
                wid = min(256, 384 - at)
                block = joined[:, at : at + wid]
                means = mean_of[:wid, :wid]
                centred = block - times(low(block), means)
                squares = low(centred * centred)
                variance = times(squares, means)
                place = 6 * pair + at // size
                pick = low(
                    jnp.where(
                        row_of((wid, LANES)) // size + place == lane_of((wid, LANES)), 1.0 / size, 0.0
                    )
                )
                compact = compact + times(squares, pick)
                hat = centred * lax.rsqrt(variance + EPSILON)
                parts.append(
                    jnp.where(is_value[:, at : at + wid] > 0, block, hat * gains[:, at : at + wid])
                )
            b0, b1, b2 = parts[0][:, :128], parts[0][:, 128:], parts[1]
            first = lane < 64
            unit = jnp.where(lane < 67, 1.0, 0.0)
            q_ref[2 * pair, here, :] = low(jnp.where(first, b0, 0.0))
            k_ref[2 * pair, here, :] = low(jnp.where(first, other_half(b0), unit))
            v_ref[2 * pair, here, :] = low(jnp.where(first, b1, unit))
            q_ref[2 * pair + 1, here, :] = low(jnp.where(first, other_half(b1), 0.0))
            k_ref[2 * pair + 1, here, :] = low(jnp.where(first, b2, unit))
            v_ref[2 * pair + 1, here, :] = low(jnp.where(first, other_half(b2), unit))
        inv_ref[here, :] = lax.rsqrt(compact + EPSILON)
        return 0

    lax.fori_loop(0, rows // stride, project, 0)
    lane = lane_of((tile, LANES))
    for ref in (q_ref, k_ref, v_ref):
        ref[:, rows:, :] = jnp.zeros((heads, padded - rows, LANES), jnp.bfloat16)

    def attend(pair, _, big):
        for start in range(0, rows, tile):
            here = slice(start, start + tile)
            if big:
                keys = slice(0, padded)
            else:
                begin, length = window_of(start // tile)
                keys = slice(begin, begin + length)
            found = []
            for side in range(2):
                head = 2 * pair + side
                queries = q_ref[head, here, :]
                scores = times_t(queries, k_ref[head, keys, :])
                if not big:
                    scores = jnp.where(
                        pair_mask(start // tile, scores.shape, keys.start), scores, -1e30
                    )
                expo = low(jnp.exp2(scores))
                out = times(expo, v_ref[head, keys, :])
                total = out[:, 64:65]
                found.append(out * (1.0 / total))
                log_total = jnp.log(total) * (-LOG2E)
                q_ref[head, here, :] = low(
                    jnp.where(lane < 64, wide(queries), three_terms(log_total, lane.shape))
                )
            att_ref[here, pl.ds(pl.multiple_of(pair * LANES, LANES), LANES)] = low(
                jnp.where(lane < 64, found[0], other_half(found[1]))
            )
        return 0

    @pl.when(flag_ref[0] > 0)
    def _():
        lax.fori_loop(0, heads // 2, functools.partial(attend, big=True), 0)

    @pl.when(flag_ref[0] <= 0)
    def _():
        lax.fori_loop(0, heads // 2, functools.partial(attend, big=False), 0)


def forward(big_images, tokens, norm_gain, w_qkv, qk_gains):
    rows, width = tokens.shape
    size = qk_gains.shape[1]
    heads = w_qkv.shape[1] // (3 * size)
    padded = -(-rows // 256) * 256
    whole = pl.BlockSpec(memory_space=VMEM)
    head_rows = jax.ShapeDtypeStruct((heads, padded, LANES), jnp.bfloat16)
    return pl.pallas_call(
        forward_kernel,
        name="forward",
        out_shape=[
            jax.ShapeDtypeStruct((rows, width), jnp.bfloat16),
            head_rows,
            head_rows,
            head_rows,
            jax.ShapeDtypeStruct((rows, heads * size), jnp.bfloat16),
            jax.ShapeDtypeStruct((rows, LANES), jnp.float32),
        ],
        in_specs=[pl.BlockSpec(memory_space=pltpu.SMEM)] + [whole] * 4,
        out_specs=[whole] * 6,
        compiler_params=pltpu.CompilerParams(vmem_limit_bytes=56 * 2**20),
        cost_estimate=cost(24),
    )(big_images, tokens, norm_gain.reshape(1, -1), w_qkv, qk_gains)


def backward_kernel(
    flag_ref, q_ref, k_ref, v_ref, do_ref, inv_ref, qk_ref, joined_ref, small_ref, dq_ref, dk_ref, dv_ref, turned_ref
):
    pair = pl.program_id(0)
    rows = inv_ref.shape[0]
    padded = q_ref.shape[1]
    tile = 2 * PATCHES
    size = qk_ref.shape[1]
    scale = size**-0.5
    zeros = jnp.zeros((1, LANES - size), jnp.float32)
    q_gain = wide(qk_ref[0:1, :])
    k_gain = wide(qk_ref[1:2, :])
    q_back = jnp.concatenate([1.0 / (q_gain * (scale * LOG2E)), zeros], axis=1)
    k_back = jnp.concatenate([1.0 / k_gain, zeros], axis=1)
    q_gain = jnp.concatenate([q_gain, zeros], axis=1)
    k_gain = jnp.concatenate([k_gain, zeros], axis=1)

    def attend(side, _, big):
        for start in range(0, rows, tile):
            here = slice(start, start + tile)
            if big:
                over = slice(0, padded)
            else:
                begin, length = window_of(start // tile)
                over = slice(begin, begin + length)
            keys = k_ref[side, here, :]
            queries = q_ref[side, over, :]
            grads = do_ref[side, over, :]
            scores = times_t(keys, queries)
            if not big:
                scores = jnp.where(pair_mask(start // tile, scores.shape, over.start), scores, -1e30)
            probs = jnp.exp2(scores)
            grad_probs = times_t(v_ref[side, here, :], grads)
            grad_scores = low(probs * grad_probs)
            dv_ref[side, here, :] = times(low(probs), grads)
            dk_ref[side, here, :] = times(grad_scores, queries)
            more = rows_t(keys, grad_scores)
            if big and start == 0:
                dq_ref[side, :, over] = more
            elif big:
                dq_ref[side, :, over] += more
            else:
                place = lane_of(more.shape) - (start - over.start)
                dq_ref[side, :, over] = jnp.where(
                    (place >= 0) & (place < tile), more, dq_ref[side, :, over]
                )
        return 0

    @pl.when(flag_ref[0] > 0)
    def _():
        lax.fori_loop(0, 2, functools.partial(attend, big=True), 0)

    @pl.when(flag_ref[0] <= 0)
    def _():
        lax.fori_loop(0, 2, functools.partial(attend, big=False), 0)

    @pl.when(pair == 0)
    def _():
        small_ref[...] = jnp.zeros_like(small_ref)

    lane = lane_of((tile, LANES))
    first = lane < 64
    shape = (2 * LANES, 2 * LANES)
    row, column = row_of(shape), lane_of(shape)
    means = (row // LANES == column // LANES) & (row % LANES < size)
    means = low(jnp.where(means, 1.0 / size, 0.0))
    gains = jnp.concatenate([q_gain * scale, k_gain * math.log(2.0)], axis=1)
    factors = jnp.concatenate([jnp.full_like(q_gain, scale), jnp.full_like(k_gain, math.log(2.0))], axis=1)
    backs = jnp.concatenate([q_back, k_back], axis=1)
    for side in range(2):
        turned_ref[side] = dq_ref[side].T
    for start in range(0, rows, tile):
        here = slice(start, start + tile)
        inverse_first, inverse_second = two_terms(inv_ref[here, :])
        blocks = []
        for side in range(2):
            shape = (LANES, 2 * LANES)
            source = 6 * pair + 3 * side + lane_of(shape) // LANES
            pick = low(jnp.where(row_of(shape) == source, 1.0, 0.0))
            inverse = times(inverse_first, pick) + times(inverse_second, pick)
            hat = jnp.concatenate([q_ref[side, here, :], k_ref[side, here, :]], axis=1)
            hat = wide(hat) * backs
            grad = jnp.concatenate([turned_ref[side, here, :], dk_ref[side, here, :]], axis=1)
            small_ref[0:1, :] += jnp.sum(grad * hat, axis=0, keepdims=True) * factors
            grad = grad * gains
            inner = times(low(grad * hat), means)
            grad = inverse * (grad - times(low(grad), means) - hat * inner)
            blocks.append((grad[:, :LANES], grad[:, LANES:], dv_ref[side, here, :]))
        (q0, k0, v0), (q1, k1, v1) = blocks
        joined_ref[here, 0:128] = low(jnp.where(first, q0, other_half(k0)))
        joined_ref[here, 128:256] = low(jnp.where(first, v0, other_half(q1)))
        joined_ref[here, 256:384] = low(jnp.where(first, k1, other_half(v1)))


def backward(big_images, q_rows, k_rows, v_rows, do_rows, inverses, qk_gains):
    heads, padded, _ = q_rows.shape
    rows = inverses.shape[0]
    pair_spec = pl.BlockSpec((2, padded, LANES), lambda pair: (pair, 0, 0))
    return pl.pallas_call(
        backward_kernel,
        name="backward",
        grid=(heads // 2,),
        out_shape=[
            jax.ShapeDtypeStruct((rows, heads * 3 * LANES // 2), jnp.bfloat16),
            jax.ShapeDtypeStruct((8, 2 * LANES), jnp.float32),
        ],
        in_specs=[pl.BlockSpec(memory_space=pltpu.SMEM)]
        + [pair_spec] * 4
        + [pl.BlockSpec((rows, LANES), lambda pair: (0, 0)), pl.BlockSpec(qk_gains.shape, lambda pair: (0, 0))],
        out_specs=[
            pl.BlockSpec((rows, 3 * LANES), lambda pair: (0, pair)),
            pl.BlockSpec((8, 2 * LANES), lambda pair: (0, 0)),
        ],
        scratch_shapes=[
            VMEM((2, LANES, padded), jnp.float32),
            VMEM((2, rows, LANES), jnp.float32),
            VMEM((2, rows, LANES), jnp.float32),
            VMEM((2, padded, LANES), jnp.float32),
        ],
        compiler_params=pltpu.CompilerParams(vmem_limit_bytes=56 * 2**20),
        cost_estimate=cost(36),
    )(big_images, q_rows, k_rows, v_rows, do_rows, inverses, qk_gains)


def in_order(mine, other):
    first = lax.axis_index("hg") == 0
    return jnp.where(first, mine, other), jnp.where(first, other, mine)


def dense_kernel(count, tiles, normed_ref, mine_ref, other_ref, *refs):
    w_in_refs, w_back_refs = refs[:count], refs[count : 2 * count]
    refs = refs[2 * count :]
    part_ref, grad_ref, dy_ref = refs[:3]
    grad_refs, refs = refs[3 : 3 + count], refs[3 + count :]
    normed_rows, dy_rows = refs[:2]
    act_refs, gup_refs = refs[2 : 2 + count], refs[2 + count :]
    step = pl.program_id(0)
    half = mine_ref.shape[1]
    curve = math.sqrt(2.0 / math.pi)
    normed = normed_ref[...]
    first, second = in_order(mine_ref[...], other_ref[...])
    dy_ref[:, :half], dy_ref[:, half:] = first, second
    dy = dy_ref[...]
    normed_rows[step] = normed
    dy_rows[step] = dy
    for w_in_ref, w_back_ref, act_ref, gup_ref in zip(w_in_refs, w_back_refs, act_refs, gup_refs):
        columns = w_in_ref.shape[1]
        width = min(256, columns)
        for at in range(0, columns, width):
            cols = slice(at, min(at + width, columns))
            up = times(normed, w_in_ref[:, cols])
            grad_act = times(dy, w_back_ref[:, cols])
            square = up * up
            bent = jnp.tanh(up * (curve + (curve * 0.044715) * square))
            gate = 0.5 + 0.5 * bent
            act = up * gate
            slope = gate + act * ((1.0 - gate) * (2 * curve + (6 * curve * 0.044715) * square))
            act_ref[step, :, cols] = low(act)
            gup_ref[step, :, cols] = low(grad_act * slope)
    total, grad = None, None
    for act_ref, w_back_ref, gup_ref, w_in_ref in zip(act_refs, w_back_refs, gup_refs, w_in_refs):
        part = times_t(act_ref[step], w_back_ref[...])
        total = part if total is None else total + part
        part = times_t(gup_ref[step], w_in_ref[...])
        grad = part if grad is None else grad + part
    part_ref[...] = total
    grad_ref[...] = low(grad)

    @pl.when(step == tiles - 1)
    def _():
        for act_ref, gup_ref, ref in zip(act_refs, gup_refs, grad_refs):
            columns = act_ref.shape[2]
            for left, right, at in ((normed_rows, gup_ref, 0), (dy_rows, act_ref, columns)):
                rows = tiles * left.shape[1]
                total = rows_t(left[...].reshape(rows, -1), right[...].reshape(rows, columns))
                ref[:, at : at + columns] = total.astype(ref.dtype)


def dense(normed, mine, other, w_in_pieces, w_back_pieces):
    rows, width = normed.shape
    tile = 2 * PATCHES
    tiles = rows // tile
    count = len(w_in_pieces)
    shape = jax.ShapeDtypeStruct
    sizes = [piece.shape[1] for piece in w_in_pieces]
    kinds = [jnp.float32] * (count - 1) + [jnp.bfloat16] if count > 1 else [jnp.float32]
    row_tile = lambda columns: pl.BlockSpec((tile, columns), lambda step: (step, 0))
    fixed = lambda columns: pl.BlockSpec((width, columns), lambda step: (0, 0))
    once = lambda columns: pl.BlockSpec((width, columns), lambda step: (0, 0), pipeline_mode=pl.Buffered(1))
    return pl.pallas_call(
        functools.partial(dense_kernel, count, tiles),
        name="dense",
        grid=(tiles,),
        out_shape=[
            shape((rows, width), jnp.float32),
            shape((rows, width), jnp.bfloat16),
            shape((rows, width), jnp.bfloat16),
        ]
        + [shape((width, 2 * size), kind) for size, kind in zip(sizes, kinds)],
        in_specs=[row_tile(width), row_tile(width // 2), row_tile(width // 2)]
        + [once(size) for size in sizes] * 2,
        out_specs=[row_tile(width)] * 3 + [fixed(2 * size) for size in sizes],
        scratch_shapes=[VMEM((tiles, tile, width), jnp.bfloat16)] * 2
        + [VMEM((tiles, tile, size), jnp.bfloat16) for size in sizes] * 2,
        compiler_params=pltpu.CompilerParams(vmem_limit_bytes=60 * 2**20),
        cost_estimate=cost(24),
    )(normed, mine, other, *w_in_pieces, *w_back_pieces)


def outputs_kernel(part_ref, tok_ref, att_ref, mine_ref, other_ref, w_out_ref, keep_ref, send_ref, do_ref):
    tile, width = part_ref.shape
    half = width // 2
    heads, padded, _ = do_ref.shape
    lane = lane_of((tile, LANES))
    attended = att_ref[...]
    left = times_t(attended, w_out_ref[...]) + part_ref[...]
    token = tok_ref[...]
    keep, send = in_order(left[:, :half], left[:, half:])
    keep_ref[...] = keep + in_order(wide(token[:, :half]), wide(token[:, half:]))[0]
    send_ref[...] = low(send)
    first, second = in_order(mine_ref[...], other_ref[...])
    grad_att = times(first, w_out_ref[:half, :]) + times(second, w_out_ref[half:, :])
    shape = (LANES, 2 * LANES)
    row, column = row_of(shape), lane_of(shape)
    inners = (row // 64 == column // LANES) & (column % LANES >= 64) & (column % LANES < 67)
    inners = low(jnp.where(inners, -1.0, 0.0))
    found = []
    for pair in range(heads // 2):
        cols = slice(pair * LANES, pair * LANES + LANES)
        low_block = wide(low(grad_att[:, cols]))
        weighed, rest = two_terms(low_block * wide(attended[:, cols]))
        inner = times(weighed, inners) + times(rest, inners)
        for side in range(2):
            value = low_block if side == 0 else other_half(low_block)
            term = spread_terms(inner[:, side * LANES : (side + 1) * LANES])
            found.append(low(jnp.where(lane < 64, value, term)))
    for step in range(3):

        @pl.when(pl.program_id(0) == step)
        def _(step=step):
            for head in range(heads):
                do_ref[head, step * tile : (step + 1) * tile, :] = found[head]
            if step == 2:
                do_ref[:, 3 * tile :, :] = jnp.zeros((heads, padded - 3 * tile, LANES), jnp.bfloat16)


def outputs(part, tokens, attended, mine, other, w_out_t):
    rows, width = tokens.shape
    tile = 2 * PATCHES
    heads = w_out_t.shape[1] // 64
    padded = -(-rows // 256) * 256
    shape = jax.ShapeDtypeStruct
    row_tile = lambda columns: pl.BlockSpec((tile, columns), lambda step: (step, 0))
    return pl.pallas_call(
        outputs_kernel,
        name="outputs",
        grid=(rows // tile,),
        out_shape=[
            shape((rows, width // 2), jnp.float32),
            shape((rows, width // 2), jnp.bfloat16),
            shape((heads, padded, LANES), jnp.bfloat16),
        ],
        in_specs=[row_tile(columns) for columns in (width, width, width // 2, width // 2, width // 2)]
        + [pl.BlockSpec(w_out_t.shape, lambda step: (0, 0))],
        out_specs=[
            row_tile(width // 2),
            row_tile(width // 2),
            pl.BlockSpec((heads, padded, LANES), lambda step: (0, 0, 0)),
        ],
        compiler_params=pltpu.CompilerParams(vmem_limit_bytes=56 * 2**20),
        cost_estimate=cost(6),
    )(part, tokens, attended, mine, other, w_out_t)


def features_kernel(joined_ref, w_ref, mlp_ref, tok_ref, sent_ref, gain_ref):
    grad = times_t(joined_ref[...], w_ref[...]) + wide(mlp_ref[...])
    sent_ref[...] = low(grad)
    x = wide(tok_ref[...])
    x = x - jnp.mean(x, axis=1, keepdims=True)
    x = x * lax.rsqrt(jnp.mean(x * x, axis=1, keepdims=True) + EPSILON)

    @pl.when(pl.program_id(0) == 0)
    def _():
        gain_ref[...] = jnp.zeros_like(gain_ref)

    gain_ref[0:1, :] += jnp.sum(grad * x, axis=0, keepdims=True)


def features(first, count, grad_joined, w_qkv, grad_mlp, tokens):
    rows, width = tokens.shape
    tile = 2 * PATCHES
    row_tile = lambda columns: pl.BlockSpec((tile, columns), lambda step: (step + first, 0))
    return pl.pallas_call(
        features_kernel,
        name="features",
        grid=(count,),
        out_shape=[
            jax.ShapeDtypeStruct((tile * count, width), jnp.bfloat16),
            jax.ShapeDtypeStruct((8, width), jnp.float32),
        ],
        in_specs=[
            row_tile(grad_joined.shape[1]),
            pl.BlockSpec(w_qkv.shape, lambda step: (0, 0)),
            row_tile(width),
            row_tile(width),
        ],
        out_specs=[
            pl.BlockSpec((tile, width), lambda step: (step, 0)),
            pl.BlockSpec((8, width), lambda step: (0, 0)),
        ],
        compiler_params=pltpu.CompilerParams(vmem_limit_bytes=40 * 2**20),
        cost_estimate=cost(0.3 * count),
    )(grad_joined, w_qkv, grad_mlp, tokens)


def weights_kernel(*refs):
    keep_ref, send_ref = refs[-2:]
    groups, rows, _ = keep_ref.shape
    first_side = lax.axis_index("hid") == 0
    at = 0
    for left_ref, right_ref in zip(refs[:-2:2], refs[1:-2:2]):
        total = rows_t(left_ref[...], right_ref[...])
        cols = slice(at, at + total.shape[1])
        at = cols.stop
        for group in range(groups):
            even, odd = (total[(2 * group + side) * rows : (2 * group + side + 1) * rows] for side in (0, 1))
            keep_ref[group, :, cols] = jnp.where(first_side, even, odd)
            send_ref[group, :, cols] = low(jnp.where(first_side, odd, even))


def weights(*pairs):
    whole = pl.BlockSpec(memory_space=VMEM)
    groups = lax.axis_size("dp")
    columns = sum(right.shape[1] for right in pairs[1::2])
    shape = (groups, pairs[0].shape[1] // (2 * groups), columns)
    return pl.pallas_call(
        weights_kernel,
        name="weights",
        out_shape=[jax.ShapeDtypeStruct(shape, jnp.float32), jax.ShapeDtypeStruct(shape, jnp.bfloat16)],
        in_specs=[whole] * len(pairs),
        out_specs=[whole] * 2,
        compiler_params=pltpu.CompilerParams(vmem_limit_bytes=48 * 2**20),
        cost_estimate=cost(1),
    )(*pairs)


def tokens_kernel(sent_ref, came_ref, tok_ref, gain_ref, mine_ref, other_ref, *refs):
    out_ref = refs[-1]
    half = mine_ref.shape[1]
    grad = (wide(sent_ref[...]) + wide(came_ref[...])) * wide(gain_ref[...])
    x = wide(tok_ref[...])
    x = x - jnp.mean(x, axis=1, keepdims=True)
    inverse = lax.rsqrt(jnp.mean(x * x, axis=1, keepdims=True) + EPSILON)
    x = x * inverse
    inner = jnp.mean(grad * x, axis=1, keepdims=True)
    grad = inverse * (grad - jnp.mean(grad, axis=1, keepdims=True) - x * inner)
    first, second = in_order(wide(mine_ref[...]), wide(other_ref[...]))
    out_ref[:, :half] = low(grad[:, :half] + first)
    out_ref[:, half:] = low(grad[:, half:] + second)


def token_rows(first, sent, came, tokens, norm_gain, mine, other, before):
    rows, width = tokens.shape
    tile = 2 * PATCHES
    count = sent.shape[0] // tile
    near = lambda columns: pl.BlockSpec((tile, columns), lambda step: (step, 0))
    far = lambda columns: pl.BlockSpec((tile, columns), lambda step: (step + first, 0))
    more = [] if before is None else [before]
    return pl.pallas_call(
        tokens_kernel,
        name="token_rows",
        grid=(count,),
        out_shape=jax.ShapeDtypeStruct((rows, width), jnp.bfloat16),
        in_specs=[
            near(width),
            near(width),
            far(width),
            pl.BlockSpec((1, width), lambda step: (0, 0)),
            far(width // 2),
            far(width // 2),
        ]
        + [pl.BlockSpec(memory_space=pl.ANY)] * len(more),
        out_specs=far(width),
        input_output_aliases={6: 0} if more else {},
        compiler_params=pltpu.CompilerParams(vmem_limit_bytes=40 * 2**20),
        cost_estimate=cost(0.3 * count),
    )(sent, came, tokens, norm_gain.reshape(1, -1), mine, other, *more)


def swap(value, axis, bit):
    size = lax.axis_size(axis)
    return lax.ppermute(value, axis, [(place, place ^ bit) for place in range(size)])


def bits_of(axis):
    size = lax.axis_size(axis)
    return [1 << place for place in range(size.bit_length() - 1)]


def gather_pieces(block, axis):
    pieces = [block]
    for bit in bits_of(axis):
        held = pieces[0] if len(pieces) == 1 else jnp.concatenate(pieces, axis=1)
        pieces.append(swap(held, axis, bit))
    return pieces


def scatter_pieces(pieces, axis):
    for bit in reversed(bits_of(axis)):
        sent = swap(low(pieces[-1]), axis, bit)
        kept, at, half = [], 0, sent.shape[1] // 2
        for piece in pieces[:-1]:
            size = piece.shape[1] // 2
            parts = (sent[:, at : at + size], sent[:, half + at : half + at + size])
            kept.append(wide(piece) + wide(jnp.concatenate(parts, axis=1) if size < half else sent))
            at += size
        pieces = kept
    return pieces[0]


def row_blocks(*pairs):
    groups, sides = lax.axis_size("dp"), lax.axis_size("hid")
    if sides == 2 and pairs[0].shape[1] % (16 * groups * sides) == 0:
        keep, send = weights(*pairs)
        return keep + wide(swap(send, "hid", 1))
    total = jnp.concatenate([rows_t(*pairs[at : at + 2]) for at in range(0, len(pairs), 2)], axis=1)
    shaped = total.reshape(groups, sides, -1, total.shape[1])
    shaped = shaped[:, lax.axis_index("hid") ^ jnp.arange(sides)]
    for bit in reversed(bits_of("hid")):
        shaped = shaped[:, :bit] + wide(swap(low(shaped[:, bit:]), "hid", bit))
    return shaped[:, 0]


def halve(shaped):
    count, rows, columns = shaped.shape
    shaped = shaped.reshape(count // 2, 2, rows, columns)
    odd = (lax.axis_index("dp") & 1) > 0
    sent = low(jnp.where(odd, shaped[:, 0], shaped[:, 1]))
    return jnp.where(odd, shaped[:, 1], shaped[:, 0]), swap(sent, "dp", 1)


def sum_rest(kept, came):
    count = lax.axis_size("dp")
    groups = [list(range(odd, count, 2)) for odd in (0, 1)]
    total = low(wide(kept) + wide(came))
    total = lax.all_to_all(total, "dp", 0, 0, axis_index_groups=groups, tiled=True)
    return jnp.sum(wide(total), axis=0)


def sum_far(kept, came):
    total = low(wide(kept) + wide(came))
    me = lax.axis_index("dp") // 2
    terms = [lax.dynamic_index_in_dim(total, me, keepdims=False)]
    for step in range(1, total.shape[0]):
        block = lax.dynamic_index_in_dim(total, me ^ step, keepdims=False)
        terms.append(swap(block, "dp", 2 * step))
    return sum(wide(term) for term in terms)


def sum_everywhere(value, axes):
    for axis in axes:
        for bit in bits_of(axis):
            value = value + swap(value, axis, bit)
    return value


def shards(tokens, big_images, norm_gain, w_qkv, qk_gains, w_out_t, w_in, w_back, cotangent):
    width = tokens.shape[1]
    size = qk_gains.shape[1]
    groups = lax.axis_size("dp")
    other = swap(cotangent, "hg", 1)
    w_in_pieces = gather_pieces(w_in, "hid")
    w_back_pieces = gather_pieces(w_back, "hid")
    normed, q_rows, k_rows, v_rows, attended, inverses = forward(
        big_images, tokens, norm_gain, w_qkv, qk_gains
    )
    part, grad_mlp, grad_out, *grads = dense(normed, cotangent, other, w_in_pieces, w_back_pieces)
    kept, sent, do_rows = outputs(part, tokens, attended, cotangent, other, w_out_t)
    out_came = swap(sent, "hg", 1)
    mlp_kept, mlp_came = halve(scatter_pieces(grads, "hid").reshape(groups, width // groups, -1))
    do_rows, mlp_kept = lax.optimization_barrier((do_rows, mlp_kept))

    grad_joined, qk_part = backward(big_images, q_rows, k_rows, v_rows, do_rows, inverses, qk_gains)
    grad_joined, out_came, mlp_came = lax.optimization_barrier((grad_joined, out_came, mlp_came))
    mine, gain_part = features(0, tokens.shape[0] // (2 * PATCHES), grad_joined, w_qkv, grad_mlp, tokens)
    came = swap(mine, "hg", 1)

    def weight_sums(normed, grad_joined, grad_out, attended, mlp_kept, mlp_came, gain_part, qk_part, kept, out_came):
        blocks = row_blocks(normed, grad_joined, grad_out, attended)
        mlp_grads = sum_rest(mlp_kept, mlp_came)
        both = sum_far(*halve(blocks))
        small = jnp.concatenate([gain_part[0], qk_part[0, :size], qk_part[0, LANES : LANES + size]])
        small = sum_everywhere(small, ("hid", "dp"))
        return mlp_grads, both, small, low(kept + wide(out_came))

    def no_sums(*operands):
        return tuple(jnp.zeros(kind.shape, kind.dtype) for kind in kinds)

    operands = (normed, grad_joined, grad_out, attended, mlp_kept, mlp_came, gain_part, qk_part, kept, out_came)
    kinds = jax.eval_shape(weight_sums, *operands)
    mlp_grads, both, small, output = lax.cond(big_images[0] >= 0, weight_sums, no_sums, *operands)
    came, small = lax.optimization_barrier((came, small))
    small = sum_everywhere(small, ("hg",))
    w_in_grad, w_back_grad = jnp.split(mlp_grads, 2, axis=1)
    w_qkv_grad, w_out_t_grad = both[:, : w_qkv.shape[1]], both[:, w_qkv.shape[1] :]
    own = lax.axis_index("dp") * lax.axis_size("hid") + lax.axis_index("hid")
    gain_rows = width // (groups * lax.axis_size("hid"))
    norm_gain_grad = lax.dynamic_slice_in_dim(small, own * gain_rows, gain_rows, 0)
    qk_gains_grad = small[width:].reshape(2, size)
    token_grad = token_rows(0, mine, came, tokens, norm_gain, cotangent, other, None)
    return (
        output,
        token_grad,
        norm_gain_grad,
        w_qkv_grad,
        qk_gains_grad,
        w_out_t_grad,
        w_in_grad,
        w_back_grad,
    )


def solution(mesh):
    return jax.shard_map(
        shards,
        mesh=mesh,
        in_specs=(
            P(("dp", "hid"), None),
            P(("dp", "hid")),
            P(),
            P(None, "hg"),
            P(),
            P(None, "hg"),
            P(None, ("hg", "hid")),
            P(None, ("hg", "hid")),
            P(("dp", "hid"), "hg"),
        ),
        out_specs=(
            P(("dp", "hid"), "hg"),
            P(("dp", "hid"), None),
            P(("dp", "hid")),
            P(("dp", "hid"), "hg"),
            P(),
            P(("dp", "hid"), "hg"),
            P("dp", ("hg", "hid")),
            P("dp", ("hg", "hid")),
        ),
        check_vma=False,
    )
```

```python
import functools
import math

import jax
import jax.numpy as jnp
from jax import lax
from jax.experimental import pallas as pl
from jax.experimental.pallas import tpu as pltpu
from jax.sharding import PartitionSpec as P

PATCHES = 196
EPSILON = 1e-06
LOG2E = math.log2(math.e)
LANES = 128
VMEM = pltpu.VMEM
SCALE = 1.0


def cost(microseconds):
    return pl.CostEstimate(
        flops=int(microseconds * SCALE * 1e9), bytes_accessed=2**20, transcendentals=0
    )


def times_t(left, right):
    return lax.dot_general(
        left, right, (((1,), (1,)), ((), ())), preferred_element_type=jnp.float32
    )


def rows_t(left, right):
    return lax.dot_general(
        left, right, (((0,), (0,)), ((), ())), preferred_element_type=jnp.float32
    )


def times(left, right):
    return jnp.dot(left, right, preferred_element_type=jnp.float32)


def low(value):
    return value.astype(jnp.bfloat16)


def wide(value):
    return value.astype(jnp.float32)


def lane_of(shape):
    return lax.broadcasted_iota(jnp.int32, shape, 1)


def row_of(shape):
    return lax.broadcasted_iota(jnp.int32, shape, 0)


def other_half(value):
    return pltpu.roll(value, LANES // 2, 1)


def spread_terms(whole):
    lane = lane_of(whole.shape)
    first = wide(low(whole))
    second = wide(low(whole - first))
    third = whole - first - second
    return jnp.where(lane == 64, first, jnp.where(lane == 65, second, jnp.where(lane == 66, third, 0.0)))


def three_terms(column, shape):
    return spread_terms(jnp.broadcast_to(column, shape))


def two_terms(value):
    first = low(value)
    return first, low(value - wide(first))


def pair_mask(block, shape, first_lane):
    start = 2 * PATCHES * block - first_lane
    place = lane_of(shape) - start
    second = row_of(shape) >= PATCHES
    begin = jnp.where(second, PATCHES, 0)
    return (place >= begin) & (place < begin + PATCHES)


def window_of(block):
    return (2 * PATCHES * block // LANES) * LANES, 4 * LANES


def forward_kernel(
    flag_ref, tok_ref, gain_ref, w_ref, qk_ref, normed_ref, q_ref, k_ref, v_ref, att_ref, inv_ref
):
    rows = tok_ref.shape[0]
    heads, padded, _ = q_ref.shape
    tile = 2 * PATCHES
    size = qk_ref.shape[1]
    columns = w_ref.shape[1]
    gain = wide(gain_ref[...])
    q_gain = wide(qk_ref[0:1, :]) * (size**-0.5 * LOG2E)
    k_gain = wide(qk_ref[1:2, :])
    ones = jnp.ones_like(k_gain)
    gains = jnp.concatenate([q_gain, k_gain, ones, q_gain, k_gain, ones], axis=1)
    is_value = jnp.concatenate([0 * ones, 0 * ones, ones, 0 * ones, 0 * ones, ones], axis=1)
    group_a = row_of((256, 256)) // size
    group_b = lane_of((256, 256)) // size
    mean_of = low(jnp.where(group_a == group_b, 1.0 / size, 0.0))
    stride = rows // (3 * LANES) and 3 * LANES
    strip = rows - (rows // stride - 1) * stride
    lane = lane_of((strip, LANES))

    def project(step, _):
        here = pl.ds(pl.multiple_of(step * stride, LANES), strip)
        x = wide(tok_ref[here, :])
        x = x - jnp.mean(x, axis=1, keepdims=True)
        x = x * lax.rsqrt(jnp.mean(x * x, axis=1, keepdims=True) + EPSILON)
        normed = low(x * gain)
        normed_ref[here, :] = normed
        compact = jnp.zeros((strip, LANES), jnp.float32)
        for pair in range(heads // 2):
            joined = times(normed, w_ref[:, 384 * pair : 384 * pair + 384])
            parts = []
            for at in (0, 256):
                wid = min(256, 384 - at)
                block = joined[:, at : at + wid]
                means = mean_of[:wid, :wid]
                centred = block - times(low(block), means)
                squares = low(centred * centred)
                variance = times(squares, means)
                place = 6 * pair + at // size
                pick = low(
                    jnp.where(
                        row_of((wid, LANES)) // size + place == lane_of((wid, LANES)), 1.0 / size, 0.0
                    )
                )
                compact = compact + times(squares, pick)
                hat = centred * lax.rsqrt(variance + EPSILON)
                parts.append(
                    jnp.where(is_value[:, at : at + wid] > 0, block, hat * gains[:, at : at + wid])
                )
            b0, b1, b2 = parts[0][:, :128], parts[0][:, 128:], parts[1]
            first = lane < 64
            unit = jnp.where(lane < 67, 1.0, 0.0)
            q_ref[2 * pair, here, :] = low(jnp.where(first, b0, 0.0))
            k_ref[2 * pair, here, :] = low(jnp.where(first, other_half(b0), unit))
            v_ref[2 * pair, here, :] = low(jnp.where(first, b1, unit))
            q_ref[2 * pair + 1, here, :] = low(jnp.where(first, other_half(b1), 0.0))
            k_ref[2 * pair + 1, here, :] = low(jnp.where(first, b2, unit))
            v_ref[2 * pair + 1, here, :] = low(jnp.where(first, other_half(b2), unit))
        inv_ref[here, :] = lax.rsqrt(compact + EPSILON)
        return 0

    lax.fori_loop(0, rows // stride, project, 0)
    lane = lane_of((tile, LANES))
    for ref in (q_ref, k_ref, v_ref):
        ref[:, rows:, :] = jnp.zeros((heads, padded - rows, LANES), jnp.bfloat16)

    def attend(pair, _, big):
        for start in range(0, rows, tile):
            here = slice(start, start + tile)
            if big:
                keys = slice(0, padded)
            else:
                begin, length = window_of(start // tile)
                keys = slice(begin, begin + length)
            found = []
            for side in range(2):
                head = 2 * pair + side
                queries = q_ref[head, here, :]
                scores = times_t(queries, k_ref[head, keys, :])
                if not big:
                    scores = jnp.where(
                        pair_mask(start // tile, scores.shape, keys.start), scores, -1e30
                    )
                expo = low(jnp.exp2(scores))
                out = times(expo, v_ref[head, keys, :])
                total = out[:, 64:65]
                found.append(out * (1.0 / total))
                log_total = jnp.log(total) * (-LOG2E)
                q_ref[head, here, :] = low(
                    jnp.where(lane < 64, wide(queries), three_terms(log_total, lane.shape))
                )
            att_ref[here, pl.ds(pl.multiple_of(pair * LANES, LANES), LANES)] = low(
                jnp.where(lane < 64, found[0], other_half(found[1]))
            )
        return 0

    @pl.when(flag_ref[0] > 0)
    def _():
        lax.fori_loop(0, heads // 2, functools.partial(attend, big=True), 0)

    @pl.when(flag_ref[0] <= 0)
    def _():
        lax.fori_loop(0, heads // 2, functools.partial(attend, big=False), 0)


def forward(big_images, tokens, norm_gain, w_qkv, qk_gains):
    rows, width = tokens.shape
    size = qk_gains.shape[1]
    heads = w_qkv.shape[1] // (3 * size)
    padded = -(-rows // 256) * 256
    whole = pl.BlockSpec(memory_space=VMEM)
    head_rows = jax.ShapeDtypeStruct((heads, padded, LANES), jnp.bfloat16)
    return pl.pallas_call(
        forward_kernel,
        name="forward",
        out_shape=[
            jax.ShapeDtypeStruct((rows, width), jnp.bfloat16),
            head_rows,
            head_rows,
            head_rows,
            jax.ShapeDtypeStruct((rows, heads * size), jnp.bfloat16),
            jax.ShapeDtypeStruct((rows, LANES), jnp.float32),
        ],
        in_specs=[pl.BlockSpec(memory_space=pltpu.SMEM)] + [whole] * 4,
        out_specs=[whole] * 6,
        compiler_params=pltpu.CompilerParams(vmem_limit_bytes=56 * 2**20),
        cost_estimate=cost(24),
    )(big_images, tokens, norm_gain.reshape(1, -1), w_qkv, qk_gains)


def backward_kernel(
    flag_ref, q_ref, k_ref, v_ref, do_ref, inv_ref, qk_ref, joined_ref, small_ref, dq_ref, dk_ref, dv_ref, turned_ref
):
    pair = pl.program_id(0)
    rows = inv_ref.shape[0]
    padded = q_ref.shape[1]
    tile = 2 * PATCHES
    size = qk_ref.shape[1]
    scale = size**-0.5
    zeros = jnp.zeros((1, LANES - size), jnp.float32)
    q_gain = wide(qk_ref[0:1, :])
    k_gain = wide(qk_ref[1:2, :])
    q_back = jnp.concatenate([1.0 / (q_gain * (scale * LOG2E)), zeros], axis=1)
    k_back = jnp.concatenate([1.0 / k_gain, zeros], axis=1)
    q_gain = jnp.concatenate([q_gain, zeros], axis=1)
    k_gain = jnp.concatenate([k_gain, zeros], axis=1)

    def attend(side, _, big):
        for start in range(0, rows, tile):
            here = slice(start, start + tile)
            if big:
                over = slice(0, padded)
            else:
                begin, length = window_of(start // tile)
                over = slice(begin, begin + length)
            keys = k_ref[side, here, :]
            queries = q_ref[side, over, :]
            grads = do_ref[side, over, :]
            scores = times_t(keys, queries)
            if not big:
                scores = jnp.where(pair_mask(start // tile, scores.shape, over.start), scores, -1e30)
            probs = jnp.exp2(scores)
            grad_probs = times_t(v_ref[side, here, :], grads)
            grad_scores = low(probs * grad_probs)
            dv_ref[side, here, :] = times(low(probs), grads)
            dk_ref[side, here, :] = times(grad_scores, queries)
            more = rows_t(keys, grad_scores)
            if big and start == 0:
                dq_ref[side, :, over] = more
            elif big:
                dq_ref[side, :, over] += more
            else:
                place = lane_of(more.shape) - (start - over.start)
                dq_ref[side, :, over] = jnp.where(
                    (place >= 0) & (place < tile), more, dq_ref[side, :, over]
                )
        return 0

    @pl.when(flag_ref[0] > 0)
    def _():
        lax.fori_loop(0, 2, functools.partial(attend, big=True), 0)

    @pl.when(flag_ref[0] <= 0)
    def _():
        lax.fori_loop(0, 2, functools.partial(attend, big=False), 0)

    @pl.when(pair == 0)
    def _():
        small_ref[...] = jnp.zeros_like(small_ref)

    lane = lane_of((tile, LANES))
    first = lane < 64
    shape = (2 * LANES, 2 * LANES)
    row, column = row_of(shape), lane_of(shape)
    means = (row // LANES == column // LANES) & (row % LANES < size)
    means = low(jnp.where(means, 1.0 / size, 0.0))
    gains = jnp.concatenate([q_gain * scale, k_gain * math.log(2.0)], axis=1)
    factors = jnp.concatenate([jnp.full_like(q_gain, scale), jnp.full_like(k_gain, math.log(2.0))], axis=1)
    backs = jnp.concatenate([q_back, k_back], axis=1)
    for side in range(2):
        turned_ref[side] = dq_ref[side].T
    for start in range(0, rows, tile):
        here = slice(start, start + tile)
        inverse_first, inverse_second = two_terms(inv_ref[here, :])
        blocks = []
        for side in range(2):
            shape = (LANES, 2 * LANES)
            source = 6 * pair + 3 * side + lane_of(shape) // LANES
            pick = low(jnp.where(row_of(shape) == source, 1.0, 0.0))
            inverse = times(inverse_first, pick) + times(inverse_second, pick)
            hat = jnp.concatenate([q_ref[side, here, :], k_ref[side, here, :]], axis=1)
            hat = wide(hat) * backs
            grad = jnp.concatenate([turned_ref[side, here, :], dk_ref[side, here, :]], axis=1)
            small_ref[0:1, :] += jnp.sum(grad * hat, axis=0, keepdims=True) * factors
            grad = grad * gains
            inner = times(low(grad * hat), means)
            grad = inverse * (grad - times(low(grad), means) - hat * inner)
            blocks.append((grad[:, :LANES], grad[:, LANES:], dv_ref[side, here, :]))
        (q0, k0, v0), (q1, k1, v1) = blocks
        joined_ref[here, 0:128] = low(jnp.where(first, q0, other_half(k0)))
        joined_ref[here, 128:256] = low(jnp.where(first, v0, other_half(q1)))
        joined_ref[here, 256:384] = low(jnp.where(first, k1, other_half(v1)))


def backward(big_images, q_rows, k_rows, v_rows, do_rows, inverses, qk_gains):
    heads, padded, _ = q_rows.shape
    rows = inverses.shape[0]
    pair_spec = pl.BlockSpec((2, padded, LANES), lambda pair: (pair, 0, 0))
    return pl.pallas_call(
        backward_kernel,
        name="backward",
        grid=(heads // 2,),
        out_shape=[
            jax.ShapeDtypeStruct((rows, heads * 3 * LANES // 2), jnp.bfloat16),
            jax.ShapeDtypeStruct((8, 2 * LANES), jnp.float32),
        ],
        in_specs=[pl.BlockSpec(memory_space=pltpu.SMEM)]
        + [pair_spec] * 4
        + [pl.BlockSpec((rows, LANES), lambda pair: (0, 0)), pl.BlockSpec(qk_gains.shape, lambda pair: (0, 0))],
        out_specs=[
            pl.BlockSpec((rows, 3 * LANES), lambda pair: (0, pair)),
            pl.BlockSpec((8, 2 * LANES), lambda pair: (0, 0)),
        ],
        scratch_shapes=[
            VMEM((2, LANES, padded), jnp.float32),
            VMEM((2, rows, LANES), jnp.float32),
            VMEM((2, rows, LANES), jnp.float32),
            VMEM((2, padded, LANES), jnp.float32),
        ],
        compiler_params=pltpu.CompilerParams(vmem_limit_bytes=56 * 2**20),
        cost_estimate=cost(36),
    )(big_images, q_rows, k_rows, v_rows, do_rows, inverses, qk_gains)


FINE = 6 * PATCHES // 7


def in_order(mine, other):
    first = lax.axis_index("hg") == 0
    return jnp.where(first, mine, other), jnp.where(first, other, mine)


def dense_kernel(count, tiles, normed_ref, mine_ref, other_ref, *refs):
    w_in_refs, w_back_refs = refs[:count], refs[count : 2 * count]
    refs = refs[2 * count :]
    part_ref, grad_ref, normed_t_ref, dy_t_ref = refs[:4]
    grad_refs, refs = refs[4 : 4 + count], refs[4 + count :]
    normed_rows, dy_rows = refs[:2]
    act_refs, gup_refs = refs[2 : 2 + count], refs[2 + count :]
    step = pl.program_id(0)
    half = mine_ref.shape[1]
    curve = math.sqrt(2.0 / math.pi)
    normed = normed_ref[...]
    dy_rows[step, :, :half], dy_rows[step, :, half:] = in_order(mine_ref[...], other_ref[...])
    dy = dy_rows[step]
    normed_rows[step] = normed
    for w_in_ref, w_back_ref, act_ref, gup_ref in zip(w_in_refs, w_back_refs, act_refs, gup_refs):
        columns = w_in_ref.shape[1]
        width = min(256, columns)
        for at in range(0, columns, width):
            cols = slice(at, min(at + width, columns))
            up = times(normed, w_in_ref[:, cols])
            grad_act = times(dy, w_back_ref[:, cols])
            square = up * up
            bent = jnp.tanh(up * (curve + (curve * 0.044715) * square))
            gate = 0.5 + 0.5 * bent
            act = up * gate
            slope = gate + act * ((1.0 - gate) * (2 * curve + (6 * curve * 0.044715) * square))
            act_ref[step, :, cols] = low(act)
            gup_ref[step, :, cols] = low(grad_act * slope)
    total, grad = None, None
    for act_ref, w_back_ref, gup_ref, w_in_ref in zip(act_refs, w_back_refs, gup_refs, w_in_refs):
        part = times_t(act_ref[step], w_back_ref[...])
        total = part if total is None else total + part
        part = times_t(gup_ref[step], w_in_ref[...])
        grad = part if grad is None else grad + part
    part_ref[...] = total
    grad_ref[...] = low(grad)

    @pl.when(step == tiles - 1)
    def _():
        rows, width = tiles * normed_rows.shape[1], normed_rows.shape[2]
        for source, turned in ((normed_rows, normed_t_ref), (dy_rows, dy_t_ref)):
            turned[:, :rows] = source[...].reshape(rows, width).T
            turned[:, rows:] = jnp.zeros((width, turned.shape[1] - rows), jnp.bfloat16)
        for act_ref, gup_ref, ref in zip(act_refs, gup_refs, grad_refs):
            columns = act_ref.shape[2]
            for turned, right, at in ((normed_t_ref, gup_ref, 0), (dy_t_ref, act_ref, columns)):
                total = times(turned[:, :rows], right[...].reshape(rows, columns))
                by_parity(total, ref, slice(at, at + columns))


def by_parity(total, ref, cols):
    halves, rows = ref.shape[1:3]
    odd = lax.axis_index("dp") & 1
    for half in range(halves):
        for side in range(2):
            start = (2 * half + side) * rows
            ref[odd ^ side, half, :, cols] = total[start : start + rows].astype(ref.dtype)


def dense(normed, mine, other, w_in_pieces, w_back_pieces):
    rows, width = normed.shape
    tile = 2 * PATCHES
    tiles = rows // tile
    count = len(w_in_pieces)
    shape = jax.ShapeDtypeStruct
    sizes = [piece.shape[1] for piece in w_in_pieces]
    groups = lax.axis_size("dp")
    padded = -(-rows // 256) * 256
    row_tile = lambda columns: pl.BlockSpec((tile, columns), lambda step: (step, 0))
    turned = pl.BlockSpec((width, padded), lambda step: (0, 0))
    once = lambda columns: pl.BlockSpec((width, columns), lambda step: (0, 0), pipeline_mode=pl.Buffered(1))
    return pl.pallas_call(
        functools.partial(dense_kernel, count, tiles),
        name="dense",
        grid=(tiles,),
        out_shape=[
            shape((rows, width), jnp.float32),
            shape((rows, width), jnp.bfloat16),
            shape((width, padded), jnp.bfloat16),
            shape((width, padded), jnp.bfloat16),
        ]
        + [shape((2, groups // 2, width // groups, 2 * size), jnp.bfloat16) for size in sizes],
        in_specs=[row_tile(width), row_tile(width // 2), row_tile(width // 2)]
        + [once(size) for size in sizes] * 2,
        out_specs=[row_tile(width)] * 2
        + [turned] * 2
        + [
            pl.BlockSpec((2, groups // 2, width // groups, 2 * size), lambda step: (0, 0, 0, 0))
            for size in sizes
        ],
        scratch_shapes=[VMEM((tiles, tile, width), jnp.bfloat16)] * 2
        + [VMEM((tiles, tile, size), jnp.bfloat16) for size in sizes] * 2,
        compiler_params=pltpu.CompilerParams(vmem_limit_bytes=60 * 2**20),
        cost_estimate=cost(24),
    )(normed, mine, other, *w_in_pieces, *w_back_pieces)


def outputs_kernel(part_ref, tok_ref, att_ref, mine_ref, other_ref, w_out_ref, keep_ref, send_ref, do_ref):
    tile, width = part_ref.shape
    half = width // 2
    heads, padded, _ = do_ref.shape
    lane = lane_of((tile, LANES))
    attended = att_ref[...]
    left = times_t(attended, w_out_ref[...]) + part_ref[...]
    token = tok_ref[...]
    keep, send = in_order(left[:, :half], left[:, half:])
    keep_ref[...] = keep + in_order(wide(token[:, :half]), wide(token[:, half:]))[0]
    send_ref[...] = low(send)
    first, second = in_order(mine_ref[...], other_ref[...])
    grad_att = times(first, w_out_ref[:half, :]) + times(second, w_out_ref[half:, :])
    shape = (LANES, 2 * LANES)
    row, column = row_of(shape), lane_of(shape)
    inners = (row // 64 == column // LANES) & (column % LANES >= 64) & (column % LANES < 67)
    inners = low(jnp.where(inners, -1.0, 0.0))
    found = []
    for pair in range(heads // 2):
        cols = slice(pair * LANES, pair * LANES + LANES)
        low_block = wide(low(grad_att[:, cols]))
        weighed, rest = two_terms(low_block * wide(attended[:, cols]))
        inner = times(weighed, inners) + times(rest, inners)
        for side in range(2):
            value = low_block if side == 0 else other_half(low_block)
            term = spread_terms(inner[:, side * LANES : (side + 1) * LANES])
            found.append(low(jnp.where(lane < 64, value, term)))
    for step in range(3):

        @pl.when(pl.program_id(0) == step)
        def _(step=step):
            for head in range(heads):
                do_ref[head, step * tile : (step + 1) * tile, :] = found[head]
            if step == 2:
                do_ref[:, 3 * tile :, :] = jnp.zeros((heads, padded - 3 * tile, LANES), jnp.bfloat16)


def outputs(part, tokens, attended, mine, other, w_out_t):
    rows, width = tokens.shape
    tile = 2 * PATCHES
    heads = w_out_t.shape[1] // 64
    padded = -(-rows // 256) * 256
    shape = jax.ShapeDtypeStruct
    row_tile = lambda columns: pl.BlockSpec((tile, columns), lambda step: (step, 0))
    return pl.pallas_call(
        outputs_kernel,
        name="outputs",
        grid=(rows // tile,),
        out_shape=[
            shape((rows, width // 2), jnp.float32),
            shape((rows, width // 2), jnp.bfloat16),
            shape((heads, padded, LANES), jnp.bfloat16),
        ],
        in_specs=[row_tile(columns) for columns in (width, width, width // 2, width // 2, width // 2)]
        + [pl.BlockSpec(w_out_t.shape, lambda step: (0, 0))],
        out_specs=[
            row_tile(width // 2),
            row_tile(width // 2),
            pl.BlockSpec((heads, padded, LANES), lambda step: (0, 0, 0)),
        ],
        compiler_params=pltpu.CompilerParams(vmem_limit_bytes=56 * 2**20),
        cost_estimate=cost(6),
    )(part, tokens, attended, mine, other, w_out_t)


def features_kernel(joined_ref, w_ref, mlp_ref, tok_ref, sent_ref, gain_ref):
    grad = times_t(joined_ref[...], w_ref[...]) + wide(mlp_ref[...])
    sent_ref[...] = low(grad)
    x = wide(tok_ref[...])
    x = x - jnp.mean(x, axis=1, keepdims=True)
    x = x * lax.rsqrt(jnp.mean(x * x, axis=1, keepdims=True) + EPSILON)

    @pl.when(pl.program_id(0) == 0)
    def _():
        gain_ref[...] = jnp.zeros_like(gain_ref)

    gain_ref[0:1, :] += jnp.sum(grad * x, axis=0, keepdims=True)


def features(first, count, grad_joined, w_qkv, grad_mlp, tokens):
    rows, width = tokens.shape
    tile = FINE
    row_tile = lambda columns: pl.BlockSpec((tile, columns), lambda step: (step + first, 0))
    return pl.pallas_call(
        features_kernel,
        name="features",
        grid=(count,),
        out_shape=[
            jax.ShapeDtypeStruct((tile * count, width), jnp.bfloat16),
            jax.ShapeDtypeStruct((8, width), jnp.float32),
        ],
        in_specs=[
            row_tile(grad_joined.shape[1]),
            pl.BlockSpec(w_qkv.shape, lambda step: (0, 0)),
            row_tile(width),
            row_tile(width),
        ],
        out_specs=[
            pl.BlockSpec((tile, width), lambda step: (step, 0)),
            pl.BlockSpec((8, width), lambda step: (0, 0)),
        ],
        compiler_params=pltpu.CompilerParams(vmem_limit_bytes=40 * 2**20),
        cost_estimate=cost(0.3 * count),
    )(grad_joined, w_qkv, grad_mlp, tokens)


def weights_kernel(chunks, normed_t_ref, dy_t_ref, joined_ref, att_ref, keep_ref, send_ref):
    halves, rows, columns = keep_ref.shape[1:]
    tokens = att_ref.shape[0]
    odd, side = lax.axis_index("dp") & 1, lax.axis_index("hid")

    def finish(left_ref, right_ref):
        total = times(left_ref[:, :tokens], right_ref[...])
        for half in range(halves):
            for parity in range(2):
                start = 2 * (2 * half + parity) * rows
                even, uneven = total[start : start + rows], total[start + rows : start + 2 * rows]
                keep_ref[odd ^ parity, half] = low(jnp.where(side == 0, even, uneven))
                send_ref[odd ^ parity, half] = low(jnp.where(side == 0, uneven, even))

    @pl.when(pl.program_id(0) < chunks)
    def _():
        finish(normed_t_ref, joined_ref)

    @pl.when(pl.program_id(0) == chunks)
    def _():
        finish(dy_t_ref, att_ref)


def weights(normed_t, dy_t, grad_joined, attended):
    groups = lax.axis_size("dp")
    rows, columns = attended.shape
    chunks = grad_joined.shape[1] // columns
    shape = (2, groups // 2, normed_t.shape[0] // (2 * groups), columns)
    whole = jax.ShapeDtypeStruct(shape[:3] + (columns * (chunks + 1),), jnp.bfloat16)
    turned = pl.BlockSpec(normed_t.shape, lambda step: (0, 0))
    out = pl.BlockSpec(shape, lambda step: (0, 0, 0, step))
    return pl.pallas_call(
        functools.partial(weights_kernel, chunks),
        name="weights",
        grid=(chunks + 1,),
        out_shape=[whole, whole],
        in_specs=[
            turned,
            turned,
            pl.BlockSpec((rows, columns), lambda step: (0, jnp.minimum(step, chunks - 1))),
            pl.BlockSpec((rows, columns), lambda step: (0, 0)),
        ],
        out_specs=[out, out],
        compiler_params=pltpu.CompilerParams(vmem_limit_bytes=48 * 2**20),
        cost_estimate=cost(1),
    )(normed_t, dy_t, grad_joined, attended)


def tokens_kernel(sent_ref, came_ref, tok_ref, gain_ref, mine_ref, other_ref, *refs):
    out_ref = refs[-1]
    half = mine_ref.shape[1]
    grad = (wide(sent_ref[...]) + wide(came_ref[...])) * wide(gain_ref[...])
    x = wide(tok_ref[...])
    x = x - jnp.mean(x, axis=1, keepdims=True)
    inverse = lax.rsqrt(jnp.mean(x * x, axis=1, keepdims=True) + EPSILON)
    x = x * inverse
    inner = jnp.mean(grad * x, axis=1, keepdims=True)
    grad = inverse * (grad - jnp.mean(grad, axis=1, keepdims=True) - x * inner)
    first, second = in_order(wide(mine_ref[...]), wide(other_ref[...]))
    out_ref[:, :half] = low(grad[:, :half] + first)
    out_ref[:, half:] = low(grad[:, half:] + second)


def token_rows(first, sent, came, tokens, norm_gain, mine, other, before):
    rows, width = tokens.shape
    tile = FINE
    count = sent.shape[0] // tile
    near = lambda columns: pl.BlockSpec((tile, columns), lambda step: (step, 0))
    far = lambda columns: pl.BlockSpec((tile, columns), lambda step: (step + first, 0))
    more = [] if before is None else [before]
    return pl.pallas_call(
        tokens_kernel,
        name="token_rows",
        grid=(count,),
        out_shape=jax.ShapeDtypeStruct((rows, width), jnp.bfloat16),
        in_specs=[
            near(width),
            near(width),
            far(width),
            pl.BlockSpec((1, width), lambda step: (0, 0)),
            far(width // 2),
            far(width // 2),
        ]
        + [pl.BlockSpec(memory_space=pl.ANY)] * len(more),
        out_specs=far(width),
        input_output_aliases={6: 0} if more else {},
        compiler_params=pltpu.CompilerParams(vmem_limit_bytes=40 * 2**20),
        cost_estimate=cost(0.3 * count),
    )(sent, came, tokens, norm_gain.reshape(1, -1), mine, other, *more)


def swap(value, axis, bit):
    size = lax.axis_size(axis)
    return lax.ppermute(value, axis, [(place, place ^ bit) for place in range(size)])


def bits_of(axis):
    size = lax.axis_size(axis)
    return [1 << place for place in range(size.bit_length() - 1)]


def gather_pieces(block, axis):
    pieces = [block]
    for bit in bits_of(axis):
        held = pieces[0] if len(pieces) == 1 else jnp.concatenate(pieces, axis=1)
        pieces.append(swap(held, axis, bit))
    return pieces


def scatter_pieces(pieces, axis):
    for bit in reversed(bits_of(axis)):
        sent = swap(low(pieces[-1]), axis, bit)
        kept, at, half = [], 0, sent.shape[-1] // 2
        for piece in pieces[:-1]:
            size = piece.shape[-1] // 2
            parts = (sent[..., at : at + size], sent[..., half + at : half + at + size])
            kept.append(wide(piece) + wide(jnp.concatenate(parts, axis=-1) if size < half else sent))
            at += size
        pieces = kept
    return pieces[0]


def row_blocks(normed_t, dy_t, grad_joined, attended):
    groups, sides = lax.axis_size("dp"), lax.axis_size("hid")
    width = normed_t.shape[0]
    if sides == 2 and width % (16 * groups * sides) == 0:
        keep, send = weights(normed_t, dy_t, grad_joined, attended)
        return wide(keep) + wide(swap(send, "hid", 1))
    tokens = attended.shape[0]
    parts = [times(normed_t[:, :tokens], grad_joined), times(dy_t[:, :tokens], attended)]
    shaped = jnp.concatenate(parts, axis=1).reshape(groups // 2, 2, sides, width // (groups * sides), -1)
    odd = lax.axis_index("dp") & 1
    shaped = shaped[:, odd ^ jnp.arange(2)][:, :, lax.axis_index("hid") ^ jnp.arange(sides)]
    shaped = shaped.transpose(1, 0, 2, 3, 4)
    for bit in reversed(bits_of("hid")):
        shaped = shaped[:, :, :bit] + wide(swap(low(shaped[:, :, bit:]), "hid", bit))
    return shaped[:, :, 0]


def halve(shaped):
    return low(shaped[0]), swap(low(shaped[1]), "dp", 1)


def sum_rest(kept, came):
    count = lax.axis_size("dp")
    groups = [list(range(odd, count, 2)) for odd in (0, 1)]
    total = low(wide(kept) + wide(came))
    total = lax.all_to_all(total, "dp", 0, 0, axis_index_groups=groups, tiled=True)
    half = total.shape[2] // 2
    return tuple(jnp.sum(wide(part), axis=0) for part in (total[:, :, :half], total[:, :, half:]))


def sum_far(kept, came, extra, extra_came, columns):
    half, rows, width = kept.shape
    extra = low(wide(extra) + wide(extra_came))
    extra = jnp.pad(extra, (0, 8 * width - extra.shape[0])).reshape(1, 8, width)
    total = low(wide(kept) + wide(came))
    total = jnp.concatenate([total, jnp.broadcast_to(extra, (half, 8, width))], axis=1)
    me = lax.axis_index("dp") // 2
    terms = [lax.dynamic_index_in_dim(total, me, keepdims=False)]
    for step in range(1, half):
        block = lax.dynamic_index_in_dim(total, me ^ step, keepdims=False)
        terms.append(swap(block, "dp", 2 * step))

    def added(part):
        values = [wide(part(term)) for term in terms]
        while len(values) > 1:
            values = [first + second for first, second in zip(values[::2], values[1::2])]
        return values[0]

    return (
        added(lambda term: term[:rows, :columns]),
        added(lambda term: term[:rows, columns:]),
        added(lambda term: term[rows]),
    )


def sum_everywhere(value, axes):
    for axis in axes:
        for bit in bits_of(axis):
            value = value + swap(value, axis, bit)
    return value


def shards(tokens, big_images, norm_gain, w_qkv, qk_gains, w_out_t, w_in, w_back, cotangent):
    width = tokens.shape[1]
    size = qk_gains.shape[1]
    groups = lax.axis_size("dp")
    other = swap(cotangent, "hg", 1)
    w_in_pieces = gather_pieces(w_in, "hid")
    w_back_pieces = gather_pieces(w_back, "hid")
    normed, q_rows, k_rows, v_rows, attended, inverses = forward(
        big_images, tokens, norm_gain, w_qkv, qk_gains
    )
    part, grad_mlp, normed_t, dy_t, *grads = dense(normed, cotangent, other, w_in_pieces, w_back_pieces)
    kept, sent, do_rows = outputs(part, tokens, attended, cotangent, other, w_out_t)
    out_came = swap(sent, "hg", 1)
    mlp_kept, mlp_came = halve(scatter_pieces(grads, "hid"))
    do_rows, mlp_kept = lax.optimization_barrier((do_rows, mlp_kept))

    grad_joined, qk_part = backward(big_images, q_rows, k_rows, v_rows, do_rows, inverses, qk_gains)
    grad_joined, out_came, mlp_came = lax.optimization_barrier((grad_joined, out_came, mlp_came))
    mine, gain_part = features(0, tokens.shape[0] // FINE, grad_joined, w_qkv, grad_mlp, tokens)
    came = swap(mine, "hg", 1)

    def weight_sums(normed_t, dy_t, grad_joined, attended, mlp_kept, mlp_came, gain_part, qk_part, kept, out_came):
        blocks = row_blocks(normed_t, dy_t, grad_joined, attended)
        mlp_grads = sum_rest(mlp_kept, mlp_came)
        small = jnp.concatenate([gain_part[0], qk_part[0, :size], qk_part[0, LANES : LANES + size]])
        small = low(sum_everywhere(small, ("hid",)))
        small, blocks = lax.optimization_barrier((small, blocks))
        blocks_kept, blocks_came = halve(blocks)
        sums = sum_far(blocks_kept, blocks_came, small, swap(small, "dp", 1), grad_joined.shape[1])
        return mlp_grads, sums, low(kept + wide(out_came))

    def no_sums(*operands):
        return jax.tree.map(lambda kind: jnp.zeros(kind.shape, kind.dtype), kinds)

    operands = (
        normed_t,
        dy_t,
        grad_joined,
        attended,
        mlp_kept,
        mlp_came,
        gain_part,
        qk_part,
        kept,
        out_came,
    )
    kinds = jax.eval_shape(weight_sums, *operands)
    mlp_grads, sums, output = lax.cond(big_images[0] >= 0, weight_sums, no_sums, *operands)
    w_in_grad, w_back_grad = mlp_grads
    w_qkv_grad, w_out_t_grad, small = sums
    came, small = lax.optimization_barrier((came, small))
    small = sum_everywhere(small, ("hg",))
    own = lax.axis_index("dp") * lax.axis_size("hid") + lax.axis_index("hid")
    gain_rows = width // (groups * lax.axis_size("hid"))
    norm_gain_grad = lax.dynamic_slice_in_dim(small, own * gain_rows, gain_rows, 0)
    qk_gains_grad = small[width : width + 2 * size].reshape(2, size)
    token_grad = token_rows(0, mine, came, tokens, norm_gain, cotangent, other, None)
    return (
        output,
        token_grad,
        norm_gain_grad,
        w_qkv_grad,
        qk_gains_grad,
        w_out_t_grad,
        w_in_grad,
        w_back_grad,
    )


def solution(mesh):
    return jax.shard_map(
        shards,
        mesh=mesh,
        in_specs=(
            P(("dp", "hid"), None),
            P(("dp", "hid")),
            P(),
            P(None, "hg"),
            P(),
            P(None, "hg"),
            P(None, ("hg", "hid")),
            P(None, ("hg", "hid")),
            P(("dp", "hid"), "hg"),
        ),
        out_specs=(
            P(("dp", "hid"), "hg"),
            P(("dp", "hid"), None),
            P(("dp", "hid")),
            P(("dp", "hid"), "hg"),
            P(),
            P(("dp", "hid"), "hg"),
            P("dp", ("hg", "hid")),
            P("dp", ("hg", "hid")),
        ),
        check_vma=False,
    )
```

```python
import functools
import math

import jax
import jax.numpy as jnp
from jax import lax
from jax.experimental import pallas as pl
from jax.experimental.pallas import tpu as pltpu
from jax.sharding import PartitionSpec as P

PATCHES = 196
EPSILON = 1e-06
LOG2E = math.log2(math.e)
LANES = 128
VMEM = pltpu.VMEM
SCALE = 1.0
ROOM = dict(forward=40, backward=24, dense=32, outputs=24, features=24, weights=24, token_rows=24)


def cost(microseconds):
    return pl.CostEstimate(
        flops=int(microseconds * SCALE * 1e9), bytes_accessed=2**20, transcendentals=0
    )


def times_t(left, right):
    return lax.dot_general(
        left, right, (((1,), (1,)), ((), ())), preferred_element_type=jnp.float32
    )


def rows_t(left, right):
    return lax.dot_general(
        left, right, (((0,), (0,)), ((), ())), preferred_element_type=jnp.float32
    )


def times(left, right):
    return jnp.dot(left, right, preferred_element_type=jnp.float32)


def low(value):
    return value.astype(jnp.bfloat16)


def wide(value):
    return value.astype(jnp.float32)


def lane_of(shape):
    return lax.broadcasted_iota(jnp.int32, shape, 1)


def row_of(shape):
    return lax.broadcasted_iota(jnp.int32, shape, 0)


def other_half(value):
    return pltpu.roll(value, LANES // 2, 1)


def spread_terms(whole):
    lane = lane_of(whole.shape)
    first = wide(low(whole))
    second = wide(low(whole - first))
    third = whole - first - second
    return jnp.where(lane == 64, first, jnp.where(lane == 65, second, jnp.where(lane == 66, third, 0.0)))


def three_terms(column, shape):
    return spread_terms(jnp.broadcast_to(column, shape))


def two_terms(value):
    first = low(value)
    return first, low(value - wide(first))


def pair_mask(block, shape, first_lane):
    start = 2 * PATCHES * block - first_lane
    place = lane_of(shape) - start
    second = row_of(shape) >= PATCHES
    begin = jnp.where(second, PATCHES, 0)
    return (place >= begin) & (place < begin + PATCHES)


def window_of(block):
    return (2 * PATCHES * block // LANES) * LANES, 4 * LANES


def forward_kernel(
    flag_ref, tok_ref, gain_ref, w_ref, qk_ref, normed_ref, q_ref, k_ref, v_ref, att_ref, inv_ref
):
    rows = tok_ref.shape[0]
    heads, padded, _ = q_ref.shape
    tile = 2 * PATCHES
    size = qk_ref.shape[1]
    columns = w_ref.shape[1]
    gain = wide(gain_ref[...])
    q_gain = wide(qk_ref[0:1, :]) * (size**-0.5 * LOG2E)
    k_gain = wide(qk_ref[1:2, :])
    ones = jnp.ones_like(k_gain)
    gains = jnp.concatenate([q_gain, k_gain, ones, q_gain, k_gain, ones], axis=1)
    is_value = jnp.concatenate([0 * ones, 0 * ones, ones, 0 * ones, 0 * ones, ones], axis=1)
    group_a = row_of((256, 256)) // size
    group_b = lane_of((256, 256)) // size
    mean_of = low(jnp.where(group_a == group_b, 1.0 / size, 0.0))
    stride = rows // (3 * LANES) and 3 * LANES
    strip = rows - (rows // stride - 1) * stride
    lane = lane_of((strip, LANES))

    def project(step, _):
        here = pl.ds(pl.multiple_of(step * stride, LANES), strip)
        x = wide(tok_ref[here, :])
        x = x - jnp.mean(x, axis=1, keepdims=True)
        x = x * lax.rsqrt(jnp.mean(x * x, axis=1, keepdims=True) + EPSILON)
        normed = low(x * gain)
        normed_ref[here, :] = normed
        compact = jnp.zeros((strip, LANES), jnp.float32)
        for pair in range(heads // 2):
            joined = times(normed, w_ref[:, 384 * pair : 384 * pair + 384])
            parts = []
            for at in (0, 256):
                wid = min(256, 384 - at)
                block = joined[:, at : at + wid]
                means = mean_of[:wid, :wid]
                centred = block - times(low(block), means)
                squares = low(centred * centred)
                variance = times(squares, means)
                place = 6 * pair + at // size
                pick = low(
                    jnp.where(
                        row_of((wid, LANES)) // size + place == lane_of((wid, LANES)), 1.0 / size, 0.0
                    )
                )
                compact = compact + times(squares, pick)
                hat = centred * lax.rsqrt(variance + EPSILON)
                parts.append(
                    jnp.where(is_value[:, at : at + wid] > 0, block, hat * gains[:, at : at + wid])
                )
            b0, b1, b2 = parts[0][:, :128], parts[0][:, 128:], parts[1]
            first = lane < 64
            unit = jnp.where(lane < 67, 1.0, 0.0)
            q_ref[2 * pair, here, :] = low(jnp.where(first, b0, 0.0))
            k_ref[2 * pair, here, :] = low(jnp.where(first, other_half(b0), unit))
            v_ref[2 * pair, here, :] = low(jnp.where(first, b1, unit))
            q_ref[2 * pair + 1, here, :] = low(jnp.where(first, other_half(b1), 0.0))
            k_ref[2 * pair + 1, here, :] = low(jnp.where(first, b2, unit))
            v_ref[2 * pair + 1, here, :] = low(jnp.where(first, other_half(b2), unit))
        inv_ref[here, :] = lax.rsqrt(compact + EPSILON)
        return 0

    lax.fori_loop(0, rows // stride, project, 0)
    lane = lane_of((tile, LANES))
    for ref in (q_ref, k_ref, v_ref):
        ref[:, rows:, :] = jnp.zeros((heads, padded - rows, LANES), jnp.bfloat16)

    def attend(pair, _, big):
        for start in range(0, rows, tile):
            here = slice(start, start + tile)
            if big:
                keys = slice(0, padded)
            else:
                begin, length = window_of(start // tile)
                keys = slice(begin, begin + length)
            found = []
            for side in range(2):
                head = 2 * pair + side
                queries = q_ref[head, here, :]
                scores = times_t(queries, k_ref[head, keys, :])
                if not big:
                    scores = jnp.where(
                        pair_mask(start // tile, scores.shape, keys.start), scores, -1e30
                    )
                expo = low(jnp.exp2(scores))
                out = times(expo, v_ref[head, keys, :])
                total = out[:, 64:65]
                found.append(out * (1.0 / total))
                log_total = jnp.log(total) * (-LOG2E)
                q_ref[head, here, :] = low(
                    jnp.where(lane < 64, wide(queries), three_terms(log_total, lane.shape))
                )
            att_ref[here, pl.ds(pl.multiple_of(pair * LANES, LANES), LANES)] = low(
                jnp.where(lane < 64, found[0], other_half(found[1]))
            )
        return 0

    @pl.when(flag_ref[0] > 0)
    def _():
        lax.fori_loop(0, heads // 2, functools.partial(attend, big=True), 0)

    @pl.when(flag_ref[0] <= 0)
    def _():
        lax.fori_loop(0, heads // 2, functools.partial(attend, big=False), 0)


def forward(big_images, tokens, norm_gain, w_qkv, qk_gains):
    rows, width = tokens.shape
    size = qk_gains.shape[1]
    heads = w_qkv.shape[1] // (3 * size)
    padded = -(-rows // 256) * 256
    whole = pl.BlockSpec(memory_space=VMEM)
    head_rows = jax.ShapeDtypeStruct((heads, padded, LANES), jnp.bfloat16)
    return pl.pallas_call(
        forward_kernel,
        name="forward",
        out_shape=[
            jax.ShapeDtypeStruct((rows, width), jnp.bfloat16),
            head_rows,
            head_rows,
            head_rows,
            jax.ShapeDtypeStruct((rows, heads * size), jnp.bfloat16),
            jax.ShapeDtypeStruct((rows, LANES), jnp.float32),
        ],
        in_specs=[pl.BlockSpec(memory_space=pltpu.SMEM)] + [whole] * 4,
        out_specs=[whole] * 6,
        compiler_params=pltpu.CompilerParams(vmem_limit_bytes=ROOM["forward"] * 2**20),
        cost_estimate=cost(24),
    )(big_images, tokens, norm_gain.reshape(1, -1), w_qkv, qk_gains)


def backward_kernel(
    flag_ref, q_ref, k_ref, v_ref, do_ref, inv_ref, qk_ref, joined_ref, small_ref, dq_ref, dk_ref, dv_ref, turned_ref
):
    pair = pl.program_id(0)
    rows = inv_ref.shape[0]
    padded = q_ref.shape[1]
    tile = 2 * PATCHES
    size = qk_ref.shape[1]
    scale = size**-0.5
    zeros = jnp.zeros((1, LANES - size), jnp.float32)
    q_gain = wide(qk_ref[0:1, :])
    k_gain = wide(qk_ref[1:2, :])
    q_back = jnp.concatenate([1.0 / (q_gain * (scale * LOG2E)), zeros], axis=1)
    k_back = jnp.concatenate([1.0 / k_gain, zeros], axis=1)
    q_gain = jnp.concatenate([q_gain, zeros], axis=1)
    k_gain = jnp.concatenate([k_gain, zeros], axis=1)

    def attend(side, _, big):
        for start in range(0, rows, tile):
            here = slice(start, start + tile)
            if big:
                over = slice(0, padded)
            else:
                begin, length = window_of(start // tile)
                over = slice(begin, begin + length)
            keys = k_ref[side, here, :]
            queries = q_ref[side, over, :]
            grads = do_ref[side, over, :]
            scores = times_t(keys, queries)
            if not big:
                scores = jnp.where(pair_mask(start // tile, scores.shape, over.start), scores, -1e30)
            probs = jnp.exp2(scores)
            grad_probs = times_t(v_ref[side, here, :], grads)
            grad_scores = low(probs * grad_probs)
            dv_ref[side, here, :] = times(low(probs), grads)
            dk_ref[side, here, :] = times(grad_scores, queries)
            more = rows_t(keys, grad_scores)
            if big and start == 0:
                dq_ref[side, :, over] = more
            elif big:
                dq_ref[side, :, over] += more
            else:
                place = lane_of(more.shape) - (start - over.start)
                dq_ref[side, :, over] = jnp.where(
                    (place >= 0) & (place < tile), more, dq_ref[side, :, over]
                )
        return 0

    @pl.when(flag_ref[0] > 0)
    def _():
        lax.fori_loop(0, 2, functools.partial(attend, big=True), 0)

    @pl.when(flag_ref[0] <= 0)
    def _():
        lax.fori_loop(0, 2, functools.partial(attend, big=False), 0)

    @pl.when(pair == 0)
    def _():
        small_ref[...] = jnp.zeros_like(small_ref)

    lane = lane_of((tile, LANES))
    first = lane < 64
    shape = (2 * LANES, 2 * LANES)
    row, column = row_of(shape), lane_of(shape)
    means = (row // LANES == column // LANES) & (row % LANES < size)
    means = low(jnp.where(means, 1.0 / size, 0.0))
    gains = jnp.concatenate([q_gain * scale, k_gain * math.log(2.0)], axis=1)
    factors = jnp.concatenate([jnp.full_like(q_gain, scale), jnp.full_like(k_gain, math.log(2.0))], axis=1)
    backs = jnp.concatenate([q_back, k_back], axis=1)
    for side in range(2):
        turned_ref[side] = dq_ref[side].T
    for start in range(0, rows, tile):
        here = slice(start, start + tile)
        inverse_first, inverse_second = two_terms(inv_ref[here, :])
        blocks = []
        for side in range(2):
            shape = (LANES, 2 * LANES)
            source = 6 * pair + 3 * side + lane_of(shape) // LANES
            pick = low(jnp.where(row_of(shape) == source, 1.0, 0.0))
            inverse = times(inverse_first, pick) + times(inverse_second, pick)
            hat = jnp.concatenate([q_ref[side, here, :], k_ref[side, here, :]], axis=1)
            hat = wide(hat) * backs
            grad = jnp.concatenate([turned_ref[side, here, :], dk_ref[side, here, :]], axis=1)
            small_ref[0:1, :] += jnp.sum(grad * hat, axis=0, keepdims=True) * factors
            grad = grad * gains
            inner = times(low(grad * hat), means)
            grad = inverse * (grad - times(low(grad), means) - hat * inner)
            blocks.append((grad[:, :LANES], grad[:, LANES:], dv_ref[side, here, :]))
        (q0, k0, v0), (q1, k1, v1) = blocks
        joined_ref[here, 0:128] = low(jnp.where(first, q0, other_half(k0)))
        joined_ref[here, 128:256] = low(jnp.where(first, v0, other_half(q1)))
        joined_ref[here, 256:384] = low(jnp.where(first, k1, other_half(v1)))


def backward(big_images, q_rows, k_rows, v_rows, do_rows, inverses, qk_gains):
    heads, padded, _ = q_rows.shape
    rows = inverses.shape[0]
    pair_spec = pl.BlockSpec((2, padded, LANES), lambda pair: (pair, 0, 0))
    return pl.pallas_call(
        backward_kernel,
        name="backward",
        grid=(heads // 2,),
        out_shape=[
            jax.ShapeDtypeStruct((rows, heads * 3 * LANES // 2), jnp.bfloat16),
            jax.ShapeDtypeStruct((8, 2 * LANES), jnp.float32),
        ],
        in_specs=[pl.BlockSpec(memory_space=pltpu.SMEM)]
        + [pair_spec] * 4
        + [pl.BlockSpec((rows, LANES), lambda pair: (0, 0)), pl.BlockSpec(qk_gains.shape, lambda pair: (0, 0))],
        out_specs=[
            pl.BlockSpec((rows, 3 * LANES), lambda pair: (0, pair)),
            pl.BlockSpec((8, 2 * LANES), lambda pair: (0, 0)),
        ],
        scratch_shapes=[
            VMEM((2, LANES, padded), jnp.float32),
            VMEM((2, rows, LANES), jnp.float32),
            VMEM((2, rows, LANES), jnp.float32),
            VMEM((2, padded, LANES), jnp.float32),
        ],
        compiler_params=pltpu.CompilerParams(vmem_limit_bytes=ROOM["backward"] * 2**20),
        cost_estimate=cost(36),
    )(big_images, q_rows, k_rows, v_rows, do_rows, inverses, qk_gains)


FINE = 2 * PATCHES


def in_order(mine, other):
    first = lax.axis_index("hg") == 0
    return jnp.where(first, mine, other), jnp.where(first, other, mine)


def dense_kernel(count, tiles, normed_ref, mine_ref, other_ref, *refs):
    w_in_refs, w_back_refs = refs[:count], refs[count : 2 * count]
    refs = refs[2 * count :]
    part_ref, grad_ref, normed_t_ref, dy_t_ref = refs[:4]
    grad_refs, refs = refs[4 : 4 + count], refs[4 + count :]
    normed_rows, dy_rows = refs[:2]
    act_refs, gup_refs = refs[2 : 2 + count], refs[2 + count :]
    step = pl.program_id(0)
    half = mine_ref.shape[1]
    curve = math.sqrt(2.0 / math.pi)
    normed = normed_ref[...]
    dy_rows[step, :, :half], dy_rows[step, :, half:] = in_order(mine_ref[...], other_ref[...])
    dy = dy_rows[step]
    normed_rows[step] = normed
    for w_in_ref, w_back_ref, act_ref, gup_ref in zip(w_in_refs, w_back_refs, act_refs, gup_refs):
        columns = w_in_ref.shape[1]
        width = min(256, columns)
        for at in range(0, columns, width):
            cols = slice(at, min(at + width, columns))
            up = times(normed, w_in_ref[:, cols])
            grad_act = times(dy, w_back_ref[:, cols])
            square = up * up
            bent = jnp.tanh(up * (curve + (curve * 0.044715) * square))
            gate = 0.5 + 0.5 * bent
            act = up * gate
            slope = gate + act * ((1.0 - gate) * (2 * curve + (6 * curve * 0.044715) * square))
            act_ref[step, :, cols] = low(act)
            gup_ref[step, :, cols] = low(grad_act * slope)
    total, grad = None, None
    for act_ref, w_back_ref, gup_ref, w_in_ref in zip(act_refs, w_back_refs, gup_refs, w_in_refs):
        part = times_t(act_ref[step], w_back_ref[...])
        total = part if total is None else total + part
        part = times_t(gup_ref[step], w_in_ref[...])
        grad = part if grad is None else grad + part
    part_ref[...] = total
    grad_ref[...] = low(grad)

    @pl.when(step == tiles - 1)
    def _():
        rows, width = tiles * normed_rows.shape[1], normed_rows.shape[2]
        for source, turned in ((normed_rows, normed_t_ref), (dy_rows, dy_t_ref)):
            turned[:, :rows] = source[...].reshape(rows, width).T
            turned[:, rows:] = jnp.zeros((width, turned.shape[1] - rows), jnp.bfloat16)
        for act_ref, gup_ref, ref in zip(act_refs, gup_refs, grad_refs):
            columns = act_ref.shape[2]
            for turned, right, at in ((normed_t_ref, gup_ref, 0), (dy_t_ref, act_ref, columns)):
                total = times(turned[:, :rows], right[...].reshape(rows, columns))
                by_parity(total, ref, slice(at, at + columns))


def by_parity(total, ref, cols):
    halves, rows = ref.shape[1:3]
    odd = lax.axis_index("dp") & 1
    for half in range(halves):
        for side in range(2):
            start = (2 * half + side) * rows
            ref[odd ^ side, half, :, cols] = total[start : start + rows].astype(ref.dtype)


def dense(normed, mine, other, w_in_pieces, w_back_pieces):
    rows, width = normed.shape
    tile = 2 * PATCHES
    tiles = rows // tile
    count = len(w_in_pieces)
    shape = jax.ShapeDtypeStruct
    sizes = [piece.shape[1] for piece in w_in_pieces]
    groups = lax.axis_size("dp")
    padded = -(-rows // 256) * 256
    row_tile = lambda columns: pl.BlockSpec((tile, columns), lambda step: (step, 0))
    turned = pl.BlockSpec((width, padded), lambda step: (0, 0))
    once = lambda columns: pl.BlockSpec((width, columns), lambda step: (0, 0), pipeline_mode=pl.Buffered(1))
    return pl.pallas_call(
        functools.partial(dense_kernel, count, tiles),
        name="dense",
        grid=(tiles,),
        out_shape=[
            shape((rows, width), jnp.float32),
            shape((rows, width), jnp.bfloat16),
            shape((width, padded), jnp.bfloat16),
            shape((width, padded), jnp.bfloat16),
        ]
        + [shape((2, groups // 2, width // groups, 2 * size), jnp.bfloat16) for size in sizes],
        in_specs=[row_tile(width), row_tile(width // 2), row_tile(width // 2)]
        + [once(size) for size in sizes] * 2,
        out_specs=[row_tile(width)] * 2
        + [turned] * 2
        + [
            pl.BlockSpec((2, groups // 2, width // groups, 2 * size), lambda step: (0, 0, 0, 0))
            for size in sizes
        ],
        scratch_shapes=[VMEM((tiles, tile, width), jnp.bfloat16)] * 2
        + [VMEM((tiles, tile, size), jnp.bfloat16) for size in sizes] * 2,
        compiler_params=pltpu.CompilerParams(vmem_limit_bytes=ROOM["dense"] * 2**20),
        cost_estimate=cost(24),
    )(normed, mine, other, *w_in_pieces, *w_back_pieces)


def outputs_kernel(part_ref, tok_ref, att_ref, mine_ref, other_ref, w_out_ref, keep_ref, send_ref, do_ref):
    tile, width = part_ref.shape
    half = width // 2
    heads, padded, _ = do_ref.shape
    lane = lane_of((tile, LANES))
    attended = att_ref[...]
    left = times_t(attended, w_out_ref[...]) + part_ref[...]
    token = tok_ref[...]
    keep, send = in_order(left[:, :half], left[:, half:])
    keep_ref[...] = keep + in_order(wide(token[:, :half]), wide(token[:, half:]))[0]
    send_ref[...] = low(send)
    first, second = in_order(mine_ref[...], other_ref[...])
    grad_att = times(first, w_out_ref[:half, :]) + times(second, w_out_ref[half:, :])
    shape = (LANES, 2 * LANES)
    row, column = row_of(shape), lane_of(shape)
    inners = (row // 64 == column // LANES) & (column % LANES >= 64) & (column % LANES < 67)
    inners = low(jnp.where(inners, -1.0, 0.0))
    found = []
    for pair in range(heads // 2):
        cols = slice(pair * LANES, pair * LANES + LANES)
        low_block = wide(low(grad_att[:, cols]))
        weighed, rest = two_terms(low_block * wide(attended[:, cols]))
        inner = times(weighed, inners) + times(rest, inners)
        for side in range(2):
            value = low_block if side == 0 else other_half(low_block)
            term = spread_terms(inner[:, side * LANES : (side + 1) * LANES])
            found.append(low(jnp.where(lane < 64, value, term)))
    for step in range(3):

        @pl.when(pl.program_id(0) == step)
        def _(step=step):
            for head in range(heads):
                do_ref[head, step * tile : (step + 1) * tile, :] = found[head]
            if step == 2:
                do_ref[:, 3 * tile :, :] = jnp.zeros((heads, padded - 3 * tile, LANES), jnp.bfloat16)


def outputs(part, tokens, attended, mine, other, w_out_t):
    rows, width = tokens.shape
    tile = 2 * PATCHES
    heads = w_out_t.shape[1] // 64
    padded = -(-rows // 256) * 256
    shape = jax.ShapeDtypeStruct
    row_tile = lambda columns: pl.BlockSpec((tile, columns), lambda step: (step, 0))
    return pl.pallas_call(
        outputs_kernel,
        name="outputs",
        grid=(rows // tile,),
        out_shape=[
            shape((rows, width // 2), jnp.float32),
            shape((rows, width // 2), jnp.bfloat16),
            shape((heads, padded, LANES), jnp.bfloat16),
        ],
        in_specs=[row_tile(columns) for columns in (width, width, width // 2, width // 2, width // 2)]
        + [pl.BlockSpec(w_out_t.shape, lambda step: (0, 0))],
        out_specs=[
            row_tile(width // 2),
            row_tile(width // 2),
            pl.BlockSpec((heads, padded, LANES), lambda step: (0, 0, 0)),
        ],
        compiler_params=pltpu.CompilerParams(vmem_limit_bytes=ROOM["outputs"] * 2**20),
        cost_estimate=cost(6),
    )(part, tokens, attended, mine, other, w_out_t)


def features_kernel(joined_ref, w_ref, mlp_ref, tok_ref, sent_ref, gain_ref):
    grad = times_t(joined_ref[...], w_ref[...]) + wide(mlp_ref[...])
    sent_ref[...] = low(grad)
    x = wide(tok_ref[...])
    x = x - jnp.mean(x, axis=1, keepdims=True)
    x = x * lax.rsqrt(jnp.mean(x * x, axis=1, keepdims=True) + EPSILON)

    @pl.when(pl.program_id(0) == 0)
    def _():
        gain_ref[...] = jnp.zeros_like(gain_ref)

    gain_ref[0:1, :] += jnp.sum(grad * x, axis=0, keepdims=True)


def features(first, count, grad_joined, w_qkv, grad_mlp, tokens):
    rows, width = tokens.shape
    tile = FINE
    row_tile = lambda columns: pl.BlockSpec((tile, columns), lambda step: (step + first, 0))
    return pl.pallas_call(
        features_kernel,
        name="features",
        grid=(count,),
        out_shape=[
            jax.ShapeDtypeStruct((tile * count, width), jnp.bfloat16),
            jax.ShapeDtypeStruct((8, width), jnp.float32),
        ],
        in_specs=[
            row_tile(grad_joined.shape[1]),
            pl.BlockSpec(w_qkv.shape, lambda step: (0, 0)),
            row_tile(width),
            row_tile(width),
        ],
        out_specs=[
            pl.BlockSpec((tile, width), lambda step: (step, 0)),
            pl.BlockSpec((8, width), lambda step: (0, 0)),
        ],
        compiler_params=pltpu.CompilerParams(vmem_limit_bytes=ROOM["features"] * 2**20),
        cost_estimate=cost(0.3 * count),
    )(grad_joined, w_qkv, grad_mlp, tokens)


def weights_kernel(*refs):
    keep_ref, send_ref = refs[-2:]
    halves, rows = keep_ref.shape[1:3]
    odd, side = lax.axis_index("dp") & 1, lax.axis_index("hid")
    at = 0
    for left_ref, right_ref in zip(refs[:-2:2], refs[1:-2:2]):
        tokens, columns = right_ref.shape
        total = times(left_ref[:, :tokens], right_ref[...])
        cols = slice(at, at + columns)
        at += columns
        for half in range(halves):
            for parity in range(2):
                start = 2 * (2 * half + parity) * rows
                even, uneven = total[start : start + rows], total[start + rows : start + 2 * rows]
                keep_ref[odd ^ parity, half, :, cols] = low(jnp.where(side == 0, even, uneven))
                send_ref[odd ^ parity, half, :, cols] = low(jnp.where(side == 0, uneven, even))


def weights(*products):
    groups = lax.axis_size("dp")
    columns = sum(size for _, _, size, _ in products)
    shape = (2, groups // 2, products[0][0].shape[0] // (2 * groups), columns)
    whole = lambda shape: pl.BlockSpec(shape, lambda step: (0,) * len(shape))
    specs, operands = [], []
    for turned, right, size, place in products:
        specs += [
            whole(turned.shape),
            pl.BlockSpec((right.shape[0], size), lambda step, place=place: (0, place)),
        ]
        operands += [turned, right]
    return pl.pallas_call(
        weights_kernel,
        name="weights",
        grid=(1,),
        out_shape=[jax.ShapeDtypeStruct(shape, jnp.bfloat16)] * 2,
        in_specs=specs,
        out_specs=[whole(shape)] * 2,
        compiler_params=pltpu.CompilerParams(vmem_limit_bytes=ROOM["weights"] * 2**20),
        cost_estimate=cost(3),
    )(*operands)


def tokens_kernel(sent_ref, came_ref, tok_ref, gain_ref, mine_ref, other_ref, *refs):
    out_ref = refs[-1]
    half = mine_ref.shape[1]
    grad = (wide(sent_ref[...]) + wide(came_ref[...])) * wide(gain_ref[...])
    x = wide(tok_ref[...])
    x = x - jnp.mean(x, axis=1, keepdims=True)
    inverse = lax.rsqrt(jnp.mean(x * x, axis=1, keepdims=True) + EPSILON)
    x = x * inverse
    inner = jnp.mean(grad * x, axis=1, keepdims=True)
    grad = inverse * (grad - jnp.mean(grad, axis=1, keepdims=True) - x * inner)
    first, second = in_order(wide(mine_ref[...]), wide(other_ref[...]))
    out_ref[:, :half] = low(grad[:, :half] + first)
    out_ref[:, half:] = low(grad[:, half:] + second)


def token_rows(first, sent, came, tokens, norm_gain, mine, other, before):
    rows, width = tokens.shape
    tile = FINE
    count = sent.shape[0] // tile
    near = lambda columns: pl.BlockSpec((tile, columns), lambda step: (step, 0))
    far = lambda columns: pl.BlockSpec((tile, columns), lambda step: (step + first, 0))
    more = [] if before is None else [before]
    return pl.pallas_call(
        tokens_kernel,
        name="token_rows",
        grid=(count,),
        out_shape=jax.ShapeDtypeStruct((rows, width), jnp.bfloat16),
        in_specs=[
            near(width),
            near(width),
            far(width),
            pl.BlockSpec((1, width), lambda step: (0, 0)),
            far(width // 2),
            far(width // 2),
        ]
        + [pl.BlockSpec(memory_space=pl.ANY)] * len(more),
        out_specs=far(width),
        input_output_aliases={6: 0} if more else {},
        compiler_params=pltpu.CompilerParams(vmem_limit_bytes=ROOM["token_rows"] * 2**20),
        cost_estimate=cost(0.3 * count),
    )(sent, came, tokens, norm_gain.reshape(1, -1), mine, other, *more)


def swap(value, axis, bit):
    size = lax.axis_size(axis)
    return lax.ppermute(value, axis, [(place, place ^ bit) for place in range(size)])


def bits_of(axis):
    size = lax.axis_size(axis)
    return [1 << place for place in range(size.bit_length() - 1)]


def gather_pieces(block, axis):
    pieces = [block]
    for bit in bits_of(axis):
        held = pieces[0] if len(pieces) == 1 else jnp.concatenate(pieces, axis=1)
        pieces.append(swap(held, axis, bit))
    return pieces


def scatter_pieces(pieces, axis):
    for bit in reversed(bits_of(axis)):
        sent = swap(low(pieces[-1]), axis, bit)
        kept, at, half = [], 0, sent.shape[-1] // 2
        for piece in pieces[:-1]:
            size = piece.shape[-1] // 2
            parts = (sent[..., at : at + size], sent[..., half + at : half + at + size])
            kept.append(wide(piece) + wide(jnp.concatenate(parts, axis=-1) if size < half else sent))
            at += size
        pieces = kept
    return pieces[0]


def row_blocks(*products):
    groups, sides = lax.axis_size("dp"), lax.axis_size("hid")
    width = products[0][0].shape[0]
    if sides == 2 and width % (16 * groups * sides) == 0:
        keep, send = weights(*products)
        return wide(keep) + wide(swap(send, "hid", 1))
    parts = []
    for turned, right, size, place in products:
        parts.append(times(turned[:, : right.shape[0]], right[:, place * size : place * size + size]))
    shaped = jnp.concatenate(parts, axis=1).reshape(groups // 2, 2, sides, width // (groups * sides), -1)
    odd = lax.axis_index("dp") & 1
    shaped = shaped[:, odd ^ jnp.arange(2)][:, :, lax.axis_index("hid") ^ jnp.arange(sides)]
    shaped = shaped.transpose(1, 0, 2, 3, 4)
    for bit in reversed(bits_of("hid")):
        shaped = shaped[:, :, :bit] + wide(swap(low(shaped[:, :, bit:]), "hid", bit))
    return shaped[:, :, 0]


def halve(shaped):
    return low(shaped[0]), swap(low(shaped[1]), "dp", 1)


def sum_rest(kept, came):
    count = lax.axis_size("dp")
    groups = [list(range(odd, count, 2)) for odd in (0, 1)]
    total = low(wide(kept) + wide(came))
    total = lax.all_to_all(total, "dp", 0, 0, axis_index_groups=groups, tiled=True)
    half = total.shape[2] // 2
    return tuple(jnp.sum(wide(part), axis=0) for part in (total[:, :, :half], total[:, :, half:]))


def far_terms(total):
    me = lax.axis_index("dp") // 2
    terms = [lax.dynamic_index_in_dim(total, me, keepdims=False)]
    for step in range(1, total.shape[0]):
        block = lax.dynamic_index_in_dim(total, me ^ step, keepdims=False)
        terms.append(swap(block, "dp", 2 * step))
    return terms


def added(terms):
    values = [wide(term) for term in terms]
    while len(values) > 1:
        values = [first + second for first, second in zip(values[::2], values[1::2])]
    return values[0]


def sum_everywhere(value, axes):
    for axis in axes:
        for bit in bits_of(axis):
            value = value + swap(value, axis, bit)
    return value


def shards(tokens, big_images, norm_gain, w_qkv, qk_gains, w_out_t, w_in, w_back, cotangent):
    width = tokens.shape[1]
    size = qk_gains.shape[1]
    groups = lax.axis_size("dp")
    other = swap(cotangent, "hg", 1)
    w_in_pieces = gather_pieces(w_in, "hid")
    w_back_pieces = gather_pieces(w_back, "hid")
    normed, q_rows, k_rows, v_rows, attended, inverses = forward(
        big_images, tokens, norm_gain, w_qkv, qk_gains
    )
    part, grad_mlp, normed_t, dy_t, *grads = dense(normed, cotangent, other, w_in_pieces, w_back_pieces)
    kept, sent, do_rows = outputs(part, tokens, attended, cotangent, other, w_out_t)
    out_came = swap(sent, "hg", 1)
    mlp_kept, mlp_came = halve(scatter_pieces(grads, "hid"))
    do_rows, mlp_kept = lax.optimization_barrier((do_rows, mlp_kept))

    grad_joined, qk_part = backward(big_images, q_rows, k_rows, v_rows, do_rows, inverses, qk_gains)
    grad_joined, out_came, mlp_came = lax.optimization_barrier((grad_joined, out_came, mlp_came))
    mine, gain_part = features(0, tokens.shape[0] // FINE, grad_joined, w_qkv, grad_mlp, tokens)
    mine, mlp_came = lax.optimization_barrier((mine, mlp_came))
    came = swap(mine, "hg", 1)
    columns = attended.shape[1]

    def weight_sums(normed_t, dy_t, grad_joined, attended, gain_part, qk_part, kept, out_came):
        first_kept, first_came = halve(row_blocks((normed_t, grad_joined, 2 * columns, 0)))
        blocks = row_blocks((normed_t, grad_joined, columns, 2), (dy_t, attended, columns, 0))
        small = jnp.concatenate([gain_part[0], qk_part[0, :size], qk_part[0, LANES : LANES + size]])
        small = low(sum_everywhere(small, ("hid",)))
        small, blocks = lax.optimization_barrier((small, blocks))
        second_kept, second_came = halve(blocks)
        small = low(wide(small) + wide(swap(small, "dp", 1)))
        small = jnp.pad(small, (0, 8 * 2 * columns - small.shape[0])).reshape(1, 8, -1)
        first = added(far_terms(low(wide(first_kept) + wide(first_came))))
        second = low(wide(second_kept) + wide(second_came))
        small = jnp.broadcast_to(small, second.shape[:1] + small.shape[1:])
        return first, jnp.concatenate([second, small], axis=1), low(kept + wide(out_came))

    def no_sums(*operands):
        return jax.tree.map(lambda kind: jnp.zeros(kind.shape, kind.dtype), kinds)

    operands = (normed_t, dy_t, grad_joined, attended, gain_part, qk_part, kept, out_came)
    kinds = jax.eval_shape(weight_sums, *operands)
    first, second, output = lax.cond(big_images[0] >= 0, weight_sums, no_sums, *operands)
    w_in_grad, w_back_grad = sum_rest(mlp_kept, mlp_came)
    terms = far_terms(second)
    token_grad = token_rows(0, mine, came, tokens, norm_gain, cotangent, other, None)
    terms[1], token_grad = lax.optimization_barrier((terms[1], token_grad))
    rows = first.shape[0]
    w_qkv_grad = jnp.concatenate([first, added([term[:rows, :columns] for term in terms])], axis=1)
    w_out_t_grad = added([term[:rows, columns:] for term in terms])
    small = added([term[rows:] for term in terms]).reshape(-1)
    small = sum_everywhere(small, ("hg",))
    own = lax.axis_index("dp") * lax.axis_size("hid") + lax.axis_index("hid")
    gain_rows = width // (groups * lax.axis_size("hid"))
    norm_gain_grad = lax.dynamic_slice_in_dim(small, own * gain_rows, gain_rows, 0)
    qk_gains_grad = small[width : width + 2 * size].reshape(2, size)
    return (
        output,
        token_grad,
        norm_gain_grad,
        w_qkv_grad,
        qk_gains_grad,
        w_out_t_grad,
        w_in_grad,
        w_back_grad,
    )


def solution(mesh):
    return jax.shard_map(
        shards,
        mesh=mesh,
        in_specs=(
            P(("dp", "hid"), None),
            P(("dp", "hid")),
            P(),
            P(None, "hg"),
            P(),
            P(None, "hg"),
            P(None, ("hg", "hid")),
            P(None, ("hg", "hid")),
            P(("dp", "hid"), "hg"),
        ),
        out_specs=(
            P(("dp", "hid"), "hg"),
            P(("dp", "hid"), None),
            P(("dp", "hid")),
            P(("dp", "hid"), "hg"),
            P(),
            P(("dp", "hid"), "hg"),
            P("dp", ("hg", "hid")),
            P("dp", ("hg", "hid")),
        ),
        check_vma=False,
    )
```

```python
import functools
import math

import jax
import jax.numpy as jnp
from jax import lax
from jax.experimental import pallas as pl
from jax.experimental.pallas import tpu as pltpu
from jax.sharding import PartitionSpec as P

PATCHES = 196
EPSILON = 1e-06
LOG2E = math.log2(math.e)
LANES = 128
VMEM = pltpu.VMEM


def pinned(value):
    return pltpu.with_memory_space_constraint(value, pltpu.HBM)


SCALE = 1.0
ROOM = dict(forward=40, backward=24, dense=32, outputs=24, features=24, weights=24, token_rows=24)


def cost(microseconds):
    return pl.CostEstimate(
        flops=int(microseconds * SCALE * 1e9), bytes_accessed=2**20, transcendentals=0
    )


def times_t(left, right):
    return lax.dot_general(
        left, right, (((1,), (1,)), ((), ())), preferred_element_type=jnp.float32
    )


def rows_t(left, right):
    return lax.dot_general(
        left, right, (((0,), (0,)), ((), ())), preferred_element_type=jnp.float32
    )


def times(left, right):
    return jnp.dot(left, right, preferred_element_type=jnp.float32)


def low(value):
    return value.astype(jnp.bfloat16)


def wide(value):
    return value.astype(jnp.float32)


def lane_of(shape):
    return lax.broadcasted_iota(jnp.int32, shape, 1)


def row_of(shape):
    return lax.broadcasted_iota(jnp.int32, shape, 0)


def other_half(value):
    return pltpu.roll(value, LANES // 2, 1)


def spread_terms(whole):
    lane = lane_of(whole.shape)
    first = wide(low(whole))
    second = wide(low(whole - first))
    third = whole - first - second
    return jnp.where(lane == 64, first, jnp.where(lane == 65, second, jnp.where(lane == 66, third, 0.0)))


def three_terms(column, shape):
    return spread_terms(jnp.broadcast_to(column, shape))


def two_terms(value):
    first = low(value)
    return first, low(value - wide(first))


def pair_mask(block, shape, first_lane):
    start = 2 * PATCHES * block - first_lane
    place = lane_of(shape) - start
    second = row_of(shape) >= PATCHES
    begin = jnp.where(second, PATCHES, 0)
    return (place >= begin) & (place < begin + PATCHES)


def window_of(block):
    return (2 * PATCHES * block // LANES) * LANES, 4 * LANES


def forward_kernel(
    flag_ref,
    tok_hbm,
    gain_ref,
    w_hbm,
    qk_ref,
    normed_ref,
    q_hbm,
    k_hbm,
    v_hbm,
    att_ref,
    inv_ref,
    tok_ref,
    w_ref,
    q_ref,
    k_ref,
    v_ref,
    in_sems,
    out_sems,
):
    rows = tok_ref.shape[0]
    heads, padded, _ = q_ref.shape
    tile = 2 * PATCHES
    size = qk_ref.shape[1]
    columns = w_ref.shape[1]
    gain = wide(gain_ref[...]).reshape(1, -1)
    q_gain = wide(qk_ref[0:1, :]) * (size**-0.5 * LOG2E)
    k_gain = wide(qk_ref[1:2, :])
    ones = jnp.ones_like(k_gain)
    gains = jnp.concatenate([q_gain, k_gain, ones, q_gain, k_gain, ones], axis=1)
    is_value = jnp.concatenate([0 * ones, 0 * ones, ones, 0 * ones, 0 * ones, ones], axis=1)
    group_a = row_of((256, 256)) // size
    group_b = lane_of((256, 256)) // size
    mean_of = low(jnp.where(group_a == group_b, 1.0 / size, 0.0))
    stride = rows // (3 * LANES) and 3 * LANES
    strip = rows - (rows // stride - 1) * stride
    strips = rows // stride
    edges = [0] + [stride * step + 32 for step in range(1, strips)] + [rows]
    token_copies = []
    for step in range(strips):
        part = pl.ds(edges[step], edges[step + 1] - edges[step])
        token_copies.append(pltpu.make_async_copy(tok_hbm.at[part], tok_ref.at[part], in_sems.at[step]))
    w_copy = pltpu.make_async_copy(w_hbm, w_ref, in_sems.at[strips])
    token_copies[0].start()
    w_copy.start()
    for copy in token_copies[1:]:
        copy.start()
    lane = lane_of((strip, LANES))

    def project(step, _):
        for place, copy in enumerate(token_copies):
            pl.when(step == place)(copy.wait)
        here = pl.ds(pl.multiple_of(step * stride, LANES), strip)
        x = wide(tok_ref[here, :])
        x = x - jnp.mean(x, axis=1, keepdims=True)
        x = x * lax.rsqrt(jnp.mean(x * x, axis=1, keepdims=True) + EPSILON)
        normed = low(x * gain)
        normed_ref[here, :] = normed
        compact = jnp.zeros((strip, LANES), jnp.float32)
        for pair in range(heads // 2):
            joined = times(normed, w_ref[:, 384 * pair : 384 * pair + 384])
            parts = []
            for at in (0, 256):
                wid = min(256, 384 - at)
                block = joined[:, at : at + wid]
                means = mean_of[:wid, :wid]
                centred = block - times(low(block), means)
                squares = low(centred * centred)
                variance = times(squares, means)
                place = 6 * pair + at // size
                pick = low(
                    jnp.where(
                        row_of((wid, LANES)) // size + place == lane_of((wid, LANES)), 1.0 / size, 0.0
                    )
                )
                compact = compact + times(squares, pick)
                hat = centred * lax.rsqrt(variance + EPSILON)
                parts.append(
                    jnp.where(is_value[:, at : at + wid] > 0, block, hat * gains[:, at : at + wid])
                )
            b0, b1, b2 = parts[0][:, :128], parts[0][:, 128:], parts[1]
            first = lane < 64
            unit = jnp.where(lane < 67, 1.0, 0.0)
            q_ref[2 * pair, here, :] = low(jnp.where(first, b0, 0.0))
            k_ref[2 * pair, here, :] = low(jnp.where(first, other_half(b0), unit))
            v_ref[2 * pair, here, :] = low(jnp.where(first, b1, unit))
            q_ref[2 * pair + 1, here, :] = low(jnp.where(first, other_half(b1), 0.0))
            k_ref[2 * pair + 1, here, :] = low(jnp.where(first, b2, unit))
            v_ref[2 * pair + 1, here, :] = low(jnp.where(first, other_half(b2), unit))
        inv_ref[here, :] = lax.rsqrt(compact + EPSILON)
        return 0

    w_copy.wait()
    lax.fori_loop(0, strips, project, 0)
    lane = lane_of((tile, LANES))
    for ref in (q_ref, k_ref, v_ref):
        ref[:, rows:, :] = jnp.zeros((heads, padded - rows, LANES), jnp.bfloat16)
    key_copy = pltpu.make_async_copy(k_ref, k_hbm, out_sems.at[0])
    value_copy = pltpu.make_async_copy(v_ref, v_hbm, out_sems.at[1])
    key_copy.start()
    value_copy.start()

    def query_copy(pair):
        part = pl.ds(2 * pair, 2)
        return pltpu.make_async_copy(q_ref.at[part], q_hbm.at[part], out_sems.at[2 + pair])

    def attend(pair, _, big):
        for start in range(0, rows, tile):
            here = slice(start, start + tile)
            if big:
                keys = slice(0, padded)
            else:
                begin, length = window_of(start // tile)
                keys = slice(begin, begin + length)
            found = []
            for side in range(2):
                head = 2 * pair + side
                queries = q_ref[head, here, :]
                scores = times_t(queries, k_ref[head, keys, :])
                if not big:
                    scores = jnp.where(
                        pair_mask(start // tile, scores.shape, keys.start), scores, -1e30
                    )
                expo = low(jnp.exp2(scores))
                out = times(expo, v_ref[head, keys, :])
                total = out[:, 64:65]
                found.append(out * (1.0 / total))
                log_total = jnp.log(total) * (-LOG2E)
                q_ref[head, here, :] = low(
                    jnp.where(lane < 64, wide(queries), three_terms(log_total, lane.shape))
                )
            att_ref[here, pl.ds(pl.multiple_of(pair * LANES, LANES), LANES)] = low(
                jnp.where(lane < 64, found[0], other_half(found[1]))
            )
        query_copy(pair).start()
        return 0

    @pl.when(flag_ref[0] > 0)
    def _():
        lax.fori_loop(0, heads // 2, functools.partial(attend, big=True), 0)

    @pl.when(flag_ref[0] <= 0)
    def _():
        lax.fori_loop(0, heads // 2, functools.partial(attend, big=False), 0)

    key_copy.wait()
    value_copy.wait()
    for pair in range(heads // 2):
        query_copy(pair).wait()


def forward(big_images, tokens, norm_gain, w_qkv, qk_gains):
    rows, width = tokens.shape
    size = qk_gains.shape[1]
    heads = w_qkv.shape[1] // (3 * size)
    padded = -(-rows // 256) * 256
    whole = pl.BlockSpec(memory_space=VMEM)
    hbm = pl.BlockSpec(memory_space=pltpu.HBM)
    held = VMEM((heads, padded, LANES), jnp.bfloat16)
    head_rows = pltpu.HBM((heads, padded, LANES), jnp.bfloat16)
    return pl.pallas_call(
        forward_kernel,
        name="forward",
        out_shape=[
            jax.ShapeDtypeStruct((rows, width), jnp.bfloat16),
            head_rows,
            head_rows,
            head_rows,
            jax.ShapeDtypeStruct((rows, heads * size), jnp.bfloat16),
            jax.ShapeDtypeStruct((rows, LANES), jnp.float32),
        ],
        in_specs=[pl.BlockSpec(memory_space=pltpu.SMEM), hbm, whole, hbm, whole],
        out_specs=[whole, hbm, hbm, hbm, whole, whole],
        scratch_shapes=[
            VMEM((rows, width), jnp.bfloat16),
            VMEM(w_qkv.shape, jnp.bfloat16),
            held,
            held,
            held,
            pltpu.SemaphoreType.DMA((rows // (3 * LANES) + 1,)),
            pltpu.SemaphoreType.DMA((2 + heads // 2,)),
        ],
        compiler_params=pltpu.CompilerParams(vmem_limit_bytes=ROOM["forward"] * 2**20),
        cost_estimate=cost(24),
    )(big_images, pinned(tokens), norm_gain, pinned(w_qkv), qk_gains)


def backward_kernel(
    flag_ref, q_ref, k_ref, v_ref, do_ref, inv_ref, qk_ref, joined_ref, small_ref, dq_ref, dk_ref, dv_ref, turned_ref
):
    pair = pl.program_id(0)
    rows = inv_ref.shape[0]
    padded = q_ref.shape[1]
    tile = 2 * PATCHES
    size = qk_ref.shape[1]
    scale = size**-0.5
    zeros = jnp.zeros((1, LANES - size), jnp.float32)
    q_gain = wide(qk_ref[0:1, :])
    k_gain = wide(qk_ref[1:2, :])
    q_back = jnp.concatenate([1.0 / (q_gain * (scale * LOG2E)), zeros], axis=1)
    k_back = jnp.concatenate([1.0 / k_gain, zeros], axis=1)
    q_gain = jnp.concatenate([q_gain, zeros], axis=1)
    k_gain = jnp.concatenate([k_gain, zeros], axis=1)

    def attend(side, _, big):
        for start in range(0, rows, tile):
            here = slice(start, start + tile)
            if big:
                over = slice(0, padded)
            else:
                begin, length = window_of(start // tile)
                over = slice(begin, begin + length)
            keys = k_ref[side, here, :]
            queries = q_ref[side, over, :]
            grads = do_ref[side, over, :]
            scores = times_t(keys, queries)
            if not big:
                scores = jnp.where(pair_mask(start // tile, scores.shape, over.start), scores, -1e30)
            probs = jnp.exp2(scores)
            grad_probs = times_t(v_ref[side, here, :], grads)
            grad_scores = low(probs * grad_probs)
            dv_ref[side, here, :] = times(low(probs), grads)
            dk_ref[side, here, :] = times(grad_scores, queries)
            more = rows_t(keys, grad_scores)
            if big and start == 0:
                dq_ref[side, :, over] = more
            elif big:
                dq_ref[side, :, over] += more
            else:
                place = lane_of(more.shape) - (start - over.start)
                dq_ref[side, :, over] = jnp.where(
                    (place >= 0) & (place < tile), more, dq_ref[side, :, over]
                )
        return 0

    @pl.when(flag_ref[0] > 0)
    def _():
        lax.fori_loop(0, 2, functools.partial(attend, big=True), 0)

    @pl.when(flag_ref[0] <= 0)
    def _():
        lax.fori_loop(0, 2, functools.partial(attend, big=False), 0)

    @pl.when(pair == 0)
    def _():
        small_ref[...] = jnp.zeros_like(small_ref)

    lane = lane_of((tile, LANES))
    first = lane < 64
    shape = (2 * LANES, 2 * LANES)
    row, column = row_of(shape), lane_of(shape)
    means = (row // LANES == column // LANES) & (row % LANES < size)
    means = low(jnp.where(means, 1.0 / size, 0.0))
    gains = jnp.concatenate([q_gain * scale, k_gain * math.log(2.0)], axis=1)
    factors = jnp.concatenate([jnp.full_like(q_gain, scale), jnp.full_like(k_gain, math.log(2.0))], axis=1)
    backs = jnp.concatenate([q_back, k_back], axis=1)
    for side in range(2):
        turned_ref[side] = dq_ref[side].T
    for start in range(0, rows, tile):
        here = slice(start, start + tile)
        inverse_first, inverse_second = two_terms(inv_ref[here, :])
        blocks = []
        for side in range(2):
            shape = (LANES, 2 * LANES)
            source = 6 * pair + 3 * side + lane_of(shape) // LANES
            pick = low(jnp.where(row_of(shape) == source, 1.0, 0.0))
            inverse = times(inverse_first, pick) + times(inverse_second, pick)
            hat = jnp.concatenate([q_ref[side, here, :], k_ref[side, here, :]], axis=1)
            hat = wide(hat) * backs
            grad = jnp.concatenate([turned_ref[side, here, :], dk_ref[side, here, :]], axis=1)
            small_ref[0:1, :] += jnp.sum(grad * hat, axis=0, keepdims=True) * factors
            grad = grad * gains
            inner = times(low(grad * hat), means)
            grad = inverse * (grad - times(low(grad), means) - hat * inner)
            blocks.append((grad[:, :LANES], grad[:, LANES:], dv_ref[side, here, :]))
        (q0, k0, v0), (q1, k1, v1) = blocks
        joined_ref[here, 0:128] = low(jnp.where(first, q0, other_half(k0)))
        joined_ref[here, 128:256] = low(jnp.where(first, v0, other_half(q1)))
        joined_ref[here, 256:384] = low(jnp.where(first, k1, other_half(v1)))


def backward(big_images, q_rows, k_rows, v_rows, do_rows, inverses, qk_gains):
    heads, padded, _ = q_rows.shape
    rows = inverses.shape[0]
    pair_spec = pl.BlockSpec((2, padded, LANES), lambda pair: (pair, 0, 0))
    return pl.pallas_call(
        backward_kernel,
        name="backward",
        grid=(heads // 2,),
        out_shape=[
            jax.ShapeDtypeStruct((rows, heads * 3 * LANES // 2), jnp.bfloat16),
            jax.ShapeDtypeStruct((8, 2 * LANES), jnp.float32),
        ],
        in_specs=[pl.BlockSpec(memory_space=pltpu.SMEM)]
        + [pair_spec] * 4
        + [pl.BlockSpec((rows, LANES), lambda pair: (0, 0)), pl.BlockSpec(qk_gains.shape, lambda pair: (0, 0))],
        out_specs=[
            pl.BlockSpec((rows, 3 * LANES), lambda pair: (0, pair)),
            pl.BlockSpec((8, 2 * LANES), lambda pair: (0, 0)),
        ],
        scratch_shapes=[
            VMEM((2, LANES, padded), jnp.float32),
            VMEM((2, rows, LANES), jnp.float32),
            VMEM((2, rows, LANES), jnp.float32),
            VMEM((2, padded, LANES), jnp.float32),
        ],
        compiler_params=pltpu.CompilerParams(vmem_limit_bytes=ROOM["backward"] * 2**20),
        cost_estimate=cost(36),
    )(big_images, pinned(q_rows), pinned(k_rows), pinned(v_rows), do_rows, inverses, qk_gains)


FINE = 2 * PATCHES


def in_order(mine, other):
    first = lax.axis_index("hg") == 0
    return jnp.where(first, mine, other), jnp.where(first, other, mine)


def dense_kernel(count, tiles, normed_ref, mine_ref, other_ref, *refs):
    w_in_refs, w_back_refs = refs[:count], refs[count : 2 * count]
    refs = refs[2 * count :]
    part_ref, grad_ref, normed_t_ref, dy_t_ref = refs[:4]
    grad_refs, refs = refs[4 : 4 + count], refs[4 + count :]
    normed_rows, dy_rows = refs[:2]
    act_refs, gup_refs = refs[2 : 2 + count], refs[2 + count :]
    step = pl.program_id(0)
    half = mine_ref.shape[1]
    curve = math.sqrt(2.0 / math.pi)
    normed = normed_ref[...]
    dy_rows[step, :, :half], dy_rows[step, :, half:] = in_order(mine_ref[...], other_ref[...])
    dy = dy_rows[step]
    normed_rows[step] = normed
    for w_in_ref, w_back_ref, act_ref, gup_ref in zip(w_in_refs, w_back_refs, act_refs, gup_refs):
        columns = w_in_ref.shape[1]
        width = min(256, columns)
        for at in range(0, columns, width):
            cols = slice(at, min(at + width, columns))
            up = times(normed, w_in_ref[:, cols])
            grad_act = times(dy, w_back_ref[:, cols])
            square = up * up
            bent = jnp.tanh(up * (curve + (curve * 0.044715) * square))
            gate = 0.5 + 0.5 * bent
            act = up * gate
            slope = gate + act * ((1.0 - gate) * (2 * curve + (6 * curve * 0.044715) * square))
            act_ref[step, :, cols] = low(act)
            gup_ref[step, :, cols] = low(grad_act * slope)
    total, grad = None, None
    for act_ref, w_back_ref, gup_ref, w_in_ref in zip(act_refs, w_back_refs, gup_refs, w_in_refs):
        part = times_t(act_ref[step], w_back_ref[...])
        total = part if total is None else total + part
        part = times_t(gup_ref[step], w_in_ref[...])
        grad = part if grad is None else grad + part
    part_ref[...] = total
    grad_ref[...] = low(grad)

    @pl.when(step == tiles - 1)
    def _():
        rows, width = tiles * normed_rows.shape[1], normed_rows.shape[2]
        for source, turned in ((normed_rows, normed_t_ref), (dy_rows, dy_t_ref)):
            turned[:, :rows] = source[...].reshape(rows, width).T
            turned[:, rows:] = jnp.zeros((width, turned.shape[1] - rows), jnp.bfloat16)
        for act_ref, gup_ref, ref in zip(act_refs, gup_refs, grad_refs):
            columns = act_ref.shape[2]
            for turned, right, at in ((normed_t_ref, gup_ref, 0), (dy_t_ref, act_ref, columns)):
                total = times(turned[:, :rows], right[...].reshape(rows, columns))
                by_parity(total, ref, slice(at, at + columns))


def by_parity(total, ref, cols):
    halves, rows = ref.shape[1:3]
    odd = lax.axis_index("dp") & 1
    for half in range(halves):
        for side in range(2):
            start = (2 * half + side) * rows
            ref[odd ^ side, half, :, cols] = total[start : start + rows].astype(ref.dtype)


def dense(normed, mine, other, w_in_pieces, w_back_pieces):
    rows, width = normed.shape
    tile = 2 * PATCHES
    tiles = rows // tile
    count = len(w_in_pieces)
    shape = jax.ShapeDtypeStruct
    sizes = [piece.shape[1] for piece in w_in_pieces]
    groups = lax.axis_size("dp")
    padded = -(-rows // 256) * 256
    row_tile = lambda columns: pl.BlockSpec((tile, columns), lambda step: (step, 0))
    turned = pl.BlockSpec((width, padded), lambda step: (0, 0))
    once = lambda columns: pl.BlockSpec((width, columns), lambda step: (0, 0), pipeline_mode=pl.Buffered(1))
    return pl.pallas_call(
        functools.partial(dense_kernel, count, tiles),
        name="dense",
        grid=(tiles,),
        out_shape=[
            shape((rows, width), jnp.float32),
            shape((rows, width), jnp.bfloat16),
            shape((width, padded), jnp.bfloat16),
            shape((width, padded), jnp.bfloat16),
        ]
        + [shape((2, groups // 2, width // groups, 2 * size), jnp.bfloat16) for size in sizes],
        in_specs=[row_tile(width), row_tile(width // 2), row_tile(width // 2)]
        + [once(size) for size in sizes] * 2,
        out_specs=[row_tile(width)] * 2
        + [turned] * 2
        + [
            pl.BlockSpec((2, groups // 2, width // groups, 2 * size), lambda step: (0, 0, 0, 0))
            for size in sizes
        ],
        scratch_shapes=[VMEM((tiles, tile, width), jnp.bfloat16)] * 2
        + [VMEM((tiles, tile, size), jnp.bfloat16) for size in sizes] * 2,
        compiler_params=pltpu.CompilerParams(vmem_limit_bytes=ROOM["dense"] * 2**20),
        cost_estimate=cost(24),
    )(normed, mine, other, *w_in_pieces, *w_back_pieces)


def outputs_kernel(part_ref, tok_ref, att_ref, mine_ref, other_ref, w_out_ref, keep_ref, send_ref, do_ref):
    tile, width = part_ref.shape
    half = width // 2
    heads, padded, _ = do_ref.shape
    lane = lane_of((tile, LANES))
    attended = att_ref[...]
    left = times_t(attended, w_out_ref[...]) + part_ref[...]
    token = tok_ref[...]
    keep, send = in_order(left[:, :half], left[:, half:])
    keep_ref[...] = keep + in_order(wide(token[:, :half]), wide(token[:, half:]))[0]
    send_ref[...] = low(send)
    first, second = in_order(mine_ref[...], other_ref[...])
    grad_att = times(first, w_out_ref[:half, :]) + times(second, w_out_ref[half:, :])
    shape = (LANES, 2 * LANES)
    row, column = row_of(shape), lane_of(shape)
    inners = (row // 64 == column // LANES) & (column % LANES >= 64) & (column % LANES < 67)
    inners = low(jnp.where(inners, -1.0, 0.0))
    found = []
    for pair in range(heads // 2):
        cols = slice(pair * LANES, pair * LANES + LANES)
        low_block = wide(low(grad_att[:, cols]))
        weighed, rest = two_terms(low_block * wide(attended[:, cols]))
        inner = times(weighed, inners) + times(rest, inners)
        for side in range(2):
            value = low_block if side == 0 else other_half(low_block)
            term = spread_terms(inner[:, side * LANES : (side + 1) * LANES])
            found.append(low(jnp.where(lane < 64, value, term)))
    for step in range(3):

        @pl.when(pl.program_id(0) == step)
        def _(step=step):
            for head in range(heads):
                do_ref[head, step * tile : (step + 1) * tile, :] = found[head]
            if step == 2:
                do_ref[:, 3 * tile :, :] = jnp.zeros((heads, padded - 3 * tile, LANES), jnp.bfloat16)


def outputs(part, tokens, attended, mine, other, w_out_t):
    rows, width = tokens.shape
    tile = 2 * PATCHES
    heads = w_out_t.shape[1] // 64
    padded = -(-rows // 256) * 256
    shape = jax.ShapeDtypeStruct
    row_tile = lambda columns: pl.BlockSpec((tile, columns), lambda step: (step, 0))
    return pl.pallas_call(
        outputs_kernel,
        name="outputs",
        grid=(rows // tile,),
        out_shape=[
            shape((rows, width // 2), jnp.float32),
            shape((rows, width // 2), jnp.bfloat16),
            shape((heads, padded, LANES), jnp.bfloat16),
        ],
        in_specs=[row_tile(columns) for columns in (width, width, width // 2, width // 2, width // 2)]
        + [pl.BlockSpec(w_out_t.shape, lambda step: (0, 0))],
        out_specs=[
            row_tile(width // 2),
            row_tile(width // 2),
            pl.BlockSpec((heads, padded, LANES), lambda step: (0, 0, 0)),
        ],
        compiler_params=pltpu.CompilerParams(vmem_limit_bytes=ROOM["outputs"] * 2**20),
        cost_estimate=cost(6),
    )(part, tokens, attended, mine, other, w_out_t)


def features_kernel(joined_ref, w_ref, mlp_ref, tok_ref, sent_ref, gain_ref):
    grad = times_t(joined_ref[...], w_ref[...]) + wide(mlp_ref[...])
    sent_ref[...] = low(grad)
    x = wide(tok_ref[...])
    x = x - jnp.mean(x, axis=1, keepdims=True)
    x = x * lax.rsqrt(jnp.mean(x * x, axis=1, keepdims=True) + EPSILON)

    @pl.when(pl.program_id(0) == 0)
    def _():
        gain_ref[...] = jnp.zeros_like(gain_ref)

    gain_ref[0:1, :] += jnp.sum(grad * x, axis=0, keepdims=True)


def features(first, count, grad_joined, w_qkv, grad_mlp, tokens):
    rows, width = tokens.shape
    tile = FINE
    row_tile = lambda columns: pl.BlockSpec((tile, columns), lambda step: (step + first, 0))
    return pl.pallas_call(
        features_kernel,
        name="features",
        grid=(count,),
        out_shape=[
            jax.ShapeDtypeStruct((tile * count, width), jnp.bfloat16),
            jax.ShapeDtypeStruct((8, width), jnp.float32),
        ],
        in_specs=[
            row_tile(grad_joined.shape[1]),
            pl.BlockSpec(w_qkv.shape, lambda step: (0, 0)),
            row_tile(width),
            row_tile(width),
        ],
        out_specs=[
            pl.BlockSpec((tile, width), lambda step: (step, 0)),
            pl.BlockSpec((8, width), lambda step: (0, 0)),
        ],
        compiler_params=pltpu.CompilerParams(vmem_limit_bytes=ROOM["features"] * 2**20),
        cost_estimate=cost(0.3 * count),
    )(grad_joined, w_qkv, grad_mlp, tokens)


def weights_kernel(*refs):
    keep_ref, send_ref = refs[-2:]
    halves, rows = keep_ref.shape[1:3]
    odd, side = lax.axis_index("dp") & 1, lax.axis_index("hid")
    at = 0
    for left_ref, right_ref in zip(refs[:-2:2], refs[1:-2:2]):
        tokens, columns = right_ref.shape
        total = times(left_ref[:, :tokens], right_ref[...])
        cols = slice(at, at + columns)
        at += columns
        for half in range(halves):
            for parity in range(2):
                start = 2 * (2 * half + parity) * rows
                even, uneven = total[start : start + rows], total[start + rows : start + 2 * rows]
                keep_ref[odd ^ parity, half, :, cols] = low(jnp.where(side == 0, even, uneven))
                send_ref[odd ^ parity, half, :, cols] = low(jnp.where(side == 0, uneven, even))


def weights(*products):
    groups = lax.axis_size("dp")
    columns = sum(size for _, _, size, _ in products)
    shape = (2, groups // 2, products[0][0].shape[0] // (2 * groups), columns)
    whole = lambda shape: pl.BlockSpec(shape, lambda step: (0,) * len(shape))
    specs, operands = [], []
    for turned, right, size, place in products:
        specs += [
            whole(turned.shape),
            pl.BlockSpec((right.shape[0], size), lambda step, place=place: (0, place)),
        ]
        operands += [turned, right]
    return pl.pallas_call(
        weights_kernel,
        name="weights",
        grid=(1,),
        out_shape=[jax.ShapeDtypeStruct(shape, jnp.bfloat16)] * 2,
        in_specs=specs,
        out_specs=[whole(shape)] * 2,
        compiler_params=pltpu.CompilerParams(vmem_limit_bytes=ROOM["weights"] * 2**20),
        cost_estimate=cost(3),
    )(*operands)


def tokens_kernel(sent_ref, came_ref, tok_ref, gain_ref, mine_ref, other_ref, *refs):
    out_ref = refs[-1]
    half = mine_ref.shape[1]
    grad = (wide(sent_ref[...]) + wide(came_ref[...])) * wide(gain_ref[...]).reshape(1, -1)
    x = wide(tok_ref[...])
    x = x - jnp.mean(x, axis=1, keepdims=True)
    inverse = lax.rsqrt(jnp.mean(x * x, axis=1, keepdims=True) + EPSILON)
    x = x * inverse
    inner = jnp.mean(grad * x, axis=1, keepdims=True)
    grad = inverse * (grad - jnp.mean(grad, axis=1, keepdims=True) - x * inner)
    first, second = in_order(wide(mine_ref[...]), wide(other_ref[...]))
    out_ref[:, :half] = low(grad[:, :half] + first)
    out_ref[:, half:] = low(grad[:, half:] + second)


def token_rows(first, sent, came, tokens, norm_gain, mine, other, before):
    rows, width = tokens.shape
    tile = FINE
    count = sent.shape[0] // tile
    near = lambda columns: pl.BlockSpec((tile, columns), lambda step: (step, 0))
    far = lambda columns: pl.BlockSpec((tile, columns), lambda step: (step + first, 0))
    more = [] if before is None else [before]
    return pl.pallas_call(
        tokens_kernel,
        name="token_rows",
        grid=(count,),
        out_shape=jax.ShapeDtypeStruct((rows, width), jnp.bfloat16),
        in_specs=[
            near(width),
            near(width),
            far(width),
            pl.BlockSpec((width,), lambda step: (0,)),
            far(width // 2),
            far(width // 2),
        ]
        + [pl.BlockSpec(memory_space=pl.ANY)] * len(more),
        out_specs=far(width),
        input_output_aliases={6: 0} if more else {},
        compiler_params=pltpu.CompilerParams(vmem_limit_bytes=ROOM["token_rows"] * 2**20),
        cost_estimate=cost(0.3 * count),
    )(sent, came, tokens, norm_gain, mine, other, *more)


def swap(value, axis, bit):
    size = lax.axis_size(axis)
    return lax.ppermute(value, axis, [(place, place ^ bit) for place in range(size)])


def bits_of(axis):
    size = lax.axis_size(axis)
    return [1 << place for place in range(size.bit_length() - 1)]


def gather_pieces(block, axis):
    pieces = [block]
    for bit in bits_of(axis):
        held = pieces[0] if len(pieces) == 1 else jnp.concatenate(pieces, axis=1)
        pieces.append(swap(held, axis, bit))
    return pieces


def scatter_pieces(pieces, axis):
    for bit in reversed(bits_of(axis)):
        sent = swap(low(pieces[-1]), axis, bit)
        kept, at, half = [], 0, sent.shape[-1] // 2
        for piece in pieces[:-1]:
            size = piece.shape[-1] // 2
            parts = (sent[..., at : at + size], sent[..., half + at : half + at + size])
            kept.append(wide(piece) + wide(jnp.concatenate(parts, axis=-1) if size < half else sent))
            at += size
        pieces = kept
    return pieces[0]


def row_blocks(*products):
    groups, sides = lax.axis_size("dp"), lax.axis_size("hid")
    width = products[0][0].shape[0]
    if sides == 2 and width % (16 * groups * sides) == 0:
        keep, send = weights(*products)
        return wide(keep) + wide(swap(send, "hid", 1))
    parts = []
    for turned, right, size, place in products:
        parts.append(times(turned[:, : right.shape[0]], right[:, place * size : place * size + size]))
    shaped = jnp.concatenate(parts, axis=1).reshape(groups // 2, 2, sides, width // (groups * sides), -1)
    odd = lax.axis_index("dp") & 1
    shaped = shaped[:, odd ^ jnp.arange(2)][:, :, lax.axis_index("hid") ^ jnp.arange(sides)]
    shaped = shaped.transpose(1, 0, 2, 3, 4)
    for bit in reversed(bits_of("hid")):
        shaped = shaped[:, :, :bit] + wide(swap(low(shaped[:, :, bit:]), "hid", bit))
    return shaped[:, :, 0]


def halve(shaped):
    return low(shaped[0]), swap(low(shaped[1]), "dp", 1)


def rest_terms(kept, came):
    count = lax.axis_size("dp")
    groups = [list(range(odd, count, 2)) for odd in (0, 1)]
    total = low(wide(kept) + wide(came))
    return lax.all_to_all(total, "dp", 0, 0, axis_index_groups=groups, tiled=True)


def far_terms(total):
    me = lax.axis_index("dp") // 2
    terms = [lax.dynamic_index_in_dim(total, me, keepdims=False)]
    for step in range(1, total.shape[0]):
        block = lax.dynamic_index_in_dim(total, me ^ step, keepdims=False)
        terms.append(swap(block, "dp", 2 * step))
    return terms


def added(terms):
    values = [wide(term) for term in terms]
    while len(values) > 1:
        values = [first + second for first, second in zip(values[::2], values[1::2])]
    return values[0]


def sum_everywhere(value, axes):
    for axis in axes:
        for bit in bits_of(axis):
            value = value + swap(value, axis, bit)
    return value


def shards(tokens, big_images, norm_gain, w_qkv, qk_gains, w_out_t, w_in, w_back, cotangent):
    width = tokens.shape[1]
    size = qk_gains.shape[1]
    groups = lax.axis_size("dp")
    other = swap(cotangent, "hg", 1)
    w_in_pieces = gather_pieces(w_in, "hid")
    w_back_pieces = gather_pieces(w_back, "hid")
    normed, q_rows, k_rows, v_rows, attended, inverses = forward(
        big_images, tokens, norm_gain, w_qkv, qk_gains
    )
    part, grad_mlp, normed_t, dy_t, *grads = dense(normed, cotangent, other, w_in_pieces, w_back_pieces)
    kept, sent, do_rows = outputs(part, tokens, attended, cotangent, other, w_out_t)
    out_came = swap(sent, "hg", 1)
    mlp_kept, mlp_came = halve(scatter_pieces(grads, "hid"))
    do_rows, mlp_kept = lax.optimization_barrier((do_rows, mlp_kept))

    grad_joined, qk_part = backward(big_images, q_rows, k_rows, v_rows, do_rows, inverses, qk_gains)
    grad_joined, out_came, mlp_came = lax.optimization_barrier((grad_joined, out_came, mlp_came))
    mine, gain_part = features(0, tokens.shape[0] // FINE, grad_joined, w_qkv, grad_mlp, tokens)
    mine, mlp_came = lax.optimization_barrier((mine, mlp_came))
    came = swap(mine, "hg", 1)
    columns = attended.shape[1]

    def weight_sums(normed_t, dy_t, grad_joined, attended, gain_part, qk_part, kept, out_came):
        first_blocks = row_blocks((normed_t, grad_joined, 2 * columns, 0))
        blocks = row_blocks((normed_t, grad_joined, columns, 2), (dy_t, attended, columns, 0))
        small = jnp.concatenate([gain_part[0], qk_part[0, :size], qk_part[0, LANES : LANES + size]])
        small = low(sum_everywhere(small, ("hid",)))
        small, first_blocks = lax.optimization_barrier((small, first_blocks))
        first_kept, first_came = halve(first_blocks)
        second_kept, second_came = halve(blocks)
        small = low(wide(small) + wide(swap(small, "dp", 1)))
        small = jnp.pad(small, (0, 8 * 4 * columns - small.shape[0])).reshape(1, 8, -1)
        first = low(wide(first_kept) + wide(first_came))
        second = low(wide(second_kept) + wide(second_came))
        small = jnp.broadcast_to(small, first.shape[:1] + small.shape[1:])
        sums = jnp.concatenate([jnp.concatenate([first, second], axis=2), small], axis=1)
        return sums, low(kept + wide(out_came))

    def no_sums(*operands):
        return jax.tree.map(lambda kind: jnp.zeros(kind.shape, kind.dtype), kinds)

    operands = (normed_t, dy_t, grad_joined, attended, gain_part, qk_part, kept, out_came)
    kinds = jax.eval_shape(weight_sums, *operands)
    sums, output = lax.cond(big_images[0] >= 0, weight_sums, no_sums, *operands)
    mlp_terms = rest_terms(mlp_kept, mlp_came)
    hidden = mlp_terms.shape[2] // 2
    w_in_grad = jnp.sum(wide(mlp_terms[:, :, :hidden]), axis=0)
    w_back_grad = jnp.sum(wide(mlp_terms[:, :, hidden:]), axis=0)
    terms = far_terms(sums)
    token_grad = token_rows(0, mine, came, tokens, norm_gain, cotangent, other, None)
    terms[1], token_grad = lax.optimization_barrier((terms[1], token_grad))
    rows = sums.shape[1] - 8
    w_qkv_grad = added([term[:rows, : 3 * columns] for term in terms])
    w_out_t_grad = added([term[:rows, 3 * columns :] for term in terms])
    small = added([term[rows : rows + 1] for term in terms]).reshape(-1)
    small = sum_everywhere(small, ("hg",))
    own = lax.axis_index("dp") * lax.axis_size("hid") + lax.axis_index("hid")
    gain_rows = width // (groups * lax.axis_size("hid"))
    norm_gain_grad = lax.dynamic_slice_in_dim(small, own * gain_rows, gain_rows, 0)
    qk_gains_grad = small[width : width + 2 * size].reshape(2, size)
    return (
        output,
        token_grad,
        norm_gain_grad,
        w_qkv_grad,
        qk_gains_grad,
        w_out_t_grad,
        w_in_grad,
        w_back_grad,
    )


def solution(mesh):
    return jax.shard_map(
        shards,
        mesh=mesh,
        in_specs=(
            P(("dp", "hid"), None),
            P(("dp", "hid")),
            P(),
            P(None, "hg"),
            P(),
            P(None, "hg"),
            P(None, ("hg", "hid")),
            P(None, ("hg", "hid")),
            P(("dp", "hid"), "hg"),
        ),
        out_specs=(
            P(("dp", "hid"), "hg"),
            P(("dp", "hid"), None),
            P(("dp", "hid")),
            P(("dp", "hid"), "hg"),
            P(),
            P(("dp", "hid"), "hg"),
            P("dp", ("hg", "hid")),
            P("dp", ("hg", "hid")),
        ),
        check_vma=False,
    )
```

```python
import functools
import math

import jax
import jax.numpy as jnp
from jax import lax
from jax.experimental import pallas as pl
from jax.experimental.pallas import tpu as pltpu
from jax.sharding import PartitionSpec as P

PATCHES = 196
EPSILON = 1e-06
LOG2E = math.log2(math.e)
LANES = 128
VMEM = pltpu.VMEM


def pinned(value):
    return pltpu.with_memory_space_constraint(value, pltpu.HBM)


SCALE = 1.0
ROOM = dict(forward=40, backward=24, dense=32, outputs=24, features=24, weights=24, token_rows=24)


def cost(microseconds):
    return pl.CostEstimate(
        flops=int(microseconds * SCALE * 1e9), bytes_accessed=2**20, transcendentals=0
    )


def times_t(left, right):
    return lax.dot_general(
        left, right, (((1,), (1,)), ((), ())), preferred_element_type=jnp.float32
    )


def rows_t(left, right):
    return lax.dot_general(
        left, right, (((0,), (0,)), ((), ())), preferred_element_type=jnp.float32
    )


def times(left, right):
    return jnp.dot(left, right, preferred_element_type=jnp.float32)


def low(value):
    return value.astype(jnp.bfloat16)


def wide(value):
    return value.astype(jnp.float32)


def lane_of(shape):
    return lax.broadcasted_iota(jnp.int32, shape, 1)


def row_of(shape):
    return lax.broadcasted_iota(jnp.int32, shape, 0)


def other_half(value):
    return pltpu.roll(value, LANES // 2, 1)


def spread_terms(whole):
    lane = lane_of(whole.shape)
    first = wide(low(whole))
    second = wide(low(whole - first))
    third = whole - first - second
    return jnp.where(lane == 64, first, jnp.where(lane == 65, second, jnp.where(lane == 66, third, 0.0)))


def three_terms(column, shape):
    return spread_terms(jnp.broadcast_to(column, shape))


def two_terms(value):
    first = low(value)
    return first, low(value - wide(first))


def pair_mask(block, shape, first_lane):
    start = 2 * PATCHES * block - first_lane
    place = lane_of(shape) - start
    second = row_of(shape) >= PATCHES
    begin = jnp.where(second, PATCHES, 0)
    return (place >= begin) & (place < begin + PATCHES)


def window_of(block):
    return (2 * PATCHES * block // LANES) * LANES, 4 * LANES


def forward_kernel(
    flag_ref,
    tok_hbm,
    gain_hbm,
    w_hbm,
    qk_hbm,
    normed_ref,
    q_hbm,
    k_hbm,
    v_hbm,
    att_ref,
    inv_ref,
    tok_ref,
    gain_ref,
    w_ref,
    qk_ref,
    q_ref,
    k_ref,
    v_ref,
    in_sems,
    out_sems,
):
    rows = tok_ref.shape[0]
    heads, padded, _ = q_ref.shape
    tile = 2 * PATCHES
    size = qk_ref.shape[1]
    group_a = row_of((256, 256)) // size
    group_b = lane_of((256, 256)) // size
    mean_of = low(jnp.where(group_a == group_b, 1.0 / size, 0.0))
    stride = rows // (3 * LANES) and 3 * LANES
    strip = rows - (rows // stride - 1) * stride
    strips = rows // stride
    edges = [0] + [stride * step + 32 for step in range(1, strips)] + [rows]
    token_copies = []
    for step in range(strips):
        part = pl.ds(edges[step], edges[step + 1] - edges[step])
        token_copies.append(pltpu.make_async_copy(tok_hbm.at[part], tok_ref.at[part], in_sems.at[step]))
    w_copy = pltpu.make_async_copy(w_hbm, w_ref, in_sems.at[strips])
    small_copies = [
        pltpu.make_async_copy(source, target, in_sems.at[strips + 1 + place])
        for place, (source, target) in enumerate(((gain_hbm, gain_ref), (qk_hbm, qk_ref)))
    ]
    for copy in small_copies:
        copy.start()
    token_copies[0].start()
    w_copy.start()
    for copy in token_copies[1:]:
        copy.start()
    lane = lane_of((strip, LANES))

    for copy in small_copies:
        copy.wait()
    gain = wide(gain_ref[...]).reshape(1, -1)
    q_gain = wide(qk_ref[0:1, :]) * (size**-0.5 * LOG2E)
    k_gain = wide(qk_ref[1:2, :])
    ones = jnp.ones_like(k_gain)
    gains = jnp.concatenate([q_gain, k_gain, ones, q_gain, k_gain, ones], axis=1)
    is_value = jnp.concatenate([0 * ones, 0 * ones, ones, 0 * ones, 0 * ones, ones], axis=1)

    def project(step, _):
        for place, copy in enumerate(token_copies):
            pl.when(step == place)(copy.wait)
        here = pl.ds(pl.multiple_of(step * stride, LANES), strip)
        x = wide(tok_ref[here, :])
        x = x - jnp.mean(x, axis=1, keepdims=True)
        x = x * lax.rsqrt(jnp.mean(x * x, axis=1, keepdims=True) + EPSILON)
        normed = low(x * gain)
        normed_ref[here, :] = normed
        every = times(normed, w_ref[...])
        for pair in range(heads // 2):
            joined = every[:, 384 * pair : 384 * pair + 384]
            parts = []
            for at in (0, 256):
                wid = min(256, 384 - at)
                block = joined[:, at : at + wid]
                means = mean_of[:wid, :wid]
                centred = block - times(low(block), means)
                squares = low(centred * centred)
                variance = times(squares, means)
                inverse = lax.rsqrt(variance + EPSILON)
                inv_ref[here, 384 * pair + at : 384 * pair + at + wid] = low(inverse)
                hat = centred * inverse
                parts.append(
                    jnp.where(is_value[:, at : at + wid] > 0, block, hat * gains[:, at : at + wid])
                )
            b0, b1, b2 = parts[0][:, :128], parts[0][:, 128:], parts[1]
            first = lane < 64
            unit = jnp.where(lane < 67, 1.0, 0.0)
            q_ref[2 * pair, here, :] = low(jnp.where(first, b0, 0.0))
            k_ref[2 * pair, here, :] = low(jnp.where(first, other_half(b0), unit))
            v_ref[2 * pair, here, :] = low(jnp.where(first, b1, unit))
            q_ref[2 * pair + 1, here, :] = low(jnp.where(first, other_half(b1), 0.0))
            k_ref[2 * pair + 1, here, :] = low(jnp.where(first, b2, unit))
            v_ref[2 * pair + 1, here, :] = low(jnp.where(first, other_half(b2), unit))
        return 0

    w_copy.wait()
    lax.fori_loop(0, strips, project, 0)
    lane = lane_of((tile, LANES))
    for ref in (q_ref, k_ref, v_ref):
        ref[:, rows:, :] = jnp.zeros((heads, padded - rows, LANES), jnp.bfloat16)
    key_copy = pltpu.make_async_copy(k_ref, k_hbm, out_sems.at[0])
    value_copy = pltpu.make_async_copy(v_ref, v_hbm, out_sems.at[1])
    key_copy.start()
    value_copy.start()

    def query_copy(pair):
        part = pl.ds(2 * pair, 2)
        return pltpu.make_async_copy(q_ref.at[part], q_hbm.at[part], out_sems.at[2 + pair])

    def attend(pair, _, big):
        for start in range(0, rows, tile):
            here = slice(start, start + tile)
            if big:
                keys = slice(0, padded)
            else:
                begin, length = window_of(start // tile)
                keys = slice(begin, begin + length)
            found = []
            for side in range(2):
                head = 2 * pair + side
                queries = q_ref[head, here, :]
                scores = times_t(queries, k_ref[head, keys, :])
                if not big:
                    scores = jnp.where(
                        pair_mask(start // tile, scores.shape, keys.start), scores, -1e30
                    )
                expo = low(jnp.exp2(scores))
                out = times(expo, v_ref[head, keys, :])
                total = out[:, 64:65]
                found.append(out * (1.0 / total))
                log_total = jnp.log(total) * (-LOG2E)
                q_ref[head, here, :] = low(
                    jnp.where(lane < 64, wide(queries), three_terms(log_total, lane.shape))
                )
            att_ref[here, pl.ds(pl.multiple_of(pair * LANES, LANES), LANES)] = low(
                jnp.where(lane < 64, found[0], other_half(found[1]))
            )
        query_copy(pair).start()
        return 0

    @pl.when(flag_ref[0] > 0)
    def _():
        lax.fori_loop(0, heads // 2, functools.partial(attend, big=True), 0)

    @pl.when(flag_ref[0] <= 0)
    def _():
        lax.fori_loop(0, heads // 2, functools.partial(attend, big=False), 0)

    key_copy.wait()
    value_copy.wait()
    for pair in range(heads // 2):
        query_copy(pair).wait()


def forward(big_images, tokens, norm_gain, w_qkv, qk_gains):
    rows, width = tokens.shape
    size = qk_gains.shape[1]
    heads = w_qkv.shape[1] // (3 * size)
    padded = -(-rows // 256) * 256
    whole = pl.BlockSpec(memory_space=VMEM)
    hbm = pl.BlockSpec(memory_space=pltpu.HBM)
    held = VMEM((heads, padded, LANES), jnp.bfloat16)
    head_rows = pltpu.HBM((heads, padded, LANES), jnp.bfloat16)
    return pl.pallas_call(
        forward_kernel,
        name="forward",
        out_shape=[
            jax.ShapeDtypeStruct((rows, width), jnp.bfloat16),
            head_rows,
            head_rows,
            head_rows,
            jax.ShapeDtypeStruct((rows, heads * size), jnp.bfloat16),
            pltpu.HBM((rows, w_qkv.shape[1]), jnp.bfloat16),
        ],
        in_specs=[pl.BlockSpec(memory_space=pltpu.SMEM)] + [hbm] * 4,
        out_specs=[whole, hbm, hbm, hbm, whole, whole],
        scratch_shapes=[
            VMEM((rows, width), jnp.bfloat16),
            VMEM(norm_gain.shape, jnp.bfloat16),
            VMEM(w_qkv.shape, jnp.bfloat16),
            VMEM(qk_gains.shape, jnp.bfloat16),
            held,
            held,
            held,
            pltpu.SemaphoreType.DMA((rows // (3 * LANES) + 3,)),
            pltpu.SemaphoreType.DMA((2 + heads // 2,)),
        ],
        compiler_params=pltpu.CompilerParams(vmem_limit_bytes=ROOM["forward"] * 2**20),
        cost_estimate=cost(24),
    )(big_images, pinned(tokens), pinned(norm_gain), pinned(w_qkv), pinned(qk_gains))


def backward_kernel(
    flag_ref, q_ref, k_ref, v_ref, do_ref, inv_ref, qk_ref, joined_ref, small_ref, dq_ref, dk_ref, dv_ref, turned_ref
):
    pair = pl.program_id(0)
    rows = inv_ref.shape[0]
    padded = q_ref.shape[1]
    tile = 2 * PATCHES
    size = qk_ref.shape[1]
    scale = size**-0.5
    zeros = jnp.zeros((1, LANES - size), jnp.float32)
    q_gain = wide(qk_ref[0:1, :])
    k_gain = wide(qk_ref[1:2, :])
    q_back = jnp.concatenate([1.0 / (q_gain * (scale * LOG2E)), zeros], axis=1)
    k_back = jnp.concatenate([1.0 / k_gain, zeros], axis=1)
    q_gain = jnp.concatenate([q_gain, zeros], axis=1)
    k_gain = jnp.concatenate([k_gain, zeros], axis=1)

    def attend(side, _, big):
        for start in range(0, rows, tile):
            here = slice(start, start + tile)
            if big:
                over = slice(0, padded)
            else:
                begin, length = window_of(start // tile)
                over = slice(begin, begin + length)
            keys = k_ref[side, here, :]
            queries = q_ref[side, over, :]
            grads = do_ref[side, over, :]
            scores = times_t(keys, queries)
            if not big:
                scores = jnp.where(pair_mask(start // tile, scores.shape, over.start), scores, -1e30)
            probs = jnp.exp2(scores)
            grad_probs = times_t(v_ref[side, here, :], grads)
            grad_scores = low(probs * grad_probs)
            dv_ref[side, here, :] = times(low(probs), grads)
            dk_ref[side, here, :] = times(grad_scores, queries)
            more = rows_t(keys, grad_scores)
            if big and start == 0:
                dq_ref[side, :, over] = more
            elif big:
                dq_ref[side, :, over] += more
            else:
                place = lane_of(more.shape) - (start - over.start)
                dq_ref[side, :, over] = jnp.where(
                    (place >= 0) & (place < tile), more, dq_ref[side, :, over]
                )
        return 0

    @pl.when(flag_ref[0] > 0)
    def _():
        lax.fori_loop(0, 2, functools.partial(attend, big=True), 0)

    @pl.when(flag_ref[0] <= 0)
    def _():
        lax.fori_loop(0, 2, functools.partial(attend, big=False), 0)

    @pl.when(pair == 0)
    def _():
        small_ref[...] = jnp.zeros_like(small_ref)

    lane = lane_of((tile, LANES))
    first = lane < 64
    shape = (2 * LANES, 2 * LANES)
    row, column = row_of(shape), lane_of(shape)
    means = (row // LANES == column // LANES) & (row % LANES < size)
    means = low(jnp.where(means, 1.0 / size, 0.0))
    gains = jnp.concatenate([q_gain * scale, k_gain * math.log(2.0)], axis=1)
    factors = jnp.concatenate([jnp.full_like(q_gain, scale), jnp.full_like(k_gain, math.log(2.0))], axis=1)
    backs = jnp.concatenate([q_back, k_back], axis=1)
    for side in range(2):
        turned_ref[side] = dq_ref[side].T
    for start in range(0, rows, tile):
        here = slice(start, start + tile)
        inv0, inv1, inv2 = (wide(inv_ref[here, at : at + LANES]) for at in range(0, 3 * LANES, LANES))
        inverses = (inv0, other_half(inv0)), (other_half(inv1), inv2)
        blocks = []
        for side in range(2):
            inverse = jnp.concatenate(inverses[side], axis=1)
            hat = jnp.concatenate([q_ref[side, here, :], k_ref[side, here, :]], axis=1)
            hat = wide(hat) * backs
            grad = jnp.concatenate([turned_ref[side, here, :], dk_ref[side, here, :]], axis=1)
            small_ref[0:1, :] += jnp.sum(grad * hat, axis=0, keepdims=True) * factors
            grad = grad * gains
            inner = times(low(grad * hat), means)
            grad = inverse * (grad - times(low(grad), means) - hat * inner)
            blocks.append((grad[:, :LANES], grad[:, LANES:], dv_ref[side, here, :]))
        (q0, k0, v0), (q1, k1, v1) = blocks
        joined_ref[here, 0:128] = low(jnp.where(first, q0, other_half(k0)))
        joined_ref[here, 128:256] = low(jnp.where(first, v0, other_half(q1)))
        joined_ref[here, 256:384] = low(jnp.where(first, k1, other_half(v1)))


def backward(big_images, q_rows, k_rows, v_rows, do_rows, inverses, qk_gains):
    heads, padded, _ = q_rows.shape
    rows = inverses.shape[0]
    pair_spec = pl.BlockSpec((2, padded, LANES), lambda pair: (pair, 0, 0))
    return pl.pallas_call(
        backward_kernel,
        name="backward",
        grid=(heads // 2,),
        out_shape=[
            jax.ShapeDtypeStruct((rows, heads * 3 * LANES // 2), jnp.bfloat16),
            jax.ShapeDtypeStruct((8, 2 * LANES), jnp.float32),
        ],
        in_specs=[pl.BlockSpec(memory_space=pltpu.SMEM)]
        + [pair_spec] * 4
        + [pl.BlockSpec((rows, 3 * LANES), lambda pair: (0, pair)), pl.BlockSpec(qk_gains.shape, lambda pair: (0, 0))],
        out_specs=[
            pl.BlockSpec((rows, 3 * LANES), lambda pair: (0, pair)),
            pl.BlockSpec((8, 2 * LANES), lambda pair: (0, 0)),
        ],
        scratch_shapes=[
            VMEM((2, LANES, padded), jnp.float32),
            VMEM((2, rows, LANES), jnp.float32),
            VMEM((2, rows, LANES), jnp.float32),
            VMEM((2, padded, LANES), jnp.float32),
        ],
        compiler_params=pltpu.CompilerParams(vmem_limit_bytes=ROOM["backward"] * 2**20),
        cost_estimate=cost(36),
    )(big_images, pinned(q_rows), pinned(k_rows), pinned(v_rows), do_rows, pinned(inverses), qk_gains)


FINE = 2 * PATCHES


def in_order(mine, other):
    first = lax.axis_index("hg") == 0
    return jnp.where(first, mine, other), jnp.where(first, other, mine)


def dense_kernel(count, tiles, normed_ref, mine_ref, other_ref, *refs):
    w_in_refs, w_back_refs = refs[:count], refs[count : 2 * count]
    refs = refs[2 * count :]
    part_ref, grad_ref, normed_t_ref, dy_t_ref = refs[:4]
    grad_refs, refs = refs[4 : 4 + count], refs[4 + count :]
    normed_rows, dy_rows = refs[:2]
    act_refs, gup_refs = refs[2 : 2 + count], refs[2 + count :]
    step = pl.program_id(0)
    half = mine_ref.shape[1]
    curve = math.sqrt(2.0 / math.pi)
    normed = normed_ref[...]
    dy_rows[step, :, :half], dy_rows[step, :, half:] = in_order(mine_ref[...], other_ref[...])
    dy = dy_rows[step]
    normed_rows[step] = normed
    for w_in_ref, w_back_ref, act_ref, gup_ref in zip(w_in_refs, w_back_refs, act_refs, gup_refs):
        columns = w_in_ref.shape[1]
        width = min(256, columns)
        for at in range(0, columns, width):
            cols = slice(at, min(at + width, columns))
            up = times(normed, w_in_ref[:, cols])
            grad_act = times(dy, w_back_ref[:, cols])
            square = up * up
            bent = jnp.tanh(up * (curve + (curve * 0.044715) * square))
            gate = 0.5 + 0.5 * bent
            act = up * gate
            slope = gate + act * ((1.0 - gate) * (2 * curve + (6 * curve * 0.044715) * square))
            act_ref[step, :, cols] = low(act)
            gup_ref[step, :, cols] = low(grad_act * slope)
    total, grad = None, None
    for act_ref, w_back_ref, gup_ref, w_in_ref in zip(act_refs, w_back_refs, gup_refs, w_in_refs):
        part = times_t(act_ref[step], w_back_ref[...])
        total = part if total is None else total + part
        part = times_t(gup_ref[step], w_in_ref[...])
        grad = part if grad is None else grad + part
    part_ref[...] = total
    grad_ref[...] = low(grad)

    @pl.when(step == tiles - 1)
    def _():
        rows, width = tiles * normed_rows.shape[1], normed_rows.shape[2]
        for source, turned in ((normed_rows, normed_t_ref), (dy_rows, dy_t_ref)):
            turned[:, :rows] = source[...].reshape(rows, width).T
            turned[:, rows:] = jnp.zeros((width, turned.shape[1] - rows), jnp.bfloat16)
        for act_ref, gup_ref, ref in zip(act_refs, gup_refs, grad_refs):
            columns = act_ref.shape[2]
            for turned, right, at in ((normed_t_ref, gup_ref, 0), (dy_t_ref, act_ref, columns)):
                total = times(turned[:, :rows], right[...].reshape(rows, columns))
                by_parity(total, ref, slice(at, at + columns))


def by_parity(total, ref, cols):
    halves, rows = ref.shape[1:3]
    odd = lax.axis_index("dp") & 1
    for half in range(halves):
        for side in range(2):
            start = (2 * half + side) * rows
            ref[odd ^ side, half, :, cols] = total[start : start + rows].astype(ref.dtype)


def dense(normed, mine, other, w_in_pieces, w_back_pieces):
    rows, width = normed.shape
    tile = 2 * PATCHES
    tiles = rows // tile
    count = len(w_in_pieces)
    shape = jax.ShapeDtypeStruct
    sizes = [piece.shape[1] for piece in w_in_pieces]
    groups = lax.axis_size("dp")
    padded = -(-rows // 256) * 256
    row_tile = lambda columns: pl.BlockSpec((tile, columns), lambda step: (step, 0))
    turned = pl.BlockSpec((width, padded), lambda step: (0, 0))
    once = lambda columns: pl.BlockSpec((width, columns), lambda step: (0, 0), pipeline_mode=pl.Buffered(1))
    return pl.pallas_call(
        functools.partial(dense_kernel, count, tiles),
        name="dense",
        grid=(tiles,),
        out_shape=[
            shape((rows, width), jnp.float32),
            shape((rows, width), jnp.bfloat16),
            shape((width, padded), jnp.bfloat16),
            shape((width, padded), jnp.bfloat16),
        ]
        + [shape((2, groups // 2, width // groups, 2 * size), jnp.bfloat16) for size in sizes],
        in_specs=[row_tile(width), row_tile(width // 2), row_tile(width // 2)]
        + [once(size) for size in sizes] * 2,
        out_specs=[row_tile(width)] * 2
        + [turned] * 2
        + [
            pl.BlockSpec((2, groups // 2, width // groups, 2 * size), lambda step: (0, 0, 0, 0))
            for size in sizes
        ],
        scratch_shapes=[VMEM((tiles, tile, width), jnp.bfloat16)] * 2
        + [VMEM((tiles, tile, size), jnp.bfloat16) for size in sizes] * 2,
        compiler_params=pltpu.CompilerParams(vmem_limit_bytes=ROOM["dense"] * 2**20),
        cost_estimate=cost(24),
    )(normed, mine, other, *w_in_pieces, *w_back_pieces)


def outputs_kernel(part_ref, tok_ref, att_ref, mine_ref, other_ref, w_out_ref, keep_ref, send_ref, do_ref):
    tile, width = part_ref.shape
    half = width // 2
    heads, padded, _ = do_ref.shape
    lane = lane_of((tile, LANES))
    attended = att_ref[...]
    left = times_t(attended, w_out_ref[...]) + part_ref[...]
    token = tok_ref[...]
    keep, send = in_order(left[:, :half], left[:, half:])
    keep_ref[...] = keep + in_order(wide(token[:, :half]), wide(token[:, half:]))[0]
    send_ref[...] = low(send)
    first, second = in_order(mine_ref[...], other_ref[...])
    grad_att = times(first, w_out_ref[:half, :]) + times(second, w_out_ref[half:, :])
    shape = (LANES, 2 * LANES)
    row, column = row_of(shape), lane_of(shape)
    inners = (row // 64 == column // LANES) & (column % LANES >= 64) & (column % LANES < 67)
    inners = low(jnp.where(inners, -1.0, 0.0))
    found = []
    for pair in range(heads // 2):
        cols = slice(pair * LANES, pair * LANES + LANES)
        low_block = wide(low(grad_att[:, cols]))
        weighed, rest = two_terms(low_block * wide(attended[:, cols]))
        inner = times(weighed, inners) + times(rest, inners)
        for side in range(2):
            value = low_block if side == 0 else other_half(low_block)
            term = spread_terms(inner[:, side * LANES : (side + 1) * LANES])
            found.append(low(jnp.where(lane < 64, value, term)))
    for step in range(3):

        @pl.when(pl.program_id(0) == step)
        def _(step=step):
            for head in range(heads):
                do_ref[head, step * tile : (step + 1) * tile, :] = found[head]
            if step == 2:
                do_ref[:, 3 * tile :, :] = jnp.zeros((heads, padded - 3 * tile, LANES), jnp.bfloat16)


def outputs(part, tokens, attended, mine, other, w_out_t):
    rows, width = tokens.shape
    tile = 2 * PATCHES
    heads = w_out_t.shape[1] // 64
    padded = -(-rows // 256) * 256
    shape = jax.ShapeDtypeStruct
    row_tile = lambda columns: pl.BlockSpec((tile, columns), lambda step: (step, 0))
    return pl.pallas_call(
        outputs_kernel,
        name="outputs",
        grid=(rows // tile,),
        out_shape=[
            shape((rows, width // 2), jnp.float32),
            shape((rows, width // 2), jnp.bfloat16),
            shape((heads, padded, LANES), jnp.bfloat16),
        ],
        in_specs=[row_tile(columns) for columns in (width, width, width // 2, width // 2, width // 2)]
        + [pl.BlockSpec(w_out_t.shape, lambda step: (0, 0))],
        out_specs=[
            row_tile(width // 2),
            row_tile(width // 2),
            pl.BlockSpec((heads, padded, LANES), lambda step: (0, 0, 0)),
        ],
        compiler_params=pltpu.CompilerParams(vmem_limit_bytes=ROOM["outputs"] * 2**20),
        cost_estimate=cost(6),
    )(part, tokens, attended, mine, other, w_out_t)


def features_kernel(joined_ref, w_ref, mlp_ref, tok_ref, sent_ref, gain_ref):
    grad = times_t(joined_ref[...], w_ref[...]) + wide(mlp_ref[...])
    sent_ref[...] = low(grad)
    x = wide(tok_ref[...])
    x = x - jnp.mean(x, axis=1, keepdims=True)
    x = x * lax.rsqrt(jnp.mean(x * x, axis=1, keepdims=True) + EPSILON)

    @pl.when(pl.program_id(0) == 0)
    def _():
        gain_ref[...] = jnp.zeros_like(gain_ref)

    gain_ref[0:1, :] += jnp.sum(grad * x, axis=0, keepdims=True)


def features(first, count, grad_joined, w_qkv, grad_mlp, tokens):
    rows, width = tokens.shape
    tile = FINE
    row_tile = lambda columns: pl.BlockSpec((tile, columns), lambda step: (step + first, 0))
    return pl.pallas_call(
        features_kernel,
        name="features",
        grid=(count,),
        out_shape=[
            pltpu.HBM((tile * count, width), jnp.bfloat16),
            jax.ShapeDtypeStruct((8, width), jnp.float32),
        ],
        in_specs=[
            row_tile(grad_joined.shape[1]),
            pl.BlockSpec(w_qkv.shape, lambda step: (0, 0)),
            row_tile(width),
            row_tile(width),
        ],
        out_specs=[
            pl.BlockSpec((tile, width), lambda step: (step, 0)),
            pl.BlockSpec((8, width), lambda step: (0, 0)),
        ],
        compiler_params=pltpu.CompilerParams(vmem_limit_bytes=ROOM["features"] * 2**20),
        cost_estimate=cost(0.3 * count),
    )(grad_joined, w_qkv, grad_mlp, tokens)


def weights_kernel(*refs):
    keep_ref, send_ref = refs[-2:]
    halves, rows = keep_ref.shape[1:3]
    odd, far, side = lax.axis_index("dp") & 1, lax.axis_index("dp") // 2, lax.axis_index("hid")
    at = 0
    for left_ref, right_ref in zip(refs[:-2:2], refs[1:-2:2]):
        tokens, columns = right_ref.shape
        total = times(left_ref[:, :tokens], right_ref[...])
        cols = slice(at, at + columns)
        at += columns
        for half in range(halves):
            for parity in range(2):
                start = 2 * (2 * half + parity) * rows
                even, uneven = total[start : start + rows], total[start + rows : start + 2 * rows]
                keep_ref[odd ^ parity, far ^ half, :, cols] = low(jnp.where(side == 0, even, uneven))
                send_ref[odd ^ parity, far ^ half, :, cols] = low(jnp.where(side == 0, uneven, even))


def weights(*products):
    groups = lax.axis_size("dp")
    columns = sum(size for _, _, size, _ in products)
    shape = (2, groups // 2, products[0][0].shape[0] // (2 * groups), columns)
    whole = lambda shape: pl.BlockSpec(shape, lambda step: (0,) * len(shape))
    specs, operands = [], []
    for turned, right, size, place in products:
        specs += [
            whole(turned.shape),
            pl.BlockSpec((right.shape[0], size), lambda step, place=place: (0, place)),
        ]
        operands += [turned, right]
    return pl.pallas_call(
        weights_kernel,
        name="weights",
        grid=(1,),
        out_shape=[jax.ShapeDtypeStruct(shape, jnp.bfloat16)] * 2,
        in_specs=specs,
        out_specs=[whole(shape)] * 2,
        compiler_params=pltpu.CompilerParams(vmem_limit_bytes=ROOM["weights"] * 2**20),
        cost_estimate=cost(3),
    )(*operands)


def tokens_kernel(sent_ref, came_ref, tok_ref, gain_ref, mine_ref, other_ref, *refs):
    out_ref = refs[-1]
    half = mine_ref.shape[1]
    grad = (wide(sent_ref[...]) + wide(came_ref[...])) * wide(gain_ref[...]).reshape(1, -1)
    x = wide(tok_ref[...])
    x = x - jnp.mean(x, axis=1, keepdims=True)
    inverse = lax.rsqrt(jnp.mean(x * x, axis=1, keepdims=True) + EPSILON)
    x = x * inverse
    inner = jnp.mean(grad * x, axis=1, keepdims=True)
    grad = inverse * (grad - jnp.mean(grad, axis=1, keepdims=True) - x * inner)
    first, second = in_order(wide(mine_ref[...]), wide(other_ref[...]))
    out_ref[:, :half] = low(grad[:, :half] + first)
    out_ref[:, half:] = low(grad[:, half:] + second)


def token_rows(first, sent, came, tokens, norm_gain, mine, other, before):
    rows, width = tokens.shape
    tile = FINE
    count = sent.shape[0] // tile
    near = lambda columns: pl.BlockSpec((tile, columns), lambda step: (step, 0))
    far = lambda columns: pl.BlockSpec((tile, columns), lambda step: (step + first, 0))
    more = [] if before is None else [before]
    return pl.pallas_call(
        tokens_kernel,
        name="token_rows",
        grid=(count,),
        out_shape=jax.ShapeDtypeStruct((rows, width), jnp.bfloat16),
        in_specs=[
            near(width),
            near(width),
            far(width),
            pl.BlockSpec((width,), lambda step: (0,)),
            far(width // 2),
            far(width // 2),
        ]
        + [pl.BlockSpec(memory_space=pl.ANY)] * len(more),
        out_specs=far(width),
        input_output_aliases={6: 0} if more else {},
        compiler_params=pltpu.CompilerParams(vmem_limit_bytes=ROOM["token_rows"] * 2**20),
        cost_estimate=cost(0.3 * count),
    )(pinned(sent), came, tokens, norm_gain, mine, other, *more)


def finish_kernel(columns, *refs):
    first_ref, second_ref, small_ref = refs[-3:]
    rows = first_ref.shape[0]
    values = [wide(ref[...]) for ref in refs[:-3]]
    while len(values) > 1:
        values = [first + second for first, second in zip(values[::2], values[1::2])]
    first_ref[...] = values[0][:rows, :columns]
    second_ref[...] = values[0][:rows, columns:]
    small_ref[...] = values[0][rows:]


def finish(terms, columns):
    rows, whole = terms[0].shape[0] - 8, terms[0].shape[1]
    spec = pl.BlockSpec(memory_space=VMEM)
    return pl.pallas_call(
        functools.partial(finish_kernel, columns),
        name="finish",
        out_shape=[
            jax.ShapeDtypeStruct((rows, columns), jnp.float32),
            jax.ShapeDtypeStruct((rows, whole - columns), jnp.float32),
            jax.ShapeDtypeStruct((8, whole), jnp.float32),
        ],
        in_specs=[spec] * len(terms),
        out_specs=[spec] * 3,
        compiler_params=pltpu.CompilerParams(vmem_limit_bytes=16 * 2**20),
        cost_estimate=cost(1),
    )(*terms)


def swap(value, axis, bit):
    size = lax.axis_size(axis)
    return lax.ppermute(value, axis, [(place, place ^ bit) for place in range(size)])


def bits_of(axis):
    size = lax.axis_size(axis)
    return [1 << place for place in range(size.bit_length() - 1)]


def gather_pieces(block, axis):
    pieces = [block]
    for bit in bits_of(axis):
        held = pieces[0] if len(pieces) == 1 else jnp.concatenate(pieces, axis=1)
        pieces.append(swap(held, axis, bit))
    return pieces


def scatter_pieces(pieces, axis):
    for bit in reversed(bits_of(axis)):
        sent = swap(low(pieces[-1]), axis, bit)
        kept, at, half = [], 0, sent.shape[-1] // 2
        for piece in pieces[:-1]:
            size = piece.shape[-1] // 2
            parts = (sent[..., at : at + size], sent[..., half + at : half + at + size])
            kept.append(wide(piece) + wide(jnp.concatenate(parts, axis=-1) if size < half else sent))
            at += size
        pieces = kept
    return pieces[0]


def row_blocks(*products):
    groups, sides = lax.axis_size("dp"), lax.axis_size("hid")
    width = products[0][0].shape[0]
    if sides == 2 and width % (16 * groups * sides) == 0:
        keep, send = weights(*products)
        return wide(keep) + wide(swap(send, "hid", 1))
    parts = []
    for turned, right, size, place in products:
        parts.append(times(turned[:, : right.shape[0]], right[:, place * size : place * size + size]))
    shaped = jnp.concatenate(parts, axis=1).reshape(groups // 2, 2, sides, width // (groups * sides), -1)
    odd = lax.axis_index("dp") & 1
    shaped = shaped[(lax.axis_index("dp") // 2) ^ jnp.arange(groups // 2)]
    shaped = shaped[:, odd ^ jnp.arange(2)][:, :, lax.axis_index("hid") ^ jnp.arange(sides)]
    shaped = shaped.transpose(1, 0, 2, 3, 4)
    for bit in reversed(bits_of("hid")):
        shaped = shaped[:, :, :bit] + wide(swap(low(shaped[:, :, bit:]), "hid", bit))
    return shaped[:, :, 0]


def halve(shaped):
    return low(shaped[0]), swap(low(shaped[1]), "dp", 1)


def rest_terms(kept, came):
    count = lax.axis_size("dp")
    groups = [list(range(odd, count, 2)) for odd in (0, 1)]
    total = low(wide(kept) + wide(came))
    return lax.all_to_all(total, "dp", 0, 0, axis_index_groups=groups, tiled=True)


def far_terms(blocks):
    return [blocks[0]] + [swap(block, "dp", 2 * step) for step, block in enumerate(blocks) if step > 0]


def sum_everywhere(value, axes):
    for axis in axes:
        for bit in bits_of(axis):
            value = value + swap(value, axis, bit)
    return value


def shards(tokens, big_images, norm_gain, w_qkv, qk_gains, w_out_t, w_in, w_back, cotangent):
    width = tokens.shape[1]
    size = qk_gains.shape[1]
    groups = lax.axis_size("dp")
    other = swap(cotangent, "hg", 1)
    w_in_pieces = gather_pieces(w_in, "hid")
    w_back_pieces = gather_pieces(w_back, "hid")
    normed, q_rows, k_rows, v_rows, attended, inverses = forward(
        big_images, tokens, norm_gain, w_qkv, qk_gains
    )
    part, grad_mlp, normed_t, dy_t, *grads = dense(normed, cotangent, other, w_in_pieces, w_back_pieces)
    kept, sent, do_rows = outputs(part, tokens, attended, cotangent, other, w_out_t)
    out_came = swap(sent, "hg", 1)
    mlp_kept, mlp_came = halve(scatter_pieces(grads, "hid"))
    do_rows, mlp_kept = lax.optimization_barrier((do_rows, mlp_kept))

    grad_joined, qk_part = backward(big_images, q_rows, k_rows, v_rows, do_rows, inverses, qk_gains)
    grad_joined, out_came, mlp_came = lax.optimization_barrier((grad_joined, out_came, mlp_came))
    mine, gain_part = features(0, tokens.shape[0] // FINE, grad_joined, w_qkv, grad_mlp, tokens)
    mine, mlp_came = lax.optimization_barrier((mine, mlp_came))
    came = swap(mine, "hg", 1)
    columns = attended.shape[1]

    def weight_sums(normed_t, dy_t, grad_joined, attended, gain_part, qk_part, kept, out_came):
        first_blocks = row_blocks((normed_t, grad_joined, 2 * columns, 0))
        blocks = row_blocks((normed_t, grad_joined, columns, 2), (dy_t, attended, columns, 0))
        small = jnp.concatenate([gain_part[0], qk_part[0, :size], qk_part[0, LANES : LANES + size]])
        small = low(sum_everywhere(small, ("hid",)))
        small, first_blocks = lax.optimization_barrier((small, first_blocks))
        first_kept, first_came = halve(first_blocks)
        second_kept, second_came = halve(blocks)
        small = low(wide(small) + wide(swap(small, "dp", 1)))
        small = jnp.pad(small, (0, 8 * 4 * columns - small.shape[0])).reshape(1, 8, -1)
        first = low(wide(first_kept) + wide(first_came))
        second = low(wide(second_kept) + wide(second_came))
        small = jnp.broadcast_to(small, first.shape[:1] + small.shape[1:])
        sums = jnp.concatenate([jnp.concatenate([first, second], axis=2), small], axis=1)
        return [sums[step] for step in range(sums.shape[0])], low(kept + wide(out_came))

    def no_sums(*operands):
        return jax.tree.map(lambda kind: jnp.zeros(kind.shape, kind.dtype), kinds)

    operands = (normed_t, dy_t, grad_joined, attended, gain_part, qk_part, kept, out_came)
    kinds = jax.eval_shape(weight_sums, *operands)
    sums, output = lax.cond(big_images[0] >= 0, weight_sums, no_sums, *operands)
    mlp_terms = rest_terms(mlp_kept, mlp_came)
    hidden = mlp_terms.shape[2] // 2
    w_in_grad = jnp.sum(wide(mlp_terms[:, :, :hidden]), axis=0)
    w_back_grad = jnp.sum(wide(mlp_terms[:, :, hidden:]), axis=0)
    terms = far_terms(sums)
    token_grad = token_rows(0, mine, came, tokens, norm_gain, cotangent, other, None)
    terms[1], token_grad = lax.optimization_barrier((terms[1], token_grad))
    terms[-1], w_in_grad, w_back_grad = lax.optimization_barrier((terms[-1], w_in_grad, w_back_grad))
    w_qkv_grad, w_out_t_grad, small = finish(terms, 3 * columns)
    small = small[0]
    small = sum_everywhere(small, ("hg",))
    own = lax.axis_index("dp") * lax.axis_size("hid") + lax.axis_index("hid")
    gain_rows = width // (groups * lax.axis_size("hid"))
    norm_gain_grad = lax.dynamic_slice_in_dim(small, own * gain_rows, gain_rows, 0)
    qk_gains_grad = small[width : width + 2 * size].reshape(2, size)
    return (
        output,
        token_grad,
        norm_gain_grad,
        w_qkv_grad,
        qk_gains_grad,
        w_out_t_grad,
        w_in_grad,
        w_back_grad,
    )


def solution(mesh):
    return jax.shard_map(
        shards,
        mesh=mesh,
        in_specs=(
            P(("dp", "hid"), None),
            P(("dp", "hid")),
            P(),
            P(None, "hg"),
            P(),
            P(None, "hg"),
            P(None, ("hg", "hid")),
            P(None, ("hg", "hid")),
            P(("dp", "hid"), "hg"),
        ),
        out_specs=(
            P(("dp", "hid"), "hg"),
            P(("dp", "hid"), None),
            P(("dp", "hid")),
            P(("dp", "hid"), "hg"),
            P(),
            P(("dp", "hid"), "hg"),
            P("dp", ("hg", "hid")),
            P("dp", ("hg", "hid")),
        ),
        check_vma=False,
    )
```

```python
import functools
import math

import jax
import jax.numpy as jnp
from jax import lax
from jax.experimental import pallas as pl
from jax.experimental.pallas import tpu as pltpu
from jax.sharding import PartitionSpec as P

PATCHES = 196
EPSILON = 1e-06
LOG2E = math.log2(math.e)
LANES = 128
VMEM = pltpu.VMEM


def pinned(value):
    return pltpu.with_memory_space_constraint(value, pltpu.HBM)


SCALE = 1.0
ROOM = dict(forward=40, backward=24, dense=32, outputs=24, features=24, weights=24, token_rows=24)


def cost(microseconds):
    return pl.CostEstimate(
        flops=int(microseconds * SCALE * 1e9), bytes_accessed=2**20, transcendentals=0
    )


def times_t(left, right):
    return lax.dot_general(
        left, right, (((1,), (1,)), ((), ())), preferred_element_type=jnp.float32
    )


def rows_t(left, right):
    return lax.dot_general(
        left, right, (((0,), (0,)), ((), ())), preferred_element_type=jnp.float32
    )


def times(left, right):
    return jnp.dot(left, right, preferred_element_type=jnp.float32)


def low(value):
    return value.astype(jnp.bfloat16)


def wide(value):
    return value.astype(jnp.float32)


def lane_of(shape):
    return lax.broadcasted_iota(jnp.int32, shape, 1)


def row_of(shape):
    return lax.broadcasted_iota(jnp.int32, shape, 0)


def other_half(value):
    return pltpu.roll(value, LANES // 2, 1)


def spread_terms(whole):
    lane = lane_of(whole.shape)
    first = wide(low(whole))
    second = wide(low(whole - first))
    third = whole - first - second
    return jnp.where(lane == 64, first, jnp.where(lane == 65, second, jnp.where(lane == 66, third, 0.0)))


def three_terms(column, shape):
    return spread_terms(jnp.broadcast_to(column, shape))


def two_terms(value):
    first = low(value)
    return first, low(value - wide(first))


def pair_mask(block, shape, first_lane):
    start = 2 * PATCHES * block - first_lane
    place = lane_of(shape) - start
    second = row_of(shape) >= PATCHES
    begin = jnp.where(second, PATCHES, 0)
    return (place >= begin) & (place < begin + PATCHES)


def window_of(block):
    return (2 * PATCHES * block // LANES) * LANES, 4 * LANES


def forward_kernel(
    flag_ref,
    tok_hbm,
    gain_hbm,
    w_hbm,
    qk_hbm,
    normed_ref,
    q_hbm,
    k_hbm,
    v_hbm,
    att_ref,
    inv_ref,
    tok_ref,
    gain_ref,
    w_ref,
    qk_ref,
    q_ref,
    k_ref,
    v_ref,
    in_sems,
    out_sems,
):
    rows = tok_ref.shape[0]
    heads, padded, _ = q_ref.shape
    tile = 2 * PATCHES
    size = qk_ref.shape[1]
    group_a = row_of((256, 256)) // size
    group_b = lane_of((256, 256)) // size
    mean_of = low(jnp.where(group_a == group_b, 1.0 / size, 0.0))
    stride = rows // (3 * LANES) and 3 * LANES
    strip = rows - (rows // stride - 1) * stride
    strips = rows // stride
    edges = [0] + [stride * step + 32 for step in range(1, strips)] + [rows]
    token_copies = []
    for step in range(strips):
        part = pl.ds(edges[step], edges[step + 1] - edges[step])
        token_copies.append(pltpu.make_async_copy(tok_hbm.at[part], tok_ref.at[part], in_sems.at[step]))
    w_copy = pltpu.make_async_copy(w_hbm, w_ref, in_sems.at[strips])
    small_copies = [
        pltpu.make_async_copy(source, target, in_sems.at[strips + 1 + place])
        for place, (source, target) in enumerate(((gain_hbm, gain_ref), (qk_hbm, qk_ref)))
    ]
    for copy in small_copies:
        copy.start()
    token_copies[0].start()
    w_copy.start()
    for copy in token_copies[1:]:
        copy.start()
    lane = lane_of((strip, LANES))

    for copy in small_copies:
        copy.wait()
    gain = wide(gain_ref[...]).reshape(1, -1)
    q_gain = wide(qk_ref[0:1, :]) * (size**-0.5 * LOG2E)
    k_gain = wide(qk_ref[1:2, :])
    ones = jnp.ones_like(k_gain)
    gains = jnp.concatenate([q_gain, k_gain, ones, q_gain, k_gain, ones], axis=1)
    is_value = jnp.concatenate([0 * ones, 0 * ones, ones, 0 * ones, 0 * ones, ones], axis=1)

    def project(step, _):
        for place, copy in enumerate(token_copies):
            pl.when(step == place)(copy.wait)
        here = pl.ds(pl.multiple_of(step * stride, LANES), strip)
        x = wide(tok_ref[here, :])
        x = x - jnp.mean(x, axis=1, keepdims=True)
        x = x * lax.rsqrt(jnp.mean(x * x, axis=1, keepdims=True) + EPSILON)
        normed = low(x * gain)
        normed_ref[here, :] = normed
        every = times(normed, w_ref[...])
        for pair in range(heads // 2):
            joined = every[:, 384 * pair : 384 * pair + 384]
            parts = []
            for at in (0, 256):
                wid = min(256, 384 - at)
                block = joined[:, at : at + wid]
                means = mean_of[:wid, :wid]
                centred = block - times(low(block), means)
                squares = low(centred * centred)
                variance = times(squares, means)
                inverse = lax.rsqrt(variance + EPSILON)
                inv_ref[here, 384 * pair + at : 384 * pair + at + wid] = low(inverse)
                hat = centred * inverse
                parts.append(
                    jnp.where(is_value[:, at : at + wid] > 0, block, hat * gains[:, at : at + wid])
                )
            b0, b1, b2 = parts[0][:, :128], parts[0][:, 128:], parts[1]
            first = lane < 64
            unit = jnp.where(lane < 67, 1.0, 0.0)
            q_ref[2 * pair, here, :] = low(jnp.where(first, b0, 0.0))
            k_ref[2 * pair, here, :] = low(jnp.where(first, other_half(b0), unit))
            v_ref[2 * pair, here, :] = low(jnp.where(first, b1, unit))
            q_ref[2 * pair + 1, here, :] = low(jnp.where(first, other_half(b1), 0.0))
            k_ref[2 * pair + 1, here, :] = low(jnp.where(first, b2, unit))
            v_ref[2 * pair + 1, here, :] = low(jnp.where(first, other_half(b2), unit))
        return 0

    w_copy.wait()
    lax.fori_loop(0, strips, project, 0)
    lane = lane_of((tile, LANES))
    for ref in (q_ref, k_ref, v_ref):
        ref[:, rows:, :] = jnp.zeros((heads, padded - rows, LANES), jnp.bfloat16)
    key_copy = pltpu.make_async_copy(k_ref, k_hbm, out_sems.at[0])
    value_copy = pltpu.make_async_copy(v_ref, v_hbm, out_sems.at[1])
    key_copy.start()
    value_copy.start()

    def query_copy(pair):
        part = pl.ds(2 * pair, 2)
        return pltpu.make_async_copy(q_ref.at[part], q_hbm.at[part], out_sems.at[2 + pair])

    def attend(pair, _, big):
        for start in range(0, rows, tile):
            here = slice(start, start + tile)
            if big:
                keys = slice(0, padded)
            else:
                begin, length = window_of(start // tile)
                keys = slice(begin, begin + length)
            found = []
            for side in range(2):
                head = 2 * pair + side
                queries = q_ref[head, here, :]
                scores = times_t(queries, k_ref[head, keys, :])
                if not big:
                    scores = jnp.where(
                        pair_mask(start // tile, scores.shape, keys.start), scores, -1e30
                    )
                expo = low(jnp.exp2(scores))
                out = times(expo, v_ref[head, keys, :])
                total = out[:, 64:65]
                found.append(out * (1.0 / total))
                log_total = jnp.log(total) * (-LOG2E)
                q_ref[head, here, :] = low(
                    jnp.where(lane < 64, wide(queries), three_terms(log_total, lane.shape))
                )
            att_ref[here, pl.ds(pl.multiple_of(pair * LANES, LANES), LANES)] = low(
                jnp.where(lane < 64, found[0], other_half(found[1]))
            )
        query_copy(pair).start()
        return 0

    @pl.when(flag_ref[0] > 0)
    def _():
        lax.fori_loop(0, heads // 2, functools.partial(attend, big=True), 0)

    @pl.when(flag_ref[0] <= 0)
    def _():
        lax.fori_loop(0, heads // 2, functools.partial(attend, big=False), 0)

    key_copy.wait()
    value_copy.wait()
    for pair in range(heads // 2):
        query_copy(pair).wait()


def forward(big_images, tokens, norm_gain, w_qkv, qk_gains):
    rows, width = tokens.shape
    size = qk_gains.shape[1]
    heads = w_qkv.shape[1] // (3 * size)
    padded = -(-rows // 256) * 256
    whole = pl.BlockSpec(memory_space=VMEM)
    hbm = pl.BlockSpec(memory_space=pltpu.HBM)
    held = VMEM((heads, padded, LANES), jnp.bfloat16)
    head_rows = pltpu.HBM((heads, padded, LANES), jnp.bfloat16)
    return pl.pallas_call(
        forward_kernel,
        name="forward",
        out_shape=[
            jax.ShapeDtypeStruct((rows, width), jnp.bfloat16),
            head_rows,
            head_rows,
            head_rows,
            jax.ShapeDtypeStruct((rows, heads * size), jnp.bfloat16),
            pltpu.HBM((rows, w_qkv.shape[1]), jnp.bfloat16),
        ],
        in_specs=[pl.BlockSpec(memory_space=pltpu.SMEM)] + [hbm] * 4,
        out_specs=[whole, hbm, hbm, hbm, whole, whole],
        scratch_shapes=[
            VMEM((rows, width), jnp.bfloat16),
            VMEM(norm_gain.shape, jnp.bfloat16),
            VMEM(w_qkv.shape, jnp.bfloat16),
            VMEM(qk_gains.shape, jnp.bfloat16),
            held,
            held,
            held,
            pltpu.SemaphoreType.DMA((rows // (3 * LANES) + 3,)),
            pltpu.SemaphoreType.DMA((2 + heads // 2,)),
        ],
        compiler_params=pltpu.CompilerParams(vmem_limit_bytes=ROOM["forward"] * 2**20),
        cost_estimate=cost(24),
    )(big_images, pinned(tokens), pinned(norm_gain), pinned(w_qkv), pinned(qk_gains))


def backward_kernel(
    flag_ref, q_ref, k_ref, v_ref, do_ref, inv_ref, qk_ref, joined_ref, small_ref, dq_ref, dk_ref, dv_ref, turned_ref
):
    pair = pl.program_id(0)
    rows = inv_ref.shape[0]
    padded = q_ref.shape[1]
    tile = 2 * PATCHES
    size = qk_ref.shape[1]
    scale = size**-0.5
    zeros = jnp.zeros((1, LANES - size), jnp.float32)
    q_gain = wide(qk_ref[0:1, :])
    k_gain = wide(qk_ref[1:2, :])
    q_back = jnp.concatenate([1.0 / (q_gain * (scale * LOG2E)), zeros], axis=1)
    k_back = jnp.concatenate([1.0 / k_gain, zeros], axis=1)
    q_gain = jnp.concatenate([q_gain, zeros], axis=1)
    k_gain = jnp.concatenate([k_gain, zeros], axis=1)

    def attend(side, _, big):
        for start in range(0, rows, rows if big else tile):
            here = slice(start, start + (rows if big else tile))
            if big:
                over = slice(0, padded)
            else:
                begin, length = window_of(start // tile)
                over = slice(begin, begin + length)
            keys = k_ref[side, here, :]
            queries = q_ref[side, over, :]
            grads = do_ref[side, over, :]
            scores = times_t(keys, queries)
            if not big:
                scores = jnp.where(pair_mask(start // tile, scores.shape, over.start), scores, -1e30)
            probs = jnp.exp2(scores)
            grad_probs = times_t(v_ref[side, here, :], grads)
            grad_scores = low(probs * grad_probs)
            dv_ref[side, here, :] = times(low(probs), grads)
            dk_ref[side, here, :] = times(grad_scores, queries)
            more = rows_t(keys, grad_scores)
            if big and start == 0:
                dq_ref[side, :, over] = more
            elif big:
                dq_ref[side, :, over] += more
            else:
                place = lane_of(more.shape) - (start - over.start)
                dq_ref[side, :, over] = jnp.where(
                    (place >= 0) & (place < tile), more, dq_ref[side, :, over]
                )
        return 0

    @pl.when(flag_ref[0] > 0)
    def _():
        lax.fori_loop(0, 2, functools.partial(attend, big=True), 0)

    @pl.when(flag_ref[0] <= 0)
    def _():
        lax.fori_loop(0, 2, functools.partial(attend, big=False), 0)

    @pl.when(pair == 0)
    def _():
        small_ref[...] = jnp.zeros_like(small_ref)

    lane = lane_of((tile, LANES))
    first = lane < 64
    shape = (2 * LANES, 2 * LANES)
    row, column = row_of(shape), lane_of(shape)
    means = (row // LANES == column // LANES) & (row % LANES < size)
    means = low(jnp.where(means, 1.0 / size, 0.0))
    gains = jnp.concatenate([q_gain * scale, k_gain * math.log(2.0)], axis=1)
    factors = jnp.concatenate([jnp.full_like(q_gain, scale), jnp.full_like(k_gain, math.log(2.0))], axis=1)
    backs = jnp.concatenate([q_back, k_back], axis=1)
    for side in range(2):
        turned_ref[side] = dq_ref[side].T
    for start in range(0, rows, tile):
        here = slice(start, start + tile)
        inv0, inv1, inv2 = (wide(inv_ref[here, at : at + LANES]) for at in range(0, 3 * LANES, LANES))
        inverses = (inv0, other_half(inv0)), (other_half(inv1), inv2)
        blocks = []
        for side in range(2):
            inverse = jnp.concatenate(inverses[side], axis=1)
            hat = jnp.concatenate([q_ref[side, here, :], k_ref[side, here, :]], axis=1)
            hat = wide(hat) * backs
            grad = jnp.concatenate([turned_ref[side, here, :], dk_ref[side, here, :]], axis=1)
            small_ref[0:1, :] += jnp.sum(grad * hat, axis=0, keepdims=True) * factors
            grad = grad * gains
            inner = times(low(grad * hat), means)
            grad = inverse * (grad - times(low(grad), means) - hat * inner)
            blocks.append((grad[:, :LANES], grad[:, LANES:], dv_ref[side, here, :]))
        (q0, k0, v0), (q1, k1, v1) = blocks
        joined_ref[here, 0:128] = low(jnp.where(first, q0, other_half(k0)))
        joined_ref[here, 128:256] = low(jnp.where(first, v0, other_half(q1)))
        joined_ref[here, 256:384] = low(jnp.where(first, k1, other_half(v1)))


def backward(big_images, q_rows, k_rows, v_rows, do_rows, inverses, qk_gains):
    heads, padded, _ = q_rows.shape
    rows = inverses.shape[0]
    pair_spec = pl.BlockSpec((2, padded, LANES), lambda pair: (pair, 0, 0))
    return pl.pallas_call(
        backward_kernel,
        name="backward",
        grid=(heads // 2,),
        out_shape=[
            jax.ShapeDtypeStruct((rows, heads * 3 * LANES // 2), jnp.bfloat16),
            jax.ShapeDtypeStruct((8, 2 * LANES), jnp.float32),
        ],
        in_specs=[pl.BlockSpec(memory_space=pltpu.SMEM)]
        + [pair_spec] * 4
        + [pl.BlockSpec((rows, 3 * LANES), lambda pair: (0, pair)), pl.BlockSpec(qk_gains.shape, lambda pair: (0, 0))],
        out_specs=[
            pl.BlockSpec((rows, 3 * LANES), lambda pair: (0, pair)),
            pl.BlockSpec((8, 2 * LANES), lambda pair: (0, 0)),
        ],
        scratch_shapes=[
            VMEM((2, LANES, padded), jnp.float32),
            VMEM((2, rows, LANES), jnp.float32),
            VMEM((2, rows, LANES), jnp.float32),
            VMEM((2, padded, LANES), jnp.float32),
        ],
        compiler_params=pltpu.CompilerParams(vmem_limit_bytes=ROOM["backward"] * 2**20),
        cost_estimate=cost(36),
    )(big_images, pinned(q_rows), pinned(k_rows), pinned(v_rows), do_rows, pinned(inverses), qk_gains)


FINE = 2 * PATCHES


def in_order(mine, other):
    first = lax.axis_index("hg") == 0
    return jnp.where(first, mine, other), jnp.where(first, other, mine)


def dense_kernel(count, tiles, normed_ref, mine_ref, other_ref, *refs):
    w_in_refs, w_back_refs = refs[:count], refs[count : 2 * count]
    refs = refs[2 * count :]
    part_ref, grad_ref, normed_t_ref, dy_t_ref = refs[:4]
    grad_refs, refs = refs[4 : 4 + count], refs[4 + count :]
    normed_rows, dy_rows = refs[:2]
    act_refs, gup_refs = refs[2 : 2 + count], refs[2 + count :]
    step = pl.program_id(0)
    half = mine_ref.shape[1]
    curve = math.sqrt(2.0 / math.pi)
    normed = normed_ref[...]
    dy_rows[step, :, :half], dy_rows[step, :, half:] = in_order(mine_ref[...], other_ref[...])
    dy = dy_rows[step]
    normed_rows[step] = normed
    for w_in_ref, w_back_ref, act_ref, gup_ref in zip(w_in_refs, w_back_refs, act_refs, gup_refs):
        columns = w_in_ref.shape[1]
        width = min(256, columns)
        for at in range(0, columns, width):
            cols = slice(at, min(at + width, columns))
            up = times(normed, w_in_ref[:, cols])
            grad_act = times(dy, w_back_ref[:, cols])
            square = up * up
            bent = jnp.tanh(up * (curve + (curve * 0.044715) * square))
            gate = 0.5 + 0.5 * bent
            act = up * gate
            slope = gate + act * ((1.0 - gate) * (2 * curve + (6 * curve * 0.044715) * square))
            act_ref[step, :, cols] = low(act)
            gup_ref[step, :, cols] = low(grad_act * slope)
    total, grad = None, None
    for act_ref, w_back_ref, gup_ref, w_in_ref in zip(act_refs, w_back_refs, gup_refs, w_in_refs):
        part = times_t(act_ref[step], w_back_ref[...])
        total = part if total is None else total + part
        part = times_t(gup_ref[step], w_in_ref[...])
        grad = part if grad is None else grad + part
    part_ref[...] = total
    grad_ref[...] = low(grad)

    @pl.when(step == tiles - 1)
    def _():
        rows, width = tiles * normed_rows.shape[1], normed_rows.shape[2]
        for source, turned in ((normed_rows, normed_t_ref), (dy_rows, dy_t_ref)):
            turned[:, :rows] = source[...].reshape(rows, width).T
            turned[:, rows:] = jnp.zeros((width, turned.shape[1] - rows), jnp.bfloat16)
        for act_ref, gup_ref, ref in zip(act_refs, gup_refs, grad_refs):
            columns = act_ref.shape[2]
            for turned, right, at in ((normed_t_ref, gup_ref, 0), (dy_t_ref, act_ref, columns)):
                total = times(turned[:, :rows], right[...].reshape(rows, columns))
                by_parity(total, ref, slice(at, at + columns))


def by_parity(total, ref, cols):
    halves, rows = ref.shape[1:3]
    odd = lax.axis_index("dp") & 1
    for half in range(halves):
        for side in range(2):
            start = (2 * half + side) * rows
            ref[odd ^ side, half, :, cols] = total[start : start + rows].astype(ref.dtype)


def dense(normed, mine, other, w_in_pieces, w_back_pieces):
    rows, width = normed.shape
    tile = 2 * PATCHES
    tiles = rows // tile
    count = len(w_in_pieces)
    shape = jax.ShapeDtypeStruct
    sizes = [piece.shape[1] for piece in w_in_pieces]
    groups = lax.axis_size("dp")
    padded = -(-rows // 256) * 256
    row_tile = lambda columns: pl.BlockSpec((tile, columns), lambda step: (step, 0))
    turned = pl.BlockSpec((width, padded), lambda step: (0, 0))
    once = lambda columns: pl.BlockSpec((width, columns), lambda step: (0, 0), pipeline_mode=pl.Buffered(1))
    return pl.pallas_call(
        functools.partial(dense_kernel, count, tiles),
        name="dense",
        grid=(tiles,),
        out_shape=[
            shape((rows, width), jnp.float32),
            shape((rows, width), jnp.bfloat16),
            shape((width, padded), jnp.bfloat16),
            shape((width, padded), jnp.bfloat16),
        ]
        + [shape((2, groups // 2, width // groups, 2 * size), jnp.bfloat16) for size in sizes],
        in_specs=[row_tile(width), row_tile(width // 2), row_tile(width // 2)]
        + [once(size) for size in sizes] * 2,
        out_specs=[row_tile(width)] * 2
        + [turned] * 2
        + [
            pl.BlockSpec((2, groups // 2, width // groups, 2 * size), lambda step: (0, 0, 0, 0))
            for size in sizes
        ],
        scratch_shapes=[VMEM((tiles, tile, width), jnp.bfloat16)] * 2
        + [VMEM((tiles, tile, size), jnp.bfloat16) for size in sizes] * 2,
        compiler_params=pltpu.CompilerParams(vmem_limit_bytes=ROOM["dense"] * 2**20),
        cost_estimate=cost(24),
    )(normed, mine, other, *w_in_pieces, *w_back_pieces)


def outputs_kernel(part_ref, tok_ref, att_ref, mine_ref, other_ref, w_out_ref, keep_ref, send_ref, do_ref):
    tile, width = part_ref.shape
    half = width // 2
    heads, padded, _ = do_ref.shape
    lane = lane_of((tile, LANES))
    attended = att_ref[...]
    left = times_t(attended, w_out_ref[...]) + part_ref[...]
    token = tok_ref[...]
    keep, send = in_order(left[:, :half], left[:, half:])
    keep_ref[...] = keep + in_order(wide(token[:, :half]), wide(token[:, half:]))[0]
    send_ref[...] = low(send)
    first, second = in_order(mine_ref[...], other_ref[...])
    grad_att = times(first, w_out_ref[:half, :]) + times(second, w_out_ref[half:, :])
    shape = (LANES, 2 * LANES)
    row, column = row_of(shape), lane_of(shape)
    inners = (row // 64 == column // LANES) & (column % LANES >= 64) & (column % LANES < 67)
    inners = low(jnp.where(inners, -1.0, 0.0))
    found = []
    for pair in range(heads // 2):
        cols = slice(pair * LANES, pair * LANES + LANES)
        low_block = wide(low(grad_att[:, cols]))
        weighed, rest = two_terms(low_block * wide(attended[:, cols]))
        inner = times(weighed, inners) + times(rest, inners)
        for side in range(2):
            value = low_block if side == 0 else other_half(low_block)
            term = spread_terms(inner[:, side * LANES : (side + 1) * LANES])
            found.append(low(jnp.where(lane < 64, value, term)))
    for step in range(3):

        @pl.when(pl.program_id(0) == step)
        def _(step=step):
            for head in range(heads):
                do_ref[head, step * tile : (step + 1) * tile, :] = found[head]
            if step == 2:
                do_ref[:, 3 * tile :, :] = jnp.zeros((heads, padded - 3 * tile, LANES), jnp.bfloat16)


def outputs(part, tokens, attended, mine, other, w_out_t):
    rows, width = tokens.shape
    tile = 2 * PATCHES
    heads = w_out_t.shape[1] // 64
    padded = -(-rows // 256) * 256
    shape = jax.ShapeDtypeStruct
    row_tile = lambda columns: pl.BlockSpec((tile, columns), lambda step: (step, 0))
    return pl.pallas_call(
        outputs_kernel,
        name="outputs",
        grid=(rows // tile,),
        out_shape=[
            shape((rows, width // 2), jnp.float32),
            shape((rows, width // 2), jnp.bfloat16),
            shape((heads, padded, LANES), jnp.bfloat16),
        ],
        in_specs=[row_tile(columns) for columns in (width, width, width // 2, width // 2, width // 2)]
        + [pl.BlockSpec(w_out_t.shape, lambda step: (0, 0))],
        out_specs=[
            row_tile(width // 2),
            row_tile(width // 2),
            pl.BlockSpec((heads, padded, LANES), lambda step: (0, 0, 0)),
        ],
        compiler_params=pltpu.CompilerParams(vmem_limit_bytes=ROOM["outputs"] * 2**20),
        cost_estimate=cost(6),
    )(part, tokens, attended, mine, other, w_out_t)


def features_kernel(joined_ref, w_ref, mlp_ref, tok_ref, sent_ref, gain_ref):
    grad = times_t(joined_ref[...], w_ref[...]) + wide(mlp_ref[...])
    sent_ref[...] = low(grad)
    x = wide(tok_ref[...])
    x = x - jnp.mean(x, axis=1, keepdims=True)
    x = x * lax.rsqrt(jnp.mean(x * x, axis=1, keepdims=True) + EPSILON)

    @pl.when(pl.program_id(0) == 0)
    def _():
        gain_ref[...] = jnp.zeros_like(gain_ref)

    gain_ref[0:1, :] += jnp.sum(grad * x, axis=0, keepdims=True)


def features(first, count, grad_joined, w_qkv, grad_mlp, tokens):
    rows, width = tokens.shape
    tile = FINE
    row_tile = lambda columns: pl.BlockSpec((tile, columns), lambda step: (step + first, 0))
    return pl.pallas_call(
        features_kernel,
        name="features",
        grid=(count,),
        out_shape=[
            pltpu.HBM((tile * count, width), jnp.bfloat16),
            jax.ShapeDtypeStruct((8, width), jnp.float32),
        ],
        in_specs=[
            row_tile(grad_joined.shape[1]),
            pl.BlockSpec(w_qkv.shape, lambda step: (0, 0)),
            row_tile(width),
            row_tile(width),
        ],
        out_specs=[
            pl.BlockSpec((tile, width), lambda step: (step, 0)),
            pl.BlockSpec((8, width), lambda step: (0, 0)),
        ],
        compiler_params=pltpu.CompilerParams(vmem_limit_bytes=ROOM["features"] * 2**20),
        cost_estimate=cost(0.3 * count),
    )(grad_joined, w_qkv, grad_mlp, tokens)


def weights_kernel(*refs):
    keep_ref, send_ref = refs[-2:]
    halves, rows = keep_ref.shape[1:3]
    odd, far, side = lax.axis_index("dp") & 1, lax.axis_index("dp") // 2, lax.axis_index("hid")
    at = 0
    for left_ref, right_ref in zip(refs[:-2:2], refs[1:-2:2]):
        tokens, columns = right_ref.shape
        total = times(left_ref[:, :tokens], right_ref[...])
        cols = slice(at, at + columns)
        at += columns
        for half in range(halves):
            for parity in range(2):
                start = 2 * (2 * half + parity) * rows
                even, uneven = total[start : start + rows], total[start + rows : start + 2 * rows]
                keep_ref[odd ^ parity, far ^ half, :, cols] = low(jnp.where(side == 0, even, uneven))
                send_ref[odd ^ parity, far ^ half, :, cols] = low(jnp.where(side == 0, uneven, even))


def weights(*products):
    groups = lax.axis_size("dp")
    columns = sum(size for _, _, size, _ in products)
    shape = (2, groups // 2, products[0][0].shape[0] // (2 * groups), columns)
    whole = lambda shape: pl.BlockSpec(shape, lambda step: (0,) * len(shape))
    specs, operands = [], []
    for turned, right, size, place in products:
        specs += [
            whole(turned.shape),
            pl.BlockSpec((right.shape[0], size), lambda step, place=place: (0, place)),
        ]
        operands += [turned, right]
    return pl.pallas_call(
        weights_kernel,
        name="weights",
        grid=(1,),
        out_shape=[jax.ShapeDtypeStruct(shape, jnp.bfloat16)] * 2,
        in_specs=specs,
        out_specs=[whole(shape)] * 2,
        compiler_params=pltpu.CompilerParams(vmem_limit_bytes=ROOM["weights"] * 2**20),
        cost_estimate=cost(3),
    )(*operands)


def tokens_kernel(sent_ref, came_ref, tok_ref, gain_ref, mine_ref, other_ref, *refs):
    out_ref = refs[-1]
    half = mine_ref.shape[1]
    grad = (wide(sent_ref[...]) + wide(came_ref[...])) * wide(gain_ref[...]).reshape(1, -1)
    x = wide(tok_ref[...])
    x = x - jnp.mean(x, axis=1, keepdims=True)
    inverse = lax.rsqrt(jnp.mean(x * x, axis=1, keepdims=True) + EPSILON)
    x = x * inverse
    inner = jnp.mean(grad * x, axis=1, keepdims=True)
    grad = inverse * (grad - jnp.mean(grad, axis=1, keepdims=True) - x * inner)
    first, second = in_order(wide(mine_ref[...]), wide(other_ref[...]))
    out_ref[:, :half] = low(grad[:, :half] + first)
    out_ref[:, half:] = low(grad[:, half:] + second)


def token_rows(first, sent, came, tokens, norm_gain, mine, other, before):
    rows, width = tokens.shape
    tile = FINE
    count = sent.shape[0] // tile
    near = lambda columns: pl.BlockSpec((tile, columns), lambda step: (step, 0))
    far = lambda columns: pl.BlockSpec((tile, columns), lambda step: (step + first, 0))
    more = [] if before is None else [before]
    return pl.pallas_call(
        tokens_kernel,
        name="token_rows",
        grid=(count,),
        out_shape=jax.ShapeDtypeStruct((rows, width), jnp.bfloat16),
        in_specs=[
            near(width),
            near(width),
            far(width),
            pl.BlockSpec((width,), lambda step: (0,)),
            far(width // 2),
            far(width // 2),
        ]
        + [pl.BlockSpec(memory_space=pl.ANY)] * len(more),
        out_specs=far(width),
        input_output_aliases={6: 0} if more else {},
        compiler_params=pltpu.CompilerParams(vmem_limit_bytes=ROOM["token_rows"] * 2**20),
        cost_estimate=cost(0.3 * count),
    )(pinned(sent), came, tokens, norm_gain, mine, other, *more)


def finish_kernel(columns, *refs):
    first_ref, second_ref, small_ref = refs[-3:]
    rows = first_ref.shape[0]
    values = [wide(ref[...]) for ref in refs[:-3]]
    while len(values) > 1:
        values = [first + second for first, second in zip(values[::2], values[1::2])]
    first_ref[...] = values[0][:rows, :columns]
    second_ref[...] = values[0][:rows, columns:]
    small_ref[...] = values[0][rows:]


def finish(terms, columns):
    rows, whole = terms[0].shape[0] - 8, terms[0].shape[1]
    spec = pl.BlockSpec(memory_space=VMEM)
    return pl.pallas_call(
        functools.partial(finish_kernel, columns),
        name="finish",
        out_shape=[
            jax.ShapeDtypeStruct((rows, columns), jnp.float32),
            jax.ShapeDtypeStruct((rows, whole - columns), jnp.float32),
            jax.ShapeDtypeStruct((8, whole), jnp.float32),
        ],
        in_specs=[spec] * len(terms),
        out_specs=[spec] * 3,
        compiler_params=pltpu.CompilerParams(vmem_limit_bytes=16 * 2**20),
        cost_estimate=cost(1),
    )(*terms)


def swap(value, axis, bit):
    size = lax.axis_size(axis)
    return lax.ppermute(value, axis, [(place, place ^ bit) for place in range(size)])


def bits_of(axis):
    size = lax.axis_size(axis)
    return [1 << place for place in range(size.bit_length() - 1)]


def gather_pieces(block, axis):
    pieces = [block]
    for bit in bits_of(axis):
        held = pieces[0] if len(pieces) == 1 else jnp.concatenate(pieces, axis=1)
        pieces.append(swap(held, axis, bit))
    return pieces


def scatter_pieces(pieces, axis):
    for bit in reversed(bits_of(axis)):
        sent = swap(low(pieces[-1]), axis, bit)
        kept, at, half = [], 0, sent.shape[-1] // 2
        for piece in pieces[:-1]:
            size = piece.shape[-1] // 2
            parts = (sent[..., at : at + size], sent[..., half + at : half + at + size])
            kept.append(wide(piece) + wide(jnp.concatenate(parts, axis=-1) if size < half else sent))
            at += size
        pieces = kept
    return pieces[0]


def row_blocks(*products):
    groups, sides = lax.axis_size("dp"), lax.axis_size("hid")
    width = products[0][0].shape[0]
    if sides == 2 and width % (16 * groups * sides) == 0:
        keep, send = weights(*products)
        return wide(keep) + wide(swap(send, "hid", 1))
    parts = []
    for turned, right, size, place in products:
        parts.append(times(turned[:, : right.shape[0]], right[:, place * size : place * size + size]))
    shaped = jnp.concatenate(parts, axis=1).reshape(groups // 2, 2, sides, width // (groups * sides), -1)
    odd = lax.axis_index("dp") & 1
    shaped = shaped[(lax.axis_index("dp") // 2) ^ jnp.arange(groups // 2)]
    shaped = shaped[:, odd ^ jnp.arange(2)][:, :, lax.axis_index("hid") ^ jnp.arange(sides)]
    shaped = shaped.transpose(1, 0, 2, 3, 4)
    for bit in reversed(bits_of("hid")):
        shaped = shaped[:, :, :bit] + wide(swap(low(shaped[:, :, bit:]), "hid", bit))
    return shaped[:, :, 0]


def halve(shaped):
    return low(shaped[0]), swap(low(shaped[1]), "dp", 1)


def rest_terms(kept, came):
    count = lax.axis_size("dp")
    groups = [list(range(odd, count, 2)) for odd in (0, 1)]
    total = low(wide(kept) + wide(came))
    return lax.all_to_all(total, "dp", 0, 0, axis_index_groups=groups, tiled=True)


def far_terms(blocks):
    return [blocks[0]] + [swap(block, "dp", 2 * step) for step, block in enumerate(blocks) if step > 0]


def sum_everywhere(value, axes):
    for axis in axes:
        for bit in bits_of(axis):
            value = value + swap(value, axis, bit)
    return value


def shards(tokens, big_images, norm_gain, w_qkv, qk_gains, w_out_t, w_in, w_back, cotangent):
    width = tokens.shape[1]
    size = qk_gains.shape[1]
    groups = lax.axis_size("dp")
    other = swap(cotangent, "hg", 1)
    w_in_pieces = gather_pieces(w_in, "hid")
    w_back_pieces = gather_pieces(w_back, "hid")
    normed, q_rows, k_rows, v_rows, attended, inverses = forward(
        big_images, tokens, norm_gain, w_qkv, qk_gains
    )
    part, grad_mlp, normed_t, dy_t, *grads = dense(normed, cotangent, other, w_in_pieces, w_back_pieces)
    kept, sent, do_rows = outputs(part, tokens, attended, cotangent, other, w_out_t)
    out_came = swap(sent, "hg", 1)
    mlp_kept, mlp_came = halve(scatter_pieces(grads, "hid"))
    do_rows, mlp_kept = lax.optimization_barrier((do_rows, mlp_kept))

    grad_joined, qk_part = backward(big_images, q_rows, k_rows, v_rows, do_rows, inverses, qk_gains)
    grad_joined, out_came, mlp_came = lax.optimization_barrier((grad_joined, out_came, mlp_came))
    mine, gain_part = features(0, tokens.shape[0] // FINE, grad_joined, w_qkv, grad_mlp, tokens)
    mine, mlp_came = lax.optimization_barrier((mine, mlp_came))
    came = swap(mine, "hg", 1)
    columns = attended.shape[1]

    def weight_sums(normed_t, dy_t, grad_joined, attended, gain_part, qk_part, kept, out_came):
        first_blocks = row_blocks((normed_t, grad_joined, 2 * columns, 0))
        blocks = row_blocks((normed_t, grad_joined, columns, 2), (dy_t, attended, columns, 0))
        small = jnp.concatenate([gain_part[0], qk_part[0, :size], qk_part[0, LANES : LANES + size]])
        small = low(sum_everywhere(small, ("hid",)))
        small, first_blocks = lax.optimization_barrier((small, first_blocks))
        first_kept, first_came = halve(first_blocks)
        second_kept, second_came = halve(blocks)
        small = low(wide(small) + wide(swap(small, "dp", 1)))
        small = jnp.pad(small, (0, 8 * 4 * columns - small.shape[0])).reshape(1, 8, -1)
        first = low(wide(first_kept) + wide(first_came))
        second = low(wide(second_kept) + wide(second_came))
        small = jnp.broadcast_to(small, first.shape[:1] + small.shape[1:])
        sums = jnp.concatenate([jnp.concatenate([first, second], axis=2), small], axis=1)
        return [sums[step] for step in range(sums.shape[0])], low(kept + wide(out_came))

    def no_sums(*operands):
        return jax.tree.map(lambda kind: jnp.zeros(kind.shape, kind.dtype), kinds)

    operands = (normed_t, dy_t, grad_joined, attended, gain_part, qk_part, kept, out_came)
    kinds = jax.eval_shape(weight_sums, *operands)
    sums, output = lax.cond(big_images[0] >= 0, weight_sums, no_sums, *operands)
    mlp_terms = rest_terms(mlp_kept, mlp_came)
    hidden = mlp_terms.shape[2] // 2
    w_in_grad = jnp.sum(wide(mlp_terms[:, :, :hidden]), axis=0)
    w_back_grad = jnp.sum(wide(mlp_terms[:, :, hidden:]), axis=0)
    terms = far_terms(sums)
    token_grad = token_rows(0, mine, came, tokens, norm_gain, cotangent, other, None)
    held = (terms[1], token_grad, w_in_grad, w_back_grad)
    terms[1], token_grad, w_in_grad, w_back_grad = lax.optimization_barrier(held)
    w_qkv_grad, w_out_t_grad, small = finish(terms, 3 * columns)
    small = small[0]
    small = sum_everywhere(small, ("hg",))
    own = lax.axis_index("dp") * lax.axis_size("hid") + lax.axis_index("hid")
    gain_rows = width // (groups * lax.axis_size("hid"))
    norm_gain_grad = lax.dynamic_slice_in_dim(small, own * gain_rows, gain_rows, 0)
    qk_gains_grad = small[width : width + 2 * size].reshape(2, size)
    return (
        output,
        token_grad,
        norm_gain_grad,
        w_qkv_grad,
        qk_gains_grad,
        w_out_t_grad,
        w_in_grad,
        w_back_grad,
    )


def solution(mesh):
    return jax.shard_map(
        shards,
        mesh=mesh,
        in_specs=(
            P(("dp", "hid"), None),
            P(("dp", "hid")),
            P(),
            P(None, "hg"),
            P(),
            P(None, "hg"),
            P(None, ("hg", "hid")),
            P(None, ("hg", "hid")),
            P(("dp", "hid"), "hg"),
        ),
        out_specs=(
            P(("dp", "hid"), "hg"),
            P(("dp", "hid"), None),
            P(("dp", "hid")),
            P(("dp", "hid"), "hg"),
            P(),
            P(("dp", "hid"), "hg"),
            P("dp", ("hg", "hid")),
            P("dp", ("hg", "hid")),
        ),
        check_vma=False,
    )
```

```python
import functools
import math

import jax
import jax.numpy as jnp
from jax import lax
from jax.experimental import pallas as pl
from jax.experimental.pallas import tpu as pltpu
from jax.sharding import PartitionSpec as P

PATCHES = 196
EPSILON = 1e-06
LOG2E = math.log2(math.e)
LANES = 128
VMEM = pltpu.VMEM


def pinned(value):
    return pltpu.with_memory_space_constraint(value, pltpu.HBM)


SCALE = 1.0
ROOM = dict(forward=40, backward=24, dense=32, outputs=24, features=24, weights=24, token_rows=24)


def cost(microseconds):
    return pl.CostEstimate(
        flops=int(microseconds * SCALE * 1e9), bytes_accessed=2**20, transcendentals=0
    )


def times_t(left, right):
    return lax.dot_general(
        left, right, (((1,), (1,)), ((), ())), preferred_element_type=jnp.float32
    )


def rows_t(left, right):
    return lax.dot_general(
        left, right, (((0,), (0,)), ((), ())), preferred_element_type=jnp.float32
    )


def times(left, right):
    return jnp.dot(left, right, preferred_element_type=jnp.float32)


def low(value):
    return value.astype(jnp.bfloat16)


def wide(value):
    return value.astype(jnp.float32)


def lane_of(shape):
    return lax.broadcasted_iota(jnp.int32, shape, 1)


def row_of(shape):
    return lax.broadcasted_iota(jnp.int32, shape, 0)


def other_half(value):
    return pltpu.roll(value, LANES // 2, 1)


def spread_terms(whole):
    lane = lane_of(whole.shape)
    first = wide(low(whole))
    second = wide(low(whole - first))
    third = whole - first - second
    return jnp.where(lane == 64, first, jnp.where(lane == 65, second, jnp.where(lane == 66, third, 0.0)))


def three_terms(column, shape):
    return spread_terms(jnp.broadcast_to(column, shape))


def two_terms(value):
    first = low(value)
    return first, low(value - wide(first))


def pair_mask(block, shape, first_lane):
    start = 2 * PATCHES * block - first_lane
    place = lane_of(shape) - start
    second = row_of(shape) >= PATCHES
    begin = jnp.where(second, PATCHES, 0)
    return (place >= begin) & (place < begin + PATCHES)


def window_of(block):
    return (2 * PATCHES * block // LANES) * LANES, 4 * LANES


def forward_kernel(
    flag_ref,
    tok_hbm,
    gain_hbm,
    w_hbm,
    qk_hbm,
    normed_ref,
    q_hbm,
    k_hbm,
    v_hbm,
    att_ref,
    inv_ref,
    tok_ref,
    gain_ref,
    w_ref,
    qk_ref,
    q_ref,
    k_ref,
    v_ref,
    in_sems,
    out_sems,
):
    rows = tok_ref.shape[0]
    heads, padded, _ = q_ref.shape
    tile = 2 * PATCHES
    size = qk_ref.shape[1]
    group_a = row_of((256, 256)) // size
    group_b = lane_of((256, 256)) // size
    mean_of = low(jnp.where(group_a == group_b, 1.0 / size, 0.0))
    stride = rows // (3 * LANES) and 3 * LANES
    strip = rows - (rows // stride - 1) * stride
    strips = rows // stride
    edges = [0] + [stride * step + 32 for step in range(1, strips)] + [rows]
    token_copies = []
    for step in range(strips):
        part = pl.ds(edges[step], edges[step + 1] - edges[step])
        token_copies.append(pltpu.make_async_copy(tok_hbm.at[part], tok_ref.at[part], in_sems.at[step]))
    w_copy = pltpu.make_async_copy(w_hbm, w_ref, in_sems.at[strips])
    small_copies = [
        pltpu.make_async_copy(source, target, in_sems.at[strips + 1 + place])
        for place, (source, target) in enumerate(((gain_hbm, gain_ref), (qk_hbm, qk_ref)))
    ]
    for copy in small_copies:
        copy.start()
    token_copies[0].start()
    w_copy.start()
    for copy in token_copies[1:]:
        copy.start()
    lane = lane_of((strip, LANES))

    for copy in small_copies:
        copy.wait()
    gain = wide(gain_ref[...]).reshape(1, -1)
    q_gain = wide(qk_ref[0:1, :]) * (size**-0.5 * LOG2E)
    k_gain = wide(qk_ref[1:2, :])
    ones = jnp.ones_like(k_gain)
    gains = jnp.concatenate([q_gain, k_gain, ones, q_gain, k_gain, ones], axis=1)
    is_value = jnp.concatenate([0 * ones, 0 * ones, ones, 0 * ones, 0 * ones, ones], axis=1)

    def project(step, _):
        for place, copy in enumerate(token_copies):
            pl.when(step == place)(copy.wait)
        here = pl.ds(pl.multiple_of(step * stride, LANES), strip)
        x = wide(tok_ref[here, :])
        x = x - jnp.mean(x, axis=1, keepdims=True)
        x = x * lax.rsqrt(jnp.mean(x * x, axis=1, keepdims=True) + EPSILON)
        normed = low(x * gain)
        normed_ref[here, :] = normed
        every = times(normed, w_ref[...])
        for pair in range(heads // 2):
            joined = every[:, 384 * pair : 384 * pair + 384]
            parts = []
            for at in (0, 256):
                wid = min(256, 384 - at)
                block = joined[:, at : at + wid]
                means = mean_of[:wid, :wid]
                centred = block - times(low(block), means)
                squares = low(centred * centred)
                variance = times(squares, means)
                inverse = lax.rsqrt(variance + EPSILON)
                inv_ref[here, 384 * pair + at : 384 * pair + at + wid] = low(inverse)
                hat = centred * inverse
                parts.append(
                    jnp.where(is_value[:, at : at + wid] > 0, block, hat * gains[:, at : at + wid])
                )
            b0, b1, b2 = parts[0][:, :128], parts[0][:, 128:], parts[1]
            first = lane < 64
            unit = jnp.where(lane < 67, 1.0, 0.0)
            q_ref[2 * pair, here, :] = low(jnp.where(first, b0, 0.0))
            k_ref[2 * pair, here, :] = low(jnp.where(first, other_half(b0), unit))
            v_ref[2 * pair, here, :] = low(jnp.where(first, b1, unit))
            q_ref[2 * pair + 1, here, :] = low(jnp.where(first, other_half(b1), 0.0))
            k_ref[2 * pair + 1, here, :] = low(jnp.where(first, b2, unit))
            v_ref[2 * pair + 1, here, :] = low(jnp.where(first, other_half(b2), unit))
        return 0

    w_copy.wait()
    lax.fori_loop(0, strips, project, 0)
    lane = lane_of((tile, LANES))
    for ref in (q_ref, k_ref, v_ref):
        ref[:, rows:, :] = jnp.zeros((heads, padded - rows, LANES), jnp.bfloat16)
    key_copy = pltpu.make_async_copy(k_ref, k_hbm, out_sems.at[0])
    value_copy = pltpu.make_async_copy(v_ref, v_hbm, out_sems.at[1])
    key_copy.start()
    value_copy.start()

    def query_copy(pair):
        part = pl.ds(2 * pair, 2)
        return pltpu.make_async_copy(q_ref.at[part], q_hbm.at[part], out_sems.at[2 + pair])

    def attend(pair, _, big):
        for start in range(0, rows, tile):
            here = slice(start, start + tile)
            if big:
                keys = slice(0, padded)
            else:
                begin, length = window_of(start // tile)
                keys = slice(begin, begin + length)
            found = []
            for side in range(2):
                head = 2 * pair + side
                queries = q_ref[head, here, :]
                scores = times_t(queries, k_ref[head, keys, :])
                if not big:
                    scores = jnp.where(
                        pair_mask(start // tile, scores.shape, keys.start), scores, -1e30
                    )
                expo = low(jnp.exp2(scores))
                out = times(expo, v_ref[head, keys, :])
                total = out[:, 64:65]
                found.append(out * (1.0 / total))
                log_total = jnp.log(total) * (-LOG2E)
                q_ref[head, here, :] = low(
                    jnp.where(lane < 64, wide(queries), three_terms(log_total, lane.shape))
                )
            att_ref[here, pl.ds(pl.multiple_of(pair * LANES, LANES), LANES)] = low(
                jnp.where(lane < 64, found[0], other_half(found[1]))
            )
        query_copy(pair).start()
        return 0

    @pl.when(flag_ref[0] > 0)
    def _():
        lax.fori_loop(0, heads // 2, functools.partial(attend, big=True), 0)

    @pl.when(flag_ref[0] <= 0)
    def _():
        lax.fori_loop(0, heads // 2, functools.partial(attend, big=False), 0)

    key_copy.wait()
    value_copy.wait()
    for pair in range(heads // 2):
        query_copy(pair).wait()


def forward(big_images, tokens, norm_gain, w_qkv, qk_gains):
    rows, width = tokens.shape
    size = qk_gains.shape[1]
    heads = w_qkv.shape[1] // (3 * size)
    padded = -(-rows // 256) * 256
    whole = pl.BlockSpec(memory_space=VMEM)
    hbm = pl.BlockSpec(memory_space=pltpu.HBM)
    held = VMEM((heads, padded, LANES), jnp.bfloat16)
    head_rows = pltpu.HBM((heads, padded, LANES), jnp.bfloat16)
    return pl.pallas_call(
        forward_kernel,
        name="forward",
        out_shape=[
            jax.ShapeDtypeStruct((rows, width), jnp.bfloat16),
            head_rows,
            head_rows,
            head_rows,
            jax.ShapeDtypeStruct((rows, heads * size), jnp.bfloat16),
            pltpu.HBM((rows, w_qkv.shape[1]), jnp.bfloat16),
        ],
        in_specs=[pl.BlockSpec(memory_space=pltpu.SMEM)] + [hbm] * 4,
        out_specs=[whole, hbm, hbm, hbm, whole, whole],
        scratch_shapes=[
            VMEM((rows, width), jnp.bfloat16),
            VMEM(norm_gain.shape, jnp.bfloat16),
            VMEM(w_qkv.shape, jnp.bfloat16),
            VMEM(qk_gains.shape, jnp.bfloat16),
            held,
            held,
            held,
            pltpu.SemaphoreType.DMA((rows // (3 * LANES) + 3,)),
            pltpu.SemaphoreType.DMA((2 + heads // 2,)),
        ],
        compiler_params=pltpu.CompilerParams(vmem_limit_bytes=ROOM["forward"] * 2**20),
        cost_estimate=cost(24),
    )(big_images, pinned(tokens), pinned(norm_gain), pinned(w_qkv), pinned(qk_gains))


def backward_kernel(
    flag_ref, q_ref, k_ref, v_ref, do_ref, inv_ref, qk_ref, joined_ref, small_ref, dq_ref, dk_ref, dv_ref, turned_ref
):
    pair = pl.program_id(0)
    rows = inv_ref.shape[0]
    padded = q_ref.shape[1]
    tile = 2 * PATCHES
    size = qk_ref.shape[1]
    scale = size**-0.5
    zeros = jnp.zeros((1, LANES - size), jnp.float32)
    q_gain = wide(qk_ref[0:1, :])
    k_gain = wide(qk_ref[1:2, :])
    q_back = jnp.concatenate([1.0 / (q_gain * (scale * LOG2E)), zeros], axis=1)
    k_back = jnp.concatenate([1.0 / k_gain, zeros], axis=1)
    q_gain = jnp.concatenate([q_gain, zeros], axis=1)
    k_gain = jnp.concatenate([k_gain, zeros], axis=1)

    def attend(side, _, big):
        for start in range(0, rows, rows if big else tile):
            here = slice(start, start + (rows if big else tile))
            if big:
                over = slice(0, padded)
            else:
                begin, length = window_of(start // tile)
                over = slice(begin, begin + length)
            keys = k_ref[side, here, :]
            queries = q_ref[side, over, :]
            grads = do_ref[side, over, :]
            scores = times_t(keys, queries)
            if not big:
                scores = jnp.where(pair_mask(start // tile, scores.shape, over.start), scores, -1e30)
            probs = jnp.exp2(scores)
            grad_probs = times_t(v_ref[side, here, :], grads)
            grad_scores = low(probs * grad_probs)
            dv_ref[side, here, :] = times(low(probs), grads)
            dk_ref[side, here, :] = times(grad_scores, queries)
            more = rows_t(keys, grad_scores)
            if big and start == 0:
                dq_ref[side, :, over] = more
            elif big:
                dq_ref[side, :, over] += more
            else:
                place = lane_of(more.shape) - (start - over.start)
                dq_ref[side, :, over] = jnp.where(
                    (place >= 0) & (place < tile), more, dq_ref[side, :, over]
                )
        return 0

    @pl.when(flag_ref[0] > 0)
    def _():
        lax.fori_loop(0, 2, functools.partial(attend, big=True), 0)

    @pl.when(flag_ref[0] <= 0)
    def _():
        lax.fori_loop(0, 2, functools.partial(attend, big=False), 0)

    @pl.when(pair == 0)
    def _():
        small_ref[...] = jnp.zeros_like(small_ref)

    lane = lane_of((tile, LANES))
    first = lane < 64
    shape = (2 * LANES, 2 * LANES)
    row, column = row_of(shape), lane_of(shape)
    means = (row // LANES == column // LANES) & (row % LANES < size)
    means = low(jnp.where(means, 1.0 / size, 0.0))
    gains = jnp.concatenate([q_gain * scale, k_gain * math.log(2.0)], axis=1)
    factors = jnp.concatenate([jnp.full_like(q_gain, scale), jnp.full_like(k_gain, math.log(2.0))], axis=1)
    backs = jnp.concatenate([q_back, k_back], axis=1)
    for side in range(2):
        turned_ref[side] = dq_ref[side].T
    for start in range(0, rows, tile):
        here = slice(start, start + tile)
        inv0, inv1, inv2 = (wide(inv_ref[here, at : at + LANES]) for at in range(0, 3 * LANES, LANES))
        inverses = (inv0, other_half(inv0)), (other_half(inv1), inv2)
        blocks = []
        for side in range(2):
            inverse = jnp.concatenate(inverses[side], axis=1)
            hat = jnp.concatenate([q_ref[side, here, :], k_ref[side, here, :]], axis=1)
            hat = wide(hat) * backs
            grad = jnp.concatenate([turned_ref[side, here, :], dk_ref[side, here, :]], axis=1)
            small_ref[0:1, :] += jnp.sum(grad * hat, axis=0, keepdims=True) * factors
            grad = grad * gains
            inner = times(low(grad * hat), means)
            grad = inverse * (grad - times(low(grad), means) - hat * inner)
            blocks.append((grad[:, :LANES], grad[:, LANES:], dv_ref[side, here, :]))
        (q0, k0, v0), (q1, k1, v1) = blocks
        joined_ref[here, 0:128] = low(jnp.where(first, q0, other_half(k0)))
        joined_ref[here, 128:256] = low(jnp.where(first, v0, other_half(q1)))
        joined_ref[here, 256:384] = low(jnp.where(first, k1, other_half(v1)))


def backward(big_images, q_rows, k_rows, v_rows, do_rows, inverses, qk_gains):
    heads, padded, _ = q_rows.shape
    rows = inverses.shape[0]
    pair_spec = pl.BlockSpec((2, padded, LANES), lambda pair: (pair, 0, 0))
    return pl.pallas_call(
        backward_kernel,
        name="backward",
        grid=(heads // 2,),
        out_shape=[
            jax.ShapeDtypeStruct((rows, heads * 3 * LANES // 2), jnp.bfloat16),
            jax.ShapeDtypeStruct((8, 2 * LANES), jnp.float32),
        ],
        in_specs=[pl.BlockSpec(memory_space=pltpu.SMEM)]
        + [pair_spec] * 4
        + [pl.BlockSpec((rows, 3 * LANES), lambda pair: (0, pair)), pl.BlockSpec(qk_gains.shape, lambda pair: (0, 0))],
        out_specs=[
            pl.BlockSpec((rows, 3 * LANES), lambda pair: (0, pair)),
            pl.BlockSpec((8, 2 * LANES), lambda pair: (0, 0)),
        ],
        scratch_shapes=[
            VMEM((2, LANES, padded), jnp.float32),
            VMEM((2, rows, LANES), jnp.float32),
            VMEM((2, rows, LANES), jnp.float32),
            VMEM((2, padded, LANES), jnp.float32),
        ],
        compiler_params=pltpu.CompilerParams(vmem_limit_bytes=ROOM["backward"] * 2**20),
        cost_estimate=cost(36),
    )(big_images, pinned(q_rows), pinned(k_rows), pinned(v_rows), do_rows, pinned(inverses), qk_gains)


FINE = 2 * PATCHES


def in_order(mine, other):
    first = lax.axis_index("hg") == 0
    return jnp.where(first, mine, other), jnp.where(first, other, mine)


def dense_kernel(count, tiles, normed_ref, mine_ref, other_ref, *refs):
    w_in_refs, w_back_refs = refs[:count], refs[count : 2 * count]
    refs = refs[2 * count :]
    part_ref, grad_ref, normed_t_ref, dy_t_ref = refs[:4]
    grad_refs, refs = refs[4 : 4 + count], refs[4 + count :]
    normed_rows, dy_rows = refs[:2]
    act_refs, gup_refs = refs[2 : 2 + count], refs[2 + count :]
    step = pl.program_id(0)
    half = mine_ref.shape[1]
    curve = math.sqrt(2.0 / math.pi)
    normed = normed_ref[...]
    dy_rows[step, :, :half], dy_rows[step, :, half:] = in_order(mine_ref[...], other_ref[...])
    dy = dy_rows[step]
    normed_rows[step] = normed
    for w_in_ref, w_back_ref, act_ref, gup_ref in zip(w_in_refs, w_back_refs, act_refs, gup_refs):
        columns = w_in_ref.shape[1]
        width = min(256, columns)
        for at in range(0, columns, width):
            cols = slice(at, min(at + width, columns))
            up = times(normed, w_in_ref[:, cols])
            grad_act = times(dy, w_back_ref[:, cols])
            square = up * up
            bent = jnp.tanh(up * (curve + (curve * 0.044715) * square))
            gate = 0.5 + 0.5 * bent
            act = up * gate
            slope = gate + act * ((1.0 - gate) * (2 * curve + (6 * curve * 0.044715) * square))
            act_ref[step, :, cols] = low(act)
            gup_ref[step, :, cols] = low(grad_act * slope)
    total, grad = None, None
    for act_ref, w_back_ref, gup_ref, w_in_ref in zip(act_refs, w_back_refs, gup_refs, w_in_refs):
        part = times_t(act_ref[step], w_back_ref[...])
        total = part if total is None else total + part
        part = times_t(gup_ref[step], w_in_ref[...])
        grad = part if grad is None else grad + part
    part_ref[...] = total
    grad_ref[...] = low(grad)

    @pl.when(step == tiles - 1)
    def _():
        rows, width = tiles * normed_rows.shape[1], normed_rows.shape[2]
        for source, turned in ((normed_rows, normed_t_ref), (dy_rows, dy_t_ref)):
            turned[:, :rows] = source[...].reshape(rows, width).T
            turned[:, rows:] = jnp.zeros((width, turned.shape[1] - rows), jnp.bfloat16)
        for act_ref, gup_ref, ref in zip(act_refs, gup_refs, grad_refs):
            columns = act_ref.shape[2]
            for turned, right, at in ((normed_t_ref, gup_ref, 0), (dy_t_ref, act_ref, columns)):
                total = times(turned[:, :rows], right[...].reshape(rows, columns))
                by_parity(total, ref, slice(at, at + columns))


def by_parity(total, ref, cols):
    halves, rows = ref.shape[1:3]
    odd = lax.axis_index("dp") & 1
    for half in range(halves):
        for side in range(2):
            start = (2 * half + side) * rows
            ref[odd ^ side, half, :, cols] = total[start : start + rows].astype(ref.dtype)


def dense(normed, mine, other, w_in_pieces, w_back_pieces):
    rows, width = normed.shape
    tile = 2 * PATCHES
    tiles = rows // tile
    count = len(w_in_pieces)
    shape = jax.ShapeDtypeStruct
    sizes = [piece.shape[1] for piece in w_in_pieces]
    groups = lax.axis_size("dp")
    padded = -(-rows // 256) * 256
    row_tile = lambda columns: pl.BlockSpec((tile, columns), lambda step: (step, 0))
    turned = pl.BlockSpec((width, padded), lambda step: (0, 0))
    once = lambda columns: pl.BlockSpec((width, columns), lambda step: (0, 0), pipeline_mode=pl.Buffered(1))
    return pl.pallas_call(
        functools.partial(dense_kernel, count, tiles),
        name="dense",
        grid=(tiles,),
        out_shape=[
            shape((rows, width), jnp.float32),
            shape((rows, width), jnp.bfloat16),
            shape((width, padded), jnp.bfloat16),
            shape((width, padded), jnp.bfloat16),
        ]
        + [shape((2, groups // 2, width // groups, 2 * size), jnp.bfloat16) for size in sizes],
        in_specs=[row_tile(width), row_tile(width // 2), row_tile(width // 2)]
        + [once(size) for size in sizes] * 2,
        out_specs=[row_tile(width)] * 2
        + [turned] * 2
        + [
            pl.BlockSpec((2, groups // 2, width // groups, 2 * size), lambda step: (0, 0, 0, 0))
            for size in sizes
        ],
        scratch_shapes=[VMEM((tiles, tile, width), jnp.bfloat16)] * 2
        + [VMEM((tiles, tile, size), jnp.bfloat16) for size in sizes] * 2,
        compiler_params=pltpu.CompilerParams(vmem_limit_bytes=ROOM["dense"] * 2**20),
        cost_estimate=cost(24),
    )(normed, mine, other, *w_in_pieces, *w_back_pieces)


def outputs_kernel(part_ref, tok_ref, att_ref, mine_ref, other_ref, w_out_ref, keep_ref, send_ref, do_ref):
    tile, width = part_ref.shape
    half = width // 2
    heads, padded, _ = do_ref.shape
    lane = lane_of((tile, LANES))
    attended = att_ref[...]
    left = times_t(attended, w_out_ref[...]) + part_ref[...]
    token = tok_ref[...]
    keep, send = in_order(left[:, :half], left[:, half:])
    keep_ref[...] = keep + in_order(wide(token[:, :half]), wide(token[:, half:]))[0]
    send_ref[...] = low(send)
    first, second = in_order(mine_ref[...], other_ref[...])
    grad_att = times(first, w_out_ref[:half, :]) + times(second, w_out_ref[half:, :])
    shape = (LANES, 2 * LANES)
    row, column = row_of(shape), lane_of(shape)
    inners = (row // 64 == column // LANES) & (column % LANES >= 64) & (column % LANES < 67)
    inners = low(jnp.where(inners, -1.0, 0.0))
    found = []
    for pair in range(heads // 2):
        cols = slice(pair * LANES, pair * LANES + LANES)
        low_block = wide(low(grad_att[:, cols]))
        weighed, rest = two_terms(low_block * wide(attended[:, cols]))
        inner = times(weighed, inners) + times(rest, inners)
        for side in range(2):
            value = low_block if side == 0 else other_half(low_block)
            term = spread_terms(inner[:, side * LANES : (side + 1) * LANES])
            found.append(low(jnp.where(lane < 64, value, term)))
    for step in range(3):

        @pl.when(pl.program_id(0) == step)
        def _(step=step):
            for head in range(heads):
                do_ref[head, step * tile : (step + 1) * tile, :] = found[head]
            if step == 2:
                do_ref[:, 3 * tile :, :] = jnp.zeros((heads, padded - 3 * tile, LANES), jnp.bfloat16)


def outputs(part, tokens, attended, mine, other, w_out_t):
    rows, width = tokens.shape
    tile = 2 * PATCHES
    heads = w_out_t.shape[1] // 64
    padded = -(-rows // 256) * 256
    shape = jax.ShapeDtypeStruct
    row_tile = lambda columns: pl.BlockSpec((tile, columns), lambda step: (step, 0))
    return pl.pallas_call(
        outputs_kernel,
        name="outputs",
        grid=(rows // tile,),
        out_shape=[
            shape((rows, width // 2), jnp.float32),
            shape((rows, width // 2), jnp.bfloat16),
            shape((heads, padded, LANES), jnp.bfloat16),
        ],
        in_specs=[row_tile(columns) for columns in (width, width, width // 2, width // 2, width // 2)]
        + [pl.BlockSpec(w_out_t.shape, lambda step: (0, 0))],
        out_specs=[
            row_tile(width // 2),
            row_tile(width // 2),
            pl.BlockSpec((heads, padded, LANES), lambda step: (0, 0, 0)),
        ],
        compiler_params=pltpu.CompilerParams(vmem_limit_bytes=ROOM["outputs"] * 2**20),
        cost_estimate=cost(6),
    )(part, tokens, attended, mine, other, w_out_t)


def features_kernel(joined_ref, w_ref, mlp_ref, tok_ref, sent_ref, gain_ref):
    grad = times_t(joined_ref[...], w_ref[...]) + wide(mlp_ref[...])
    sent_ref[...] = low(grad)
    x = wide(tok_ref[...])
    x = x - jnp.mean(x, axis=1, keepdims=True)
    x = x * lax.rsqrt(jnp.mean(x * x, axis=1, keepdims=True) + EPSILON)

    @pl.when(pl.program_id(0) == 0)
    def _():
        gain_ref[...] = jnp.zeros_like(gain_ref)

    gain_ref[0:1, :] += jnp.sum(grad * x, axis=0, keepdims=True)


def features(first, count, grad_joined, w_qkv, grad_mlp, tokens):
    rows, width = tokens.shape
    tile = FINE
    row_tile = lambda columns: pl.BlockSpec((tile, columns), lambda step: (step + first, 0))
    return pl.pallas_call(
        features_kernel,
        name="features",
        grid=(count,),
        out_shape=[
            pltpu.HBM((tile * count, width), jnp.bfloat16),
            jax.ShapeDtypeStruct((8, width), jnp.float32),
        ],
        in_specs=[
            row_tile(grad_joined.shape[1]),
            pl.BlockSpec(w_qkv.shape, lambda step: (0, 0)),
            row_tile(width),
            row_tile(width),
        ],
        out_specs=[
            pl.BlockSpec((tile, width), lambda step: (step, 0)),
            pl.BlockSpec((8, width), lambda step: (0, 0)),
        ],
        compiler_params=pltpu.CompilerParams(vmem_limit_bytes=ROOM["features"] * 2**20),
        cost_estimate=cost(0.3 * count),
    )(grad_joined, w_qkv, grad_mlp, tokens)


def weights_kernel(*refs):
    keep_ref, send_ref = refs[-2:]
    halves, rows = keep_ref.shape[1:3]
    odd, far, side = lax.axis_index("dp") & 1, lax.axis_index("dp") // 2, lax.axis_index("hid")
    at = 0
    for left_ref, right_ref in zip(refs[:-2:2], refs[1:-2:2]):
        tokens, columns = right_ref.shape
        total = times(left_ref[:, :tokens], right_ref[...])
        cols = slice(at, at + columns)
        at += columns
        for half in range(halves):
            for parity in range(2):
                start = 2 * (2 * half + parity) * rows
                even, uneven = total[start : start + rows], total[start + rows : start + 2 * rows]
                keep_ref[odd ^ parity, far ^ half, :, cols] = low(jnp.where(side == 0, even, uneven))
                send_ref[odd ^ parity, far ^ half, :, cols] = low(jnp.where(side == 0, uneven, even))


def weights(*products):
    groups = lax.axis_size("dp")
    columns = sum(size for _, _, size, _ in products)
    shape = (2, groups // 2, products[0][0].shape[0] // (2 * groups), columns)
    whole = lambda shape: pl.BlockSpec(shape, lambda step: (0,) * len(shape))
    specs, operands = [], []
    for turned, right, size, place in products:
        specs += [
            whole(turned.shape),
            pl.BlockSpec((right.shape[0], size), lambda step, place=place: (0, place)),
        ]
        operands += [turned, right]
    return pl.pallas_call(
        weights_kernel,
        name="weights",
        grid=(1,),
        out_shape=[jax.ShapeDtypeStruct(shape, jnp.bfloat16)] * 2,
        in_specs=specs,
        out_specs=[whole(shape)] * 2,
        compiler_params=pltpu.CompilerParams(vmem_limit_bytes=ROOM["weights"] * 2**20),
        cost_estimate=cost(3),
    )(*operands)


def tokens_kernel(sent_ref, came_ref, tok_ref, gain_ref, mine_ref, other_ref, *refs):
    out_ref = refs[-1]
    half = mine_ref.shape[1]
    grad = (wide(sent_ref[...]) + wide(came_ref[...])) * wide(gain_ref[...]).reshape(1, -1)
    x = wide(tok_ref[...])
    x = x - jnp.mean(x, axis=1, keepdims=True)
    inverse = lax.rsqrt(jnp.mean(x * x, axis=1, keepdims=True) + EPSILON)
    x = x * inverse
    inner = jnp.mean(grad * x, axis=1, keepdims=True)
    grad = inverse * (grad - jnp.mean(grad, axis=1, keepdims=True) - x * inner)
    first, second = in_order(wide(mine_ref[...]), wide(other_ref[...]))
    out_ref[:, :half] = low(grad[:, :half] + first)
    out_ref[:, half:] = low(grad[:, half:] + second)


def token_rows(first, sent, came, tokens, norm_gain, mine, other, before):
    rows, width = tokens.shape
    tile = FINE
    count = sent.shape[0] // tile
    near = lambda columns: pl.BlockSpec((tile, columns), lambda step: (step, 0))
    far = lambda columns: pl.BlockSpec((tile, columns), lambda step: (step + first, 0))
    more = [] if before is None else [before]
    return pl.pallas_call(
        tokens_kernel,
        name="token_rows",
        grid=(count,),
        out_shape=jax.ShapeDtypeStruct((rows, width), jnp.bfloat16),
        in_specs=[
            near(width),
            near(width),
            far(width),
            pl.BlockSpec((width,), lambda step: (0,)),
            far(width // 2),
            far(width // 2),
        ]
        + [pl.BlockSpec(memory_space=pl.ANY)] * len(more),
        out_specs=far(width),
        input_output_aliases={6: 0} if more else {},
        compiler_params=pltpu.CompilerParams(vmem_limit_bytes=ROOM["token_rows"] * 2**20),
        cost_estimate=cost(0.3 * count),
    )(pinned(sent), came, tokens, norm_gain, mine, other, *more)


def finish_kernel(columns, *refs):
    first_ref, second_ref, small_ref = refs[-3:]
    rows = first_ref.shape[0]
    values = [wide(ref[...]) for ref in refs[:-3]]
    while len(values) > 1:
        values = [first + second for first, second in zip(values[::2], values[1::2])]
    first_ref[...] = values[0][:rows, :columns]
    second_ref[...] = values[0][:rows, columns:]
    small_ref[...] = values[0][rows:]


def finish(terms, columns):
    rows, whole = terms[0].shape[0] - 8, terms[0].shape[1]
    spec = pl.BlockSpec(memory_space=VMEM)
    return pl.pallas_call(
        functools.partial(finish_kernel, columns),
        name="finish",
        out_shape=[
            jax.ShapeDtypeStruct((rows, columns), jnp.float32),
            jax.ShapeDtypeStruct((rows, whole - columns), jnp.float32),
            jax.ShapeDtypeStruct((8, whole), jnp.float32),
        ],
        in_specs=[spec] * len(terms),
        out_specs=[spec] * 3,
        compiler_params=pltpu.CompilerParams(vmem_limit_bytes=16 * 2**20),
        cost_estimate=cost(1),
    )(*terms)


def swap(value, axis, bit):
    size = lax.axis_size(axis)
    return lax.ppermute(value, axis, [(place, place ^ bit) for place in range(size)])


def bits_of(axis):
    size = lax.axis_size(axis)
    return [1 << place for place in range(size.bit_length() - 1)]


def gather_pieces(block, axis):
    pieces = [block]
    for bit in bits_of(axis):
        held = pieces[0] if len(pieces) == 1 else jnp.concatenate(pieces, axis=1)
        pieces.append(swap(held, axis, bit))
    return pieces


def scatter_pieces(pieces, axis):
    for bit in reversed(bits_of(axis)):
        sent = swap(low(pieces[-1]), axis, bit)
        kept, at, half = [], 0, sent.shape[-1] // 2
        for piece in pieces[:-1]:
            size = piece.shape[-1] // 2
            parts = (sent[..., at : at + size], sent[..., half + at : half + at + size])
            kept.append(wide(piece) + wide(jnp.concatenate(parts, axis=-1) if size < half else sent))
            at += size
        pieces = kept
    return pieces[0]


def row_blocks(*products):
    groups, sides = lax.axis_size("dp"), lax.axis_size("hid")
    width = products[0][0].shape[0]
    if sides == 2 and width % (16 * groups * sides) == 0:
        keep, send = weights(*products)
        return wide(keep) + wide(swap(send, "hid", 1))
    parts = []
    for turned, right, size, place in products:
        parts.append(times(turned[:, : right.shape[0]], right[:, place * size : place * size + size]))
    shaped = jnp.concatenate(parts, axis=1).reshape(groups // 2, 2, sides, width // (groups * sides), -1)
    odd = lax.axis_index("dp") & 1
    shaped = shaped[(lax.axis_index("dp") // 2) ^ jnp.arange(groups // 2)]
    shaped = shaped[:, odd ^ jnp.arange(2)][:, :, lax.axis_index("hid") ^ jnp.arange(sides)]
    shaped = shaped.transpose(1, 0, 2, 3, 4)
    for bit in reversed(bits_of("hid")):
        shaped = shaped[:, :, :bit] + wide(swap(low(shaped[:, :, bit:]), "hid", bit))
    return shaped[:, :, 0]


def halve(shaped):
    return low(shaped[0]), swap(low(shaped[1]), "dp", 1)


def rest_terms(kept, came):
    count = lax.axis_size("dp")
    groups = [list(range(odd, count, 2)) for odd in (0, 1)]
    total = low(wide(kept) + wide(came))
    return lax.all_to_all(total, "dp", 0, 0, axis_index_groups=groups, tiled=True)


def far_terms(blocks):
    return [blocks[0]] + [swap(block, "dp", 2 * step) for step, block in enumerate(blocks) if step > 0]


def sum_everywhere(value, axes):
    for axis in axes:
        for bit in bits_of(axis):
            value = value + swap(value, axis, bit)
    return value


def shards(tokens, big_images, norm_gain, w_qkv, qk_gains, w_out_t, w_in, w_back, cotangent):
    width = tokens.shape[1]
    size = qk_gains.shape[1]
    groups = lax.axis_size("dp")
    other = swap(cotangent, "hg", 1)
    w_in_pieces = gather_pieces(w_in, "hid")
    w_back_pieces = gather_pieces(w_back, "hid")
    normed, q_rows, k_rows, v_rows, attended, inverses = forward(
        big_images, tokens, norm_gain, w_qkv, qk_gains
    )
    part, grad_mlp, normed_t, dy_t, *grads = dense(normed, cotangent, other, w_in_pieces, w_back_pieces)
    kept, sent, do_rows = outputs(part, tokens, attended, cotangent, other, w_out_t)
    out_came = swap(sent, "hg", 1)
    mlp_kept, mlp_came = halve(scatter_pieces(grads, "hid"))
    do_rows, mlp_kept = lax.optimization_barrier((do_rows, mlp_kept))

    grad_joined, qk_part = backward(big_images, q_rows, k_rows, v_rows, do_rows, inverses, qk_gains)
    grad_joined, out_came, mlp_came = lax.optimization_barrier((grad_joined, out_came, mlp_came))
    mine, gain_part = features(0, tokens.shape[0] // FINE, grad_joined, w_qkv, grad_mlp, tokens)
    mine, mlp_came = lax.optimization_barrier((mine, mlp_came))
    came = swap(mine, "hg", 1)
    columns = attended.shape[1]

    def weight_sums(normed_t, dy_t, grad_joined, attended, gain_part, qk_part, kept, out_came):
        parts = (
            row_blocks((normed_t, grad_joined, columns, 0)),
            row_blocks((normed_t, grad_joined, columns, 1)),
            row_blocks((normed_t, grad_joined, columns, 2), (dy_t, attended, columns, 0)),
        )
        small = jnp.concatenate([gain_part[0], qk_part[0, :size], qk_part[0, LANES : LANES + size]])
        small = low(sum_everywhere(small, ("hid",)))
        small, first = lax.optimization_barrier((small, parts[0]))
        halves = [halve(part) for part in (first,) + parts[1:]]
        small = low(wide(small) + wide(swap(small, "dp", 1)))
        small = jnp.pad(small, (0, 8 * 4 * columns - small.shape[0])).reshape(1, 8, -1)
        sums = jnp.concatenate([low(wide(stays) + wide(comes)) for stays, comes in halves], axis=2)
        small = jnp.broadcast_to(small, sums.shape[:1] + small.shape[1:])
        sums = jnp.concatenate([sums, small], axis=1)
        return [sums[step] for step in range(sums.shape[0])], low(kept + wide(out_came))

    def no_sums(*operands):
        return jax.tree.map(lambda kind: jnp.zeros(kind.shape, kind.dtype), kinds)

    operands = (normed_t, dy_t, grad_joined, attended, gain_part, qk_part, kept, out_came)
    kinds = jax.eval_shape(weight_sums, *operands)
    sums, output = lax.cond(big_images[0] >= 0, weight_sums, no_sums, *operands)
    mlp_terms = rest_terms(mlp_kept, mlp_came)
    mlp_terms, came = lax.optimization_barrier((mlp_terms, came))
    hidden = mlp_terms.shape[2] // 2
    w_in_grad = jnp.sum(wide(mlp_terms[:, :, :hidden]), axis=0)
    w_back_grad = jnp.sum(wide(mlp_terms[:, :, hidden:]), axis=0)
    terms = far_terms(sums)
    token_grad = token_rows(0, mine, came, tokens, norm_gain, cotangent, other, None)
    held = (terms[1], token_grad, w_in_grad, w_back_grad)
    terms[1], token_grad, w_in_grad, w_back_grad = lax.optimization_barrier(held)
    w_qkv_grad, w_out_t_grad, small = finish(terms, 3 * columns)
    small = small[0]
    small = sum_everywhere(small, ("hg",))
    own = lax.axis_index("dp") * lax.axis_size("hid") + lax.axis_index("hid")
    gain_rows = width // (groups * lax.axis_size("hid"))
    norm_gain_grad = lax.dynamic_slice_in_dim(small, own * gain_rows, gain_rows, 0)
    qk_gains_grad = small[width : width + 2 * size].reshape(2, size)
    return (
        output,
        token_grad,
        norm_gain_grad,
        w_qkv_grad,
        qk_gains_grad,
        w_out_t_grad,
        w_in_grad,
        w_back_grad,
    )


def solution(mesh):
    return jax.shard_map(
        shards,
        mesh=mesh,
        in_specs=(
            P(("dp", "hid"), None),
            P(("dp", "hid")),
            P(),
            P(None, "hg"),
            P(),
            P(None, "hg"),
            P(None, ("hg", "hid")),
            P(None, ("hg", "hid")),
            P(("dp", "hid"), "hg"),
        ),
        out_specs=(
            P(("dp", "hid"), "hg"),
            P(("dp", "hid"), None),
            P(("dp", "hid")),
            P(("dp", "hid"), "hg"),
            P(),
            P(("dp", "hid"), "hg"),
            P("dp", ("hg", "hid")),
            P("dp", ("hg", "hid")),
        ),
        check_vma=False,
    )
```

```python
import functools
import math

import jax
import jax.numpy as jnp
from jax import lax
from jax.experimental import pallas as pl
from jax.experimental.pallas import tpu as pltpu
from jax.sharding import PartitionSpec as P

PATCHES = 196
EPSILON = 1e-06
LOG2E = math.log2(math.e)
LANES = 128
VMEM = pltpu.VMEM


def pinned(value):
    return pltpu.with_memory_space_constraint(value, pltpu.HBM)


SCALE = 1.0
ROOM = dict(forward=40, backward=24, dense=32, outputs=24, features=24, weights=24, token_rows=24)


def cost(microseconds):
    return pl.CostEstimate(
        flops=int(microseconds * SCALE * 1e9), bytes_accessed=2**20, transcendentals=0
    )


def times_t(left, right):
    return lax.dot_general(
        left, right, (((1,), (1,)), ((), ())), preferred_element_type=jnp.float32
    )


def rows_t(left, right):
    return lax.dot_general(
        left, right, (((0,), (0,)), ((), ())), preferred_element_type=jnp.float32
    )


def times(left, right):
    return jnp.dot(left, right, preferred_element_type=jnp.float32)


def low(value):
    return value.astype(jnp.bfloat16)


def wide(value):
    return value.astype(jnp.float32)


def lane_of(shape):
    return lax.broadcasted_iota(jnp.int32, shape, 1)


def row_of(shape):
    return lax.broadcasted_iota(jnp.int32, shape, 0)


def other_half(value):
    return pltpu.roll(value, LANES // 2, 1)


def spread_terms(whole):
    lane = lane_of(whole.shape)
    first = wide(low(whole))
    second = wide(low(whole - first))
    third = whole - first - second
    return jnp.where(lane == 64, first, jnp.where(lane == 65, second, jnp.where(lane == 66, third, 0.0)))


def three_terms(column, shape):
    return spread_terms(jnp.broadcast_to(column, shape))


def two_terms(value):
    first = low(value)
    return first, low(value - wide(first))


def pair_mask(block, shape, first_lane):
    start = 2 * PATCHES * block - first_lane
    place = lane_of(shape) - start
    second = row_of(shape) >= PATCHES
    begin = jnp.where(second, PATCHES, 0)
    return (place >= begin) & (place < begin + PATCHES)


def window_of(block):
    return (2 * PATCHES * block // LANES) * LANES, 4 * LANES


def forward_kernel(
    flag_ref,
    tok_hbm,
    gain_hbm,
    w_hbm,
    qk_hbm,
    normed_ref,
    q_hbm,
    k_hbm,
    v_hbm,
    att_ref,
    inv_ref,
    tok_ref,
    gain_ref,
    w_ref,
    qk_ref,
    q_ref,
    k_ref,
    v_ref,
    in_sems,
    out_sems,
):
    rows = tok_ref.shape[0]
    heads, padded, _ = q_ref.shape
    tile = 2 * PATCHES
    size = qk_ref.shape[1]
    group_a = row_of((256, 256)) // size
    group_b = lane_of((256, 256)) // size
    mean_of = low(jnp.where(group_a == group_b, 1.0 / size, 0.0))
    stride = rows // (3 * LANES) and 3 * LANES
    strip = rows - (rows // stride - 1) * stride
    strips = rows // stride
    edges = [0] + [stride * step + 32 for step in range(1, strips)] + [rows]
    token_copies = []
    for step in range(strips):
        part = pl.ds(edges[step], edges[step + 1] - edges[step])
        token_copies.append(pltpu.make_async_copy(tok_hbm.at[part], tok_ref.at[part], in_sems.at[step]))
    w_copy = pltpu.make_async_copy(w_hbm, w_ref, in_sems.at[strips])
    small_copies = [
        pltpu.make_async_copy(source, target, in_sems.at[strips + 1 + place])
        for place, (source, target) in enumerate(((gain_hbm, gain_ref), (qk_hbm, qk_ref)))
    ]
    for copy in small_copies:
        copy.start()
    token_copies[0].start()
    w_copy.start()
    for copy in token_copies[1:]:
        copy.start()
    lane = lane_of((strip, LANES))

    for copy in small_copies:
        copy.wait()
    gain = wide(gain_ref[...]).reshape(1, -1)
    q_gain = wide(qk_ref[0:1, :]) * (size**-0.5 * LOG2E)
    k_gain = wide(qk_ref[1:2, :])
    ones = jnp.ones_like(k_gain)
    gains = jnp.concatenate([q_gain, k_gain, ones, q_gain, k_gain, ones], axis=1)
    is_value = jnp.concatenate([0 * ones, 0 * ones, ones, 0 * ones, 0 * ones, ones], axis=1)

    def project(step, _):
        for place, copy in enumerate(token_copies):
            pl.when(step == place)(copy.wait)
        here = pl.ds(pl.multiple_of(step * stride, LANES), strip)
        x = wide(tok_ref[here, :])
        x = x - jnp.mean(x, axis=1, keepdims=True)
        x = x * lax.rsqrt(jnp.mean(x * x, axis=1, keepdims=True) + EPSILON)
        normed = low(x * gain)
        normed_ref[here, :] = normed
        every = times(normed, w_ref[...])
        for pair in range(heads // 2):
            joined = every[:, 384 * pair : 384 * pair + 384]
            parts = []
            for at in (0, 256):
                wid = min(256, 384 - at)
                block = joined[:, at : at + wid]
                means = mean_of[:wid, :wid]
                centred = block - times(low(block), means)
                squares = low(centred * centred)
                variance = times(squares, means)
                inverse = lax.rsqrt(variance + EPSILON)
                inv_ref[here, 384 * pair + at : 384 * pair + at + wid] = low(inverse)
                hat = centred * inverse
                parts.append(
                    jnp.where(is_value[:, at : at + wid] > 0, block, hat * gains[:, at : at + wid])
                )
            b0, b1, b2 = parts[0][:, :128], parts[0][:, 128:], parts[1]
            first = lane < 64
            unit = jnp.where(lane < 67, 1.0, 0.0)
            q_ref[2 * pair, here, :] = low(jnp.where(first, b0, 0.0))
            k_ref[2 * pair, here, :] = low(jnp.where(first, other_half(b0), unit))
            v_ref[2 * pair, here, :] = low(jnp.where(first, b1, unit))
            q_ref[2 * pair + 1, here, :] = low(jnp.where(first, other_half(b1), 0.0))
            k_ref[2 * pair + 1, here, :] = low(jnp.where(first, b2, unit))
            v_ref[2 * pair + 1, here, :] = low(jnp.where(first, other_half(b2), unit))
        return 0

    w_copy.wait()
    lax.fori_loop(0, strips, project, 0)
    lane = lane_of((tile, LANES))
    for ref in (q_ref, k_ref, v_ref):
        ref[:, rows:, :] = jnp.zeros((heads, padded - rows, LANES), jnp.bfloat16)
    key_copy = pltpu.make_async_copy(k_ref, k_hbm, out_sems.at[0])
    value_copy = pltpu.make_async_copy(v_ref, v_hbm, out_sems.at[1])
    key_copy.start()
    value_copy.start()

    def query_copy(pair):
        part = pl.ds(2 * pair, 2)
        return pltpu.make_async_copy(q_ref.at[part], q_hbm.at[part], out_sems.at[2 + pair])

    def attend(pair, _, big):
        for start in range(0, rows, tile):
            here = slice(start, start + tile)
            if big:
                keys = slice(0, padded)
            else:
                begin, length = window_of(start // tile)
                keys = slice(begin, begin + length)
            found = []
            for side in range(2):
                head = 2 * pair + side
                queries = q_ref[head, here, :]
                scores = times_t(queries, k_ref[head, keys, :])
                if not big:
                    scores = jnp.where(
                        pair_mask(start // tile, scores.shape, keys.start), scores, -1e30
                    )
                expo = low(jnp.exp2(scores))
                out = times(expo, v_ref[head, keys, :])
                total = out[:, 64:65]
                found.append(out * (1.0 / total))
                log_total = jnp.log(total) * (-LOG2E)
                q_ref[head, here, :] = low(
                    jnp.where(lane < 64, wide(queries), three_terms(log_total, lane.shape))
                )
            att_ref[here, pl.ds(pl.multiple_of(pair * LANES, LANES), LANES)] = low(
                jnp.where(lane < 64, found[0], other_half(found[1]))
            )
        query_copy(pair).start()
        return 0

    @pl.when(flag_ref[0] > 0)
    def _():
        lax.fori_loop(0, heads // 2, functools.partial(attend, big=True), 0)

    @pl.when(flag_ref[0] <= 0)
    def _():
        lax.fori_loop(0, heads // 2, functools.partial(attend, big=False), 0)

    key_copy.wait()
    value_copy.wait()
    for pair in range(heads // 2):
        query_copy(pair).wait()


def forward(big_images, tokens, norm_gain, w_qkv, qk_gains):
    rows, width = tokens.shape
    size = qk_gains.shape[1]
    heads = w_qkv.shape[1] // (3 * size)
    padded = -(-rows // 256) * 256
    whole = pl.BlockSpec(memory_space=VMEM)
    hbm = pl.BlockSpec(memory_space=pltpu.HBM)
    held = VMEM((heads, padded, LANES), jnp.bfloat16)
    head_rows = pltpu.HBM((heads, padded, LANES), jnp.bfloat16)
    return pl.pallas_call(
        forward_kernel,
        name="forward",
        out_shape=[
            jax.ShapeDtypeStruct((rows, width), jnp.bfloat16),
            head_rows,
            head_rows,
            head_rows,
            jax.ShapeDtypeStruct((rows, heads * size), jnp.bfloat16),
            pltpu.HBM((rows, w_qkv.shape[1]), jnp.bfloat16),
        ],
        in_specs=[pl.BlockSpec(memory_space=pltpu.SMEM)] + [hbm] * 4,
        out_specs=[whole, hbm, hbm, hbm, whole, whole],
        scratch_shapes=[
            VMEM((rows, width), jnp.bfloat16),
            VMEM(norm_gain.shape, jnp.bfloat16),
            VMEM(w_qkv.shape, jnp.bfloat16),
            VMEM(qk_gains.shape, jnp.bfloat16),
            held,
            held,
            held,
            pltpu.SemaphoreType.DMA((rows // (3 * LANES) + 3,)),
            pltpu.SemaphoreType.DMA((2 + heads // 2,)),
        ],
        compiler_params=pltpu.CompilerParams(vmem_limit_bytes=ROOM["forward"] * 2**20),
        cost_estimate=cost(24),
    )(big_images, pinned(tokens), pinned(norm_gain), pinned(w_qkv), pinned(qk_gains))


def backward_kernel(
    flag_ref, q_ref, k_ref, v_ref, do_ref, inv_ref, qk_ref, joined_ref, small_ref, dq_ref, dk_ref, dv_ref, turned_ref
):
    pair = pl.program_id(0)
    rows = inv_ref.shape[0]
    padded = q_ref.shape[1]
    tile = 2 * PATCHES
    size = qk_ref.shape[1]
    scale = size**-0.5
    zeros = jnp.zeros((1, LANES - size), jnp.float32)
    q_gain = wide(qk_ref[0:1, :])
    k_gain = wide(qk_ref[1:2, :])
    q_back = jnp.concatenate([1.0 / (q_gain * (scale * LOG2E)), zeros], axis=1)
    k_back = jnp.concatenate([1.0 / k_gain, zeros], axis=1)
    q_gain = jnp.concatenate([q_gain, zeros], axis=1)
    k_gain = jnp.concatenate([k_gain, zeros], axis=1)

    def attend(side, _, big):
        for start in range(0, rows, rows if big else tile):
            here = slice(start, start + (rows if big else tile))
            if big:
                over = slice(0, padded)
            else:
                begin, length = window_of(start // tile)
                over = slice(begin, begin + length)
            keys = k_ref[side, here, :]
            queries = q_ref[side, over, :]
            grads = do_ref[side, over, :]
            scores = times_t(keys, queries)
            if not big:
                scores = jnp.where(pair_mask(start // tile, scores.shape, over.start), scores, -1e30)
            probs = jnp.exp2(scores)
            grad_probs = times_t(v_ref[side, here, :], grads)
            grad_scores = low(probs * grad_probs)
            dv_ref[side, here, :] = times(low(probs), grads)
            dk_ref[side, here, :] = times(grad_scores, queries)
            more = rows_t(keys, grad_scores)
            if big and start == 0:
                dq_ref[side, :, over] = more
            elif big:
                dq_ref[side, :, over] += more
            else:
                place = lane_of(more.shape) - (start - over.start)
                dq_ref[side, :, over] = jnp.where(
                    (place >= 0) & (place < tile), more, dq_ref[side, :, over]
                )
        return 0

    @pl.when(flag_ref[0] > 0)
    def _():
        lax.fori_loop(0, 2, functools.partial(attend, big=True), 0)

    @pl.when(flag_ref[0] <= 0)
    def _():
        lax.fori_loop(0, 2, functools.partial(attend, big=False), 0)

    @pl.when(pair == 0)
    def _():
        small_ref[...] = jnp.zeros_like(small_ref)

    lane = lane_of((tile, LANES))
    first = lane < 64
    shape = (2 * LANES, 2 * LANES)
    row, column = row_of(shape), lane_of(shape)
    means = (row // LANES == column // LANES) & (row % LANES < size)
    means = low(jnp.where(means, 1.0 / size, 0.0))
    gains = jnp.concatenate([q_gain * scale, k_gain * math.log(2.0)], axis=1)
    factors = jnp.concatenate([jnp.full_like(q_gain, scale), jnp.full_like(k_gain, math.log(2.0))], axis=1)
    backs = jnp.concatenate([q_back, k_back], axis=1)
    for side in range(2):
        turned_ref[side] = dq_ref[side].T
    for start in range(0, rows, tile):
        here = slice(start, start + tile)
        inv0, inv1, inv2 = (wide(inv_ref[here, at : at + LANES]) for at in range(0, 3 * LANES, LANES))
        inverses = (inv0, other_half(inv0)), (other_half(inv1), inv2)
        blocks = []
        for side in range(2):
            inverse = jnp.concatenate(inverses[side], axis=1)
            hat = jnp.concatenate([q_ref[side, here, :], k_ref[side, here, :]], axis=1)
            hat = wide(hat) * backs
            grad = jnp.concatenate([turned_ref[side, here, :], dk_ref[side, here, :]], axis=1)
            small_ref[0:1, :] += jnp.sum(grad * hat, axis=0, keepdims=True) * factors
            grad = grad * gains
            inner = times(low(grad * hat), means)
            grad = inverse * (grad - times(low(grad), means) - hat * inner)
            blocks.append((grad[:, :LANES], grad[:, LANES:], dv_ref[side, here, :]))
        (q0, k0, v0), (q1, k1, v1) = blocks
        joined_ref[here, 0:128] = low(jnp.where(first, q0, other_half(k0)))
        joined_ref[here, 128:256] = low(jnp.where(first, v0, other_half(q1)))
        joined_ref[here, 256:384] = low(jnp.where(first, k1, other_half(v1)))


def backward(big_images, q_rows, k_rows, v_rows, do_rows, inverses, qk_gains):
    heads, padded, _ = q_rows.shape
    rows = inverses.shape[0]
    pair_spec = pl.BlockSpec((2, padded, LANES), lambda pair: (pair, 0, 0))
    return pl.pallas_call(
        backward_kernel,
        name="backward",
        grid=(heads // 2,),
        out_shape=[
            jax.ShapeDtypeStruct((rows, heads * 3 * LANES // 2), jnp.bfloat16),
            jax.ShapeDtypeStruct((8, 2 * LANES), jnp.float32),
        ],
        in_specs=[pl.BlockSpec(memory_space=pltpu.SMEM)]
        + [pair_spec] * 4
        + [pl.BlockSpec((rows, 3 * LANES), lambda pair: (0, pair)), pl.BlockSpec(qk_gains.shape, lambda pair: (0, 0))],
        out_specs=[
            pl.BlockSpec((rows, 3 * LANES), lambda pair: (0, pair)),
            pl.BlockSpec((8, 2 * LANES), lambda pair: (0, 0)),
        ],
        scratch_shapes=[
            VMEM((2, LANES, padded), jnp.float32),
            VMEM((2, rows, LANES), jnp.float32),
            VMEM((2, rows, LANES), jnp.float32),
            VMEM((2, padded, LANES), jnp.float32),
        ],
        compiler_params=pltpu.CompilerParams(vmem_limit_bytes=ROOM["backward"] * 2**20),
        cost_estimate=cost(36),
    )(big_images, pinned(q_rows), pinned(k_rows), pinned(v_rows), do_rows, pinned(inverses), qk_gains)


FINE = 2 * PATCHES


def in_order(mine, other):
    first = lax.axis_index("hg") == 0
    return jnp.where(first, mine, other), jnp.where(first, other, mine)


def dense_kernel(count, tiles, normed_ref, mine_ref, other_ref, *refs):
    w_in_refs, w_back_refs = refs[:count], refs[count : 2 * count]
    refs = refs[2 * count :]
    part_ref, grad_ref, normed_t_ref, dy_t_ref = refs[:4]
    grad_refs, refs = refs[4 : 4 + count], refs[4 + count :]
    normed_rows, dy_rows = refs[:2]
    act_refs, gup_refs = refs[2 : 2 + count], refs[2 + count :]
    step = pl.program_id(0)
    half = mine_ref.shape[1]
    curve = math.sqrt(2.0 / math.pi)
    normed = normed_ref[...]
    dy_rows[step, :, :half], dy_rows[step, :, half:] = in_order(mine_ref[...], other_ref[...])
    dy = dy_rows[step]
    normed_rows[step] = normed
    for w_in_ref, w_back_ref, act_ref, gup_ref in zip(w_in_refs, w_back_refs, act_refs, gup_refs):
        columns = w_in_ref.shape[1]
        width = min(256, columns)
        for at in range(0, columns, width):
            cols = slice(at, min(at + width, columns))
            up = times(normed, w_in_ref[:, cols])
            grad_act = times(dy, w_back_ref[:, cols])
            square = up * up
            bent = jnp.tanh(up * (curve + (curve * 0.044715) * square))
            gate = 0.5 + 0.5 * bent
            act = up * gate
            slope = gate + act * ((1.0 - gate) * (2 * curve + (6 * curve * 0.044715) * square))
            act_ref[step, :, cols] = low(act)
            gup_ref[step, :, cols] = low(grad_act * slope)
    total, grad = None, None
    for act_ref, w_back_ref, gup_ref, w_in_ref in zip(act_refs, w_back_refs, gup_refs, w_in_refs):
        part = times_t(act_ref[step], w_back_ref[...])
        total = part if total is None else total + part
        part = times_t(gup_ref[step], w_in_ref[...])
        grad = part if grad is None else grad + part
    part_ref[...] = total
    grad_ref[...] = low(grad)

    @pl.when(step == tiles - 1)
    def _():
        rows, width = tiles * normed_rows.shape[1], normed_rows.shape[2]
        for source, turned in ((normed_rows, normed_t_ref), (dy_rows, dy_t_ref)):
            turned[:, :rows] = source[...].reshape(rows, width).T
            turned[:, rows:] = jnp.zeros((width, turned.shape[1] - rows), jnp.bfloat16)
        for act_ref, gup_ref, ref in zip(act_refs, gup_refs, grad_refs):
            columns = act_ref.shape[2]
            for turned, right, at in ((normed_t_ref, gup_ref, 0), (dy_t_ref, act_ref, columns)):
                total = times(turned[:, :rows], right[...].reshape(rows, columns))
                by_parity(total, ref, slice(at, at + columns))


def by_parity(total, ref, cols):
    halves, rows = ref.shape[1:3]
    odd = lax.axis_index("dp") & 1
    for half in range(halves):
        for side in range(2):
            start = (2 * half + side) * rows
            ref[odd ^ side, half, :, cols] = total[start : start + rows].astype(ref.dtype)


def dense(normed, mine, other, w_in_pieces, w_back_pieces):
    rows, width = normed.shape
    tile = 2 * PATCHES
    tiles = rows // tile
    count = len(w_in_pieces)
    shape = jax.ShapeDtypeStruct
    sizes = [piece.shape[1] for piece in w_in_pieces]
    groups = lax.axis_size("dp")
    padded = -(-rows // 256) * 256
    row_tile = lambda columns: pl.BlockSpec((tile, columns), lambda step: (step, 0))
    turned = pl.BlockSpec((width, padded), lambda step: (0, 0))
    once = lambda columns: pl.BlockSpec((width, columns), lambda step: (0, 0), pipeline_mode=pl.Buffered(1))
    return pl.pallas_call(
        functools.partial(dense_kernel, count, tiles),
        name="dense",
        grid=(tiles,),
        out_shape=[
            shape((rows, width), jnp.float32),
            shape((rows, width), jnp.bfloat16),
            shape((width, padded), jnp.bfloat16),
            shape((width, padded), jnp.bfloat16),
        ]
        + [shape((2, groups // 2, width // groups, 2 * size), jnp.bfloat16) for size in sizes],
        in_specs=[row_tile(width), row_tile(width // 2), row_tile(width // 2)]
        + [once(size) for size in sizes] * 2,
        out_specs=[row_tile(width)] * 2
        + [turned] * 2
        + [
            pl.BlockSpec((2, groups // 2, width // groups, 2 * size), lambda step: (0, 0, 0, 0))
            for size in sizes
        ],
        scratch_shapes=[VMEM((tiles, tile, width), jnp.bfloat16)] * 2
        + [VMEM((tiles, tile, size), jnp.bfloat16) for size in sizes] * 2,
        compiler_params=pltpu.CompilerParams(vmem_limit_bytes=ROOM["dense"] * 2**20),
        cost_estimate=cost(24),
    )(normed, mine, other, *w_in_pieces, *w_back_pieces)


def outputs_kernel(part_ref, tok_ref, att_ref, mine_ref, other_ref, w_out_ref, keep_ref, send_ref, do_ref):
    tile, width = part_ref.shape
    half = width // 2
    heads, padded, _ = do_ref.shape
    lane = lane_of((tile, LANES))
    attended = att_ref[...]
    left = times_t(attended, w_out_ref[...]) + part_ref[...]
    token = tok_ref[...]
    keep, send = in_order(left[:, :half], left[:, half:])
    keep_ref[...] = keep + in_order(wide(token[:, :half]), wide(token[:, half:]))[0]
    send_ref[...] = low(send)
    first, second = in_order(mine_ref[...], other_ref[...])
    grad_att = times(first, w_out_ref[:half, :]) + times(second, w_out_ref[half:, :])
    shape = (LANES, 2 * LANES)
    row, column = row_of(shape), lane_of(shape)
    inners = (row // 64 == column // LANES) & (column % LANES >= 64) & (column % LANES < 67)
    inners = low(jnp.where(inners, -1.0, 0.0))
    found = []
    for pair in range(heads // 2):
        cols = slice(pair * LANES, pair * LANES + LANES)
        low_block = wide(low(grad_att[:, cols]))
        weighed, rest = two_terms(low_block * wide(attended[:, cols]))
        inner = times(weighed, inners) + times(rest, inners)
        for side in range(2):
            value = low_block if side == 0 else other_half(low_block)
            term = spread_terms(inner[:, side * LANES : (side + 1) * LANES])
            found.append(low(jnp.where(lane < 64, value, term)))
    for step in range(3):

        @pl.when(pl.program_id(0) == step)
        def _(step=step):
            for head in range(heads):
                do_ref[head, step * tile : (step + 1) * tile, :] = found[head]
            if step == 2:
                do_ref[:, 3 * tile :, :] = jnp.zeros((heads, padded - 3 * tile, LANES), jnp.bfloat16)


def outputs(part, tokens, attended, mine, other, w_out_t):
    rows, width = tokens.shape
    tile = 2 * PATCHES
    heads = w_out_t.shape[1] // 64
    padded = -(-rows // 256) * 256
    shape = jax.ShapeDtypeStruct
    row_tile = lambda columns: pl.BlockSpec((tile, columns), lambda step: (step, 0))
    return pl.pallas_call(
        outputs_kernel,
        name="outputs",
        grid=(rows // tile,),
        out_shape=[
            shape((rows, width // 2), jnp.float32),
            shape((rows, width // 2), jnp.bfloat16),
            shape((heads, padded, LANES), jnp.bfloat16),
        ],
        in_specs=[row_tile(columns) for columns in (width, width, width // 2, width // 2, width // 2)]
        + [pl.BlockSpec(w_out_t.shape, lambda step: (0, 0))],
        out_specs=[
            row_tile(width // 2),
            row_tile(width // 2),
            pl.BlockSpec((heads, padded, LANES), lambda step: (0, 0, 0)),
        ],
        compiler_params=pltpu.CompilerParams(vmem_limit_bytes=ROOM["outputs"] * 2**20),
        cost_estimate=cost(6),
    )(part, tokens, attended, mine, other, w_out_t)


def features_kernel(joined_ref, w_ref, mlp_ref, tok_ref, sent_ref, gain_ref):
    grad = times_t(joined_ref[...], w_ref[...]) + wide(mlp_ref[...])
    sent_ref[...] = low(grad)
    x = wide(tok_ref[...])
    x = x - jnp.mean(x, axis=1, keepdims=True)
    x = x * lax.rsqrt(jnp.mean(x * x, axis=1, keepdims=True) + EPSILON)

    @pl.when(pl.program_id(0) == 0)
    def _():
        gain_ref[...] = jnp.zeros_like(gain_ref)

    gain_ref[0:1, :] += jnp.sum(grad * x, axis=0, keepdims=True)


def features(first, count, grad_joined, w_qkv, grad_mlp, tokens):
    rows, width = tokens.shape
    tile = FINE
    row_tile = lambda columns: pl.BlockSpec((tile, columns), lambda step: (step + first, 0))
    return pl.pallas_call(
        features_kernel,
        name="features",
        grid=(count,),
        out_shape=[
            pltpu.HBM((tile * count, width), jnp.bfloat16),
            jax.ShapeDtypeStruct((8, width), jnp.float32),
        ],
        in_specs=[
            row_tile(grad_joined.shape[1]),
            pl.BlockSpec(w_qkv.shape, lambda step: (0, 0)),
            row_tile(width),
            row_tile(width),
        ],
        out_specs=[
            pl.BlockSpec((tile, width), lambda step: (step, 0)),
            pl.BlockSpec((8, width), lambda step: (0, 0)),
        ],
        compiler_params=pltpu.CompilerParams(vmem_limit_bytes=ROOM["features"] * 2**20),
        cost_estimate=cost(0.3 * count),
    )(grad_joined, w_qkv, grad_mlp, tokens)


def weights_kernel(*refs):
    keep_ref, send_ref = refs[-2:]
    halves, rows = keep_ref.shape[1:3]
    odd, far, side = lax.axis_index("dp") & 1, lax.axis_index("dp") // 2, lax.axis_index("hid")
    at = 0
    for left_ref, right_ref in zip(refs[:-2:2], refs[1:-2:2]):
        tokens, columns = right_ref.shape
        total = times(left_ref[:, :tokens], right_ref[...])
        cols = slice(at, at + columns)
        at += columns
        for half in range(halves):
            for parity in range(2):
                start = 2 * (2 * half + parity) * rows
                even, uneven = total[start : start + rows], total[start + rows : start + 2 * rows]
                keep_ref[odd ^ parity, far ^ half, :, cols] = low(jnp.where(side == 0, even, uneven))
                send_ref[odd ^ parity, far ^ half, :, cols] = low(jnp.where(side == 0, uneven, even))


def weights(*products):
    groups = lax.axis_size("dp")
    columns = sum(size for _, _, size, _ in products)
    shape = (2, groups // 2, products[0][0].shape[0] // (2 * groups), columns)
    whole = lambda shape: pl.BlockSpec(shape, lambda step: (0,) * len(shape))
    specs, operands = [], []
    for turned, right, size, place in products:
        specs += [
            whole(turned.shape),
            pl.BlockSpec((right.shape[0], size), lambda step, place=place: (0, place)),
        ]
        operands += [turned, right]
    return pl.pallas_call(
        weights_kernel,
        name="weights",
        grid=(1,),
        out_shape=[jax.ShapeDtypeStruct(shape, jnp.bfloat16)] * 2,
        in_specs=specs,
        out_specs=[whole(shape)] * 2,
        compiler_params=pltpu.CompilerParams(vmem_limit_bytes=ROOM["weights"] * 2**20),
        cost_estimate=cost(3),
    )(*operands)


def tokens_kernel(sent_ref, came_ref, tok_ref, gain_ref, mine_ref, other_ref, *refs):
    out_ref = refs[-1]
    half = mine_ref.shape[1]
    grad = (wide(sent_ref[...]) + wide(came_ref[...])) * wide(gain_ref[...]).reshape(1, -1)
    x = wide(tok_ref[...])
    x = x - jnp.mean(x, axis=1, keepdims=True)
    inverse = lax.rsqrt(jnp.mean(x * x, axis=1, keepdims=True) + EPSILON)
    x = x * inverse
    inner = jnp.mean(grad * x, axis=1, keepdims=True)
    grad = inverse * (grad - jnp.mean(grad, axis=1, keepdims=True) - x * inner)
    first, second = in_order(wide(mine_ref[...]), wide(other_ref[...]))
    out_ref[:, :half] = low(grad[:, :half] + first)
    out_ref[:, half:] = low(grad[:, half:] + second)


def token_rows(first, sent, came, tokens, norm_gain, mine, other, before):
    rows, width = tokens.shape
    tile = FINE
    count = sent.shape[0] // tile
    near = lambda columns: pl.BlockSpec((tile, columns), lambda step: (step, 0))
    far = lambda columns: pl.BlockSpec((tile, columns), lambda step: (step + first, 0))
    more = [] if before is None else [before]
    return pl.pallas_call(
        tokens_kernel,
        name="token_rows",
        grid=(count,),
        out_shape=jax.ShapeDtypeStruct((rows, width), jnp.bfloat16),
        in_specs=[
            near(width),
            near(width),
            far(width),
            pl.BlockSpec((width,), lambda step: (0,)),
            far(width // 2),
            far(width // 2),
        ]
        + [pl.BlockSpec(memory_space=pl.ANY)] * len(more),
        out_specs=far(width),
        input_output_aliases={6: 0} if more else {},
        compiler_params=pltpu.CompilerParams(vmem_limit_bytes=ROOM["token_rows"] * 2**20),
        cost_estimate=cost(0.3 * count),
    )(pinned(sent), came, tokens, norm_gain, mine, other, *more)


def finish_kernel(columns, *refs):
    first_ref, second_ref, small_ref = refs[-3:]
    rows = first_ref.shape[0]
    values = [wide(ref[...]) for ref in refs[:-3]]
    while len(values) > 1:
        values = [first + second for first, second in zip(values[::2], values[1::2])]
    first_ref[...] = values[0][:rows, :columns]
    second_ref[...] = values[0][:rows, columns:]
    small_ref[...] = values[0][rows:]


def finish(terms, columns):
    rows, whole = terms[0].shape[0] - 8, terms[0].shape[1]
    spec = pl.BlockSpec(memory_space=VMEM)
    return pl.pallas_call(
        functools.partial(finish_kernel, columns),
        name="finish",
        out_shape=[
            jax.ShapeDtypeStruct((rows, columns), jnp.float32),
            jax.ShapeDtypeStruct((rows, whole - columns), jnp.float32),
            jax.ShapeDtypeStruct((8, whole), jnp.float32),
        ],
        in_specs=[spec] * len(terms),
        out_specs=[spec] * 3,
        compiler_params=pltpu.CompilerParams(vmem_limit_bytes=16 * 2**20),
        cost_estimate=cost(1),
    )(*terms)


def swap(value, axis, bit):
    size = lax.axis_size(axis)
    return lax.ppermute(value, axis, [(place, place ^ bit) for place in range(size)])


def bits_of(axis):
    size = lax.axis_size(axis)
    return [1 << place for place in range(size.bit_length() - 1)]


def gather_pieces(block, axis):
    pieces = [block]
    for bit in bits_of(axis):
        held = pieces[0] if len(pieces) == 1 else jnp.concatenate(pieces, axis=1)
        pieces.append(swap(held, axis, bit))
    return pieces


def scatter_pieces(pieces, axis):
    for bit in reversed(bits_of(axis)):
        sent = swap(low(pieces[-1]), axis, bit)
        kept, at, half = [], 0, sent.shape[-1] // 2
        for piece in pieces[:-1]:
            size = piece.shape[-1] // 2
            parts = (sent[..., at : at + size], sent[..., half + at : half + at + size])
            kept.append(wide(piece) + wide(jnp.concatenate(parts, axis=-1) if size < half else sent))
            at += size
        pieces = kept
    return pieces[0]


def row_blocks(*products):
    groups, sides = lax.axis_size("dp"), lax.axis_size("hid")
    width = products[0][0].shape[0]
    if sides == 2 and width % (16 * groups * sides) == 0:
        keep, send = weights(*products)
        return wide(keep) + wide(swap(send, "hid", 1))
    parts = []
    for turned, right, size, place in products:
        parts.append(times(turned[:, : right.shape[0]], right[:, place * size : place * size + size]))
    shaped = jnp.concatenate(parts, axis=1).reshape(groups // 2, 2, sides, width // (groups * sides), -1)
    odd = lax.axis_index("dp") & 1
    shaped = shaped[(lax.axis_index("dp") // 2) ^ jnp.arange(groups // 2)]
    shaped = shaped[:, odd ^ jnp.arange(2)][:, :, lax.axis_index("hid") ^ jnp.arange(sides)]
    shaped = shaped.transpose(1, 0, 2, 3, 4)
    for bit in reversed(bits_of("hid")):
        shaped = shaped[:, :, :bit] + wide(swap(low(shaped[:, :, bit:]), "hid", bit))
    return shaped[:, :, 0]


def halve(shaped):
    return low(shaped[0]), swap(low(shaped[1]), "dp", 1)


def rest_terms(kept, came):
    count = lax.axis_size("dp")
    groups = [list(range(odd, count, 2)) for odd in (0, 1)]
    total = low(wide(kept) + wide(came))
    return lax.all_to_all(total, "dp", 0, 0, axis_index_groups=groups, tiled=True)


def far_terms(blocks):
    return [blocks[0]] + [swap(block, "dp", 2 * step) for step, block in enumerate(blocks) if step > 0]


def sum_everywhere(value, axes):
    for axis in axes:
        for bit in bits_of(axis):
            value = value + swap(value, axis, bit)
    return value


def shards(tokens, big_images, norm_gain, w_qkv, qk_gains, w_out_t, w_in, w_back, cotangent):
    width = tokens.shape[1]
    size = qk_gains.shape[1]
    groups = lax.axis_size("dp")
    other = swap(cotangent, "hg", 1)
    w_in_pieces = gather_pieces(w_in, "hid")
    w_back_pieces = gather_pieces(w_back, "hid")
    normed, q_rows, k_rows, v_rows, attended, inverses = forward(
        big_images, tokens, norm_gain, w_qkv, qk_gains
    )
    part, grad_mlp, normed_t, dy_t, *grads = dense(normed, cotangent, other, w_in_pieces, w_back_pieces)
    kept, sent, do_rows = outputs(part, tokens, attended, cotangent, other, w_out_t)
    out_came = swap(sent, "hg", 1)
    mlp_kept, mlp_came = halve(scatter_pieces(grads, "hid"))
    do_rows, mlp_kept = lax.optimization_barrier((do_rows, mlp_kept))

    grad_joined, qk_part = backward(big_images, q_rows, k_rows, v_rows, do_rows, inverses, qk_gains)
    grad_joined, out_came, mlp_came = lax.optimization_barrier((grad_joined, out_came, mlp_came))
    mine, gain_part = features(0, tokens.shape[0] // FINE, grad_joined, w_qkv, grad_mlp, tokens)
    mine, mlp_came = lax.optimization_barrier((mine, mlp_came))
    came = swap(mine, "hg", 1)
    columns = attended.shape[1]

    def weight_sums(normed_t, dy_t, grad_joined, attended, gain_part, qk_part, kept, out_came):
        parts = (
            row_blocks((normed_t, grad_joined, columns, 0)),
            row_blocks((normed_t, grad_joined, columns, 1)),
            row_blocks((normed_t, grad_joined, columns, 2), (dy_t, attended, columns, 0)),
        )
        small = jnp.concatenate([gain_part[0], qk_part[0, :size], qk_part[0, LANES : LANES + size]])
        small = low(sum_everywhere(small, ("hid",)))
        small, first = lax.optimization_barrier((small, parts[0]))
        halves = [halve(part) for part in (first,) + parts[1:]]
        small = low(wide(small) + wide(swap(small, "dp", 1)))
        small = jnp.pad(small, (0, 8 * 4 * columns - small.shape[0])).reshape(1, 8, -1)
        sums = jnp.concatenate([low(wide(stays) + wide(comes)) for stays, comes in halves], axis=2)
        small = jnp.broadcast_to(small, sums.shape[:1] + small.shape[1:])
        sums = jnp.concatenate([sums, small], axis=1)
        return [sums[step] for step in range(sums.shape[0])], low(kept + wide(out_came))

    def no_sums(*operands):
        return jax.tree.map(lambda kind: jnp.zeros(kind.shape, kind.dtype), kinds)

    operands = (normed_t, dy_t, grad_joined, attended, gain_part, qk_part, kept, out_came)
    kinds = jax.eval_shape(weight_sums, *operands)
    sums, output = lax.cond(big_images[0] >= 0, weight_sums, no_sums, *operands)
    mlp_terms = rest_terms(mlp_kept, mlp_came)
    hidden = mlp_terms.shape[2] // 2
    w_in_grad = jnp.sum(wide(mlp_terms[:, :, :hidden]), axis=0)
    w_back_grad = jnp.sum(wide(mlp_terms[:, :, hidden:]), axis=0)
    terms = far_terms(sums)
    token_grad = token_rows(0, mine, came, tokens, norm_gain, cotangent, other, None)
    held = (terms[1], token_grad, w_in_grad, w_back_grad)
    terms[1], token_grad, w_in_grad, w_back_grad = lax.optimization_barrier(held)
    w_qkv_grad, w_out_t_grad, small = finish(terms, 3 * columns)
    small = small[0]
    small = sum_everywhere(small, ("hg",))
    own = lax.axis_index("dp") * lax.axis_size("hid") + lax.axis_index("hid")
    gain_rows = width // (groups * lax.axis_size("hid"))
    norm_gain_grad = lax.dynamic_slice_in_dim(small, own * gain_rows, gain_rows, 0)
    qk_gains_grad = small[width : width + 2 * size].reshape(2, size)
    return (
        output,
        token_grad,
        norm_gain_grad,
        w_qkv_grad,
        qk_gains_grad,
        w_out_t_grad,
        w_in_grad,
        w_back_grad,
    )


def solution(mesh):
    return jax.shard_map(
        shards,
        mesh=mesh,
        in_specs=(
            P(("dp", "hid"), None),
            P(("dp", "hid")),
            P(),
            P(None, "hg"),
            P(),
            P(None, "hg"),
            P(None, ("hg", "hid")),
            P(None, ("hg", "hid")),
            P(("dp", "hid"), "hg"),
        ),
        out_specs=(
            P(("dp", "hid"), "hg"),
            P(("dp", "hid"), None),
            P(("dp", "hid")),
            P(("dp", "hid"), "hg"),
            P(),
            P(("dp", "hid"), "hg"),
            P("dp", ("hg", "hid")),
            P("dp", ("hg", "hid")),
        ),
        check_vma=False,
    )
```
